32 devices in a mesh: client: 8 (over z, y), tensor: 4 (over x, core).
Axes of the slice: x: 2, y: 2, z: 4, core: 2. Of those that a mesh axis runs over, the one named last changes fastest.
Arguments:
- pool: bfloat16 [256, 196, 768], P('client'), may hold values from -6 to 6
- index: int32 [8, 4, 4], P('client'), may hold values from 0 to 31
- tau: int32 [8], P('client'), may hold values from 1 to 4, as said below
- counts: int32 [8], P('client'), may hold values from 100 to 999
- labels: int32 [256], P('client'), may hold values from 0 to 99
- in_bf: bfloat16 [7, 768, 768], P(None, 'client', 'tensor'), may hold values from -0.21875 to 0.21875
- out_bf: bfloat16 [5, 768, 768], P(None, 'tensor', 'client'), as said below
- table_bf: bfloat16 [1074, 768], P(None, 'client'), as said below
- bias_bf: bfloat16 [4, 768], P(None, 'tensor'), may hold values from -3 to 3
- in_master: float32 [7, 768, 768], P(None, 'client', 'tensor'), may hold values from -0.21875 to 0.21875
- out_master: float32 [5, 768, 768], P(None, 'tensor', 'client'), as said below
- table_master: float32 [1074, 768], P(None, 'client'), as said below
- bias_master: float32 [4, 768], P(None, 'tensor'), may hold values from -3 to 3
- in_first: float32 [7, 768, 768], P(None, 'client', 'tensor')
- out_first: float32 [5, 768, 768], P(None, 'tensor', 'client')
- table_first: float32 [1074, 768], P(None, 'client')
- bias_first: float32 [4, 768], P(None, 'tensor')
- in_second: float32 [7, 768, 768], P(None, 'client', 'tensor'), as said below
- out_second: float32 [5, 768, 768], P(None, 'tensor', 'client'), as said below
- table_second: float32 [1074, 768], P(None, 'client'), as said below
- bias_second: float32 [4, 768], P(None, 'tensor'), as said below
Outputs:
- loss: float32 [], replicated
- clip_norms: float32 [8, 4], P('client')
- new_in_master: float32 [7, 768, 768], P(None, 'client', 'tensor')
- new_out_master: float32 [5, 768, 768], P(None, 'tensor', 'client')
- new_table_master: float32 [1074, 768], P(None, 'client')
- new_bias_master: float32 [4, 768], P(None, 'tensor')
- new_in_first: float32 [7, 768, 768], P(None, 'client', 'tensor')
- new_out_first: float32 [5, 768, 768], P(None, 'tensor', 'client')
- new_table_first: float32 [1074, 768], P(None, 'client')
- new_bias_first: float32 [4, 768], P(None, 'tensor')
- new_in_second: float32 [7, 768, 768], P(None, 'client', 'tensor')
- new_out_second: float32 [5, 768, 768], P(None, 'tensor', 'client')
- new_table_second: float32 [1074, 768], P(None, 'client')
- new_bias_second: float32 [4, 768], P(None, 'tensor')
- new_in_bf: bfloat16 [7, 768, 768], P(None, 'client', 'tensor')
- new_out_bf: bfloat16 [5, 768, 768], P(None, 'tensor', 'client')
- new_table_bf: bfloat16 [1074, 768], P(None, 'client')
- new_bias_bf: bfloat16 [4, 768], P(None, 'tensor')
The draws below stay inside these ranges and needn't reach their ends.
Inputs may be any that keep to these rules, and one draw needn't show every extreme that they name: `index`: each entry names an image of the client's own pool of 32. `tau`: some client takes 4 steps in every draw. `out_bf`: output-side matrices of unit-order products. `out_master`: output-side matrices of unit-order products. `table_bf`: gains near one, small shifts and biases. `table_master`: gains near one, small shifts and biases. `in_second`: positive. `out_second`: positive. `table_second`: positive. `bias_second`: positive.
All inputs are finite; a program needn't handle non-finite values.
Results may differ from the reference program's by a relative error of at most 0.0075.
The reference program's roundings to bfloat16 on the way count: a program that leaves them out, or rounds other values in their place, can miss the bound.
Values may be sent and summed in bfloat16 or wider, within the bound.
A program may use at most 192 MiB of HBM per device.

```python
import math
import jax
import jax.numpy as jnp
import numpy as np
from jax import lax

D = 768
HEADS = 12
HEAD_DIM = 64
FF = 3072
PATCH_FEAT = 768
PATCHES = 196
CLASSES = 100
IMGS = 4
TAU_MAX = 4
ROUND = 5
SEQ = 197
POOL = 32
CLIENTS = 8
ROWS = 1074
N_TENSOR = 4


LOCAL_MOVE = 0.125


def draw_tau(key, part):
    base = jax.random.randint(key, (CLIENTS,), 1, TAU_MAX + 1)
    chosen = jax.random.randint(jax.random.fold_in(key, 11), (), 0, CLIENTS)
    return jnp.where(jnp.arange(CLIENTS) == chosen, TAU_MAX, base).astype(jnp.int32)


def out_values(key):
    noise = jax.random.normal(key, (5, D, D), jnp.float32)
    slab_scale = jnp.where(jnp.arange(5) == 0, 4.0 * D ** (-0.5), FF ** (-0.5))
    return noise * slab_scale[:, None, None]


def draw_out_bf(key, part):
    return out_values(jax.random.fold_in(key, 3)).astype(jnp.bfloat16)


def draw_out_master(key, part):
    return out_values(jax.random.fold_in(key, 4))


def table_values(key):
    keys = jax.random.split(key, 4)
    embed = jax.random.normal(keys[0], (PATCH_FEAT, D), jnp.float32) * PATCH_FEAT ** (-0.5)
    positions = jax.random.normal(keys[1], (SEQ, D), jnp.float32) * 0.5
    noise = jax.random.normal(keys[2], (9, D), jnp.float32)
    rows = jnp.arange(9)
    is_gain = (rows % 2 == 0) & (rows < 6)
    vectors = jnp.where(is_gain[:, None], 1.0 + 0.1 * noise, 0.1 * noise)
    head = jax.random.normal(keys[3], (CLASSES, D), jnp.float32) * D ** (-0.5)
    return jnp.concatenate([embed, positions, vectors, head], 0)


def draw_table_bf(key, part):
    return table_values(jax.random.fold_in(key, 5)).astype(jnp.bfloat16)


def draw_table_master(key, part):
    return table_values(jax.random.fold_in(key, 6))


def table_scale():
    rows = jnp.arange(ROWS)
    return jnp.where(rows >= ROWS - CLASSES, LOCAL_MOVE * 0.9 / math.sqrt(CLASSES * D), LOCAL_MOVE * 0.3 / math.sqrt((ROWS - CLASSES) * D))[:, None]


def first_values(key, shape, scale):
    return jax.random.normal(key, shape, jnp.float32) * scale


def second_values(key, shape, scale):
    factor = jnp.exp(jax.random.uniform(key, shape, jnp.float32, math.log(0.5), math.log(8.0)))
    return 0.3 / 0.7 * scale * scale * factor


def draw_in_first(key, part):
    return first_values(key, (7, D, D), LOCAL_MOVE * 0.2 / math.sqrt(7 * D * D))


def draw_out_first(key, part):
    return first_values(key, (5, D, D), LOCAL_MOVE * 0.2 / math.sqrt(5 * D * D))


def draw_table_first(key, part):
    return first_values(key, (ROWS, D), table_scale())


def draw_bias_first(key, part):
    return first_values(key, (4, D), LOCAL_MOVE * 0.01 / math.sqrt(4 * D))


def draw_in_second(key, part):
    return second_values(key, (7, D, D), LOCAL_MOVE * 0.2 / math.sqrt(7 * D * D))


def draw_out_second(key, part):
    return second_values(key, (5, D, D), LOCAL_MOVE * 0.2 / math.sqrt(5 * D * D))


def draw_table_second(key, part):
    return second_values(key, (ROWS, D), table_scale())


def draw_bias_second(key, part):
    return second_values(key, (4, D), LOCAL_MOVE * 0.01 / math.sqrt(4 * D))


def plant(values, own_key, smallest, top_value):
    spot = [jax.random.randint(jax.random.fold_in(own_key, axis), (), 0, length) for axis, length in enumerate(values.shape)]
    main_axis = values.shape.index(max(values.shape))
    next_to = spot[:main_axis] + [(spot[main_axis] + 1) % values.shape[main_axis]] + spot[main_axis + 1:]
    return values.at[tuple(spot)].set(smallest).at[tuple(next_to)].set(top_value)


def block_scale(rng, shape, pieces, low, high):
    level = 1.0
    for dim, blocks in pieces:
        draws = jax.random.uniform(jax.random.fold_in(jax.random.fold_in(rng, 6), dim), (blocks,), jnp.float32, low / len(pieces), high / len(pieces))
        level = level * jnp.repeat(jnp.exp(draws), shape[dim] // blocks).reshape((-1,) + (1,) * (len(shape) - 1 - dim))
    return level


def cumulative_ranks(count, skew):
    weights = [(1 << 20) // math.isqrt(grade ** skew) + 1 for grade in range(1, count + 1)]
    width = 1 + sum(weights) // (1 << 30)
    return np.cumsum(np.array([max(1, weight // width) for weight in weights]))


def ranked_ids(own_key, shape, number_of, lean):
    table = cumulative_ranks(number_of, lean)
    ticket = jax.random.randint(jax.random.fold_in(own_key, 1), shape, 0, int(table[number_of - 1]))
    grade = jnp.searchsorted(jnp.asarray(table, jnp.int32), ticket, side="right")
    return jax.random.permutation(jax.random.fold_in(own_key, 2), number_of)[grade].astype(jnp.int32)


def centred(rng, dims, width, limit, shards=(), dtype=jnp.bfloat16):
    loudness = block_scale(rng, dims, shards, -0.22, 0.18) if shards else 1.0
    array = jax.random.normal(rng, dims, jnp.float32) * width * loudness
    return jnp.minimum(jnp.maximum(array, -limit), limit).astype(dtype)


def setup_inputs(seed: int = 0) -> dict:
    arg_keys = jax.random.split(jax.random.key(seed), 22)
    pool = centred(arg_keys[0], (CLIENTS * POOL, PATCHES, PATCH_FEAT), 1.0, 6.0, ((0, 8),))
    index = plant(ranked_ids(arg_keys[1], (CLIENTS, TAU_MAX, IMGS), POOL, 2), jax.random.fold_in(arg_keys[1], 3), 0, POOL - 1).astype(jnp.int32)
    tau = draw_tau(jax.random.fold_in(arg_keys[21], 71), 0)
    counts = plant(jax.random.randint(arg_keys[3], (CLIENTS,), 100, 1000), jax.random.fold_in(arg_keys[3], 1), 100, 999).astype(jnp.int32)
    labels = plant(jax.random.randint(arg_keys[4], (CLIENTS * POOL,), 0, CLASSES), jax.random.fold_in(arg_keys[4], 1), 0, CLASSES - 1).astype(jnp.int32)
    in_bf = centred(arg_keys[5], (7, D, D), D ** -0.5, 0.21875, ((1, 8), (2, 4)))
    out_bf = draw_out_bf(jax.random.fold_in(arg_keys[21], 71), 0)
    table_bf = draw_table_bf(jax.random.fold_in(arg_keys[21], 71), 0)
    bias_bf = centred(arg_keys[8], (4, D), 0.3, 3.0, ((1, 4),))
    in_master = centred(arg_keys[9], (7, D, D), D ** -0.5, 0.21875, ((1, 8), (2, 4)), jnp.float32)
    out_master = draw_out_master(jax.random.fold_in(arg_keys[21], 71), 0)
    table_master = draw_table_master(jax.random.fold_in(arg_keys[21], 71), 0)
    bias_master = centred(arg_keys[12], (4, D), 0.3, 3.0, ((1, 4),), jnp.float32)
    in_first = draw_in_first(jax.random.fold_in(arg_keys[21], 71), 0)
    out_first = draw_out_first(jax.random.fold_in(arg_keys[21], 71), 0)
    table_first = draw_table_first(jax.random.fold_in(arg_keys[21], 71), 0)
    bias_first = draw_bias_first(jax.random.fold_in(arg_keys[21], 71), 0)
    in_second = draw_in_second(jax.random.fold_in(arg_keys[21], 71), 0)
    out_second = draw_out_second(jax.random.fold_in(arg_keys[21], 71), 0)
    table_second = draw_table_second(jax.random.fold_in(arg_keys[21], 71), 0)
    bias_second = draw_bias_second(jax.random.fold_in(arg_keys[21], 71), 0)
    return {"pool": pool, "index": index, "tau": tau, "counts": counts, "labels": labels, "in_bf": in_bf, "out_bf": out_bf, "table_bf": table_bf, "bias_bf": bias_bf, "in_master": in_master, "out_master": out_master, "table_master": table_master, "bias_master": bias_master, "in_first": in_first, "out_first": out_first, "table_first": table_first, "bias_first": bias_first, "in_second": in_second, "out_second": out_second, "table_second": table_second, "bias_second": bias_second}


EPS_NORM = 1e-06
MOMENTUM_RHO = 0.9
LOCAL_RATE = 0.05
CLIP_LIMIT = 1.0
BETA_ONE = 0.5
BETA_TWO = 0.7
ADAM_EPS = 1e-08
WEIGHT_DECAY = 0.05
SERVER_RATE = 0.05

@jax.custom_vjp
def low(v):
    return lax.optimization_barrier(v.astype(jnp.bfloat16)).astype(jnp.float32)

@jax.custom_vjp
def low_back(v):
    return v

def low_keep(v):
    return (low(v), None)

def low_pass(kept, grad):
    return (grad,)

def back_keep(v):
    return (v, None)

def back_low(kept, grad):
    return (low(grad),)
low.defvjp(low_keep, low_pass)
low_back.defvjp(back_keep, back_low)

def product(form, left, right):
    return jnp.einsum(form, left, right, precision=lax.Precision.HIGHEST)

def layer_norm(value, gain, shift):
    centre = value - lax.optimization_barrier(jnp.mean(value, -1, keepdims=True))
    return centre * lax.rsqrt(lax.optimization_barrier(jnp.mean(centre * centre, -1, keepdims=True)) + EPS_NORM) * gain + shift

def forward(in_w, out_w, table, bias, patches, target):
    images = patches.shape[0]
    w_emb = low(table[:PATCH_FEAT])
    positions = table[PATCH_FEAT:PATCH_FEAT + SEQ]
    vectors = table[PATCH_FEAT + SEQ:PATCH_FEAT + SEQ + 9]
    w_head = low(table[PATCH_FEAT + SEQ + 9:])
    w_in = low(in_w)
    w_out = low(out_w)
    group = D // N_TENSOR
    heads = HEADS // N_TENSOR
    embedded = low_back(product('npe,ed->npd', patches, w_emb)) + vectors[6]
    first = jnp.broadcast_to(positions[None, :1], (images, 1, D))
    state0 = jnp.concatenate([first, embedded + positions[None, 1:]], 1)
    normed = low(layer_norm(state0, vectors[0], vectors[1]))
    attn = jnp.zeros((images, SEQ, D), jnp.float32)
    for member in range(N_TENSOR):
        cols = slice(member * group, (member + 1) * group)
        normed_g = low_back(normed)
        parts = [low(low_back(product('nld,dc->nlc', normed_g, w_in[slab][:, cols]))).reshape(images, SEQ, heads, HEAD_DIM) for slab in range(3)]
        scores = low_back(product('nqhe,nkhe->nhqk', parts[0], parts[1]) * HEAD_DIM ** (-0.5))
        expd = jnp.exp(scores - lax.optimization_barrier(jnp.max(scores, -1, keepdims=True)))
        prob = low(expd / lax.optimization_barrier(jnp.sum(expd, -1, keepdims=True)))
        context = low(low_back(product('nhqk,nkhe->nqhe', prob, parts[2]))).reshape(images, SEQ, group)
        attn = attn + low(product('nlc,cd->nld', context, w_out[0][cols]))
    state1 = state0 + low_back(attn) + vectors[7]
    upper = low(layer_norm(state1, vectors[2], vectors[3]))
    mlp = jnp.zeros((images, SEQ, D), jnp.float32)
    for member in range(N_TENSOR):
        cols = slice(member * group, (member + 1) * group)
        upper_g = low_back(upper)
        pre = low_back(product('nld,sdc->nlsc', upper_g, w_in[3:, :, cols]) + bias[None, None, :, cols])
        act = low(pre * 0.5 * (1.0 + lax.erf(pre * 0.7071067811865476)))
        mlp = mlp + low(product('nlsc,scd->nld', act, w_out[1:, cols]))
    state2 = state1 + low_back(mlp) + vectors[8]
    pooled = low(layer_norm(lax.optimization_barrier(jnp.mean(state2, 1)), vectors[4], vectors[5]))
    logits = low_back(product('nd,cd->nc', pooled, w_head))
    top = lax.optimization_barrier(jnp.max(logits, -1, keepdims=True))
    lse = top[:, 0] + jnp.log(lax.optimization_barrier(jnp.sum(jnp.exp(logits - top), -1)))
    onehot = (target[:, None] == jnp.arange(CLASSES)[None, :]).astype(jnp.float32)
    return jnp.mean(lse - lax.optimization_barrier(jnp.sum(logits * onehot, -1)))

def local_round(start, pool_c, index_c, labels_c, tau_c):
    slots = jnp.arange(POOL)

    def step(carry, which):
        weights, buffers, loss_sum = carry
        onehot = index_c[which][:, None] == slots[None, :]
        patches = product('ip,pqe->iqe', onehot.astype(jnp.float32), pool_c)
        target = lax.optimization_barrier(jnp.sum(onehot.astype(jnp.int32) * labels_c[None, :], 1))
        loss, pull = jax.vjp(lambda w0, w1, w2, w3: forward(w0, w1, w2, w3, patches, target), *weights)
        grads = pull(jnp.ones_like(loss))
        norm = jnp.sqrt(sum((jnp.sum(grad * grad) for grad in grads)))
        factor = CLIP_LIMIT / jnp.maximum(norm, CLIP_LIMIT)
        live = which < tau_c
        new_buffers = tuple((jnp.where(live, MOMENTUM_RHO * old_b + factor * grad, old_b) for old_b, grad in zip(buffers, grads)))
        new_weights = tuple((jnp.where(live, weight - LOCAL_RATE * buffer_v, weight) for weight, buffer_v in zip(weights, new_buffers)))
        return ((new_weights, new_buffers, loss_sum + jnp.where(live, loss, 0.0)), jnp.where(live, norm, 0.0))
    zeros = tuple((jnp.zeros_like(weight) for weight in start))
    (finish, unused, loss_sum), norms = lax.scan(step, (start, zeros, jnp.zeros((), jnp.float32)), jnp.arange(TAU_MAX))
    return (finish, loss_sum, norms)

def adam(master, first, second, grad):
    first2 = BETA_ONE * first + (1.0 - BETA_ONE) * grad
    second2 = BETA_TWO * second + (1.0 - BETA_TWO) * grad * grad
    moved = first2 / (1.0 - BETA_ONE ** ROUND) / (jnp.sqrt(second2 / (1.0 - BETA_TWO ** ROUND)) + ADAM_EPS)
    fresh = master - SERVER_RATE * (moved + WEIGHT_DECAY * master)
    return (fresh, first2, second2, fresh.astype(jnp.bfloat16))

def reference(pool, index, tau, counts, labels, in_bf, out_bf, table_bf, bias_bf, in_master, out_master, table_master, bias_master, in_first, out_first, table_first, bias_first, in_second, out_second, table_second, bias_second):
    start = (in_bf.astype(jnp.float32), out_bf.astype(jnp.float32), table_bf.astype(jnp.float32), bias_bf.astype(jnp.float32))
    pool_r = pool.astype(jnp.float32).reshape(CLIENTS, POOL, PATCHES, PATCH_FEAT)
    labels_r = labels.reshape(CLIENTS, POOL)
    ladder = jnp.arange(TAU_MAX)

    def one_client(carry, item):
        sums, weighted_loss, weighted_factor, total = carry
        pool_c, index_c, labels_c, tau_c, count_c = item
        finish, loss_sum, norms = local_round(start, pool_c, index_c, labels_c, tau_c)
        factor_c = jnp.sum(jnp.where(ladder < tau_c, (1.0 - MOMENTUM_RHO ** (ladder + 1)) / (1.0 - MOMENTUM_RHO), 0.0))
        examples = count_c.astype(jnp.float32)
        share = examples / factor_c
        sums = tuple((acc + share * (begin - end) for acc, begin, end in zip(sums, start, finish)))
        new_carry = (sums, weighted_loss + examples * loss_sum / tau_c.astype(jnp.float32), weighted_factor + examples * factor_c, total + examples)
        return (new_carry, norms)
    zero_scalar = jnp.zeros((), jnp.float32)
    init = (tuple((jnp.zeros_like(weight) for weight in start)), zero_scalar, zero_scalar, zero_scalar)
    (sums, weighted_loss, weighted_factor, total), clip_norms = lax.scan(one_client, init, (pool_r, index, labels_r, tau, counts))
    scale = weighted_factor / total / total
    masters = (in_master, out_master, table_master, bias_master)
    firsts = (in_first, out_first, table_first, bias_first)
    seconds = (in_second, out_second, table_second, bias_second)
    results = [adam(mst, fst, snd, scale * acc) for mst, fst, snd, acc in zip(masters, firsts, seconds, sums)]
    return (weighted_loss / total, clip_norms, results[0][0], results[1][0], results[2][0], results[3][0], results[0][1], results[1][1], results[2][1], results[3][1], results[0][2], results[1][2], results[2][2], results[3][2], results[0][3], results[1][3], results[2][3], results[3][3])
```

```python
import jax
import jax.numpy as jnp
from jax import lax
from jax.sharding import PartitionSpec as P

HEAD_DIM = 64
ROUND = 5


EPS_NORM = 1e-06
MOMENTUM_RHO = 0.9
LOCAL_RATE = 0.05
CLIP_LIMIT = 1.0
BETA_ONE = 0.5
BETA_TWO = 0.7
ADAM_EPS = 1e-08
WEIGHT_DECAY = 0.05
SERVER_RATE = 0.05
SQRT_HALF = 0.7071067811865476
INV_ROOT_TAU = 0.3989422804014327


def cut_along(value, dim, count):
    dims = value.shape
    parts = value.reshape(*dims[:dim], count, dims[dim] // count, *dims[dim + 1 :])
    return jnp.moveaxis(parts, dim, 0)


def sum_at_owner(value, axis, dim):
    parts = cut_along(value, dim, lax.axis_size(axis))
    arrived = lax.all_to_all(parts, axis, split_axis=0, concat_axis=0, tiled=True)
    return arrived.astype(jnp.float32).sum(axis=0)


def product(form, left, right):
    return jnp.einsum(form, left, right, preferred_element_type=jnp.float32)


def layer_norm(value, gain, shift):
    centre = value - jnp.mean(value, -1, keepdims=True)
    inverse = lax.rsqrt(jnp.mean(centre * centre, -1, keepdims=True) + EPS_NORM)
    normed = centre * inverse
    return (normed * gain + shift, (normed, inverse))


def norm_back(grad, gain, kept):
    normed, inverse = kept
    scaled = grad * gain
    inner = (
        scaled
        - jnp.mean(scaled, -1, keepdims=True)
        - normed * jnp.mean(scaled * normed, -1, keepdims=True)
    )
    leading = tuple(range(grad.ndim - 1))
    return (inverse * inner, jnp.sum(grad * normed, leading), jnp.sum(grad, leading))


def gelu_parts(value):
    normal_cdf = 0.5 * (1.0 + lax.erf(value * SQRT_HALF))
    return (value * normal_cdf, normal_cdf + value * jnp.exp(-0.5 * value * value) * INV_ROOT_TAU)


def train_step(weights, patches, target):
    in_w, out_w, table, bias = weights
    images, patch_rows, features = patches.shape
    length = patch_rows + 1
    width = table.shape[1]
    group = in_w.shape[2]
    heads = group // HEAD_DIM
    scale = HEAD_DIM ** (-0.5)
    w_in = in_w.astype(jnp.bfloat16)
    w_out = out_w.astype(jnp.bfloat16)
    w_emb = table[:features].astype(jnp.bfloat16)
    positions = table[features : features + length]
    vectors = table[features + length : features + length + 9]
    w_head = table[features + length + 9 :].astype(jnp.bfloat16)
    classes = w_head.shape[0]
    embedded = product("npe,ed->npd", patches, w_emb) + vectors[6]
    first = jnp.broadcast_to(positions[None, :1], (images, 1, width))
    state0 = jnp.concatenate([first, embedded + positions[None, 1:]], 1)
    normed, kept_a = layer_norm(state0, vectors[0], vectors[1])
    normed_b = normed.astype(jnp.bfloat16)
    qkv = product("nld,sdc->snlc", normed_b, w_in[:3]).astype(jnp.bfloat16)
    queries = qkv[0].reshape(images, length, heads, HEAD_DIM)
    keys_b = qkv[1].reshape(images, length, heads, HEAD_DIM)
    values_b = qkv[2].reshape(images, length, heads, HEAD_DIM)
    scores = product("nqhe,nkhe->nhqk", queries, keys_b) * scale
    top = jnp.max(scores, -1, keepdims=True)
    expd = jnp.exp(scores - top)
    total = jnp.sum(expd, -1, keepdims=True)
    lse = top + jnp.log(total)
    prob_b = (expd / total).astype(jnp.bfloat16)
    context = (
        product("nhqk,nkhe->nqhe", prob_b, values_b)
        .astype(jnp.bfloat16)
        .reshape(images, length, group)
    )
    attn = lax.psum(
        product("nlc,cd->nld", context, w_out[0]).astype(jnp.bfloat16), "tensor"
    ).astype(jnp.float32)
    state1 = state0 + attn + vectors[7]
    upper, kept_u = layer_norm(state1, vectors[2], vectors[3])
    upper_b = upper.astype(jnp.bfloat16)
    pre = product("nld,sdc->nlsc", upper_b, w_in[3:]) + bias[None, None]
    act, slope = gelu_parts(pre)
    act_b = act.astype(jnp.bfloat16)
    act_sum = jnp.sum(act_b.astype(jnp.float32), 1)
    mlp_sum = lax.psum(
        jnp.einsum(
            "nsc,scd->nd",
            act_sum,
            w_out[1:].astype(jnp.float32),
            precision=lax.Precision.HIGHEST,
        ),
        "tensor",
    )
    average2 = jnp.mean(state1, 1) + mlp_sum / length + vectors[8]
    pooled, kept_y = layer_norm(average2, vectors[4], vectors[5])
    pooled_b = pooled.astype(jnp.bfloat16)
    logits = product("nd,cd->nc", pooled_b, w_head)
    top_l = jnp.max(logits, -1, keepdims=True)
    exp_l = jnp.exp(logits - top_l)
    total_l = jnp.sum(exp_l, -1, keepdims=True)
    onehot = (target[:, None] == jnp.arange(classes, dtype=jnp.int32)[None, :]).astype(jnp.float32)
    loss = jnp.mean(top_l[:, 0] + jnp.log(total_l[:, 0]) - jnp.sum(logits * onehot, -1))
    d_logits = ((exp_l / total_l - onehot) / images).astype(jnp.bfloat16)
    d_head = product("nc,nd->cd", d_logits, pooled_b)
    d_pooled = product("nc,cd->nd", d_logits, w_head)
    d_average, d_gain3, d_shift3 = norm_back(d_pooled, vectors[4], kept_y)
    d_token = d_average / length
    d_mlp = d_token.astype(jnp.bfloat16)
    d_act = product("nd,scd->nsc", d_mlp, w_out[1:])
    d_w2 = jnp.einsum(
        "nsc,nd->scd", act_sum, d_mlp.astype(jnp.float32), precision=lax.Precision.HIGHEST
    )
    d_pre = (d_act[:, None] * slope).astype(jnp.bfloat16)
    d_bias = jnp.sum(d_pre.astype(jnp.float32), (0, 1))
    d_w1 = product("nld,nlsc->sdc", upper_b, d_pre)
    d_upper = lax.psum(
        product("nlsc,sdc->nld", d_pre, w_in[3:]).astype(jnp.bfloat16), "tensor"
    ).astype(jnp.float32)
    d_norm2, d_gain2, d_shift2 = norm_back(d_upper, vectors[2], kept_u)
    d_state1 = d_token[:, None] + d_norm2
    d_attn = d_state1.astype(jnp.bfloat16)
    d_context = (
        product("nld,cd->nlc", d_attn, w_out[0])
        .astype(jnp.bfloat16)
        .reshape(images, length, heads, HEAD_DIM)
    )
    d_wo = product("nlc,nld->cd", context, d_attn)
    again = jnp.exp(product("nqhe,nkhe->nhqk", queries, keys_b) * scale - lse)
    d_prob = product("nqhe,nkhe->nhqk", d_context, values_b)
    d_values = product("nhqk,nqhe->nkhe", again.astype(jnp.bfloat16), d_context)
    d_scores = (again * (d_prob - jnp.sum(d_prob * again, -1, keepdims=True))).astype(jnp.bfloat16)
    d_queries = product("nhqk,nkhe->nqhe", d_scores, keys_b) * scale
    d_keys = product("nhqk,nqhe->nkhe", d_scores, queries) * scale
    d_qkv = (
        jnp.stack([d_queries, d_keys, d_values])
        .reshape(3, images, length, group)
        .astype(jnp.bfloat16)
    )
    d_wqkv = product("nld,snlc->sdc", normed_b, d_qkv)
    d_normed = lax.psum(
        product("snlc,sdc->nld", d_qkv, w_in[:3]).astype(jnp.bfloat16), "tensor"
    ).astype(jnp.float32)
    d_norm1, d_gain1, d_shift1 = norm_back(d_normed, vectors[0], kept_a)
    d_state0 = d_state1 + d_norm1
    d_positions = jnp.sum(d_state0, 0)
    d_embedded = d_state0[:, 1:]
    d_wemb = product("npe,npd->ed", patches, d_embedded.astype(jnp.bfloat16))
    d_vectors = jnp.stack(
        [
            d_gain1,
            d_shift1,
            d_gain2,
            d_shift2,
            d_gain3,
            d_shift3,
            jnp.sum(d_embedded, (0, 1)),
            jnp.sum(d_state1, (0, 1)),
            jnp.sum(d_average, 0),
        ]
    )
    d_table = jnp.concatenate([d_wemb, d_positions, d_vectors, d_head], 0)
    d_in = jnp.concatenate([d_wqkv, d_w1], 0)
    d_out = jnp.concatenate([d_wo[None], d_w2], 0)
    return (loss, (d_in, d_out, d_table, d_bias))


def adam(master, first, second, grad):
    first2 = BETA_ONE * first + (1.0 - BETA_ONE) * grad
    second2 = BETA_TWO * second + (1.0 - BETA_TWO) * grad * grad
    moved = (
        first2 / (1.0 - BETA_ONE**ROUND) / (jnp.sqrt(second2 / (1.0 - BETA_TWO**ROUND)) + ADAM_EPS)
    )
    fresh = master - SERVER_RATE * (moved + WEIGHT_DECAY * master)
    return (fresh, first2, second2, fresh.astype(jnp.bfloat16))


def on_device(
    pool,
    index,
    tau,
    counts,
    labels,
    in_bf,
    out_bf,
    table_bf,
    bias_bf,
    in_master,
    out_master,
    table_master,
    bias_master,
    in_first,
    out_first,
    table_first,
    bias_first,
    in_second,
    out_second,
    table_second,
    bias_second,
):
    in_full, out_full, table_full = (
        lax.all_gather(in_bf, "client", axis=1, tiled=True),
        lax.all_gather(out_bf, "client", axis=2, tiled=True),
        lax.all_gather(table_bf, "client", axis=1, tiled=True),
    )
    start = (
        in_full.astype(jnp.float32),
        out_full.astype(jnp.float32),
        table_full.astype(jnp.float32),
        bias_bf.astype(jnp.float32),
    )
    images = index.shape[2]
    steps_cap = index.shape[1]
    pool_size = pool.shape[0]
    flat_pool = pool.reshape(pool_size, pool.shape[1] * pool.shape[2])
    slots = jnp.arange(pool_size, dtype=jnp.int32)
    taken = tau[0]

    def local_step(which, carry):
        weights, buffers, loss_sum, norms = carry
        chosen = lax.dynamic_index_in_dim(index[0], which, 0, keepdims=False)
        onehot = chosen[:, None] == slots[None, :]
        patches = jnp.dot(
            onehot.astype(jnp.bfloat16), flat_pool, preferred_element_type=jnp.float32
        )
        patches = patches.astype(jnp.bfloat16).reshape(images, pool.shape[1], pool.shape[2])
        target = jnp.sum(onehot.astype(jnp.int32) * labels[None, :], 1)
        loss, grads = train_step(weights, patches, target)
        split_squares = (
            jnp.sum(grads[0] * grads[0])
            + jnp.sum(grads[1] * grads[1])
            + jnp.sum(grads[3] * grads[3])
        )
        shared_squares = jnp.sum(grads[2] * grads[2]) / lax.axis_size("tensor")
        norm = jnp.sqrt(lax.psum(split_squares + shared_squares, "tensor"))
        factor = CLIP_LIMIT / jnp.maximum(norm, CLIP_LIMIT)
        live = which < taken
        buffers = tuple(
            (
                jnp.where(live, MOMENTUM_RHO * previous + factor * gradient, previous)
                for previous, gradient in zip(buffers, grads)
            )
        )
        weights = tuple(
            (
                jnp.where(live, weight - LOCAL_RATE * buffer_v, weight)
                for weight, buffer_v in zip(weights, buffers)
            )
        )
        norms = lax.dynamic_update_index_in_dim(norms, jnp.where(live, norm, 0.0), which, 0)
        return (weights, buffers, loss_sum + jnp.where(live, loss, 0.0), norms)

    zeros = tuple((jnp.zeros_like(weight) for weight in start))
    init = (start, zeros, jnp.zeros((), jnp.float32), jnp.zeros((steps_cap,), jnp.float32))
    finish, unused, loss_sum, norms = lax.fori_loop(0, steps_cap, local_step, init)
    ladder = jnp.arange(steps_cap, dtype=jnp.int32)
    factor_sum = jnp.sum(
        jnp.where(
            ladder < taken,
            (1.0 - MOMENTUM_RHO ** (ladder + 1).astype(jnp.float32)) / (1.0 - MOMENTUM_RHO),
            0.0,
        )
    )
    examples = counts[0].astype(jnp.float32)
    share = examples / factor_sum
    moved = tuple((share * (begin - end) for begin, end in zip(start, finish)))
    total, weighted_loss, weighted_factor, bias_delta = lax.psum(
        (
            examples,
            examples * loss_sum / taken.astype(jnp.float32),
            examples * factor_sum,
            moved[3],
        ),
        "client",
    )
    in_delta, out_delta = (
        lax.psum_scatter(
            moved[0].astype(jnp.bfloat16), "client", scatter_dimension=1, tiled=True
        ).astype(jnp.float32),
        lax.psum_scatter(
            moved[1].astype(jnp.bfloat16), "client", scatter_dimension=2, tiled=True
        ).astype(jnp.float32),
    )
    table_delta = sum_at_owner(moved[2].astype(jnp.bfloat16), "client", 1)
    server_scale = weighted_factor / total / total
    masters = (in_master, out_master, table_master, bias_master)
    firsts = (in_first, out_first, table_first, bias_first)
    seconds = (in_second, out_second, table_second, bias_second)
    deltas = (in_delta, out_delta, table_delta, bias_delta)
    results = [
        adam(mst, fst, snd, server_scale * dlt)
        for mst, fst, snd, dlt in zip(masters, firsts, seconds, deltas)
    ]
    return (
        weighted_loss / total,
        norms[None],
        results[0][0],
        results[1][0],
        results[2][0],
        results[3][0],
        results[0][1],
        results[1][1],
        results[2][1],
        results[3][1],
        results[0][2],
        results[1][2],
        results[2][2],
        results[3][2],
        results[0][3],
        results[1][3],
        results[2][3],
        results[3][3],
    )


def solution(mesh):
    in_specs = (
        P("client", None, None),
        P("client", None, None),
        P("client"),
        P("client"),
        P("client"),
        P(None, "client", "tensor"),
        P(None, "tensor", "client"),
        P(None, "client"),
        P(None, "tensor"),
        P(None, "client", "tensor"),
        P(None, "tensor", "client"),
        P(None, "client"),
        P(None, "tensor"),
        P(None, "client", "tensor"),
        P(None, "tensor", "client"),
        P(None, "client"),
        P(None, "tensor"),
        P(None, "client", "tensor"),
        P(None, "tensor", "client"),
        P(None, "client"),
        P(None, "tensor"),
    )
    out_specs = (
        P(),
        P("client", None),
        P(None, "client", "tensor"),
        P(None, "tensor", "client"),
        P(None, "client"),
        P(None, "tensor"),
        P(None, "client", "tensor"),
        P(None, "tensor", "client"),
        P(None, "client"),
        P(None, "tensor"),
        P(None, "client", "tensor"),
        P(None, "tensor", "client"),
        P(None, "client"),
        P(None, "tensor"),
        P(None, "client", "tensor"),
        P(None, "tensor", "client"),
        P(None, "client"),
        P(None, "tensor"),
    )
    return jax.shard_map(
        on_device, mesh=mesh, in_specs=in_specs, out_specs=out_specs, check_vma=False
    )
```

```python
import functools

import jax
import jax.numpy as jnp
from jax import lax
from jax.experimental import pallas as pl
from jax.experimental.pallas import tpu as pltpu
from jax.sharding import PartitionSpec as P

HEAD_DIM = 64
ROUND = 5
EPS_NORM = 1e-06
MOMENTUM_RHO = 0.9
LOCAL_RATE = 0.05
CLIP_LIMIT = 1.0
BETA_ONE = 0.5
BETA_TWO = 0.7
ADAM_EPS = 1e-08
WEIGHT_DECAY = 0.05
SERVER_RATE = 0.05
SQRT_HALF = 0.7071067811865476
INV_ROOT_TAU = 0.3989422804014327
MESH = pl.DeviceIdType.MESH
F32 = jnp.float32
BF16 = jnp.bfloat16
NEG = -1e30
LANE = 256
SMALL = 16
VMEM_LIMIT = 67043328


def dot(left, right, dims):
    return lax.dot_general(left, right, (dims, ((), ())), preferred_element_type=F32)


def nn(left, right):
    return dot(left, right, ((1,), (0,)))


def nt(left, right):
    return dot(left, right, ((1,), (1,)))


def tn(left, right):
    return dot(left, right, ((0,), (0,)))


def fold(value):
    rows, width = value.shape
    return jnp.sum(value.reshape(rows // 8, 8, width), 0)


def total(value):
    return jnp.sum(jnp.sum(value, 1, keepdims=True), 0, keepdims=True)


def normalise(value):
    centre = value - jnp.mean(value, -1, keepdims=True)
    inverse = lax.rsqrt(jnp.mean(centre * centre, -1, keepdims=True) + EPS_NORM)
    return (centre * inverse, inverse)


def norm_grad(grad, gain, normed, inverse):
    scaled = grad * gain
    return inverse * (
        scaled
        - jnp.mean(scaled, -1, keepdims=True)
        - normed * jnp.mean(scaled * normed, -1, keepdims=True)
    )


def split_two(value):
    high = value.astype(BF16)
    return (high, (value - high.astype(F32)).astype(BF16))


def train_kernel(
    sizes,
    live_ref,
    x_hbm,
    hot_ref,
    wqkv_in,
    w1_in,
    wot_in,
    w2t_in,
    wet_in,
    head_in,
    pos_in,
    vec_in,
    bias_in,
    dqkv_out,
    dw1_out,
    dwot_out,
    dwet_out,
    dpos_out,
    dhead_out,
    dvec_out,
    dbias_out,
    low_d_out,
    low_a_out,
    loss_out,
    norm_out,
    wqkv, w1, wot, w2t, wet, head,
    wqkv_f, w1_f, wot_f, wet_f, pos_f, head_f, vec_f, bias_f,
    wqkv_m, w1_m, wot_m, wet_m, pos_m, head_m, vec_m, bias_m,
    wqkv_g, wot_g, pos_g, head_g, vec_g,
    xbuf, h0, slope, prob, abuf, qkv, oall, ubuf, dpre, h1own, datt, chip,
    hsum, asum, dact, bsum, vacc, ssq,
    low_d, low_a, low_b, low_w, scal,
    s1, r1, s2, r2, mx_s, mx_r, nx_s, nx_r, pos_r, vec_r,
    wsem, xsem, o_ps, o_xs, o_fs, o_pr, o_xr, o_fr,
    a1s, a1r, a2s, a2r, das, dar, pvs, pvr, mxs, mxr, nxs, nxr, osem,
):
    steps, seq, pad, classes = sizes
    width = 768
    rows_all = 4 * pad
    me = lax.axis_index("tensor")
    core = lax.rem(me, 2)
    mate = me + 1 - 2 * core
    across = lax.rem(me + 2, 4)
    own0 = 2 * core
    oth0 = 2 - 2 * core

    def rows(n):
        return pl.ds(pl.multiple_of(n * pad, 16), pad)

    def remote(src, dst, send, recv, device):
        return pltpu.make_async_remote_copy(
            src_ref=src, dst_ref=dst, send_sem=send, recv_sem=recv,
            device_id={"tensor": device}, device_id_type=MESH,
        )

    weights_in = (wqkv_in, w1_in, wot_in, w2t_in, wet_in, head_in)
    weights = (wqkv, w1, wot, w2t, wet, head)

    def load(which):
        return pltpu.make_async_copy(weights_in[which], weights[which], wsem.at[which])

    def fetch(step, slot):
        return pltpu.make_async_copy(x_hbm.at[step], xbuf.at[slot], xsem.at[slot])

    barrier = pltpu.get_barrier_semaphore()
    for shift in (1, 2, 3):
        pl.semaphore_signal(
            barrier, inc=1, device_id={"tensor": lax.rem(me + shift, 4)}, device_id_type=MESH
        )
    fetch(0, 0).start()
    for which in range(6):
        load(which).start()
    pos_load = pltpu.make_async_copy(pos_in, pos_f, wsem.at[6])
    pos_load.start()
    vec_f[...] = vec_in[...]
    bias_f[...] = bias_in[...]
    for zero in (pos_m, head_m, vec_m, bias_m, low_a, low_b, low_w, loss_out):
        zero[...] = jnp.zeros_like(zero)
    low_d[...] = jnp.zeros_like(low_d)
    for which in range(6):
        load(which).wait()
    pos_load.wait()
    head_f[...] = head[...].astype(F32)

    def start_rows(j, carry):
        at = pl.ds(pl.multiple_of(j * 32, 32), 32)
        for low, full, mom in (
            (wqkv, wqkv_f, wqkv_m), (w1, w1_f, w1_m), (wot, wot_f, wot_m), (wet, wet_f, wet_m)
        ):
            full[at, :] = low[at, :].astype(F32)
            mom[at, :] = jnp.zeros((32, mom.shape[1]), F32)
        return carry

    lax.fori_loop(0, width // 32, start_rows, 0)
    pl.semaphore_wait(barrier, 3)

    row_id = lax.broadcasted_iota(jnp.int32, (pad, 1), 0)
    token = row_id < seq
    key_ok = lax.broadcasted_iota(jnp.int32, (1, pad), 1) < seq
    lane_head = lax.broadcasted_iota(jnp.int32, (1, LANE), 1) // HEAD_DIM
    small_ok = lax.broadcasted_iota(jnp.int32, (SMALL, 1), 0) < 4
    scale = HEAD_DIM ** (-0.5)

    def of_head(value, h):
        return jnp.where(lane_head == h, value, jnp.zeros_like(value))

    def o_place(n, group):
        return oall.at[rows(n), pl.ds(pl.multiple_of(group * LANE, LANE), LANE)]

    def o_to_mate(n):
        place = o_place(n, me)
        return remote(place, place, o_ps.at[n], o_pr.at[n], mate)

    def o_across(n):
        place = o_place(n, me)
        return remote(place, place, o_xs.at[n], o_xr.at[n], across)

    def o_forward(n):
        place = o_place(n, across)
        return remote(place, place, o_fs.at[n], o_fr.at[n], mate)

    def to_mate(n):
        return remote(s1.at[n], r1.at[n], a1s.at[n], a1r.at[n], mate)

    def to_across(which, n):
        return remote(s2.at[n], r2.at[2 * which + n], a2s.at[2 * which + n], a2r.at[2 * which + n], across)

    def gradient_to_mate(buffer, which, image, k):
        return remote(
            buffer.at[rows(image)], buffer.at[rows(image)],
            das.at[2 * which + k], dar.at[2 * which + k], mate,
        )

    def pos_to_mate():
        return remote(pos_g, pos_r, pvs.at[0], pvr.at[0], mate)

    def vec_to_mate():
        return remote(vacc, vec_r, pvs.at[1], pvr.at[1], mate)

    def spread(src, dst, send, recv, shift):
        return remote(
            src, dst.at[me], send.at[shift - 1], recv.at[shift - 1], lax.rem(me + shift, 4)
        )

    def one_step(step, carry):
        slot = lax.rem(step, 2)
        fetch(step, slot).wait()

        @pl.when(step < steps - 1)
        def _():
            fetch(step + 1, 1 - slot).start()

        gain1, shift1 = vec_f[0:1, :], vec_f[1:2, :]
        gain2, shift2 = vec_f[2:3, :], vec_f[3:4, :]
        gain3, shift3 = vec_f[4:5, :], vec_f[5:6, :]

        def attend(n, carry):
            @pl.when(n >= 1)
            def _():
                remote(
                    o_place(n - 1, across), o_place(n - 1, across), o_xs.at[n - 1], o_xr.at[n - 1], across
                ).wait_recv()
                o_forward(n - 1).start()

            inside = (row_id >= 1) & token
            state = (
                nt(xbuf[slot, rows(n), :], wet[...])
                + pos_f[...]
                + jnp.where(inside, vec_f[6:7, :], 0.0)
            )
            h0[rows(n), :] = state
            normed, _ = normalise(state)
            a = (normed * gain1 + shift1).astype(BF16)
            abuf[rows(n), :] = a
            projected = nn(a, wqkv[...]).astype(BF16)
            qkv[rows(n), :] = projected
            q, k, v = projected[:, :LANE], projected[:, LANE : 2 * LANE], projected[:, 2 * LANE :]
            out = jnp.zeros((pad, LANE), F32)
            for h in range(3):
                scores = jnp.where(key_ok, nt(of_head(q, h), k) * scale, NEG)
                expd = jnp.exp(scores - jnp.max(scores, -1, keepdims=True))
                p = (expd / jnp.sum(expd, -1, keepdims=True)).astype(BF16)
                prob[n * 3 + h] = p
                out = out + nn(p, of_head(v, h))
            o_place(n, me)[...] = out.astype(BF16)
            o_to_mate(n).start()
            o_across(n).start()
            return carry

        lax.fori_loop(0, 4, attend, 0)

        def feed(n, carry):
            @pl.when(n == 1)
            def _():
                remote(
                    o_place(3, across), o_place(3, across), o_xs.at[3], o_xr.at[3], across
                ).wait_recv()
                o_forward(3).start()

            remote(o_place(n, mate), o_place(n, mate), o_ps.at[n], o_pr.at[n], mate).wait_recv()
            diagonal = lax.rem(mate + 2, 4)
            remote(
                o_place(n, diagonal), o_place(n, diagonal), o_fs.at[n], o_fr.at[n], mate
            ).wait_recv()
            state = h0[rows(n), :] + nt(oall[rows(n), :], wot[...]) + vec_f[7:8, :]

            @pl.when(n // 2 == core)
            def _():
                h1own[lax.rem(n, 2)] = state

            hsum[n] = fold(jnp.where(token, state, 0.0))
            normed, _ = normalise(state)
            u = (normed * gain2 + shift2).astype(BF16)
            ubuf[rows(n), :] = u
            z = nn(u, w1[...]) + bias_f[0:1, :]
            cdf = 0.5 * (1.0 + lax.erf(z * SQRT_HALF))
            act = (z * cdf).astype(BF16).astype(F32)
            asum[n] = fold(jnp.where(token, act, 0.0))
            tail = cdf + z * jnp.exp(-0.5 * z * z) * INV_ROOT_TAU
            slope[rows(n), :] = jnp.where(token, tail, 0.0)
            return carry

        lax.fori_loop(0, 4, feed, 0)

        def stack(ref):
            parts = [jnp.sum(ref[n], 0, keepdims=True) for n in range(4)]
            return jnp.concatenate(parts + [jnp.zeros((SMALL - 4, width), F32)], 0)

        act_sum = stack(asum)
        act_hi, act_lo = split_two(act_sum)
        both = nt(jnp.concatenate([act_hi, act_lo], 0), w2t[...])
        mx_s[...] = both[:SMALL] + both[SMALL:]
        for shift in (1, 2, 3):
            spread(mx_s, mx_r, mxs, mxr, shift).start()
        mx_r[me] = mx_s[...]
        h_mean = stack(hsum) * (1.0 / seq)
        for shift in (1, 2, 3):
            remote(
                mx_s, mx_r.at[lax.rem(me + 4 - shift, 4)], mxs.at[shift - 1], mxr.at[shift - 1], mate
            ).wait_recv()
        mlp = mx_r[0] + mx_r[1] + mx_r[2] + mx_r[3]
        average = h_mean + mlp * (1.0 / seq) + vec_f[8:9, :]
        normed3, inverse3 = normalise(average)
        pooled = (normed3 * gain3 + shift3).astype(BF16)
        logits = nt(pooled, head[...])
        class_ok = lax.broadcasted_iota(jnp.int32, (1, head.shape[0]), 1) < classes
        logits = jnp.where(class_ok, logits, NEG)
        top = jnp.max(logits, -1, keepdims=True)
        exp_l = jnp.exp(logits - top)
        total_l = jnp.sum(exp_l, -1, keepdims=True)
        hot = hot_ref[step]
        each = top + jnp.log(total_l) - jnp.sum(jnp.where(class_ok, logits, 0.0) * hot, -1, keepdims=True)
        loss = jnp.sum(jnp.where(small_ok, each, 0.0), 0, keepdims=True) * 0.25
        live = live_ref[0, step]
        rho = live_ref[1, step]
        loss_out[...] = loss_out[...] + live * loss
        d_logits = jnp.where(small_ok, (exp_l / total_l - hot) * 0.25, 0.0).astype(BF16)
        d_head = tn(d_logits, pooled)
        head_g[...] = d_head
        d_pooled = nn(d_logits, head[...])
        d_average = norm_grad(d_pooled, gain3, normed3, inverse3)
        d_token = d_average * (1.0 / seq)
        d_mlp = d_token.astype(BF16)
        dact[...] = nn(d_mlp, w2t[...])
        for r in range(4):
            scal[r] = jnp.broadcast_to(d_token[r : r + 1, :], (8, width))
        vec_g[...] = jnp.zeros_like(vec_g)
        vec_g[4:5, :] = jnp.sum(d_pooled * normed3, 0, keepdims=True)
        vec_g[5:6, :] = jnp.sum(d_pooled, 0, keepdims=True)
        vec_g[8:9, :] = jnp.sum(d_average, 0, keepdims=True)
        low_at = pl.ds(pl.multiple_of(step * SMALL, SMALL), SMALL)
        low_d[low_at, :] = d_mlp
        low_a[low_at, :] = act_sum
        gram_d = nt(d_mlp, d_mlp)
        gram_a = nt(act_hi, act_hi) + nt(act_hi, act_lo) + nt(act_lo, act_hi)
        own_squares = total(gram_d * gram_a)

        for n in range(4):
            scal[4 + n] = jnp.broadcast_to(dact[n : n + 1, :], (8, width))
        bsum[...] = jnp.zeros_like(bsum)
        vacc[...] = jnp.zeros_like(vacc)

        def upper_partial(n):
            g = (scal[4 + n][0:1, :] * slope[rows(n), :]).astype(BF16)
            dpre[rows(n), :] = g
            bsum[...] = bsum[...] + fold(g.astype(F32))
            return nt(g, w1[...])

        for k in (0, 1):
            s1[k] = upper_partial(oth0 + k).astype(BF16)
            to_mate(k).start()
            own = upper_partial(own0 + k)
            to_mate(k).wait_recv()
            own = own + r1[k].astype(F32)
            chip[k] = own
            s2[k] = own.astype(BF16)
            to_across(0, k).start()

        ssq[...] = jnp.zeros_like(ssq)
        w1_g = slope

        def weight_grad(left, right, out, which):
            def tile(j, carry):
                at = pl.ds(pl.multiple_of(j * LANE, LANE), LANE)
                g = tn(left[:, at], right[...])
                out[at, :] = g
                if g.shape[1] > width:
                    squares = fold(g * g)
                    ssq[which] = ssq[which] + squares[:, :width]
                    ssq[which, :, : g.shape[1] - width] = (
                        ssq[which, :, : g.shape[1] - width] + squares[:, width:]
                    )
                else:
                    ssq[which] = ssq[which] + fold(g * g)
                return carry

            lax.fori_loop(0, width // LANE, tile, 0)

        weight_grad(ubuf, dpre, w1_g, 0)

        def attention_partial(n):
            d_ctx = nn(
                datt[rows(n), :], wot[:, pl.ds(pl.multiple_of(me * LANE, LANE), LANE)]
            ).astype(BF16)
            projected = qkv[rows(n), :]
            q, k, v = projected[:, :LANE], projected[:, LANE : 2 * LANE], projected[:, 2 * LANE :]
            d_q = jnp.zeros((pad, LANE), F32)
            d_k = jnp.zeros((pad, LANE), F32)
            d_v = jnp.zeros((pad, LANE), F32)
            for h in range(3):
                part = of_head(d_ctx, h)
                p = prob[n * 3 + h]
                again = p.astype(F32)
                d_p = nt(part, v)
                inner = d_p - jnp.sum(d_p * again, -1, keepdims=True)
                d_s = (again * inner).astype(BF16)
                d_v = d_v + tn(p, part)
                d_q = d_q + nn(d_s, of_head(k, h))
                d_k = d_k + tn(d_s, of_head(q, h))
            d_all = jnp.concatenate([d_q * scale, d_k * scale, d_v], 1).astype(BF16)
            qkv[rows(n), :] = d_all
            return nt(d_all, wqkv[...])

        for k in (0, 1):
            to_across(0, k).wait_recv()
            d_upper = chip[k] + r2[k].astype(F32)
            normed, inverse = normalise(h1own[k])
            d_state = norm_grad(d_upper, gain2, normed, inverse) + scal[own0 + k][0:1, :]
            d_state = jnp.where(token, d_state, 0.0)
            h1own[k] = d_state
            datt[rows(own0 + k), :] = d_state.astype(BF16)
            gradient_to_mate(datt, 0, own0 + k, k).start()
            vacc[0] = vacc[0] + fold(d_upper * normed)
            vacc[1] = vacc[1] + fold(d_upper)
            vacc[2] = vacc[2] + fold(d_state)
            own = attention_partial(own0 + k)
            remote(
                datt.at[rows(oth0 + k)], datt.at[rows(oth0 + k)], das.at[k], dar.at[k], mate
            ).wait_recv()
            other = attention_partial(oth0 + k)
            to_mate(k).wait_send()
            s1[k] = other.astype(BF16)
            to_mate(k).start()
            to_mate(k).wait_recv()
            own = own + r1[k].astype(F32)
            chip[k] = own
            to_across(0, k).wait_send()
            s2[k] = own.astype(BF16)
            to_across(1, k).start()

        weight_grad(datt, oall, wot_g, 1)
        weight_grad(abuf, qkv, wqkv_g, 2)

        d_emb = ubuf
        d_pos = jnp.zeros((pad, width), F32)
        for k in (0, 1):
            to_across(1, k).wait_recv()
            d_normed = chip[k] + r2[2 + k].astype(F32)
            normed, inverse = normalise(h0[rows(own0 + k), :])
            d_state = h1own[k] + norm_grad(d_normed, gain1, normed, inverse)
            d_emb[rows(own0 + k), :] = d_state.astype(BF16)
            gradient_to_mate(d_emb, 1, own0 + k, k).start()
            vacc[3] = vacc[3] + fold(d_normed * normed)
            vacc[4] = vacc[4] + fold(d_normed)
            vacc[5] = vacc[5] + fold(jnp.where(row_id >= 1, d_state, 0.0))
            d_pos = d_pos + d_state
        pos_g[...] = d_pos
        pos_to_mate().start()
        vec_to_mate().start()
        wet_g = h0
        for k in (0, 1):
            remote(
                d_emb.at[rows(oth0 + k)], d_emb.at[rows(oth0 + k)], das.at[2 + k], dar.at[2 + k], mate
            ).wait_recv()
        weight_grad(d_emb, xbuf.at[slot], wet_g, 3)
        pos_to_mate().wait()
        vec_to_mate().wait()
        pos_g[...] = pos_g[...] + pos_r[...]
        sums = [jnp.sum(vacc[r] + vec_r[r], 0, keepdims=True) for r in range(6)]
        vec_g[0:1, :] = sums[3]
        vec_g[1:2, :] = sums[4]
        vec_g[2:3, :] = sums[0]
        vec_g[3:4, :] = sums[1]
        vec_g[6:7, :] = sums[5]
        vec_g[7:8, :] = sums[2]
        d_bias = jnp.sum(bsum[...], 0, keepdims=True)
        shared = (
            total(ssq[1] + ssq[3] + fold(pos_g[...] * pos_g[...]) + fold(head_g[...] * head_g[...]))
            + total(vec_g[...] * vec_g[...])
        )
        own_squares = own_squares + total(ssq[0] + ssq[2]) + total(d_bias * d_bias)
        for n in range(4):
            o_to_mate(n).wait_send()
            o_across(n).wait_send()
            o_forward(n).wait_send()
        for k in (0, 1):
            to_mate(k).wait_send()
            to_across(1, k).wait_send()
            gradient_to_mate(datt, 0, own0 + k, k).wait_send()
            gradient_to_mate(d_emb, 1, own0 + k, k).wait_send()
        for shift in (1, 2, 3):
            spread(mx_s, mx_r, mxs, mxr, shift).wait_send()
        nx_s[...] = jnp.broadcast_to(own_squares + 0.25 * shared, (8, 128))
        for shift in (1, 2, 3):
            spread(nx_s, nx_r, nxs, nxr, shift).start()
        nx_r[me] = nx_s[...]

        load(3).start()

        @pl.when(step == steps - 1)
        def _():
            for which in (0, 1, 2, 4, 5):
                load(which).start()

        for shift in (1, 2, 3):
            remote(
                nx_s, nx_r.at[lax.rem(me + 4 - shift, 4)], nxs.at[shift - 1], nxr.at[shift - 1], mate
            ).wait_recv()
        norm = jnp.sqrt((nx_r[0] + nx_r[1] + nx_r[2] + nx_r[3]))
        factor = live * (CLIP_LIMIT / jnp.maximum(norm, CLIP_LIMIT))
        norm_out[step] = live * norm
        for shift in (1, 2, 3):
            spread(nx_s, nx_r, nxs, nxr, shift).wait_send()
        fac = factor[0:1, 0:1]

        low_row = lax.broadcasted_iota(jnp.int32, low_b.shape, 0) // SMALL
        low_b[...] = jnp.where(low_row == step, fac, rho * low_b[...])
        low_w[...] = low_w[...] + live * low_b[...]
        factors = (LOCAL_RATE * low_w[:, 0:1]) * low_a[...]
        low_hi, low_lo = split_two(factors)
        pair = jnp.concatenate([low_hi, low_lo], 0)
        load(3).wait()

        def low_rank(j, carry):
            at = pl.ds(pl.multiple_of(j * LANE, LANE), LANE)
            moved = tn(jnp.concatenate([low_d[:, at], low_d[:, at]], 0), pair)
            w2t[at, :] = (w2t[at, :].astype(F32) - moved).astype(BF16)
            return carry

        lax.fori_loop(0, width // LANE, low_rank, 0)

        def small_update(full, mom, grad):
            mom[...] = rho * mom[...] + fac * grad
            full[...] = full[...] - (live * LOCAL_RATE) * mom[...]

        small_update(pos_f, pos_m, pos_g[...])
        small_update(vec_f, vec_m, vec_g[...])
        small_update(bias_f, bias_m, jnp.broadcast_to(d_bias, (8, width)))
        small_update(head_f, head_m, head_g[...])
        table = (
            (wqkv, wqkv_f, wqkv_m, wqkv_g),
            (w1, w1_f, w1_m, w1_g),
            (wot, wot_f, wot_m, wot_g),
            (wet, wet_f, wet_m, wet_g),
        )

        @pl.when(step < steps - 1)
        def _():
            head[...] = head_f[...].astype(BF16)

            def update(j, carry):
                at = pl.ds(pl.multiple_of(j * 16, 16), 16)
                for low, full, mom, grad in table:
                    m = rho * mom[at, :] + fac * grad[at, :]
                    mom[at, :] = m
                    w = full[at, :] - (live * LOCAL_RATE) * m
                    full[at, :] = w
                    low[at, :] = w.astype(BF16)
                return carry

            lax.fori_loop(0, width // 16, update, 0)

        @pl.when(step == steps - 1)
        def _():
            share = live_ref[2, 0]
            pos_again = pltpu.make_async_copy(pos_in, pos_r, wsem.at[7])
            pos_again.start()
            for which in (0, 1, 2, 4, 5):
                load(which).wait()

            def finish(j, carry):
                at = pl.ds(pl.multiple_of(j * 16, 16), 16)
                for low, full, mom, grad in table:
                    m = rho * mom[at, :] + fac * grad[at, :]
                    w = full[at, :] - (live * LOCAL_RATE) * m
                    low[at, :] = (share * (low[at, :].astype(F32) - w)).astype(BF16)
                return carry

            lax.fori_loop(0, width // 16, finish, 0)
            outs = (
                (wqkv, dqkv_out),
                (w1, dw1_out),
                (wot.at[:, pl.ds(pl.multiple_of(me * LANE, LANE), LANE)], dwot_out),
                (wet, dwet_out),
                (pos_g, dpos_out),
                (head_g, dhead_out),
            )
            pos_again.wait()
            pos_g[...] = share * (pos_r[...] - pos_f[...])
            head_g[...] = share * (head[...].astype(F32) - head_f[...])
            copies = [
                pltpu.make_async_copy(src, dst, osem.at[i]) for i, (src, dst) in enumerate(outs)
            ]
            for copy in copies:
                copy.start()
            dvec_out[...] = share * (vec_in[...] - vec_f[...])
            dbias_out[...] = share * (bias_in[...] - bias_f[...])
            low_d_out[...] = low_d[...]
            low_a_out[...] = share * factors
            for copy in copies:
                copy.wait()

        return carry

    lax.fori_loop(0, steps, one_step, 0)


def local_training(live, patches, hot, wqkv, w1, wot, w2t, wet, head, pos, vec, bias, seq, classes):
    steps = patches.shape[0]
    pad = pos.shape[0]
    width = pos.shape[1]
    n_all = 4 * pad
    wide = wot.shape[1]
    n_head = head.shape[0]
    n_low = steps * SMALL
    vmem = pltpu.VMEM
    dma = pltpu.SemaphoreType.DMA
    anywhere = pl.BlockSpec(memory_space=pl.ANY)
    inside = pl.BlockSpec(memory_space=pltpu.VMEM)
    square = (width, width)
    out_shape = (
        jax.ShapeDtypeStruct(square, BF16),
        jax.ShapeDtypeStruct(square, BF16),
        jax.ShapeDtypeStruct((width, LANE), BF16),
        jax.ShapeDtypeStruct(square, BF16),
        jax.ShapeDtypeStruct((pad, width), F32),
        jax.ShapeDtypeStruct((n_head, width), F32),
        jax.ShapeDtypeStruct((SMALL, width), F32),
        jax.ShapeDtypeStruct((8, width), F32),
        jax.ShapeDtypeStruct((n_low, width), BF16),
        jax.ShapeDtypeStruct((n_low, width), F32),
        jax.ShapeDtypeStruct((8, 128), F32),
        jax.ShapeDtypeStruct((steps, 8, 128), F32),
    )
    scratch = [
        vmem(square, BF16), vmem(square, BF16), vmem((width, wide), BF16), vmem(square, BF16),
        vmem(square, BF16), vmem((n_head, width), BF16),
    ]
    for _ in range(2):
        scratch += [
            vmem(square, F32), vmem(square, F32), vmem((width, wide), F32), vmem(square, F32),
            vmem((pad, width), F32), vmem((n_head, width), F32), vmem((SMALL, width), F32),
            vmem((8, width), F32),
        ]
    scratch += [
        vmem(square, F32), vmem((width, wide), F32), vmem((pad, width), F32),
        vmem((n_head, width), F32), vmem((SMALL, width), F32),
        vmem((2, n_all, width), BF16), vmem((n_all, width), F32), vmem((n_all, width), F32),
        vmem((12, pad, pad), BF16), vmem((n_all, width), BF16), vmem((n_all, width), BF16),
        vmem((n_all, wide), BF16), vmem((n_all, width), BF16), vmem((n_all, width), BF16),
        vmem((2, pad, width), F32), vmem((n_all, width), BF16), vmem((2, pad, width), F32),
        vmem((4, 8, width), F32), vmem((4, 8, width), F32), vmem((SMALL, width), F32),
        vmem((8, width), F32), vmem((6, 8, width), F32), vmem((4, 8, width), F32),
        vmem((n_low, width), BF16), vmem((n_low, width), F32), vmem((n_low, 128), F32),
        vmem((n_low, 128), F32), vmem((8, 8, width), F32),
        vmem((2, pad, width), BF16), vmem((2, pad, width), BF16), vmem((2, pad, width), BF16),
        vmem((4, pad, width), BF16), vmem((SMALL, width), F32), vmem((4, SMALL, width), F32),
        vmem((8, 128), F32), vmem((4, 8, 128), F32), vmem((pad, width), F32),
        vmem((6, 8, width), F32),
        dma((8,)), dma((2,)), dma((4,)), dma((4,)), dma((4,)), dma((4,)), dma((4,)), dma((4,)),
        dma((2,)), dma((2,)), dma((4,)), dma((4,)), dma((4,)), dma((4,)), dma((2,)), dma((2,)),
        dma((3,)), dma((3,)), dma((3,)), dma((3,)), dma((6,)),
    ]
    return pl.pallas_call(
        functools.partial(train_kernel, (steps, seq, pad, classes)),
        out_shape=out_shape,
        in_specs=[pl.BlockSpec(memory_space=pltpu.SMEM), anywhere, inside]
        + [anywhere] * 7 + [inside] * 2,
        out_specs=(anywhere,) * 6 + (inside,) * 6,
        scratch_shapes=scratch,
        compiler_params=pltpu.CompilerParams(
            collective_id=0, has_side_effects=True, vmem_limit_bytes=VMEM_LIMIT
        ),
        name="local_training",
    )(live, patches, hot, wqkv, w1, wot, w2t, wet, head, pos, vec, bias)


def place_patches(chosen_ref, pool_ref, out_ref):
    seq_rows, width = pool_ref.shape[1], pool_ref.shape[2]
    pad = out_ref.shape[1]
    below = jnp.zeros((pad - 1 - seq_rows, width), F32)
    whole = jnp.concatenate([jnp.zeros((1, width), F32), pool_ref[0].astype(F32), below], 0)
    out_ref[0] = whole.astype(BF16)


def pick_patches(pool, chosen, pad):
    count = chosen.shape[0]
    _, patch_rows, width = pool.shape
    return pl.pallas_call(
        place_patches,
        out_shape=jax.ShapeDtypeStruct((count, pad, width), BF16),
        grid_spec=pltpu.PrefetchScalarGridSpec(
            num_scalar_prefetch=1,
            grid=(count,),
            in_specs=[pl.BlockSpec((1, patch_rows, width), lambda i, ids: (ids[i], 0, 0))],
            out_specs=pl.BlockSpec((1, pad, width), lambda i, ids: (i, 0, 0)),
        ),
        name="pick_patches",
    )(chosen, pool)


def adam(master, first, second, grad):
    first2 = BETA_ONE * first + (1.0 - BETA_ONE) * grad
    second2 = BETA_TWO * second + (1.0 - BETA_TWO) * grad * grad
    moved = (
        first2 / (1.0 - BETA_ONE**ROUND) / (jnp.sqrt(second2 / (1.0 - BETA_TWO**ROUND)) + ADAM_EPS)
    )
    fresh = master - SERVER_RATE * (moved + WEIGHT_DECAY * master)
    return (fresh, first2, second2, fresh.astype(jnp.bfloat16))


def on_device(
    pool, index, tau, counts, labels,
    in_bf, out_bf, table_bf, bias_bf,
    in_master, out_master, table_master, bias_master,
    in_first, out_first, table_first, bias_first,
    in_second, out_second, table_second, bias_second,
):
    clients = lax.axis_size("client")
    group = in_bf.shape[2]
    steps, images = index.shape[1], index.shape[2]
    patch_rows, features = pool.shape[1], pool.shape[2]
    seq = patch_rows + 1
    pad = (seq + 15) // 16 * 16
    in_full = lax.all_gather(in_bf, "client", axis=1, tiled=True)
    out_t = jnp.transpose(out_bf, (2, 0, 1))
    out_full = lax.all_gather(out_t, "client", axis=0, tiled=True)
    table_full = lax.all_gather(table_bf.T, "client", axis=0, tiled=True)
    width = in_full.shape[1]
    classes = table_full.shape[1] - features - seq - 9

    def lanes(value):
        return jnp.pad(value, [(0, 0)] * (value.ndim - 1) + [(0, LANE - group)])

    wqkv = jnp.transpose(lanes(in_full[:3]), (1, 0, 2)).reshape(width, 3 * LANE)
    w1 = jnp.transpose(in_full[3:], (1, 0, 2)).reshape(width, 4 * group)
    w2t = out_full[:, 1:].reshape(width, 4 * group)
    wot_own = lanes(out_full[:, 0])
    wot = lax.all_gather(wot_own, "tensor", axis=1, tiled=True)
    wet = table_full[:, :features]
    rest = table_full[:, features:].T
    head_rows = (classes + 127) // 128 * 128
    pos = jnp.pad(rest[:seq].astype(F32), ((0, pad - seq), (0, 0)))
    vec = jnp.pad(rest[seq : seq + 9].astype(F32), ((0, SMALL - 9), (0, 0)))
    head = jnp.pad(rest[seq + 9 :], ((0, head_rows - classes), (0, 0)))
    bias = jnp.broadcast_to(bias_bf.astype(F32).reshape(1, 4 * group), (8, 4 * group))

    taken = tau[0]
    ladder = jnp.arange(steps, dtype=jnp.int32)
    live = (ladder < taken).astype(F32)
    factor_sum = jnp.sum(
        jnp.where(
            ladder < taken,
            (1.0 - MOMENTUM_RHO ** (ladder + 1).astype(F32)) / (1.0 - MOMENTUM_RHO),
            0.0,
        )
    )
    examples = counts[0].astype(F32)
    share = examples / factor_sum
    scalars = jnp.stack(
        [live, jnp.where(ladder < taken, MOMENTUM_RHO, 1.0), jnp.full((steps,), share)]
    )
    patches = pick_patches(pool, index[0].reshape(steps * images), pad)
    patches = patches.reshape(steps, images * pad, features)
    slots = jnp.arange(pool.shape[0], dtype=jnp.int32)
    picked = index[0][:, :, None] == slots[None, None, :]
    target = jnp.sum(picked.astype(jnp.int32) * labels[None, None, :], 2)
    hot = (target[:, :, None] == jnp.arange(head_rows, dtype=jnp.int32)).astype(F32)
    hot = jnp.pad(hot, ((0, 0), (0, SMALL - images), (0, 0)))

    (
        d_wqkv, d_w1, d_wot, d_wet, d_pos, d_head, d_vec, d_bias, low_d, low_a, loss_sum, norms,
    ) = local_training(
        scalars, patches, hot, wqkv, w1, wot, w2t, wet, head, pos, vec, bias, seq, classes
    )

    first_member = (lax.axis_index("tensor") == 0).astype(F32)
    norms = lax.psum(norms[:, 0, 0] * first_member, "tensor")
    loss_sum = loss_sum[0, 0]
    total_c, weighted_factor, bias_delta = lax.psum(
        (examples, examples * factor_sum, d_bias[:1].reshape(4, group)), "client"
    )
    weighted_loss = lax.psum(
        first_member * examples * loss_sum / taken.astype(F32), ("client", "tensor")
    )

    def scatter(value):
        return lax.psum_scatter(
            value.astype(BF16), "client", scatter_dimension=0, tiled=True
        ).astype(F32)

    mine = scatter(jnp.concatenate([d_wqkv, d_w1, d_wot], 1))
    own = mine.shape[0]
    d_qkv = jnp.transpose(mine[:, : 3 * LANE].reshape(own, 3, LANE)[..., :group], (1, 0, 2))
    d_up = jnp.transpose(mine[:, 3 * LANE : 3 * LANE + 4 * group].reshape(own, 4, group), (1, 0, 2))
    in_delta = jnp.concatenate([d_qkv, d_up], 0)
    d_wo = mine[:, 3 * LANE + 4 * group :][:, :group].T
    all_d = lax.all_gather(low_d, "client", axis=0, tiled=True)
    all_a = lax.all_gather(low_a, "client", axis=0, tiled=True)
    at = lax.axis_index("client") * own
    part_d = lax.dynamic_slice_in_dim(all_d, at, own, 1).astype(F32)
    d_w2 = jnp.einsum("rc,rd->cd", all_a, part_d, precision=lax.Precision.HIGHEST)
    out_delta = jnp.concatenate([d_wo[None], d_w2.reshape(4, group, own)], 0)
    small = jnp.concatenate([d_pos[:seq], d_vec[:9], d_head[:classes]], 0).T.astype(BF16)
    d_table = jnp.concatenate([d_wet, small], 1)
    d_table = jnp.where(first_member > 0, d_table, jnp.zeros_like(d_table))
    table_delta = lax.psum(scatter(d_table), "tensor").T
    server_scale = weighted_factor / total_c / total_c
    masters = (in_master, out_master, table_master, bias_master)
    firsts = (in_first, out_first, table_first, bias_first)
    seconds = (in_second, out_second, table_second, bias_second)
    deltas = (in_delta, out_delta, table_delta, bias_delta)
    results = [
        adam(mst, fst, snd, server_scale * dlt)
        for mst, fst, snd, dlt in zip(masters, firsts, seconds, deltas)
    ]
    return (
        weighted_loss / total_c,
        norms[None],
        *[r[0] for r in results],
        *[r[1] for r in results],
        *[r[2] for r in results],
        *[r[3] for r in results],
    )


def solution(mesh):
    by_client = P("client", None, None)
    state = (P(None, "client", "tensor"), P(None, "tensor", "client"), P(None, "client"), P(None, "tensor"))
    in_specs = (by_client, by_client, P("client"), P("client"), P("client")) + state * 4
    out_specs = (P(), P("client", None)) + state * 4
    return jax.shard_map(
        on_device, mesh=mesh, in_specs=in_specs, out_specs=out_specs, check_vma=False
    )
```

```python
import functools

import jax
import jax.numpy as jnp
from jax import lax
from jax.experimental import pallas as pl
from jax.experimental.pallas import tpu as pltpu
from jax.sharding import PartitionSpec as P

HEAD_DIM = 64
ROUND = 5
EPS_NORM = 1e-06
MOMENTUM_RHO = 0.9
LOCAL_RATE = 0.05
CLIP_LIMIT = 1.0
BETA_ONE = 0.5
BETA_TWO = 0.7
ADAM_EPS = 1e-08
WEIGHT_DECAY = 0.05
SERVER_RATE = 0.05
SQRT_HALF = 0.7071067811865476
INV_ROOT_TAU = 0.3989422804014327
MESH = pl.DeviceIdType.MESH
F32 = jnp.float32
BF16 = jnp.bfloat16
NEG = -1e30
LANE = 256
SMALL = 16
REST = 512
VMEM_LIMIT = 67043328


def dot(left, right, dims):
    return lax.dot_general(left, right, (dims, ((), ())), preferred_element_type=F32)


def nn(left, right):
    return dot(left, right, ((1,), (0,)))


def nt(left, right):
    return dot(left, right, ((1,), (1,)))


def tn(left, right):
    return dot(left, right, ((0,), (0,)))


def fold(value):
    rows, width = value.shape
    return jnp.sum(value.reshape(rows // 8, 8, width), 0)


def total(value):
    return jnp.sum(jnp.sum(value, 1, keepdims=True), 0, keepdims=True)


def normalise(value):
    centre = value - jnp.mean(value, -1, keepdims=True)
    inverse = lax.rsqrt(jnp.mean(centre * centre, -1, keepdims=True) + EPS_NORM)
    return (centre * inverse, inverse)


def norm_grad(grad, gain, normed, inverse):
    scaled = grad * gain
    return inverse * (
        scaled
        - jnp.mean(scaled, -1, keepdims=True)
        - normed * jnp.mean(scaled * normed, -1, keepdims=True)
    )


def split_two(value):
    high = value.astype(BF16)
    return (high, (value - high.astype(F32)).astype(BF16))


def train_kernel(
    sizes,
    live_ref,
    x_hbm,
    hot_ref,
    main_in,
    wot_in,
    table_in,
    bias_in,
    main_out,
    table_out,
    dbias_out,
    low_d_out,
    low_a_out,
    loss_out,
    norm_out,
    wqkv, w1, wot, w2t, wet, head,
    wqkv_f, w1_f, wot_f, wet_f, pos_f, head_f, vec_f, bias_f,
    wqkv_m, w1_m, wot_m, wet_m, pos_m, head_m, vec_m, bias_m,
    wqkv_g, wot_g, pos_g, head_g, vec_g,
    xbuf, h0, slope, prob, abuf, qkv, oall, ubuf, dpre, h1own, datt, chip,
    hsum, asum, dact, bsum, vacc, ssq,
    low_d, low_a, low_b, low_w, scal,
    s1, r1, s2, r2, mx_s, mx_r, nx_s, nx_r, pos_r, vec_r,
    wsem, xsem, o_ps, o_xs, o_fs, o_pr, o_xr, o_fr,
    a1s, a1r, a2s, a2r, das, dar, pvs, pvr, mxs, mxr, nxs, nxr, osem,
):
    steps, seq, pad, classes = sizes
    width = 768
    rows_all = 4 * pad
    me = lax.axis_index("tensor")
    core = lax.rem(me, 2)
    mate = me + 1 - 2 * core
    across = lax.rem(me + 2, 4)
    own0 = 2 * core
    oth0 = 2 - 2 * core

    def rows(n):
        return pl.ds(pl.multiple_of(n * pad, 16), pad)

    def remote(src, dst, send, recv, device):
        return pltpu.make_async_remote_copy(
            src_ref=src, dst_ref=dst, send_sem=send, recv_sem=recv,
            device_id={"tensor": device}, device_id_type=MESH,
        )

    rest = dpre.at[0:width, 0:REST]
    weights_in = (
        main_in.at[:, 0:width],
        main_in.at[:, width : 2 * width],
        wot_in,
        main_in.at[:, 2 * width : 3 * width],
        table_in.at[:, 0:width],
        table_in.at[:, width : width + REST],
    )
    weights = (wqkv, w1, wot, w2t, wet, rest)

    def load(which):
        return pltpu.make_async_copy(weights_in[which], weights[which], wsem.at[which])

    def fetch(step, slot):
        return pltpu.make_async_copy(x_hbm.at[step], xbuf.at[slot], xsem.at[slot])

    barrier = pltpu.get_barrier_semaphore()
    for shift in (1, 2, 3):
        pl.semaphore_signal(
            barrier, inc=1, device_id={"tensor": lax.rem(me + shift, 4)}, device_id_type=MESH
        )
    fetch(0, 0).start()
    for which in range(6):
        load(which).start()
    bias_f[...] = bias_in[...]
    for zero in (pos_m, head_m, vec_m, bias_m, low_a, low_b, low_w, loss_out):
        zero[...] = jnp.zeros_like(zero)
    low_d[...] = jnp.zeros_like(low_d)
    for which in range(6):
        load(which).wait()
    vec_at, head_at = pad, pad + SMALL
    n_head = head.shape[0]
    turned = jnp.transpose(rest[...].astype(F32))
    pos_f[...] = turned[:pad]
    vec_f[...] = turned[vec_at : vec_at + SMALL]
    head_f[...] = turned[head_at : head_at + n_head]
    head[...] = turned[head_at : head_at + n_head].astype(BF16)

    def start_rows(j, carry):
        at = pl.ds(pl.multiple_of(j * 32, 32), 32)
        for low, full, mom in (
            (wqkv, wqkv_f, wqkv_m), (w1, w1_f, w1_m), (wot, wot_f, wot_m), (wet, wet_f, wet_m)
        ):
            full[at, :] = low[at, :].astype(F32)
            mom[at, :] = jnp.zeros((32, mom.shape[1]), F32)
        return carry

    lax.fori_loop(0, width // 32, start_rows, 0)
    pl.semaphore_wait(barrier, 3)

    row_id = lax.broadcasted_iota(jnp.int32, (pad, 1), 0)
    token = row_id < seq
    key_ok = lax.broadcasted_iota(jnp.int32, (1, pad), 1) < seq
    lane_head = lax.broadcasted_iota(jnp.int32, (1, LANE), 1) // HEAD_DIM
    small_ok = lax.broadcasted_iota(jnp.int32, (SMALL, 1), 0) < 4
    scale = HEAD_DIM ** (-0.5)

    def of_head(value, h):
        return jnp.where(lane_head == h, value, jnp.zeros_like(value))

    def o_place(n, group):
        return oall.at[rows(n), pl.ds(pl.multiple_of(group * LANE, LANE), LANE)]

    def o_to_mate(n):
        place = o_place(n, me)
        return remote(place, place, o_ps.at[n], o_pr.at[n], mate)

    def o_across(n):
        place = o_place(n, me)
        return remote(place, place, o_xs.at[n], o_xr.at[n], across)

    def o_forward(n):
        place = o_place(n, across)
        return remote(place, place, o_fs.at[n], o_fr.at[n], mate)

    def to_mate(n):
        return remote(s1.at[n], r1.at[n], a1s.at[n], a1r.at[n], mate)

    def to_across(which, n):
        return remote(s2.at[n], r2.at[2 * which + n], a2s.at[2 * which + n], a2r.at[2 * which + n], across)

    def gradient_to_mate(buffer, which, image, k):
        return remote(
            buffer.at[rows(image)], buffer.at[rows(image)],
            das.at[2 * which + k], dar.at[2 * which + k], mate,
        )

    def pos_to_mate():
        return remote(pos_g, pos_r, pvs.at[0], pvr.at[0], mate)

    def vec_to_mate():
        return remote(vacc, vec_r, pvs.at[1], pvr.at[1], mate)

    def spread(src, dst, send, recv, shift):
        return remote(
            src, dst.at[me], send.at[shift - 1], recv.at[shift - 1], lax.rem(me + shift, 4)
        )

    def one_step(step, carry):
        slot = lax.rem(step, 2)
        fetch(step, slot).wait()

        @pl.when(step < steps - 1)
        def _():
            fetch(step + 1, 1 - slot).start()

        gain1, shift1 = vec_f[0:1, :], vec_f[1:2, :]
        gain2, shift2 = vec_f[2:3, :], vec_f[3:4, :]
        gain3, shift3 = vec_f[4:5, :], vec_f[5:6, :]

        def attend(n, carry):
            @pl.when(n >= 1)
            def _():
                remote(
                    o_place(n - 1, across), o_place(n - 1, across), o_xs.at[n - 1], o_xr.at[n - 1], across
                ).wait_recv()
                o_forward(n - 1).start()

            inside = (row_id >= 1) & token
            state = (
                nt(xbuf[slot, rows(n), :], wet[...])
                + pos_f[...]
                + jnp.where(inside, vec_f[6:7, :], 0.0)
            )
            h0[rows(n), :] = state
            normed, _ = normalise(state)
            a = (normed * gain1 + shift1).astype(BF16)
            abuf[rows(n), :] = a
            projected = nn(a, wqkv[...]).astype(BF16)
            qkv[rows(n), :] = projected
            q, k, v = projected[:, :LANE], projected[:, LANE : 2 * LANE], projected[:, 2 * LANE :]
            out = jnp.zeros((pad, LANE), F32)
            for h in range(3):
                scores = jnp.where(key_ok, nt(of_head(q, h), k) * scale, NEG)
                expd = jnp.exp(scores - jnp.max(scores, -1, keepdims=True))
                p = (expd / jnp.sum(expd, -1, keepdims=True)).astype(BF16)
                prob[n * 3 + h] = p
                out = out + nn(p, of_head(v, h))
            o_place(n, me)[...] = out.astype(BF16)
            o_to_mate(n).start()
            o_across(n).start()
            return carry

        lax.fori_loop(0, 4, attend, 0)

        def feed(n, carry):
            @pl.when(n == 1)
            def _():
                remote(
                    o_place(3, across), o_place(3, across), o_xs.at[3], o_xr.at[3], across
                ).wait_recv()
                o_forward(3).start()

            remote(o_place(n, mate), o_place(n, mate), o_ps.at[n], o_pr.at[n], mate).wait_recv()
            diagonal = lax.rem(mate + 2, 4)
            remote(
                o_place(n, diagonal), o_place(n, diagonal), o_fs.at[n], o_fr.at[n], mate
            ).wait_recv()
            state = h0[rows(n), :] + nt(oall[rows(n), :], wot[...]) + vec_f[7:8, :]

            @pl.when(n // 2 == core)
            def _():
                h1own[lax.rem(n, 2)] = state

            hsum[n] = fold(jnp.where(token, state, 0.0))
            normed, _ = normalise(state)
            u = (normed * gain2 + shift2).astype(BF16)
            ubuf[rows(n), :] = u
            z = nn(u, w1[...]) + bias_f[0:1, :]
            cdf = 0.5 * (1.0 + lax.erf(z * SQRT_HALF))
            act = (z * cdf).astype(BF16).astype(F32)
            asum[n] = fold(jnp.where(token, act, 0.0))
            tail = cdf + z * jnp.exp(-0.5 * z * z) * INV_ROOT_TAU
            slope[rows(n), :] = jnp.where(token, tail, 0.0)
            return carry

        lax.fori_loop(0, 4, feed, 0)

        def stack(ref):
            parts = [jnp.sum(ref[n], 0, keepdims=True) for n in range(4)]
            return jnp.concatenate(parts + [jnp.zeros((SMALL - 4, width), F32)], 0)

        act_sum = stack(asum)
        act_hi, act_lo = split_two(act_sum)
        both = nt(jnp.concatenate([act_hi, act_lo], 0), w2t[...])
        mx_s[...] = both[:SMALL] + both[SMALL:]
        for shift in (1, 2, 3):
            spread(mx_s, mx_r, mxs, mxr, shift).start()
        mx_r[me] = mx_s[...]
        h_mean = stack(hsum) * (1.0 / seq)
        for shift in (1, 2, 3):
            remote(
                mx_s, mx_r.at[lax.rem(me + 4 - shift, 4)], mxs.at[shift - 1], mxr.at[shift - 1], mate
            ).wait_recv()
        mlp = mx_r[0] + mx_r[1] + mx_r[2] + mx_r[3]
        average = h_mean + mlp * (1.0 / seq) + vec_f[8:9, :]
        normed3, inverse3 = normalise(average)
        pooled = (normed3 * gain3 + shift3).astype(BF16)
        logits = nt(pooled, head[...])
        class_ok = lax.broadcasted_iota(jnp.int32, (1, head.shape[0]), 1) < classes
        logits = jnp.where(class_ok, logits, NEG)
        top = jnp.max(logits, -1, keepdims=True)
        exp_l = jnp.exp(logits - top)
        total_l = jnp.sum(exp_l, -1, keepdims=True)
        hot = hot_ref[step]
        each = top + jnp.log(total_l) - jnp.sum(jnp.where(class_ok, logits, 0.0) * hot, -1, keepdims=True)
        loss = jnp.sum(jnp.where(small_ok, each, 0.0), 0, keepdims=True) * 0.25
        live = live_ref[0, step]
        rho = live_ref[1, step]
        loss_tile = live * loss
        d_logits = jnp.where(small_ok, (exp_l / total_l - hot) * 0.25, 0.0).astype(BF16)
        d_head = tn(d_logits, pooled)
        head_g[...] = d_head
        d_pooled = nn(d_logits, head[...])
        d_average = norm_grad(d_pooled, gain3, normed3, inverse3)
        d_token = d_average * (1.0 / seq)
        d_mlp = d_token.astype(BF16)
        dact[...] = nn(d_mlp, w2t[...])
        for r in range(4):
            scal[r] = jnp.broadcast_to(d_token[r : r + 1, :], (8, width))
        vec_g[...] = jnp.zeros_like(vec_g)
        vec_g[4:5, :] = jnp.sum(d_pooled * normed3, 0, keepdims=True)
        vec_g[5:6, :] = jnp.sum(d_pooled, 0, keepdims=True)
        vec_g[8:9, :] = jnp.sum(d_average, 0, keepdims=True)
        low_at = pl.ds(pl.multiple_of(step * SMALL, SMALL), SMALL)
        low_d[low_at, :] = d_mlp
        low_a[low_at, :] = act_sum
        gram_d = nt(d_mlp, d_mlp)
        gram_a = nt(act_hi, act_hi) + nt(act_hi, act_lo) + nt(act_lo, act_hi)
        own_squares = total(gram_d * gram_a)

        for n in range(4):
            scal[4 + n] = jnp.broadcast_to(dact[n : n + 1, :], (8, width))
        bsum[...] = jnp.zeros_like(bsum)
        vacc[...] = jnp.zeros_like(vacc)

        def upper_partial(n):
            g = (scal[4 + n][0:1, :] * slope[rows(n), :]).astype(BF16)
            dpre[rows(n), :] = g
            bsum[...] = bsum[...] + fold(g.astype(F32))
            return nt(g, w1[...])

        for k in (0, 1):
            s1[k] = upper_partial(oth0 + k).astype(BF16)
            to_mate(k).start()
            own = upper_partial(own0 + k)
            to_mate(k).wait_recv()
            own = own + r1[k].astype(F32)
            chip[k] = own
            s2[k] = own.astype(BF16)
            to_across(0, k).start()

        ssq[...] = jnp.zeros_like(ssq)
        w1_g = slope

        def weight_grad(left, right, out, which):
            def tile(j, carry):
                at = pl.ds(pl.multiple_of(j * LANE, LANE), LANE)
                g = tn(left[:, at], right[...])
                out[at, :] = g
                if g.shape[1] > width:
                    squares = fold(g * g)
                    ssq[which] = ssq[which] + squares[:, :width]
                    ssq[which, :, : g.shape[1] - width] = (
                        ssq[which, :, : g.shape[1] - width] + squares[:, width:]
                    )
                else:
                    ssq[which] = ssq[which] + fold(g * g)
                return carry

            lax.fori_loop(0, width // LANE, tile, 0)

        weight_grad(ubuf, dpre, w1_g, 0)

        def attention_partial(n):
            d_ctx = nn(
                datt[rows(n), :], wot[:, pl.ds(pl.multiple_of(me * LANE, LANE), LANE)]
            ).astype(BF16)
            projected = qkv[rows(n), :]
            q, k, v = projected[:, :LANE], projected[:, LANE : 2 * LANE], projected[:, 2 * LANE :]
            d_q = jnp.zeros((pad, LANE), F32)
            d_k = jnp.zeros((pad, LANE), F32)
            d_v = jnp.zeros((pad, LANE), F32)
            for h in range(3):
                part = of_head(d_ctx, h)
                p = prob[n * 3 + h]
                again = p.astype(F32)
                d_p = nt(part, v)
                inner = d_p - jnp.sum(d_p * again, -1, keepdims=True)
                d_s = (again * inner).astype(BF16)
                d_v = d_v + tn(p, part)
                d_q = d_q + nn(d_s, of_head(k, h))
                d_k = d_k + tn(d_s, of_head(q, h))
            d_all = jnp.concatenate([d_q * scale, d_k * scale, d_v], 1).astype(BF16)
            qkv[rows(n), :] = d_all
            return nt(d_all, wqkv[...])

        for k in (0, 1):
            to_across(0, k).wait_recv()
            d_upper = chip[k] + r2[k].astype(F32)
            normed, inverse = normalise(h1own[k])
            d_state = norm_grad(d_upper, gain2, normed, inverse) + scal[own0 + k][0:1, :]
            d_state = jnp.where(token, d_state, 0.0)
            h1own[k] = d_state
            datt[rows(own0 + k), :] = d_state.astype(BF16)
            gradient_to_mate(datt, 0, own0 + k, k).start()
            vacc[0] = vacc[0] + fold(d_upper * normed)
            vacc[1] = vacc[1] + fold(d_upper)
            vacc[2] = vacc[2] + fold(d_state)
            own = attention_partial(own0 + k)
            remote(
                datt.at[rows(oth0 + k)], datt.at[rows(oth0 + k)], das.at[k], dar.at[k], mate
            ).wait_recv()
            other = attention_partial(oth0 + k)
            to_mate(k).wait_send()
            s1[k] = other.astype(BF16)
            to_mate(k).start()
            to_mate(k).wait_recv()
            own = own + r1[k].astype(F32)
            chip[k] = own
            to_across(0, k).wait_send()
            s2[k] = own.astype(BF16)
            to_across(1, k).start()

        weight_grad(datt, oall, wot_g, 1)
        weight_grad(abuf, qkv, wqkv_g, 2)

        d_emb = ubuf
        d_pos = jnp.zeros((pad, width), F32)
        for k in (0, 1):
            to_across(1, k).wait_recv()
            d_normed = chip[k] + r2[2 + k].astype(F32)
            normed, inverse = normalise(h0[rows(own0 + k), :])
            d_state = h1own[k] + norm_grad(d_normed, gain1, normed, inverse)
            d_emb[rows(own0 + k), :] = d_state.astype(BF16)
            gradient_to_mate(d_emb, 1, own0 + k, k).start()
            vacc[3] = vacc[3] + fold(d_normed * normed)
            vacc[4] = vacc[4] + fold(d_normed)
            vacc[5] = vacc[5] + fold(jnp.where(row_id >= 1, d_state, 0.0))
            d_pos = d_pos + d_state
        pos_g[...] = d_pos
        pos_to_mate().start()
        vec_to_mate().start()
        wet_g = h0
        for k in (0, 1):
            remote(
                d_emb.at[rows(oth0 + k)], d_emb.at[rows(oth0 + k)], das.at[2 + k], dar.at[2 + k], mate
            ).wait_recv()
        weight_grad(d_emb, xbuf.at[slot], wet_g, 3)
        pos_to_mate().wait()
        vec_to_mate().wait()
        pos_g[...] = pos_g[...] + pos_r[...]
        sums = [jnp.sum(vacc[r] + vec_r[r], 0, keepdims=True) for r in range(6)]
        vec_g[0:1, :] = sums[3]
        vec_g[1:2, :] = sums[4]
        vec_g[2:3, :] = sums[0]
        vec_g[3:4, :] = sums[1]
        vec_g[6:7, :] = sums[5]
        vec_g[7:8, :] = sums[2]
        d_bias = jnp.sum(bsum[...], 0, keepdims=True)
        shared = (
            total(ssq[1] + ssq[3] + fold(pos_g[...] * pos_g[...]) + fold(head_g[...] * head_g[...]))
            + total(vec_g[...] * vec_g[...])
        )
        own_squares = own_squares + total(ssq[0] + ssq[2]) + total(d_bias * d_bias)
        for n in range(4):
            o_to_mate(n).wait_send()
            o_across(n).wait_send()
            o_forward(n).wait_send()
        for k in (0, 1):
            to_mate(k).wait_send()
            to_across(1, k).wait_send()
            gradient_to_mate(datt, 0, own0 + k, k).wait_send()
            gradient_to_mate(d_emb, 1, own0 + k, k).wait_send()
        for shift in (1, 2, 3):
            spread(mx_s, mx_r, mxs, mxr, shift).wait_send()
        first_lane = lax.broadcasted_iota(jnp.int32, (8, 128), 1) < 64
        nx_s[...] = jnp.where(first_lane, own_squares + 0.25 * shared, loss_tile)
        for shift in (1, 2, 3):
            spread(nx_s, nx_r, nxs, nxr, shift).start()
        nx_r[me] = nx_s[...]

        load(3).start()

        @pl.when(step == steps - 1)
        def _():
            for which in (0, 1, 2, 4, 5):
                load(which).start()

        for shift in (1, 2, 3):
            remote(
                nx_s, nx_r.at[lax.rem(me + 4 - shift, 4)], nxs.at[shift - 1], nxr.at[shift - 1], mate
            ).wait_recv()
        norm = jnp.sqrt((nx_r[0] + nx_r[1] + nx_r[2] + nx_r[3]))
        factor = live * (CLIP_LIMIT / jnp.maximum(norm, CLIP_LIMIT))
        norm_out[step] = live * norm
        loss_out[...] = loss_out[...] + nx_r[0]
        for shift in (1, 2, 3):
            spread(nx_s, nx_r, nxs, nxr, shift).wait_send()
        fac = factor[0:1, 0:1]

        low_row = lax.broadcasted_iota(jnp.int32, low_b.shape, 0) // SMALL
        low_b[...] = jnp.where(low_row == step, fac, rho * low_b[...])
        low_w[...] = low_w[...] + live * low_b[...]
        factors = (LOCAL_RATE * low_w[:, 0:1]) * low_a[...]
        low_hi, low_lo = split_two(factors)
        pair = jnp.concatenate([low_hi, low_lo], 0)
        load(3).wait()

        def low_rank(j, carry):
            at = pl.ds(pl.multiple_of(j * LANE, LANE), LANE)
            moved = tn(jnp.concatenate([low_d[:, at], low_d[:, at]], 0), pair)
            w2t[at, :] = (w2t[at, :].astype(F32) - moved).astype(BF16)
            return carry

        lax.fori_loop(0, width // LANE, low_rank, 0)

        def small_update(full, mom, grad):
            mom[...] = rho * mom[...] + fac * grad
            full[...] = full[...] - (live * LOCAL_RATE) * mom[...]

        small_update(pos_f, pos_m, pos_g[...])
        small_update(vec_f, vec_m, vec_g[...])
        small_update(bias_f, bias_m, jnp.broadcast_to(d_bias, (8, width)))
        small_update(head_f, head_m, head_g[...])
        table = (
            (wqkv, wqkv_f, wqkv_m, wqkv_g),
            (w1, w1_f, w1_m, w1_g),
            (wot, wot_f, wot_m, wot_g),
            (wet, wet_f, wet_m, wet_g),
        )

        @pl.when(step < steps - 1)
        def _():
            head[...] = head_f[...].astype(BF16)

            def update(j, carry):
                at = pl.ds(pl.multiple_of(j * 16, 16), 16)
                for low, full, mom, grad in table:
                    m = rho * mom[at, :] + fac * grad[at, :]
                    mom[at, :] = m
                    w = full[at, :] - (live * LOCAL_RATE) * m
                    full[at, :] = w
                    low[at, :] = w.astype(BF16)
                return carry

            lax.fori_loop(0, width // 16, update, 0)

        @pl.when(step == steps - 1)
        def _():
            share = live_ref[2, 0]
            for which in (0, 1, 2, 4, 5):
                load(which).wait()

            def finish(j, carry):
                at = pl.ds(pl.multiple_of(j * 16, 16), 16)
                for low, full, mom, grad in table:
                    m = rho * mom[at, :] + fac * grad[at, :]
                    w = full[at, :] - (live * LOCAL_RATE) * m
                    low[at, :] = (share * (low[at, :].astype(F32) - w)).astype(BF16)
                return carry

            lax.fori_loop(0, width // 16, finish, 0)
            h0[0:REST, :] = jnp.transpose(rest[...].astype(F32))
            for ref, low_row, count in ((pos_f, 0, pad), (vec_f, vec_at, SMALL), (head_f, head_at, n_head)):
                place = pl.ds(low_row, count)
                h0[place, :] = share * (h0[place, :] - ref[...])
            rest[...] = jnp.transpose(h0[0:REST, :]).astype(BF16)
            outs = (
                (wqkv, main_out.at[:, 0:width]),
                (w1, main_out.at[:, width : 2 * width]),
                (
                    wot.at[:, pl.ds(pl.multiple_of(me * LANE, LANE), LANE)],
                    main_out.at[:, 2 * width : 2 * width + LANE],
                ),
                (wet, table_out.at[:, 0:width]),
                (rest, table_out.at[:, width : width + REST]),
            )
            copies = [
                pltpu.make_async_copy(src, dst, osem.at[i]) for i, (src, dst) in enumerate(outs)
            ]
            for copy in copies:
                copy.start()
            dbias_out[...] = share * (bias_in[...] - bias_f[...])
            low_d_out[...] = low_d[...]
            low_a_out[...] = share * factors
            for copy in copies:
                copy.wait()

        return carry

    lax.fori_loop(0, steps, one_step, 0)


def local_training(live, patches, hot, main, wot, table, bias, pad, seq, classes):
    steps = patches.shape[0]
    width = main.shape[0]
    n_all = 4 * pad
    wide = wot.shape[1]
    n_head = hot.shape[2]
    n_low = steps * SMALL
    vmem = pltpu.VMEM
    dma = pltpu.SemaphoreType.DMA
    anywhere = pl.BlockSpec(memory_space=pl.ANY)
    inside = pl.BlockSpec(memory_space=pltpu.VMEM)
    square = (width, width)
    out_shape = (
        jax.ShapeDtypeStruct((width, 2 * width + LANE), BF16),
        jax.ShapeDtypeStruct(table.shape, BF16),
        jax.ShapeDtypeStruct((8, width), F32),
        jax.ShapeDtypeStruct((n_low, width), BF16),
        jax.ShapeDtypeStruct((n_low, width), F32),
        jax.ShapeDtypeStruct((8, 128), F32),
        jax.ShapeDtypeStruct((steps, 8, 128), F32),
    )
    scratch = [
        vmem(square, BF16), vmem(square, BF16), vmem((width, wide), BF16), vmem(square, BF16),
        vmem(square, BF16), vmem((n_head, width), BF16),
    ]
    for _ in range(2):
        scratch += [
            vmem(square, F32), vmem(square, F32), vmem((width, wide), F32), vmem(square, F32),
            vmem((pad, width), F32), vmem((n_head, width), F32), vmem((SMALL, width), F32),
            vmem((8, width), F32),
        ]
    scratch += [
        vmem(square, F32), vmem((width, wide), F32), vmem((pad, width), F32),
        vmem((n_head, width), F32), vmem((SMALL, width), F32),
        vmem((2, n_all, width), BF16), vmem((n_all, width), F32), vmem((n_all, width), F32),
        vmem((12, pad, pad), BF16), vmem((n_all, width), BF16), vmem((n_all, width), BF16),
        vmem((n_all, wide), BF16), vmem((n_all, width), BF16), vmem((n_all, width), BF16),
        vmem((2, pad, width), F32), vmem((n_all, width), BF16), vmem((2, pad, width), F32),
        vmem((4, 8, width), F32), vmem((4, 8, width), F32), vmem((SMALL, width), F32),
        vmem((8, width), F32), vmem((6, 8, width), F32), vmem((4, 8, width), F32),
        vmem((n_low, width), BF16), vmem((n_low, width), F32), vmem((n_low, 128), F32),
        vmem((n_low, 128), F32), vmem((8, 8, width), F32),
        vmem((2, pad, width), BF16), vmem((2, pad, width), BF16), vmem((2, pad, width), BF16),
        vmem((4, pad, width), BF16), vmem((SMALL, width), F32), vmem((4, SMALL, width), F32),
        vmem((8, 128), F32), vmem((4, 8, 128), F32), vmem((pad, width), F32),
        vmem((6, 8, width), F32),
        dma((8,)), dma((2,)), dma((4,)), dma((4,)), dma((4,)), dma((4,)), dma((4,)), dma((4,)),
        dma((2,)), dma((2,)), dma((4,)), dma((4,)), dma((4,)), dma((4,)), dma((2,)), dma((2,)),
        dma((3,)), dma((3,)), dma((3,)), dma((3,)), dma((6,)),
    ]
    return pl.pallas_call(
        functools.partial(train_kernel, (steps, seq, pad, classes)),
        out_shape=out_shape,
        in_specs=[pl.BlockSpec(memory_space=pltpu.SMEM), anywhere, inside]
        + [anywhere] * 3 + [inside],
        out_specs=(anywhere,) * 2 + (inside,) * 5,
        scratch_shapes=scratch,
        compiler_params=pltpu.CompilerParams(
            collective_id=0, has_side_effects=True, vmem_limit_bytes=VMEM_LIMIT
        ),
        name="local_training",
    )(live, patches, hot, main, wot, table, bias)


def place_patches(chosen_ref, pool_ref, out_ref):
    seq_rows, width = pool_ref.shape[1], pool_ref.shape[2]
    pad = out_ref.shape[1]
    below = jnp.zeros((pad - 1 - seq_rows, width), F32)
    whole = jnp.concatenate([jnp.zeros((1, width), F32), pool_ref[0].astype(F32), below], 0)
    out_ref[0] = whole.astype(BF16)


def pick_patches(pool, chosen, pad):
    count = chosen.shape[0]
    _, patch_rows, width = pool.shape
    return pl.pallas_call(
        place_patches,
        out_shape=jax.ShapeDtypeStruct((count, pad, width), BF16),
        grid_spec=pltpu.PrefetchScalarGridSpec(
            num_scalar_prefetch=1,
            grid=(count,),
            in_specs=[pl.BlockSpec((1, patch_rows, width), lambda i, ids: (ids[i], 0, 0))],
            out_specs=pl.BlockSpec((1, pad, width), lambda i, ids: (i, 0, 0)),
        ),
        name="pick_patches",
    )(chosen, pool)


def ring_places(clients):
    depth = clients // 2
    client = lax.axis_index("client")
    member = lax.axis_index("tensor")
    core = lax.rem(member, 2)
    return (
        depth, client, client // 2, lax.rem(client, 2), member, core, member // 2,
        member + 1 - 2 * core, lax.rem(member + 2, 4),
    )


def send(src, dst, send_sem, recv_sem, client, member):
    return pltpu.make_async_remote_copy(
        src_ref=src, dst_ref=dst, send_sem=send_sem, recv_sem=recv_sem,
        device_id={"client": client, "tensor": member}, device_id_type=MESH,
    )


def span(start, size, unit):
    return pl.ds(pl.multiple_of(start, unit), size)


def gather_kernel(
    clients, main_ref, wo_ref, table_ref, main_out, wo_out, table_out,
    up_s, up_r, down_s, down_r, y_s, y_r, mate_s, mate_r, x_s, x_r, on_s, on_r, own_sem,
):
    depth, client, z, y, member, core, chip_x, mate, across = ring_places(clients)
    block = main_ref.shape[0]
    half = block // 2
    columns = table_ref.shape[1] // 2
    peer = client + 1 - 2 * y

    def shared(origin, who):
        who_x, who_core = who // 2, lax.rem(who, 2)
        return (
            wo_out.at[span(origin * block, block, block), span(who * LANE, LANE, LANE)],
            table_out.at[
                span(origin * block + who_x * half, half, half),
                span(who_core * columns, columns, 128),
            ],
        )

    def landed(origin):
        return (main_out.at[span(origin * block, block, block), :],) + shared(origin, member)

    own_pieces = (
        main_ref, wo_ref, table_ref.at[span(chip_x * half, half, half), span(core * columns, columns, 128)]
    )

    def pieces(origin, mine):
        return own_pieces if mine else landed(origin)

    def message(origin, mine, send_sem, recv_sem, index, to):
        return [
            send(src, dst, send_sem.at[p, index], recv_sem.at[p, index], to, member)
            for p, (src, dst) in enumerate(zip(pieces(origin, mine), landed(origin)))
        ]

    def up(origin, i, mine=False):
        return message(origin, mine, up_s, up_r, i, client + 2)

    def down(origin, i, mine=False):
        return message(origin, mine, down_s, down_r, i, client - 2)

    def over(origin, mine=False):
        return message(origin, mine, y_s, y_r, origin // 2, peer)

    def give(origin, mine, send_sem, recv_sem, to):
        return [
            send(src, dst, send_sem.at[p, origin], recv_sem.at[p, origin], client, to)
            for p, (src, dst) in enumerate(zip(pieces(origin, mine)[1:], shared(origin, member)))
        ]

    def share(origin, mine=False):
        return give(origin, mine, mate_s, mate_r, mate) + give(origin, mine, x_s, x_r, across)

    def from_across(origin):
        return [
            send(dst, dst, x_s.at[p, origin], x_r.at[p, origin], client, across)
            for p, dst in enumerate(shared(origin, across))
        ]

    def pass_on(origin):
        return [
            send(dst, dst, on_s.at[p, origin], on_r.at[p, origin], client, mate)
            for p, dst in enumerate(shared(origin, across))
        ]

    def start(copies):
        for copy in copies:
            copy.start()

    def arrived(copies):
        for copy in copies:
            copy.wait_recv()

    def sent(copies):
        for copy in copies:
            copy.wait_send()

    has_up, has_down = z < depth - 1, z > 0

    barrier = pltpu.get_barrier_semaphore()

    def hello(to_client, to_member):
        pl.semaphore_signal(
            barrier, inc=1, device_id={"client": to_client, "tensor": to_member}, device_id_type=MESH
        )

    hello(peer, member)
    for shift in (1, 2, 3):
        hello(client, lax.rem(member + shift, 4))
    for shift in range(1, depth):
        hello(2 * lax.rem(z + shift, depth) + y, member)
    pl.semaphore_wait(barrier, 3 + depth)

    start(over(client, True))

    @pl.when(has_up)
    def _():
        start(up(client, 0, True))

    @pl.when(has_down)
    def _():
        start(down(client, 0, True))

    start(share(client, True))
    local = [
        pltpu.make_async_copy(src, dst, own_sem.at[p])
        for p, (src, dst) in enumerate(zip(own_pieces, landed(client)))
    ]
    start(local)

    def line(d, act):
        @pl.when(z >= d)
        def _():
            act(client - 2 * d, True)

        @pl.when(z < depth - d)
        def _():
            act(client + 2 * d, False)

    def across_line(d, act):
        if d == 0:
            act(peer, True)
            return

        @pl.when(z >= d)
        def _():
            act(peer - 2 * d, True)

        @pl.when(z < depth - d)
        def _():
            act(peer + 2 * d, False)

    def line_in(d):
        def act(origin, below):
            if below:
                arrived(message(origin, False, up_s, up_r, d - 1, peer))
                if d < depth - 1:

                    @pl.when(has_up)
                    def _():
                        start(up(origin, d))
            else:
                arrived(message(origin, False, down_s, down_r, d - 1, peer))
                if d < depth - 1:

                    @pl.when(has_down)
                    def _():
                        start(down(origin, d))
            start(over(origin))
            start(share(origin))

        return act

    def y_in(origin, below):
        arrived(over(origin))
        start(share(origin))

    def forward(origin, below=True):
        arrived(from_across(origin))
        start(pass_on(origin))

    for d in range(1, depth + 1):
        if d < depth:
            line(d, line_in(d))
        across_line(d - 1, y_in)
        if d == 1:
            forward(client)
        else:
            line(d - 1, forward)
            across_line(d - 2, forward)
    across_line(depth - 1, forward)

    for copy in local:
        copy.wait()
    for origin in range(clients):
        sent(share(origin))
        sent(pass_on(origin))
        arrived([
            send(dst, dst, mate_s.at[p, origin], mate_r.at[p, origin], client, mate)
            for p, dst in enumerate(shared(origin, mate))
        ])
        arrived([
            send(dst, dst, on_s.at[p, origin], on_r.at[p, origin], client, mate)
            for p, dst in enumerate(shared(origin, lax.rem(mate + 2, 4)))
        ])
    for d in range(depth):
        sent(over(2 * d + y))

        @pl.when(has_up & (z >= d))
        def _():
            if d < depth - 1:
                sent(up(client - 2 * d, d))

        @pl.when(has_down & (z < depth - d))
        def _():
            if d < depth - 1:
                sent(down(client + 2 * d, d))


def gather_weights(clients, main, wo, table):
    depth = clients // 2
    dma = pltpu.SemaphoreType.DMA
    anywhere = pl.BlockSpec(memory_space=pl.ANY)
    inside = pl.BlockSpec(memory_space=pltpu.VMEM)
    width = main.shape[0] * clients
    hops = depth - 1
    return pl.pallas_call(
        functools.partial(gather_kernel, clients),
        out_shape=(
            jax.ShapeDtypeStruct((width, main.shape[1]), BF16),
            jax.ShapeDtypeStruct((width, 4 * wo.shape[1]), BF16),
            jax.ShapeDtypeStruct((width, table.shape[1]), BF16),
        ),
        in_specs=[inside] * 3,
        out_specs=(anywhere,) * 3,
        scratch_shapes=[
            dma((3, hops)), dma((3, hops)), dma((3, hops)), dma((3, hops)), dma((3, depth)),
            dma((3, depth)),
        ] + [dma((2, clients))] * 6 + [dma((3,))],
        compiler_params=pltpu.CompilerParams(collective_id=1, has_side_effects=True),
        name="gather_weights",
    )(main, wo, table)


def reduce_kernel(
    clients, main_in, table_in, low_in, tile_in, main_out, table_out, low_out, tile_out,
    own_main, own_table, y_main, y_table, zs_main, zs_table, zr_main, zr_table, whole, low_all, tile_all,
    own_sem, y_s, y_r, z_s, z_r, low_s, low_r, tile_s, tile_r, q_s, q_r,
):
    depth, client, z, y, member, core, chip_x, mate, across = ring_places(clients)
    block = own_main.shape[1]
    half, columns = own_table.shape[1], own_table.shape[2]
    peer = client + 1 - 2 * y

    def main_rows(owner):
        return main_in.at[span(owner * block, block, block), :]

    def table_part(owner):
        return table_in.at[
            span(owner * block + chip_x * half, half, half), span(core * columns, columns, 128)
        ]

    def own_load(level):
        owner = 2 * level + y
        return [
            pltpu.make_async_copy(main_rows(owner), own_main.at[level], own_sem.at[0, level]),
            pltpu.make_async_copy(table_part(owner), own_table.at[level], own_sem.at[1, level]),
        ]

    def over(level):
        owner = 2 * level + 1 - y
        return [
            send(main_rows(owner), y_main.at[level], y_s.at[0, level], y_r.at[0, level], peer, member),
            send(table_part(owner), y_table.at[level], y_s.at[1, level], y_r.at[1, level], peer, member),
        ]

    def onward(i):
        owner = 2 * lax.rem(z + 1 + i, depth) + y
        return [
            send(zs_main.at[i], zr_main.at[i], z_s.at[0, i], z_r.at[0, i], owner, member),
            send(zs_table.at[i], zr_table.at[i], z_s.at[1, i], z_r.at[1, i], owner, member),
        ]

    def small(shift):
        to = lax.rem(client + shift, clients)
        return [
            send(low_in.at[to], low_all.at[client], low_s.at[shift - 1], low_r.at[shift - 1], to, member),
            send(tile_in, tile_all.at[client], tile_s.at[shift - 1], tile_r.at[shift - 1], to, member),
        ]

    def small_from(shift):
        source = lax.rem(client + clients - shift, clients)
        return [
            send(low_in.at[source], low_all.at[source], low_s.at[shift - 1], low_r.at[shift - 1], source, member),
            send(tile_in, tile_all.at[source], tile_s.at[shift - 1], tile_r.at[shift - 1], source, member),
        ]

    def quarter(who):
        return whole.at[span((who // 2) * half, half, half), span(lax.rem(who, 2) * columns, columns, 128)]

    def pass_quarter(who, index, to):
        return send(quarter(who), quarter(who), q_s.at[index], q_r.at[index], client, to)

    barrier = pltpu.get_barrier_semaphore()
    for shift in range(1, clients):
        pl.semaphore_signal(
            barrier, inc=1,
            device_id={"client": lax.rem(client + shift, clients), "tensor": member}, device_id_type=MESH,
        )
    for shift in (1, 2, 3):
        pl.semaphore_signal(
            barrier, inc=1,
            device_id={"client": client, "tensor": lax.rem(member + shift, 4)}, device_id_type=MESH,
        )
    for i in range(depth):
        for copy in own_load(lax.rem(z + 1 + i, depth)):
            copy.start()
    pl.semaphore_wait(barrier, clients - 1 + 3)
    for i in range(depth):
        for copy in over(lax.rem(z + 1 + i, depth)):
            copy.start()
    for shift in range(1, clients):
        for copy in small(shift):
            copy.start()
    low_all[client] = low_in[client]
    tile_all[client] = tile_in[...]
    for i in range(depth):
        level = lax.rem(z + 1 + i, depth)
        for copy in own_load(level):
            copy.wait()
        for copy in over(level):
            copy.wait_recv()
        for own, came, out, last in (
            (own_main, y_main, zs_main, main_out), (own_table, y_table, zs_table, quarter(member))
        ):
            pair = own[level].astype(F32) + came[level].astype(F32)
            if i < depth - 1:
                out[i] = pair.astype(BF16)
            else:
                last[...] = pair
        if i < depth - 1:
            for copy in onward(i):
                copy.start()
    mine = quarter(member)
    for i in range(depth - 1):
        for copy in onward(i):
            copy.wait_recv()
        main_out[...] = main_out[...] + zr_main[i].astype(F32)
        mine[...] = mine[...] + zr_table[i].astype(F32)
    first = [pass_quarter(member, 0, mate), pass_quarter(member, 1, across)]
    for copy in first:
        copy.start()
    for shift in range(1, clients):
        for copy in small_from(shift):
            copy.wait_recv()
    low_out[...] = low_all[...]
    tile_out[...] = tile_all[...]
    pass_quarter(across, 1, across).wait_recv()
    second = pass_quarter(across, 2, mate)
    second.start()
    pass_quarter(mate, 0, mate).wait_recv()
    pass_quarter(lax.rem(mate + 2, 4), 2, mate).wait_recv()
    table_out[...] = whole[...]
    for copy in first + [second]:
        copy.wait_send()
    for shift in range(1, clients):
        for copy in small(shift):
            copy.wait_send()
    for i in range(depth):
        for copy in over(i):
            copy.wait_send()
        if i < depth - 1:
            for copy in onward(i):
                copy.wait_send()


def reduce_deltas(clients, main, table, low, tile):
    depth = clients // 2
    dma = pltpu.SemaphoreType.DMA
    vmem = pltpu.VMEM
    anywhere = pl.BlockSpec(memory_space=pl.ANY)
    inside = pl.BlockSpec(memory_space=pltpu.VMEM)
    block = main.shape[0] // clients
    half, columns = block // 2, table.shape[1] // 2
    wide = main.shape[1]
    hops = depth - 1
    return pl.pallas_call(
        functools.partial(reduce_kernel, clients),
        out_shape=(
            jax.ShapeDtypeStruct((block, wide), F32),
            jax.ShapeDtypeStruct((block, table.shape[1]), F32),
            jax.ShapeDtypeStruct(low.shape, BF16),
            jax.ShapeDtypeStruct((clients,) + tile.shape, F32),
        ),
        in_specs=[anywhere, anywhere, inside, inside],
        out_specs=(inside,) * 4,
        scratch_shapes=[
            vmem((depth, block, wide), BF16), vmem((depth, half, columns), BF16),
            vmem((depth, block, wide), BF16), vmem((depth, half, columns), BF16),
            vmem((hops, block, wide), BF16), vmem((hops, half, columns), BF16),
            vmem((hops, block, wide), BF16), vmem((hops, half, columns), BF16),
            vmem((block, table.shape[1]), F32), vmem(low.shape, BF16),
            vmem((clients,) + tile.shape, F32),
            dma((2, depth)), dma((2, depth)), dma((2, depth)), dma((2, hops)), dma((2, hops)),
            dma((clients - 1,)), dma((clients - 1,)), dma((clients - 1,)), dma((clients - 1,)),
            dma((3,)), dma((3,)),
        ],
        compiler_params=pltpu.CompilerParams(collective_id=2, has_side_effects=True),
        name="reduce_deltas",
    )(main, table, low, tile)


def adam(master, first, second, grad):
    first2 = BETA_ONE * first + (1.0 - BETA_ONE) * grad
    second2 = BETA_TWO * second + (1.0 - BETA_TWO) * grad * grad
    moved = (
        first2 / (1.0 - BETA_ONE**ROUND) / (jnp.sqrt(second2 / (1.0 - BETA_TWO**ROUND)) + ADAM_EPS)
    )
    fresh = master - SERVER_RATE * (moved + WEIGHT_DECAY * master)
    return (fresh, first2, second2, fresh.astype(jnp.bfloat16))


def on_device(
    pool, index, tau, counts, labels,
    in_bf, out_bf, table_bf, bias_bf,
    in_master, out_master, table_master, bias_master,
    in_first, out_first, table_first, bias_first,
    in_second, out_second, table_second, bias_second,
):
    clients = lax.axis_size("client")
    group = in_bf.shape[2]
    steps, images = index.shape[1], index.shape[2]
    patch_rows, features = pool.shape[1], pool.shape[2]
    seq = patch_rows + 1
    pad = (seq + 15) // 16 * 16
    own = in_bf.shape[1]
    width = own * clients
    rows_total = table_bf.shape[0]
    classes = rows_total - features - seq - 9
    head_rows = (classes + 127) // 128 * 128
    vec_at, head_at = pad, pad + SMALL

    def lanes(value):
        return jnp.pad(value, [(0, 0)] * (value.ndim - 1) + [(0, LANE - group)])

    in_rows = jnp.transpose(in_bf, (1, 0, 2))
    out_rows = jnp.transpose(out_bf, (2, 0, 1))
    main_own = jnp.concatenate(
        [
            lanes(in_rows[:, :3]).reshape(own, 3 * LANE),
            in_rows[:, 3:].reshape(own, 4 * group),
            out_rows[:, 1:].reshape(own, 4 * group),
        ],
        1,
    )
    wo_own = lanes(out_rows[:, 0])
    empty = functools.partial(jnp.zeros, dtype=BF16)
    table_own = jnp.concatenate(
        [
            table_bf[: features + seq],
            empty((pad - seq, own)),
            table_bf[features + seq : features + seq + 9],
            empty((SMALL - 9, own)),
            table_bf[features + seq + 9 :],
            empty((REST - head_at - classes, own)),
        ],
        0,
    ).T
    direct = clients == 8
    if direct:
        main, wot, table = gather_weights(clients, main_own, wo_own, table_own)
    else:
        main = lax.all_gather(main_own, "client", axis=0, tiled=True)
        table = lax.all_gather(table_own, "client", axis=0, tiled=True)
        wot = lax.all_gather(
            lax.all_gather(wo_own, "client", axis=0, tiled=True), "tensor", axis=1, tiled=True
        )
    bias = jnp.broadcast_to(bias_bf.astype(F32).reshape(1, 4 * group), (8, 4 * group))

    taken = tau[0]
    ladder = jnp.arange(steps, dtype=jnp.int32)
    live = (ladder < taken).astype(F32)
    factor_sum = jnp.sum(
        jnp.where(
            ladder < taken,
            (1.0 - MOMENTUM_RHO ** (ladder + 1).astype(F32)) / (1.0 - MOMENTUM_RHO),
            0.0,
        )
    )
    examples = counts[0].astype(F32)
    share = examples / factor_sum
    scalars = jnp.stack(
        [live, jnp.where(ladder < taken, MOMENTUM_RHO, 1.0), jnp.full((steps,), share)]
    )
    patches = pick_patches(pool, index[0].reshape(steps * images), pad)
    patches = patches.reshape(steps, images * pad, features)
    slots = jnp.arange(pool.shape[0], dtype=jnp.int32)
    picked = index[0][:, :, None] == slots[None, None, :]
    target = jnp.sum(picked.astype(jnp.int32) * labels[None, None, :], 2)
    hot = (target[:, :, None] == jnp.arange(head_rows, dtype=jnp.int32)).astype(F32)
    hot = jnp.pad(hot, ((0, 0), (0, SMALL - images), (0, 0)))

    d_main, d_table, d_bias, low_d, low_a, loss_sum, norms = local_training(
        scalars, patches, hot, main, wot, table, bias, pad, seq, classes
    )
    norms = norms[:, 0, 0]
    loss_sum = loss_sum[0, 64]
    used = steps * images

    def squeeze(value):
        return value.reshape(steps, SMALL, width)[:, :images].reshape(used, width)

    low_d, low_a = squeeze(low_d), squeeze(low_a).astype(BF16)
    own_scalars = jnp.stack([examples, examples * loss_sum / taken.astype(F32), examples * factor_sum])
    if direct:
        parts = jnp.pad(
            jnp.transpose(low_d.reshape(used, clients, own), (1, 0, 2)),
            ((0, 0), (0, 0), (0, 128 - own)),
        )
        low = jnp.concatenate([jnp.broadcast_to(low_a[None], (clients, used, width)), parts], 2)
        bias_rows = width // 128
        tile = jnp.concatenate(
            [
                d_bias[:1].reshape(bias_rows, 128),
                jnp.pad(own_scalars.reshape(1, 3), ((0, 7 - bias_rows), (0, 125))),
                jnp.zeros((1, 128), F32),
            ],
            0,
        )
        mine, table_sum, low_all, tile_all = reduce_deltas(clients, d_main, d_table, low, tile)
        all_a = low_all[:, :, :width].reshape(clients * used, width).astype(F32)
        part_d = low_all[:, :, width : width + own].reshape(clients * used, own).astype(F32)
        tile_sum = jnp.sum(tile_all, 0)
        bias_delta = tile_sum[:bias_rows].reshape(4, group)
        total_c, weighted_loss, weighted_factor = (tile_sum[bias_rows, i] for i in range(3))
    else:
        sums = lax.psum((own_scalars, d_bias[:1].reshape(4, group)), "client")
        total_c, weighted_loss, weighted_factor = (sums[0][i] for i in range(3))
        bias_delta = sums[1]
        mine = lax.psum_scatter(d_main, "client", scatter_dimension=0, tiled=True).astype(F32)
        first_member = lax.axis_index("tensor") == 0
        d_table = jnp.where(first_member, d_table, jnp.zeros_like(d_table))
        table_sum = lax.psum(
            lax.psum_scatter(d_table, "client", scatter_dimension=0, tiled=True).astype(F32), "tensor"
        )
        all_a = lax.all_gather(low_a, "client", axis=0, tiled=True).astype(F32)
        all_d = lax.all_gather(low_d, "client", axis=0, tiled=True)
        part_d = lax.dynamic_slice_in_dim(all_d, lax.axis_index("client") * own, own, 1).astype(F32)
    d_qkv = jnp.transpose(mine[:, : 3 * LANE].reshape(own, 3, LANE)[..., :group], (1, 0, 2))
    d_up = jnp.transpose(mine[:, 3 * LANE : 3 * LANE + 4 * group].reshape(own, 4, group), (1, 0, 2))
    in_delta = jnp.concatenate([d_qkv, d_up], 0)
    d_wo = mine[:, 3 * LANE + 4 * group :][:, :group].T
    d_w2 = jnp.einsum("rc,rd->cd", all_a, part_d, precision=lax.Precision.HIGHEST)
    out_delta = jnp.concatenate([d_wo[None], d_w2.reshape(4, group, own)], 0)
    turned = table_sum.T
    table_delta = jnp.concatenate(
        [
            turned[: features + seq],
            turned[features + vec_at : features + vec_at + 9],
            turned[features + head_at : features + head_at + classes],
        ],
        0,
    )
    server_scale = weighted_factor / total_c / total_c
    masters = (in_master, out_master, table_master, bias_master)
    firsts = (in_first, out_first, table_first, bias_first)
    seconds = (in_second, out_second, table_second, bias_second)
    deltas = (in_delta, out_delta, table_delta, bias_delta)
    results = [
        adam(mst, fst, snd, server_scale * dlt)
        for mst, fst, snd, dlt in zip(masters, firsts, seconds, deltas)
    ]
    return (
        weighted_loss / total_c,
        norms[None],
        *[r[0] for r in results],
        *[r[1] for r in results],
        *[r[2] for r in results],
        *[r[3] for r in results],
    )


def solution(mesh):
    by_client = P("client", None, None)
    state = (P(None, "client", "tensor"), P(None, "tensor", "client"), P(None, "client"), P(None, "tensor"))
    in_specs = (by_client, by_client, P("client"), P("client"), P("client")) + state * 4
    out_specs = (P(), P("client", None)) + state * 4
    return jax.shard_map(
        on_device, mesh=mesh, in_specs=in_specs, out_specs=out_specs, check_vma=False
    )
```

```python
import functools

import jax
import jax.numpy as jnp
from jax import lax
from jax.experimental import pallas as pl
from jax.experimental.pallas import tpu as pltpu
from jax.sharding import PartitionSpec as P

HEAD_DIM = 64
ROUND = 5
EPS_NORM = 1e-06
MOMENTUM_RHO = 0.9
LOCAL_RATE = 0.05
CLIP_LIMIT = 1.0
BETA_ONE = 0.5
BETA_TWO = 0.7
ADAM_EPS = 1e-08
WEIGHT_DECAY = 0.05
SERVER_RATE = 0.05
SQRT_HALF = 0.7071067811865476
INV_ROOT_TAU = 0.3989422804014327
MESH = pl.DeviceIdType.MESH
F32 = jnp.float32
BF16 = jnp.bfloat16
NEG = -1e30
LANE = 256
SMALL = 16
REST = 512
VMEM_LIMIT = 67043328


def dot(left, right, dims):
    return lax.dot_general(left, right, (dims, ((), ())), preferred_element_type=F32)


def nn(left, right):
    return dot(left, right, ((1,), (0,)))


def nt(left, right):
    return dot(left, right, ((1,), (1,)))


def tn(left, right):
    return dot(left, right, ((0,), (0,)))


def fold(value):
    rows, width = value.shape
    return jnp.sum(value.reshape(rows // 8, 8, width), 0)


def total(value):
    return jnp.sum(jnp.sum(value, 1, keepdims=True), 0, keepdims=True)


def normalise(value):
    centre = value - jnp.mean(value, -1, keepdims=True)
    inverse = lax.rsqrt(jnp.mean(centre * centre, -1, keepdims=True) + EPS_NORM)
    return (centre * inverse, inverse)


def norm_grad(grad, gain, normed, inverse):
    scaled = grad * gain
    return inverse * (
        scaled
        - jnp.mean(scaled, -1, keepdims=True)
        - normed * jnp.mean(scaled * normed, -1, keepdims=True)
    )


def split_two(value):
    high = value.astype(BF16)
    return (high, (value - high.astype(F32)).astype(BF16))


def train_kernel(
    sizes,
    live_ref,
    x_hbm,
    hot_ref,
    main_in,
    wot_in,
    table_in,
    bias_in,
    main_out,
    table_out,
    dbias_out,
    low_d_out,
    low_a_out,
    loss_out,
    norm_out,
    wqkv, w1, wot, w2t, wet, head,
    wqkv_f, w1_f, wot_f, wet_f, pos_f, head_f, vec_f, bias_f,
    wqkv_m, w1_m, wot_m, wet_m, pos_m, head_m, vec_m, bias_m,
    wqkv_g, wot_g, pos_g, head_g, vec_g,
    xbuf, h0, slope, prob, abuf, qkv, oall, ubuf, dpre, h1own, datt, chip,
    hsum, asum, dact, bsum, vacc, ssq,
    low_d, low_a, low_b, low_w, scal,
    s1, r1, s2, r2, mx_s, mx_r, nx_s, nx_r, pos_r, vec_r,
    wsem, xsem, o_ps, o_xs, o_fs, o_pr, o_xr, o_fr,
    a1s, a1r, a2s, a2r, das, dar, pvs, pvr, mxs, mxr, nxs, nxr, osem,
):
    steps, seq, pad, classes = sizes
    width = 768
    kept = (seq + 7) // 8 * 8
    me = lax.axis_index("tensor")
    core = lax.rem(me, 2)
    mate = me + 1 - 2 * core
    across = lax.rem(me + 2, 4)
    own0 = 2 * core
    oth0 = 2 - 2 * core

    def rows(n):
        return pl.ds(pl.multiple_of(n * pad, 16), pad)

    def sent_rows(n):
        return pl.ds(pl.multiple_of(n * pad, 16), kept)

    def remote(src, dst, send, recv, device):
        return pltpu.make_async_remote_copy(
            src_ref=src, dst_ref=dst, send_sem=send, recv_sem=recv,
            device_id={"tensor": device}, device_id_type=MESH,
        )

    rest = dpre.at[0:width, 0:REST]
    weights_in = (
        main_in.at[:, 0:width],
        main_in.at[:, width : 2 * width],
        wot_in,
        main_in.at[:, 2 * width : 3 * width],
        table_in.at[:, 0:width],
        table_in.at[:, width : width + REST],
    )
    weights = (wqkv, w1, wot, w2t, wet, rest)

    def load(which):
        return pltpu.make_async_copy(weights_in[which], weights[which], wsem.at[which])

    def fetch(step, slot):
        return pltpu.make_async_copy(x_hbm.at[step], xbuf.at[slot], xsem.at[slot])

    barrier = pltpu.get_barrier_semaphore()
    fetch(0, 0).start()
    for which in range(6):
        load(which).start()
    for zero in (r1, r2, oall, datt):
        zero[...] = jnp.zeros_like(zero)
    for shift in (1, 2, 3):
        pl.semaphore_signal(
            barrier, inc=1, device_id={"tensor": lax.rem(me + shift, 4)}, device_id_type=MESH
        )
    bias_f[...] = bias_in[...]
    for zero in (pos_m, head_m, vec_m, bias_m, low_a, low_b, low_w, loss_out):
        zero[...] = jnp.zeros_like(zero)
    low_d[...] = jnp.zeros_like(low_d)
    for which in range(6):
        load(which).wait()
    vec_at, head_at = pad, pad + SMALL
    n_head = head.shape[0]
    turned = jnp.transpose(rest[...].astype(F32))
    pos_f[...] = turned[:pad]
    vec_f[...] = turned[vec_at : vec_at + SMALL]
    head_f[...] = turned[head_at : head_at + n_head]
    head[...] = turned[head_at : head_at + n_head].astype(BF16)

    def start_rows(j, carry):
        at = pl.ds(pl.multiple_of(j * 32, 32), 32)
        for low, full, mom in (
            (wqkv, wqkv_f, wqkv_m), (w1, w1_f, w1_m), (wot, wot_f, wot_m), (wet, wet_f, wet_m)
        ):
            full[at, :] = low[at, :].astype(F32)
            mom[at, :] = jnp.zeros((32, mom.shape[1]), F32)
        return carry

    lax.fori_loop(0, width // 32, start_rows, 0)
    pl.semaphore_wait(barrier, 3)

    row_id = lax.broadcasted_iota(jnp.int32, (pad, 1), 0)
    token = row_id < seq
    key_ok = lax.broadcasted_iota(jnp.int32, (1, pad), 1) < seq
    lane_head = lax.broadcasted_iota(jnp.int32, (1, LANE), 1) // HEAD_DIM
    small_ok = lax.broadcasted_iota(jnp.int32, (SMALL, 1), 0) < 4
    scale = HEAD_DIM ** (-0.5)

    def of_head(value, h):
        return jnp.where(lane_head == h, value, jnp.zeros_like(value))

    def o_place(n, group):
        return oall.at[rows(n), pl.ds(pl.multiple_of(group * LANE, LANE), LANE)]

    def o_part(n, group):
        return oall.at[sent_rows(n), pl.ds(pl.multiple_of(group * LANE, LANE), LANE)]

    def o_to_mate(n):
        place = o_part(n, me)
        return remote(place, place, o_ps.at[n], o_pr.at[n], mate)

    def o_across(n):
        place = o_part(n, me)
        return remote(place, place, o_xs.at[n], o_xr.at[n], across)

    def o_forward(n):
        place = o_part(n, across)
        return remote(place, place, o_fs.at[n], o_fr.at[n], mate)

    def relay_o(n):
        place = o_part(n, across)
        remote(place, place, o_xs.at[n], o_xr.at[n], across).wait_recv()
        o_forward(n).start()

    def to_mate(n):
        return remote(s1.at[n, 0:kept], r1.at[n, 0:kept], a1s.at[n], a1r.at[n], mate)

    def to_across(which, n):
        return remote(s2.at[n, 0:kept], r2.at[2 * which + n, 0:kept], a2s.at[2 * which + n], a2r.at[2 * which + n], across)

    def gradient_to_mate(buffer, which, image, k):
        return remote(
            buffer.at[sent_rows(image)], buffer.at[sent_rows(image)],
            das.at[2 * which + k], dar.at[2 * which + k], mate,
        )

    def pos_to_mate():
        return remote(pos_g, pos_r, pvs.at[0], pvr.at[0], mate)

    def vec_to_mate():
        return remote(vacc, vec_r, pvs.at[1], pvr.at[1], mate)

    def spread(src, dst, send, recv, shift):
        return remote(
            src, dst.at[me], send.at[shift - 1], recv.at[shift - 1], lax.rem(me + shift, 4)
        )

    def one_step(step, carry):
        slot = lax.rem(step, 2)
        fetch(step, slot).wait()

        @pl.when(step < steps - 1)
        def _():
            fetch(step + 1, 1 - slot).start()

        gain1, shift1 = vec_f[0:1, :], vec_f[1:2, :]
        gain2, shift2 = vec_f[2:3, :], vec_f[3:4, :]
        gain3, shift3 = vec_f[4:5, :], vec_f[5:6, :]

        def attend(n, carry):
            @pl.when(n >= 2)
            def _():
                relay_o(n - 2)

            inside = (row_id >= 1) & token
            state = (
                nt(xbuf[slot, rows(n), :], wet[...])
                + pos_f[...]
                + jnp.where(inside, vec_f[6:7, :], 0.0)
            )
            h0[rows(n), :] = state
            normed, _ = normalise(state)
            a = (normed * gain1 + shift1).astype(BF16)
            abuf[rows(n), :] = a
            projected = nn(a, wqkv[...]).astype(BF16)
            qkv[rows(n), :] = projected
            q, k, v = projected[:, :LANE], projected[:, LANE : 2 * LANE], projected[:, 2 * LANE :]
            out = jnp.zeros((pad, LANE), F32)
            for h in range(3):
                scores = jnp.where(key_ok, nt(of_head(q, h), k) * scale, NEG)
                expd = jnp.exp(scores - jnp.max(scores, -1, keepdims=True))
                p = (expd / jnp.sum(expd, -1, keepdims=True)).astype(BF16)
                prob[n * 3 + h] = p
                out = out + nn(p, of_head(v, h))
            o_place(n, me)[...] = out.astype(BF16)
            o_to_mate(n).start()
            o_across(n).start()
            return carry

        lax.fori_loop(0, 4, attend, 0)

        def feed(n, carry):
            @pl.when((n == 1) | (n == 2))
            def _():
                relay_o(n + 1)

            remote(o_part(n, mate), o_part(n, mate), o_ps.at[n], o_pr.at[n], mate).wait_recv()
            diagonal = lax.rem(mate + 2, 4)
            remote(
                o_part(n, diagonal), o_part(n, diagonal), o_fs.at[n], o_fr.at[n], mate
            ).wait_recv()
            state = h0[rows(n), :] + nt(oall[rows(n), :], wot[...]) + vec_f[7:8, :]

            @pl.when(n // 2 == core)
            def _():
                h1own[lax.rem(n, 2)] = state

            hsum[n] = fold(jnp.where(token, state, 0.0))
            normed, _ = normalise(state)
            u = (normed * gain2 + shift2).astype(BF16)
            ubuf[rows(n), :] = u
            z = nn(u, w1[...]) + bias_f[0:1, :]
            cdf = 0.5 * (1.0 + lax.erf(z * SQRT_HALF))
            act = (z * cdf).astype(BF16).astype(F32)
            asum[n] = fold(jnp.where(token, act, 0.0))
            tail = cdf + z * jnp.exp(-0.5 * z * z) * INV_ROOT_TAU
            slope[rows(n), :] = jnp.where(token, tail, 0.0)
            return carry

        lax.fori_loop(0, 4, feed, 0)

        def stack(ref):
            parts = [jnp.sum(ref[n], 0, keepdims=True) for n in range(4)]
            return jnp.concatenate(parts + [jnp.zeros((SMALL - 4, width), F32)], 0)

        act_sum = stack(asum)
        act_hi, act_lo = split_two(act_sum)
        both = nt(jnp.concatenate([act_hi, act_lo], 0), w2t[...])
        mx_s[...] = both[:SMALL] + both[SMALL:]
        for shift in (1, 2, 3):
            spread(mx_s, mx_r, mxs, mxr, shift).start()
        mx_r[me] = mx_s[...]
        h_mean = stack(hsum) * (1.0 / seq)
        for shift in (1, 2, 3):
            remote(
                mx_s, mx_r.at[lax.rem(me + 4 - shift, 4)], mxs.at[shift - 1], mxr.at[shift - 1], mate
            ).wait_recv()
        mlp = mx_r[0] + mx_r[1] + mx_r[2] + mx_r[3]
        average = h_mean + mlp * (1.0 / seq) + vec_f[8:9, :]
        normed3, inverse3 = normalise(average)
        pooled = (normed3 * gain3 + shift3).astype(BF16)
        logits = nt(pooled, head[...])
        class_ok = lax.broadcasted_iota(jnp.int32, (1, head.shape[0]), 1) < classes
        logits = jnp.where(class_ok, logits, NEG)
        top = jnp.max(logits, -1, keepdims=True)
        exp_l = jnp.exp(logits - top)
        total_l = jnp.sum(exp_l, -1, keepdims=True)
        hot = hot_ref[step]
        each = top + jnp.log(total_l) - jnp.sum(jnp.where(class_ok, logits, 0.0) * hot, -1, keepdims=True)
        loss = jnp.sum(jnp.where(small_ok, each, 0.0), 0, keepdims=True) * 0.25
        live = live_ref[0, step]
        rho = live_ref[1, step]
        loss_tile = live * loss
        d_logits = jnp.where(small_ok, (exp_l / total_l - hot) * 0.25, 0.0).astype(BF16)
        d_head = tn(d_logits, pooled)
        head_g[...] = d_head
        d_pooled = nn(d_logits, head[...])
        d_average = norm_grad(d_pooled, gain3, normed3, inverse3)
        d_token = d_average * (1.0 / seq)
        d_mlp = d_token.astype(BF16)
        dact[...] = nn(d_mlp, w2t[...])
        for r in range(4):
            scal[r] = jnp.broadcast_to(d_token[r : r + 1, :], (8, width))
        vec_g[...] = jnp.zeros_like(vec_g)
        vec_g[4:5, :] = jnp.sum(d_pooled * normed3, 0, keepdims=True)
        vec_g[5:6, :] = jnp.sum(d_pooled, 0, keepdims=True)
        vec_g[8:9, :] = jnp.sum(d_average, 0, keepdims=True)
        low_at = pl.ds(pl.multiple_of(step * SMALL, SMALL), SMALL)
        low_d[low_at, :] = d_mlp
        low_a[low_at, :] = act_sum
        gram_d = nt(d_mlp, d_mlp)
        gram_a = nt(act_hi, act_hi) + nt(act_hi, act_lo) + nt(act_lo, act_hi)
        own_squares = total(gram_d * gram_a)

        for n in range(4):
            scal[4 + n] = jnp.broadcast_to(dact[n : n + 1, :], (8, width))
        bsum[...] = jnp.zeros_like(bsum)
        vacc[...] = jnp.zeros_like(vacc)

        def upper_partial(n):
            g = (scal[4 + n][0:1, :] * slope[rows(n), :]).astype(BF16)
            dpre[rows(n), :] = g
            bsum[...] = bsum[...] + fold(g.astype(F32))
            return nt(g, w1[...])

        for k in (0, 1):
            s1[k] = upper_partial(oth0 + k).astype(BF16)
            to_mate(k).start()
        for k in (0, 1):
            own = upper_partial(own0 + k)
            to_mate(k).wait_recv()
            own = own + r1[k].astype(F32)
            chip[k] = own
            s2[k] = own.astype(BF16)
            to_across(0, k).start()

        ssq[...] = jnp.zeros_like(ssq)
        w1_g = slope

        def weight_grad(left, right, out, which):
            def tile(j, carry):
                at = pl.ds(pl.multiple_of(j * LANE, LANE), LANE)
                g = tn(left[:, at], right[...])
                out[at, :] = g
                if g.shape[1] > width:
                    squares = fold(g * g)
                    ssq[which] = ssq[which] + squares[:, :width]
                    ssq[which, :, : g.shape[1] - width] = (
                        ssq[which, :, : g.shape[1] - width] + squares[:, width:]
                    )
                else:
                    ssq[which] = ssq[which] + fold(g * g)
                return carry

            lax.fori_loop(0, width // LANE, tile, 0)

        weight_grad(ubuf, dpre, w1_g, 0)

        def attention_partial(n):
            d_ctx = nn(
                datt[rows(n), :], wot[:, pl.ds(pl.multiple_of(me * LANE, LANE), LANE)]
            ).astype(BF16)
            projected = qkv[rows(n), :]
            q, k, v = projected[:, :LANE], projected[:, LANE : 2 * LANE], projected[:, 2 * LANE :]
            d_q = jnp.zeros((pad, LANE), F32)
            d_k = jnp.zeros((pad, LANE), F32)
            d_v = jnp.zeros((pad, LANE), F32)
            for h in range(3):
                part = of_head(d_ctx, h)
                p = prob[n * 3 + h]
                again = p.astype(F32)
                d_p = nt(part, v)
                inner = d_p - jnp.sum(d_p * again, -1, keepdims=True)
                d_s = (again * inner).astype(BF16)
                d_v = d_v + tn(p, part)
                d_q = d_q + nn(d_s, of_head(k, h))
                d_k = d_k + tn(d_s, of_head(q, h))
            d_all = jnp.concatenate([d_q * scale, d_k * scale, d_v], 1).astype(BF16)
            qkv[rows(n), :] = d_all
            return nt(d_all, wqkv[...])

        for k in (0, 1):
            to_across(0, k).wait_recv()
            d_upper = chip[k] + r2[k].astype(F32)
            normed, inverse = normalise(h1own[k])
            d_state = norm_grad(d_upper, gain2, normed, inverse) + scal[own0 + k][0:1, :]
            d_state = jnp.where(token, d_state, 0.0)
            h1own[k] = d_state
            datt[rows(own0 + k), :] = d_state.astype(BF16)
            gradient_to_mate(datt, 0, own0 + k, k).start()
            vacc[0] = vacc[0] + fold(d_upper * normed)
            vacc[1] = vacc[1] + fold(d_upper)
            vacc[2] = vacc[2] + fold(d_state)
            own = attention_partial(own0 + k)
            remote(
                datt.at[sent_rows(oth0 + k)], datt.at[sent_rows(oth0 + k)], das.at[k], dar.at[k], mate
            ).wait_recv()
            other = attention_partial(oth0 + k)
            to_mate(k).wait_send()
            s1[k] = other.astype(BF16)
            to_mate(k).start()
            to_mate(k).wait_recv()
            own = own + r1[k].astype(F32)
            chip[k] = own
            to_across(0, k).wait_send()
            s2[k] = own.astype(BF16)
            to_across(1, k).start()

        weight_grad(datt, oall, wot_g, 1)
        weight_grad(abuf, qkv, wqkv_g, 2)

        d_emb = ubuf
        d_pos = jnp.zeros((pad, width), F32)
        for k in (0, 1):
            to_across(1, k).wait_recv()
            d_normed = chip[k] + r2[2 + k].astype(F32)
            normed, inverse = normalise(h0[rows(own0 + k), :])
            d_state = h1own[k] + norm_grad(d_normed, gain1, normed, inverse)
            d_emb[rows(own0 + k), :] = d_state.astype(BF16)
            gradient_to_mate(d_emb, 1, own0 + k, k).start()
            vacc[3] = vacc[3] + fold(d_normed * normed)
            vacc[4] = vacc[4] + fold(d_normed)
            vacc[5] = vacc[5] + fold(jnp.where(row_id >= 1, d_state, 0.0))
            d_pos = d_pos + d_state
        pos_g[...] = d_pos
        pos_to_mate().start()
        vec_to_mate().start()
        wet_g = h0
        for k in (0, 1):
            remote(
                d_emb.at[sent_rows(oth0 + k)], d_emb.at[sent_rows(oth0 + k)], das.at[2 + k], dar.at[2 + k], mate
            ).wait_recv()
        weight_grad(d_emb, xbuf.at[slot], wet_g, 3)
        pos_to_mate().wait()
        vec_to_mate().wait()
        pos_g[...] = pos_g[...] + pos_r[...]
        sums = [jnp.sum(vacc[r] + vec_r[r], 0, keepdims=True) for r in range(6)]
        vec_g[0:1, :] = sums[3]
        vec_g[1:2, :] = sums[4]
        vec_g[2:3, :] = sums[0]
        vec_g[3:4, :] = sums[1]
        vec_g[6:7, :] = sums[5]
        vec_g[7:8, :] = sums[2]
        d_bias = jnp.sum(bsum[...], 0, keepdims=True)
        shared = (
            total(ssq[1] + ssq[3] + fold(pos_g[...] * pos_g[...]) + fold(head_g[...] * head_g[...]))
            + total(vec_g[...] * vec_g[...])
        )
        own_squares = own_squares + total(ssq[0] + ssq[2]) + total(d_bias * d_bias)
        for n in range(4):
            o_to_mate(n).wait_send()
            o_across(n).wait_send()
            o_forward(n).wait_send()
        for k in (0, 1):
            to_mate(k).wait_send()
            to_across(1, k).wait_send()
            gradient_to_mate(datt, 0, own0 + k, k).wait_send()
            gradient_to_mate(d_emb, 1, own0 + k, k).wait_send()
        for shift in (1, 2, 3):
            spread(mx_s, mx_r, mxs, mxr, shift).wait_send()
        first_lane = lax.broadcasted_iota(jnp.int32, (8, 128), 1) < 64
        nx_s[...] = jnp.where(first_lane, own_squares + 0.25 * shared, loss_tile)
        for shift in (1, 2, 3):
            spread(nx_s, nx_r, nxs, nxr, shift).start()
        nx_r[me] = nx_s[...]

        load(3).start()

        @pl.when(step == steps - 1)
        def _():
            for which in (0, 1, 2, 4, 5):
                load(which).start()

        for shift in (1, 2, 3):
            remote(
                nx_s, nx_r.at[lax.rem(me + 4 - shift, 4)], nxs.at[shift - 1], nxr.at[shift - 1], mate
            ).wait_recv()
        norm = jnp.sqrt((nx_r[0] + nx_r[1] + nx_r[2] + nx_r[3]))
        factor = live * (CLIP_LIMIT / jnp.maximum(norm, CLIP_LIMIT))
        norm_out[step] = live * norm
        loss_out[...] = loss_out[...] + nx_r[0]
        for shift in (1, 2, 3):
            spread(nx_s, nx_r, nxs, nxr, shift).wait_send()
        fac = factor[0:1, 0:1]

        low_row = lax.broadcasted_iota(jnp.int32, low_b.shape, 0) // SMALL
        low_b[...] = jnp.where(low_row == step, fac, rho * low_b[...])
        low_w[...] = low_w[...] + live * low_b[...]
        factors = (LOCAL_RATE * low_w[:, 0:1]) * low_a[...]
        low_hi, low_lo = split_two(factors)
        pair = jnp.concatenate([low_hi, low_lo], 0)
        load(3).wait()

        def low_rank(j, carry):
            at = pl.ds(pl.multiple_of(j * LANE, LANE), LANE)
            moved = tn(jnp.concatenate([low_d[:, at], low_d[:, at]], 0), pair)
            w2t[at, :] = (w2t[at, :].astype(F32) - moved).astype(BF16)
            return carry

        lax.fori_loop(0, width // LANE, low_rank, 0)

        def small_update(full, mom, grad):
            mom[...] = rho * mom[...] + fac * grad
            full[...] = full[...] - (live * LOCAL_RATE) * mom[...]

        small_update(pos_f, pos_m, pos_g[...])
        small_update(vec_f, vec_m, vec_g[...])
        small_update(bias_f, bias_m, jnp.broadcast_to(d_bias, (8, width)))
        small_update(head_f, head_m, head_g[...])
        table = (
            (wqkv, wqkv_f, wqkv_m, wqkv_g),
            (w1, w1_f, w1_m, w1_g),
            (wot, wot_f, wot_m, wot_g),
            (wet, wet_f, wet_m, wet_g),
        )

        @pl.when(step < steps - 1)
        def _():
            head[...] = head_f[...].astype(BF16)

            def update(j, carry):
                at = pl.ds(pl.multiple_of(j * 16, 16), 16)
                for low, full, mom, grad in table:
                    m = rho * mom[at, :] + fac * grad[at, :]
                    mom[at, :] = m
                    w = full[at, :] - (live * LOCAL_RATE) * m
                    full[at, :] = w
                    low[at, :] = w.astype(BF16)
                return carry

            lax.fori_loop(0, width // 16, update, 0)

        @pl.when(step == steps - 1)
        def _():
            share = live_ref[2, 0]
            for which in (0, 1, 2, 4, 5):
                load(which).wait()

            def finish(j, carry):
                at = pl.ds(pl.multiple_of(j * 16, 16), 16)
                for low, full, mom, grad in table:
                    m = rho * mom[at, :] + fac * grad[at, :]
                    w = full[at, :] - (live * LOCAL_RATE) * m
                    low[at, :] = (share * (low[at, :].astype(F32) - w)).astype(BF16)
                return carry

            lax.fori_loop(0, width // 16, finish, 0)
            h0[0:REST, :] = jnp.transpose(rest[...].astype(F32))
            for ref, low_row, count in ((pos_f, 0, pad), (vec_f, vec_at, SMALL), (head_f, head_at, n_head)):
                place = pl.ds(low_row, count)
                h0[place, :] = share * (h0[place, :] - ref[...])
            rest[...] = jnp.transpose(h0[0:REST, :]).astype(BF16)
            outs = (
                (wqkv, main_out.at[:, 0:width]),
                (w1, main_out.at[:, width : 2 * width]),
                (
                    wot.at[:, pl.ds(pl.multiple_of(me * LANE, LANE), LANE)],
                    main_out.at[:, 2 * width : 2 * width + LANE],
                ),
                (wet, table_out.at[:, 0:width]),
                (rest, table_out.at[:, width : width + REST]),
            )
            copies = [
                pltpu.make_async_copy(src, dst, osem.at[i]) for i, (src, dst) in enumerate(outs)
            ]
            for copy in copies:
                copy.start()
            dbias_out[...] = share * (bias_in[...] - bias_f[...])
            low_d_out[...] = low_d[...]
            low_a_out[...] = share * factors
            for copy in copies:
                copy.wait()

        return carry

    lax.fori_loop(0, steps, one_step, 0)


def local_training(live, patches, hot, main, wot, table, bias, pad, seq, classes):
    steps = patches.shape[0]
    width = main.shape[0]
    n_all = 4 * pad
    wide = wot.shape[1]
    n_head = hot.shape[2]
    n_low = steps * SMALL
    vmem = pltpu.VMEM
    dma = pltpu.SemaphoreType.DMA
    anywhere = pl.BlockSpec(memory_space=pl.ANY)
    inside = pl.BlockSpec(memory_space=pltpu.VMEM)
    square = (width, width)
    out_shape = (
        jax.ShapeDtypeStruct((width, 2 * width + LANE), BF16),
        jax.ShapeDtypeStruct(table.shape, BF16),
        jax.ShapeDtypeStruct((8, width), F32),
        jax.ShapeDtypeStruct((n_low, width), BF16),
        jax.ShapeDtypeStruct((n_low, width), F32),
        jax.ShapeDtypeStruct((8, 128), F32),
        jax.ShapeDtypeStruct((steps, 8, 128), F32),
    )
    scratch = [
        vmem(square, BF16), vmem(square, BF16), vmem((width, wide), BF16), vmem(square, BF16),
        vmem(square, BF16), vmem((n_head, width), BF16),
    ]
    for _ in range(2):
        scratch += [
            vmem(square, F32), vmem(square, F32), vmem((width, wide), F32), vmem(square, F32),
            vmem((pad, width), F32), vmem((n_head, width), F32), vmem((SMALL, width), F32),
            vmem((8, width), F32),
        ]
    scratch += [
        vmem(square, F32), vmem((width, wide), F32), vmem((pad, width), F32),
        vmem((n_head, width), F32), vmem((SMALL, width), F32),
        vmem((2, n_all, width), BF16), vmem((n_all, width), F32), vmem((n_all, width), F32),
        vmem((12, pad, pad), BF16), vmem((n_all, width), BF16), vmem((n_all, width), BF16),
        vmem((n_all, wide), BF16), vmem((n_all, width), BF16), vmem((n_all, width), BF16),
        vmem((2, pad, width), F32), vmem((n_all, width), BF16), vmem((2, pad, width), F32),
        vmem((4, 8, width), F32), vmem((4, 8, width), F32), vmem((SMALL, width), F32),
        vmem((8, width), F32), vmem((6, 8, width), F32), vmem((4, 8, width), F32),
        vmem((n_low, width), BF16), vmem((n_low, width), F32), vmem((n_low, 128), F32),
        vmem((n_low, 128), F32), vmem((8, 8, width), F32),
        vmem((2, pad, width), BF16), vmem((2, pad, width), BF16), vmem((2, pad, width), BF16),
        vmem((4, pad, width), BF16), vmem((SMALL, width), F32), vmem((4, SMALL, width), F32),
        vmem((8, 128), F32), vmem((4, 8, 128), F32), vmem((pad, width), F32),
        vmem((6, 8, width), F32),
        dma((8,)), dma((2,)), dma((4,)), dma((4,)), dma((4,)), dma((4,)), dma((4,)), dma((4,)),
        dma((2,)), dma((2,)), dma((4,)), dma((4,)), dma((4,)), dma((4,)), dma((2,)), dma((2,)),
        dma((3,)), dma((3,)), dma((3,)), dma((3,)), dma((6,)),
    ]
    return pl.pallas_call(
        functools.partial(train_kernel, (steps, seq, pad, classes)),
        out_shape=out_shape,
        in_specs=[pl.BlockSpec(memory_space=pltpu.SMEM), anywhere, inside]
        + [anywhere] * 3 + [inside],
        out_specs=(anywhere,) * 2 + (inside,) * 5,
        scratch_shapes=scratch,
        compiler_params=pltpu.CompilerParams(
            collective_id=0, has_side_effects=True, vmem_limit_bytes=VMEM_LIMIT
        ),
        name="local_training",
    )(live, patches, hot, main, wot, table, bias)


def place_patches(chosen_ref, pool_ref, out_ref):
    seq_rows, width = pool_ref.shape[1], pool_ref.shape[2]
    pad = out_ref.shape[1]
    below = jnp.zeros((pad - 1 - seq_rows, width), F32)
    whole = jnp.concatenate([jnp.zeros((1, width), F32), pool_ref[0].astype(F32), below], 0)
    out_ref[0] = whole.astype(BF16)


def pick_patches(pool, chosen, pad):
    count = chosen.shape[0]
    _, patch_rows, width = pool.shape
    return pl.pallas_call(
        place_patches,
        out_shape=jax.ShapeDtypeStruct((count, pad, width), BF16),
        grid_spec=pltpu.PrefetchScalarGridSpec(
            num_scalar_prefetch=1,
            grid=(count,),
            in_specs=[pl.BlockSpec((1, patch_rows, width), lambda i, ids: (ids[i], 0, 0))],
            out_specs=pl.BlockSpec((1, pad, width), lambda i, ids: (i, 0, 0)),
        ),
        name="pick_patches",
    )(chosen, pool)


def ring_places(clients):
    depth = clients // 2
    client = lax.axis_index("client")
    member = lax.axis_index("tensor")
    core = lax.rem(member, 2)
    return (
        depth, client, client // 2, lax.rem(client, 2), member, core, member // 2,
        member + 1 - 2 * core, lax.rem(member + 2, 4),
    )


def send(src, dst, send_sem, recv_sem, client, member):
    return pltpu.make_async_remote_copy(
        src_ref=src, dst_ref=dst, send_sem=send_sem, recv_sem=recv_sem,
        device_id={"client": client, "tensor": member}, device_id_type=MESH,
    )


def span(start, size, unit):
    return pl.ds(pl.multiple_of(start, unit), size)


def gather_kernel(
    clients, main_ref, wo_ref, table_ref, chosen_ref, pool_ref, main_out, wo_out, table_out, x_out,
    pool_buf, x_buf, pool_sem, x_sem, up_s, up_r, down_s, down_r, y_s, y_r, mate_s, mate_r, x_s, x_r, on_s, on_r, own_sem,
):
    depth, client, z, y, member, core, chip_x, mate, across = ring_places(clients)
    block = main_ref.shape[0]
    half = block // 2
    columns = table_ref.shape[1] // 2
    peer = client + 1 - 2 * y

    def shared(origin, who):
        who_x, who_core = who // 2, lax.rem(who, 2)
        return (
            wo_out.at[span(origin * block, block, block), span(who * LANE, LANE, LANE)],
            table_out.at[
                span(origin * block + who_x * half, half, half),
                span(who_core * columns, columns, 128),
            ],
        )

    def landed(origin):
        return (main_out.at[span(origin * block, block, block), :],) + shared(origin, member)

    own_pieces = (
        main_ref, wo_ref, table_ref.at[span(chip_x * half, half, half), span(core * columns, columns, 128)]
    )

    def pieces(origin, mine):
        return own_pieces if mine else landed(origin)

    def message(origin, mine, send_sem, recv_sem, index, to):
        return [
            send(src, dst, send_sem.at[p, index], recv_sem.at[p, index], to, member)
            for p, (src, dst) in enumerate(zip(pieces(origin, mine), landed(origin)))
        ]

    def up(origin, i, mine=False):
        return message(origin, mine, up_s, up_r, i, client + 2)

    def down(origin, i, mine=False):
        return message(origin, mine, down_s, down_r, i, client - 2)

    def over(origin, mine=False):
        return message(origin, mine, y_s, y_r, origin // 2, peer)

    def give(origin, mine, send_sem, recv_sem, to):
        return [
            send(src, dst, send_sem.at[p, origin], recv_sem.at[p, origin], client, to)
            for p, (src, dst) in enumerate(zip(pieces(origin, mine)[1:], shared(origin, member)))
        ]

    def share(origin, mine=False):
        return give(origin, mine, mate_s, mate_r, mate) + give(origin, mine, x_s, x_r, across)

    def from_across(origin):
        return [
            send(dst, dst, x_s.at[p, origin], x_r.at[p, origin], client, across)
            for p, dst in enumerate(shared(origin, across))
        ]

    def pass_on(origin):
        return [
            send(dst, dst, on_s.at[p, origin], on_r.at[p, origin], client, mate)
            for p, dst in enumerate(shared(origin, across))
        ]

    def start(copies):
        for copy in copies:
            copy.start()

    def arrived(copies):
        for copy in copies:
            copy.wait_recv()

    def sent(copies):
        for copy in copies:
            copy.wait_send()

    has_up, has_down = z < depth - 1, z > 0

    barrier = pltpu.get_barrier_semaphore()

    def hello(to_client, to_member):
        pl.semaphore_signal(
            barrier, inc=1, device_id={"client": to_client, "tensor": to_member}, device_id_type=MESH
        )

    hello(peer, member)
    for shift in (1, 2, 3):
        hello(client, lax.rem(member + shift, 4))
    for shift in range(1, depth):
        hello(2 * lax.rem(z + shift, depth) + y, member)
    pl.semaphore_wait(barrier, 3 + depth)

    start(over(client, True))

    @pl.when(has_up)
    def _():
        start(up(client, 0, True))

    @pl.when(has_down)
    def _():
        start(down(client, 0, True))

    start(share(client, True))
    local = [
        pltpu.make_async_copy(src, dst, own_sem.at[p])
        for p, (src, dst) in enumerate(zip(own_pieces, landed(client)))
    ]
    start(local)

    images = chosen_ref.shape[0] // 8
    pool_size = pool_buf.shape[1] // 8
    patch_rows = pool_ref.shape[0] // pool_size
    pad = x_out.shape[1]

    def base(b):
        return lax.min(lax.max(8 * b - 1, 0), patch_rows - 8)

    deep = pool_buf.shape[0]

    def pool_load(b):
        k = lax.rem(b, deep)
        return pltpu.make_async_copy(
            pool_ref.at[span(base(b) * pool_size, 8 * pool_size, 32), :], pool_buf.at[k], pool_sem.at[k]
        )

    def x_store(b):
        k = lax.rem(b, deep)
        return pltpu.make_async_copy(x_buf.at[k], x_out.at[:, span(8 * b, 8, 8), :], x_sem.at[k])

    for b in range(deep - 1):
        pool_load(b).start()
    lane = lax.broadcasted_iota(jnp.int32, (8 * images, 8 * pool_size), 1)
    line_row = lax.rem(lax.broadcasted_iota(jnp.int32, (8 * images, 1), 0), 8)

    def pick(b, carry):
        k = lax.rem(b, deep)
        pool_load(b).wait()

        @pl.when(b < pad // 8 - (deep - 1))
        def _():
            pool_load(b + deep - 1).start()

        wanted = (8 * b - 1 + line_row - base(b)) * pool_size + chosen_ref[...]
        picked = nn((lane == wanted).astype(BF16), pool_buf[k]).astype(BF16)

        @pl.when(b >= deep)
        def _():
            x_store(b - deep).wait()

        x_buf[k] = picked.reshape(images, 8, picked.shape[1])
        x_store(b).start()
        return carry

    lax.fori_loop(0, pad // 8, pick, 0)
    for b in range(pad // 8 - deep, pad // 8):
        x_store(b).wait()

    def line(d, act):
        @pl.when(z >= d)
        def _():
            act(client - 2 * d, True)

        @pl.when(z < depth - d)
        def _():
            act(client + 2 * d, False)

    def across_line(d, act):
        if d == 0:
            act(peer, True)
            return

        @pl.when(z >= d)
        def _():
            act(peer - 2 * d, True)

        @pl.when(z < depth - d)
        def _():
            act(peer + 2 * d, False)

    def line_in(d):
        def act(origin, below):
            if below:
                arrived(message(origin, False, up_s, up_r, d - 1, peer))
                if d < depth - 1:

                    @pl.when(has_up)
                    def _():
                        start(up(origin, d))
            else:
                arrived(message(origin, False, down_s, down_r, d - 1, peer))
                if d < depth - 1:

                    @pl.when(has_down)
                    def _():
                        start(down(origin, d))
            start(over(origin))
            start(share(origin))

        return act

    def y_in(origin, below):
        arrived(over(origin))
        start(share(origin))

    def forward(origin, below=True):
        arrived(from_across(origin))
        start(pass_on(origin))

    for d in range(1, depth + 1):
        if d < depth:
            line(d, line_in(d))
        across_line(d - 1, y_in)
        if d == 1:
            forward(client)
        else:
            line(d - 1, forward)
            across_line(d - 2, forward)
    across_line(depth - 1, forward)

    for copy in local:
        copy.wait()
    for origin in range(clients):
        sent(share(origin))
        sent(pass_on(origin))
        arrived([
            send(dst, dst, mate_s.at[p, origin], mate_r.at[p, origin], client, mate)
            for p, dst in enumerate(shared(origin, mate))
        ])
        arrived([
            send(dst, dst, on_s.at[p, origin], on_r.at[p, origin], client, mate)
            for p, dst in enumerate(shared(origin, lax.rem(mate + 2, 4)))
        ])
    for d in range(depth):
        sent(over(2 * d + y))

        @pl.when(has_up & (z >= d))
        def _():
            if d < depth - 1:
                sent(up(client - 2 * d, d))

        @pl.when(has_down & (z < depth - d))
        def _():
            if d < depth - 1:
                sent(down(client + 2 * d, d))


def gather_weights(clients, main, wo, table, chosen, pool, pad):
    depth = clients // 2
    dma = pltpu.SemaphoreType.DMA
    anywhere = pl.BlockSpec(memory_space=pl.ANY)
    inside = pl.BlockSpec(memory_space=pltpu.VMEM)
    width = main.shape[0] * clients
    hops = depth - 1
    pool_size, patch_rows, features = pool.shape
    images = chosen.shape[0]
    rows = jnp.transpose(pool, (1, 0, 2)).reshape(patch_rows * pool_size, features)
    column = jnp.repeat(chosen, 8).reshape(8 * images, 1)
    return pl.pallas_call(
        functools.partial(gather_kernel, clients),
        out_shape=(
            jax.ShapeDtypeStruct((width, main.shape[1]), BF16),
            jax.ShapeDtypeStruct((width, 4 * wo.shape[1]), BF16),
            jax.ShapeDtypeStruct((width, table.shape[1]), BF16),
            jax.ShapeDtypeStruct((images, pad, features), BF16),
        ),
        in_specs=[inside] * 4 + [anywhere],
        out_specs=(anywhere,) * 4,
        scratch_shapes=[
            pltpu.VMEM((6, 8 * pool_size, features), BF16), pltpu.VMEM((6, images, 8, features), BF16),
            dma((6,)), dma((6,)),
            dma((3, hops)), dma((3, hops)), dma((3, hops)), dma((3, hops)), dma((3, depth)),
            dma((3, depth)),
        ] + [dma((2, clients))] * 6 + [dma((3,))],
        compiler_params=pltpu.CompilerParams(collective_id=1, has_side_effects=True),
        name="gather_weights",
    )(main, wo, table, column, rows)


def reduce_kernel(
    clients, main_in, table_in, low_in, tile_in, main_out, table_out, low_out, tile_out,
    own_main, own_table, y_main, y_table, zs_main, zs_table, zr_main, zr_table, whole, low_all, tile_all,
    own_sem, y_s, y_r, z_s, z_r, low_s, low_r, tile_s, tile_r, q_s, q_r,
):
    depth, client, z, y, member, core, chip_x, mate, across = ring_places(clients)
    block = own_main.shape[1]
    half, columns = own_table.shape[1], own_table.shape[2]
    peer = client + 1 - 2 * y

    def main_rows(owner):
        return main_in.at[span(owner * block, block, block), :]

    def table_part(owner):
        return table_in.at[
            span(owner * block + chip_x * half, half, half), span(core * columns, columns, 128)
        ]

    def own_load(level):
        owner = 2 * level + y
        return [
            pltpu.make_async_copy(main_rows(owner), own_main.at[level], own_sem.at[0, level]),
            pltpu.make_async_copy(table_part(owner), own_table.at[level], own_sem.at[1, level]),
        ]

    def over(level):
        owner = 2 * level + 1 - y
        return [
            send(main_rows(owner), y_main.at[level], y_s.at[0, level], y_r.at[0, level], peer, member),
            send(table_part(owner), y_table.at[level], y_s.at[1, level], y_r.at[1, level], peer, member),
        ]

    def onward(i):
        owner = 2 * lax.rem(z + 1 + i, depth) + y
        return [
            send(zs_main.at[i], zr_main.at[i], z_s.at[0, i], z_r.at[0, i], owner, member),
            send(zs_table.at[i], zr_table.at[i], z_s.at[1, i], z_r.at[1, i], owner, member),
        ]

    def small(shift):
        to = lax.rem(client + shift, clients)
        return [
            send(low_in.at[to], low_all.at[client], low_s.at[shift - 1], low_r.at[shift - 1], to, member),
            send(tile_in, tile_all.at[client], tile_s.at[shift - 1], tile_r.at[shift - 1], to, member),
        ]

    def small_from(shift):
        source = lax.rem(client + clients - shift, clients)
        return [
            send(low_in.at[source], low_all.at[source], low_s.at[shift - 1], low_r.at[shift - 1], source, member),
            send(tile_in, tile_all.at[source], tile_s.at[shift - 1], tile_r.at[shift - 1], source, member),
        ]

    def quarter(who):
        return whole.at[span((who // 2) * half, half, half), span(lax.rem(who, 2) * columns, columns, 128)]

    def pass_quarter(who, index, to):
        return send(quarter(who), quarter(who), q_s.at[index], q_r.at[index], client, to)

    barrier = pltpu.get_barrier_semaphore()
    for shift in range(1, clients):
        pl.semaphore_signal(
            barrier, inc=1,
            device_id={"client": lax.rem(client + shift, clients), "tensor": member}, device_id_type=MESH,
        )
    for shift in (1, 2, 3):
        pl.semaphore_signal(
            barrier, inc=1,
            device_id={"client": client, "tensor": lax.rem(member + shift, 4)}, device_id_type=MESH,
        )
    for i in range(depth):
        for copy in own_load(lax.rem(z + 1 + i, depth)):
            copy.start()
    pl.semaphore_wait(barrier, clients - 1 + 3)
    for i in range(depth):
        for copy in over(lax.rem(z + 1 + i, depth)):
            copy.start()
    for shift in range(1, clients):
        for copy in small(shift):
            copy.start()
    low_all[client] = low_in[client]
    tile_all[client] = tile_in[...]
    for i in range(depth):
        level = lax.rem(z + 1 + i, depth)
        for copy in own_load(level):
            copy.wait()
        for copy in over(level):
            copy.wait_recv()
        for own, came, out, last in (
            (own_main, y_main, zs_main, main_out), (own_table, y_table, zs_table, quarter(member))
        ):
            pair = own[level].astype(F32) + came[level].astype(F32)
            if i < depth - 1:
                out[i] = pair.astype(BF16)
            else:
                last[...] = pair
        if i < depth - 1:
            for copy in onward(i):
                copy.start()
    mine = quarter(member)
    for i in range(depth - 1):
        for copy in onward(i):
            copy.wait_recv()
        main_out[...] = main_out[...] + zr_main[i].astype(F32)
        mine[...] = mine[...] + zr_table[i].astype(F32)
    first = [pass_quarter(member, 0, mate), pass_quarter(member, 1, across)]
    for copy in first:
        copy.start()
    for shift in range(1, clients):
        for copy in small_from(shift):
            copy.wait_recv()
    low_out[...] = low_all[...]
    tile_out[...] = tile_all[...]
    pass_quarter(across, 1, across).wait_recv()
    second = pass_quarter(across, 2, mate)
    second.start()
    pass_quarter(mate, 0, mate).wait_recv()
    pass_quarter(lax.rem(mate + 2, 4), 2, mate).wait_recv()
    table_out[...] = whole[...]
    for copy in first + [second]:
        copy.wait_send()
    for shift in range(1, clients):
        for copy in small(shift):
            copy.wait_send()
    for i in range(depth):
        for copy in over(i):
            copy.wait_send()
        if i < depth - 1:
            for copy in onward(i):
                copy.wait_send()


def reduce_deltas(clients, main, table, low, tile):
    depth = clients // 2
    dma = pltpu.SemaphoreType.DMA
    vmem = pltpu.VMEM
    anywhere = pl.BlockSpec(memory_space=pl.ANY)
    inside = pl.BlockSpec(memory_space=pltpu.VMEM)
    block = main.shape[0] // clients
    half, columns = block // 2, table.shape[1] // 2
    wide = main.shape[1]
    hops = depth - 1
    return pl.pallas_call(
        functools.partial(reduce_kernel, clients),
        out_shape=(
            jax.ShapeDtypeStruct((block, wide), F32),
            jax.ShapeDtypeStruct((block, table.shape[1]), F32),
            jax.ShapeDtypeStruct(low.shape, BF16),
            jax.ShapeDtypeStruct((clients,) + tile.shape, F32),
        ),
        in_specs=[anywhere, anywhere, inside, inside],
        out_specs=(inside,) * 4,
        scratch_shapes=[
            vmem((depth, block, wide), BF16), vmem((depth, half, columns), BF16),
            vmem((depth, block, wide), BF16), vmem((depth, half, columns), BF16),
            vmem((hops, block, wide), BF16), vmem((hops, half, columns), BF16),
            vmem((hops, block, wide), BF16), vmem((hops, half, columns), BF16),
            vmem((block, table.shape[1]), F32), vmem(low.shape, BF16),
            vmem((clients,) + tile.shape, F32),
            dma((2, depth)), dma((2, depth)), dma((2, depth)), dma((2, hops)), dma((2, hops)),
            dma((clients - 1,)), dma((clients - 1,)), dma((clients - 1,)), dma((clients - 1,)),
            dma((3,)), dma((3,)),
        ],
        compiler_params=pltpu.CompilerParams(collective_id=2, has_side_effects=True),
        name="reduce_deltas",
    )(main, table, low, tile)


def adam(master, first, second, grad):
    first2 = BETA_ONE * first + (1.0 - BETA_ONE) * grad
    second2 = BETA_TWO * second + (1.0 - BETA_TWO) * grad * grad
    moved = (
        first2 / (1.0 - BETA_ONE**ROUND) / (jnp.sqrt(second2 / (1.0 - BETA_TWO**ROUND)) + ADAM_EPS)
    )
    fresh = master - SERVER_RATE * (moved + WEIGHT_DECAY * master)
    return (fresh, first2, second2, fresh.astype(jnp.bfloat16))


def on_device(
    pool, index, tau, counts, labels,
    in_bf, out_bf, table_bf, bias_bf,
    in_master, out_master, table_master, bias_master,
    in_first, out_first, table_first, bias_first,
    in_second, out_second, table_second, bias_second,
):
    clients = lax.axis_size("client")
    group = in_bf.shape[2]
    steps, images = index.shape[1], index.shape[2]
    patch_rows, features = pool.shape[1], pool.shape[2]
    seq = patch_rows + 1
    pad = (seq + 15) // 16 * 16
    own = in_bf.shape[1]
    width = own * clients
    rows_total = table_bf.shape[0]
    classes = rows_total - features - seq - 9
    head_rows = (classes + 127) // 128 * 128
    vec_at, head_at = pad, pad + SMALL

    def lanes(value):
        return jnp.pad(value, [(0, 0)] * (value.ndim - 1) + [(0, LANE - group)])

    in_rows = jnp.transpose(in_bf, (1, 0, 2))
    out_rows = jnp.transpose(out_bf, (2, 0, 1))
    main_own = jnp.concatenate(
        [
            lanes(in_rows[:, :3]).reshape(own, 3 * LANE),
            in_rows[:, 3:].reshape(own, 4 * group),
            out_rows[:, 1:].reshape(own, 4 * group),
        ],
        1,
    )
    wo_own = lanes(out_rows[:, 0])
    empty = functools.partial(jnp.zeros, dtype=BF16)
    table_own = jnp.concatenate(
        [
            table_bf[: features + seq],
            empty((pad - seq, own)),
            table_bf[features + seq : features + seq + 9],
            empty((SMALL - 9, own)),
            table_bf[features + seq + 9 :],
            empty((REST - head_at - classes, own)),
        ],
        0,
    ).T
    direct = clients == 8
    if direct:
        main, wot, table, patches = gather_weights(
            clients, main_own, wo_own, table_own, index[0].reshape(steps * images), pool, pad
        )
    else:
        main = lax.all_gather(main_own, "client", axis=0, tiled=True)
        table = lax.all_gather(table_own, "client", axis=0, tiled=True)
        wot = lax.all_gather(
            lax.all_gather(wo_own, "client", axis=0, tiled=True), "tensor", axis=1, tiled=True
        )
        patches = pick_patches(pool, index[0].reshape(steps * images), pad)
    bias = jnp.broadcast_to(bias_bf.astype(F32).reshape(1, 4 * group), (8, 4 * group))

    taken = tau[0]
    ladder = jnp.arange(steps, dtype=jnp.int32)
    live = (ladder < taken).astype(F32)
    factor_sum = jnp.sum(
        jnp.where(
            ladder < taken,
            (1.0 - MOMENTUM_RHO ** (ladder + 1).astype(F32)) / (1.0 - MOMENTUM_RHO),
            0.0,
        )
    )
    examples = counts[0].astype(F32)
    share = examples / factor_sum
    scalars = jnp.stack(
        [live, jnp.where(ladder < taken, MOMENTUM_RHO, 1.0), jnp.full((steps,), share)]
    )
    patches = patches.reshape(steps, images * pad, features)
    slots = jnp.arange(pool.shape[0], dtype=jnp.int32)
    picked = index[0][:, :, None] == slots[None, None, :]
    target = jnp.sum(picked.astype(jnp.int32) * labels[None, None, :], 2)
    hot = (target[:, :, None] == jnp.arange(head_rows, dtype=jnp.int32)).astype(F32)
    hot = jnp.pad(hot, ((0, 0), (0, SMALL - images), (0, 0)))

    d_main, d_table, d_bias, low_d, low_a, loss_sum, norms = local_training(
        scalars, patches, hot, main, wot, table, bias, pad, seq, classes
    )
    norms = norms[:, 0, 0]
    loss_sum = loss_sum[0, 64]
    used = steps * images

    def squeeze(value):
        return value.reshape(steps, SMALL, width)[:, :images].reshape(used, width)

    low_d, low_a = squeeze(low_d), squeeze(low_a).astype(BF16)
    own_scalars = jnp.stack([examples, examples * loss_sum / taken.astype(F32), examples * factor_sum])
    if direct:
        parts = jnp.pad(
            jnp.transpose(low_d.reshape(used, clients, own), (1, 0, 2)),
            ((0, 0), (0, 0), (0, 128 - own)),
        )
        low = jnp.concatenate([jnp.broadcast_to(low_a[None], (clients, used, width)), parts], 2)
        bias_rows = width // 128
        tile = jnp.concatenate(
            [
                d_bias[:1].reshape(bias_rows, 128),
                jnp.pad(own_scalars.reshape(1, 3), ((0, 7 - bias_rows), (0, 125))),
                jnp.zeros((1, 128), F32),
            ],
            0,
        )
        mine, table_sum, low_all, tile_all = reduce_deltas(clients, d_main, d_table, low, tile)
        all_a = low_all[:, :, :width].reshape(clients * used, width).astype(F32)
        part_d = low_all[:, :, width : width + own].reshape(clients * used, own).astype(F32)
        tile_sum = jnp.sum(tile_all, 0)
        bias_delta = tile_sum[:bias_rows].reshape(4, group)
        total_c, weighted_loss, weighted_factor = (tile_sum[bias_rows, i] for i in range(3))
    else:
        sums = lax.psum((own_scalars, d_bias[:1].reshape(4, group)), "client")
        total_c, weighted_loss, weighted_factor = (sums[0][i] for i in range(3))
        bias_delta = sums[1]
        mine = lax.psum_scatter(d_main, "client", scatter_dimension=0, tiled=True).astype(F32)
        first_member = lax.axis_index("tensor") == 0
        d_table = jnp.where(first_member, d_table, jnp.zeros_like(d_table))
        table_sum = lax.psum(
            lax.psum_scatter(d_table, "client", scatter_dimension=0, tiled=True).astype(F32), "tensor"
        )
        all_a = lax.all_gather(low_a, "client", axis=0, tiled=True).astype(F32)
        all_d = lax.all_gather(low_d, "client", axis=0, tiled=True)
        part_d = lax.dynamic_slice_in_dim(all_d, lax.axis_index("client") * own, own, 1).astype(F32)
    d_qkv = jnp.transpose(mine[:, : 3 * LANE].reshape(own, 3, LANE)[..., :group], (1, 0, 2))
    d_up = jnp.transpose(mine[:, 3 * LANE : 3 * LANE + 4 * group].reshape(own, 4, group), (1, 0, 2))
    in_delta = jnp.concatenate([d_qkv, d_up], 0)
    d_wo = mine[:, 3 * LANE + 4 * group :][:, :group].T
    d_w2 = jnp.einsum("rc,rd->cd", all_a, part_d, precision=lax.Precision.HIGHEST)
    out_delta = jnp.concatenate([d_wo[None], d_w2.reshape(4, group, own)], 0)
    turned = table_sum.T
    table_delta = jnp.concatenate(
        [
            turned[: features + seq],
            turned[features + vec_at : features + vec_at + 9],
            turned[features + head_at : features + head_at + classes],
        ],
        0,
    )
    server_scale = weighted_factor / total_c / total_c
    masters = (in_master, out_master, table_master, bias_master)
    firsts = (in_first, out_first, table_first, bias_first)
    seconds = (in_second, out_second, table_second, bias_second)
    deltas = (in_delta, out_delta, table_delta, bias_delta)
    results = [
        adam(mst, fst, snd, server_scale * dlt)
        for mst, fst, snd, dlt in zip(masters, firsts, seconds, deltas)
    ]
    return (
        weighted_loss / total_c,
        norms[None],
        *[r[0] for r in results],
        *[r[1] for r in results],
        *[r[2] for r in results],
        *[r[3] for r in results],
    )


def solution(mesh):
    by_client = P("client", None, None)
    state = (P(None, "client", "tensor"), P(None, "tensor", "client"), P(None, "client"), P(None, "tensor"))
    in_specs = (by_client, by_client, P("client"), P("client"), P("client")) + state * 4
    out_specs = (P(), P("client", None)) + state * 4
    return jax.shard_map(
        on_device, mesh=mesh, in_specs=in_specs, out_specs=out_specs, check_vma=False
    )
```

```python
import functools

import jax
import jax.numpy as jnp
from jax import lax
from jax.experimental import pallas as pl
from jax.experimental.pallas import tpu as pltpu
from jax.sharding import PartitionSpec as P

HEAD_DIM = 64
ROUND = 5
EPS_NORM = 1e-06
MOMENTUM_RHO = 0.9
LOCAL_RATE = 0.05
CLIP_LIMIT = 1.0
BETA_ONE = 0.5
BETA_TWO = 0.7
ADAM_EPS = 1e-08
WEIGHT_DECAY = 0.05
SERVER_RATE = 0.05
SQRT_HALF = 0.7071067811865476
INV_ROOT_TAU = 0.3989422804014327
MESH = pl.DeviceIdType.MESH
F32 = jnp.float32
BF16 = jnp.bfloat16
NEG = -1e30
LANE = 256
SMALL = 16
REST = 512
VMEM_LIMIT = 67043328


def dot(left, right, dims):
    return lax.dot_general(left, right, (dims, ((), ())), preferred_element_type=F32)


def nn(left, right):
    return dot(left, right, ((1,), (0,)))


def nt(left, right):
    return dot(left, right, ((1,), (1,)))


def tn(left, right):
    return dot(left, right, ((0,), (0,)))


def fold(value):
    rows, width = value.shape
    return jnp.sum(value.reshape(rows // 8, 8, width), 0)


def total(value):
    return jnp.sum(jnp.sum(value, 1, keepdims=True), 0, keepdims=True)


def normalise(value):
    centre = value - jnp.mean(value, -1, keepdims=True)
    inverse = lax.rsqrt(jnp.mean(centre * centre, -1, keepdims=True) + EPS_NORM)
    return (centre * inverse, inverse)


def norm_grad(grad, gain, normed, inverse):
    scaled = grad * gain
    return inverse * (
        scaled
        - jnp.mean(scaled, -1, keepdims=True)
        - normed * jnp.mean(scaled * normed, -1, keepdims=True)
    )


def split_two(value):
    high = value.astype(BF16)
    return (high, (value - high.astype(F32)).astype(BF16))


def swap(tile):
    return pltpu.roll(tile, HEAD_DIM, 1)


def tiles(value):
    return [value[:, i : i + 128] for i in range(0, value.shape[1], 128)]


def low_half(shape):
    return lax.broadcasted_iota(jnp.int32, shape, 1) < HEAD_DIM


def pack_two(left, right):
    low = low_half(left[0].shape)
    return [
        left[0],
        jnp.where(low, left[1], swap(right[0])),
        jnp.where(low, swap(right[0]), swap(right[1])),
    ]


def unpack_two(packed):
    low = low_half(packed[0].shape)
    nothing = jnp.zeros_like(packed[0])
    middle, last = swap(packed[1]), swap(packed[2])
    return (
        [packed[0], jnp.where(low, packed[1], nothing)],
        [jnp.where(low, middle, last), jnp.where(low, last, nothing)],
    )


def train_kernel(
    sizes,
    live_ref,
    x_hbm,
    hot_ref,
    main_in,
    wo_in,
    table_in,
    bias_in,
    main_out,
    table_out,
    dbias_out,
    low_d_out,
    low_a_out,
    loss_out,
    norm_out,
    wqkv, w1, wot, w2t, wet, head,
    wqkv_f, w1_f, wot_f, wet_f, pos_f, head_f, vec_f, bias_f,
    wqkv_m, w1_m, wot_m, wet_m, pos_m, head_m, vec_m, bias_m,
    wqkv_g, wot_g, wet_g, pos_g, head_g, vec_g,
    xbuf, h0, slope, prob, abuf, qkv, oall, third, ubuf, dpre, h1own, datt, chip, inverses,
    hsum, asum, dact, bsum, vacc, ssq,
    low_d, low_a, low_b, low_w, scal,
    s1, r1, s2, r2, mx_s, mx_r, nx_s, nx_r, pos_r, vec_r,
    wsem, xsem, o_ps, o_xs, o_fs, o_pr, o_xr, o_fr,
    a1s, a1r, a2s, a2r, das, dar, pvs, pvr, mxs, mxr, nxs, nxr, osem,
):
    steps, seq, pad, classes = sizes
    width = 768
    kept = (seq + 7) // 8 * 8
    me = lax.axis_index("tensor")
    core = lax.rem(me, 2)
    mate = me + 1 - 2 * core
    across = lax.rem(me + 2, 4)
    own0 = 2 * core
    oth0 = 2 - 2 * core

    def rows(n):
        return pl.ds(pl.multiple_of(n * pad, 16), pad)

    def sent_rows(n):
        return pl.ds(pl.multiple_of(n * pad, 16), kept)

    def remote(src, dst, send, recv, device):
        return pltpu.make_async_remote_copy(
            src_ref=src, dst_ref=dst, send_sem=send, recv_sem=recv,
            device_id={"tensor": device}, device_id_type=MESH,
        )

    rest = dpre.at[0:width, 0:REST]
    square_rows = pl.ds(0, width)
    raw = abuf.at[square_rows, :]
    wo_raw = [ubuf.at[square_rows, pl.ds(g * LANE, LANE)] for g in range(3)] + [
        qkv.at[square_rows, pl.ds(0, LANE)]
    ]
    weights_in = [
        main_in.at[:, 2 * width : 3 * width],
        main_in.at[:, 0:width],
        main_in.at[:, width : 2 * width],
        table_in.at[:, 0:width],
        table_in.at[:, width : width + REST],
    ] + [wo_in.at[:, g * LANE : (g + 1) * LANE] for g in range(4)]
    weights = [raw, w1, w2t, wet, rest] + wo_raw

    def load(which):
        return pltpu.make_async_copy(weights_in[which], weights[which], wsem.at[which])

    def fetch(step, slot):
        return pltpu.make_async_copy(x_hbm.at[step], xbuf.at[slot], xsem.at[slot])

    barrier = pltpu.get_barrier_semaphore()
    fetch(0, 0).start()
    for which in range(9):
        load(which).start()
    for zero in (r1, r2, oall, third, datt):
        zero[...] = jnp.zeros_like(zero)
    for shift in (1, 2, 3):
        pl.semaphore_signal(
            barrier, inc=1, device_id={"tensor": lax.rem(me + shift, 4)}, device_id_type=MESH
        )
    bias_f[...] = bias_in[...]
    for zero in (pos_m, head_m, vec_m, bias_m, low_a, low_b, low_w, loss_out):
        zero[...] = jnp.zeros_like(zero)
    low_d[...] = jnp.zeros_like(low_d)
    for which in range(9):
        load(which).wait()
    vec_at, head_at = pad, pad + SMALL
    n_head = head.shape[0]
    turned = jnp.transpose(rest[...].astype(F32))
    pos_f[...] = turned[:pad]
    vec_f[...] = turned[vec_at : vec_at + SMALL]
    head_f[...] = turned[head_at : head_at + n_head]
    head[...] = turned[head_at : head_at + n_head].astype(BF16)

    def join(parts):
        return jnp.concatenate(parts, 1)

    def start_rows(j, carry):
        at = pl.ds(pl.multiple_of(j * 32, 32), 32)
        packed = tiles(raw[at, :].astype(F32))
        q, k = unpack_two(packed[:3])
        v, _ = unpack_two(packed[3:])
        all_three = join(q + k + v)
        wqkv_f[at, :] = all_three
        wqkv[at, :] = all_three.astype(BF16)
        pieces = [tiles(piece[at, :].astype(F32)) for piece in wo_raw]
        low = low_half((32, 128))
        first = [jnp.where(low, swap(p[0]), swap(p[1])) for p in pieces]
        last = [
            jnp.where(low, swap(pieces[g][1]), pieces[g + 1][1]) for g in (0, 2)
        ]
        wo_rows = join(first + last)
        wot_f[at, :] = wo_rows
        wot[at, :] = wo_rows.astype(BF16)
        for low_ref, full in ((w1, w1_f), (wet, wet_f)):
            full[at, :] = low_ref[at, :].astype(F32)
        for mom in (wqkv_m, w1_m, wot_m, wet_m):
            mom[at, :] = jnp.zeros((32, mom.shape[1]), F32)
        return carry

    lax.fori_loop(0, width // 32, start_rows, 0)
    pl.semaphore_wait(barrier, 3)

    row_id = lax.broadcasted_iota(jnp.int32, (pad, 1), 0)
    token = row_id < seq
    key_ok = lax.broadcasted_iota(jnp.int32, (1, pad), 1) < seq
    lane_head = lax.broadcasted_iota(jnp.int32, (1, LANE), 1) // HEAD_DIM
    small_ok = lax.broadcasted_iota(jnp.int32, (SMALL, 1), 0) < 4
    scale = HEAD_DIM ** (-0.5)

    def of_head(value, h):
        return jnp.where(lane_head == h, value, jnp.zeros_like(value))

    def o_part(message, group):
        lanes = pl.ds(pl.multiple_of(group * 128, 128), 128)
        pair, which = message // 3, message % 3
        if which == 2:
            return third.at[pair, 0:kept, lanes]
        return oall.at[pl.ds((2 * pair + which) * pad, kept), lanes]

    def o_to_mate(message):
        place = o_part(message, me)
        return remote(place, place, o_ps.at[message], o_pr.at[message], mate)

    def o_across(message):
        place = o_part(message, me)
        return remote(place, place, o_xs.at[message], o_xr.at[message], across)

    def o_forward(message):
        place = o_part(message, across)
        return remote(place, place, o_fs.at[message], o_fr.at[message], mate)

    def relay_o(message):
        place = o_part(message, across)
        remote(place, place, o_xs.at[message], o_xr.at[message], across).wait_recv()
        o_forward(message).start()

    def o_here(message):
        direct = o_part(message, mate)
        remote(direct, direct, o_ps.at[message], o_pr.at[message], mate).wait_recv()
        passed = o_part(message, lax.rem(mate + 2, 4))
        remote(passed, passed, o_fs.at[message], o_fr.at[message], mate).wait_recv()

    def to_mate(n):
        return remote(s1.at[n, 0:kept], r1.at[n, 0:kept], a1s.at[n], a1r.at[n], mate)

    def to_across(which, n):
        return remote(s2.at[n, 0:kept], r2.at[2 * which + n, 0:kept], a2s.at[2 * which + n], a2r.at[2 * which + n], across)

    def gradient_to_mate(buffer, which, image, k):
        return remote(
            buffer.at[sent_rows(image)], buffer.at[sent_rows(image)],
            das.at[2 * which + k], dar.at[2 * which + k], mate,
        )

    def pos_to_mate():
        return remote(pos_g, pos_r, pvs.at[0], pvr.at[0], mate)

    def vec_to_mate():
        return remote(vacc, vec_r, pvs.at[1], pvr.at[1], mate)

    def spread(src, dst, send, recv, shift):
        return remote(
            src, dst.at[me], send.at[shift - 1], recv.at[shift - 1], lax.rem(me + shift, 4)
        )

    def one_step(step, carry):
        slot = lax.rem(step, 2)
        fetch(step, slot).wait()

        @pl.when(step < steps - 1)
        def _():
            fetch(step + 1, 1 - slot).start()

        gain1, shift1 = vec_f[0:1, :], vec_f[1:2, :]
        gain2, shift2 = vec_f[2:3, :], vec_f[3:4, :]
        gain3, shift3 = vec_f[4:5, :], vec_f[5:6, :]

        def attend(pair):
            two = slice(2 * pair * pad, 2 * (pair + 1) * pad)
            inside = (row_id >= 1) & token
            added = pos_f[...] + jnp.where(inside, vec_f[6:7, :], 0.0)
            state = nt(xbuf[slot, two, :], wet[...]) + jnp.concatenate([added, added], 0)
            h0[two, :] = state
            normed, _ = normalise(state)
            a = (normed * gain1 + shift1).astype(BF16)
            abuf[two, :] = a
            both = nn(a, wqkv[...]).astype(BF16)
            qkv[two, :] = both
            mine = pl.ds(pl.multiple_of(me * 128, 128), 128)
            thirds = []
            for i in range(2):
                projected = both[i * pad : (i + 1) * pad]
                q, k, v = projected[:, :LANE], projected[:, LANE : 2 * LANE], projected[:, 2 * LANE :]
                out = jnp.zeros((pad, LANE), F32)
                for h in range(3):
                    scores = jnp.where(key_ok, nt(of_head(q, h), k) * scale, NEG)
                    expd = jnp.exp(scores - jnp.max(scores, -1, keepdims=True))
                    p = (expd / jnp.sum(expd, -1, keepdims=True)).astype(BF16)
                    prob[(2 * pair + i) * 3 + h] = p
                    out = out + nn(p, of_head(v, h))
                oall[(2 * pair + i) * pad : (2 * pair + i + 1) * pad, mine] = out[:, :128].astype(BF16)
                thirds.append(out[:, 128:])
                o_to_mate(3 * pair + i).start()
                o_across(3 * pair + i).start()
            third[pair, :, mine] = (thirds[0] + swap(thirds[1])).astype(BF16)
            o_to_mate(3 * pair + 2).start()
            o_across(3 * pair + 2).start()

        attend(0)
        attend(1)
        for message in range(3):
            relay_o(message)

        def feed(pair):
            for message in range(3):
                o_here(3 * pair + message)
            two = slice(2 * pair * pad, 2 * (pair + 1) * pad)
            side = tiles(third[pair].astype(F32))
            low = low_half((pad, 128))
            for i in range(2):
                for g in (0, 2):
                    if i == 0:
                        tile = jnp.where(low, side[g], swap(side[g + 1]))
                    else:
                        tile = jnp.where(low, swap(side[g]), side[g + 1])
                    at = 4 * 128 + g * HEAD_DIM
                    oall[(2 * pair + i) * pad : (2 * pair + i + 1) * pad, at : at + 128] = tile.astype(BF16)
            state = h0[two, :] + nt(oall[two, :], wot[...]) + vec_f[7:8, :]
            differs = (pair + core) - 2 * pair * core
            for i in range(2):
                part = state[i * pad : (i + 1) * pad]
                h1own[i * (1 - differs) + 2 * differs] = part
                hsum[2 * pair + i] = fold(jnp.where(token, part, 0.0))
            normed, _ = normalise(state)
            u = (normed * gain2 + shift2).astype(BF16)
            ubuf[two, :] = u
            if pair == 0:
                relay_o(3)
                relay_o(4)
            z = nn(u, w1[...]) + bias_f[0:1, :]
            cdf = 0.5 * (1.0 + lax.erf(z * SQRT_HALF))
            act = (z * cdf).astype(BF16).astype(F32)
            tail = cdf + z * jnp.exp(-0.5 * z * z) * INV_ROOT_TAU
            for i in range(2):
                part = slice(i * pad, (i + 1) * pad)
                asum[2 * pair + i] = fold(jnp.where(token, act[part], 0.0))
                slope[(2 * pair + i) * pad : (2 * pair + i + 1) * pad, :] = jnp.where(token, tail[part], 0.0)
            if pair == 0:
                relay_o(5)

        feed(0)
        feed(1)

        def stack(ref):
            parts = [jnp.sum(ref[n], 0, keepdims=True) for n in range(4)]
            return jnp.concatenate(parts + [jnp.zeros((SMALL - 4, width), F32)], 0)

        act_sum = stack(asum)
        act_hi, act_lo = split_two(act_sum)
        both = nt(jnp.concatenate([act_hi, act_lo], 0), w2t[...])
        mx_s[...] = both[:8] + both[SMALL : SMALL + 8]
        for shift in (1, 2, 3):
            spread(mx_s, mx_r, mxs, mxr, shift).start()
        mx_r[me] = mx_s[...]
        h_mean = stack(hsum) * (1.0 / seq)
        for shift in (1, 2, 3):
            remote(
                mx_s, mx_r.at[lax.rem(me + 4 - shift, 4)], mxs.at[shift - 1], mxr.at[shift - 1], mate
            ).wait_recv()
        mlp = jnp.concatenate(
            [mx_r[0] + mx_r[1] + mx_r[2] + mx_r[3], jnp.zeros((SMALL - 8, width), F32)], 0
        )
        average = h_mean + mlp * (1.0 / seq) + vec_f[8:9, :]
        normed3, inverse3 = normalise(average)
        pooled = (normed3 * gain3 + shift3).astype(BF16)
        logits = nt(pooled, head[...])
        class_ok = lax.broadcasted_iota(jnp.int32, (1, head.shape[0]), 1) < classes
        logits = jnp.where(class_ok, logits, NEG)
        top = jnp.max(logits, -1, keepdims=True)
        exp_l = jnp.exp(logits - top)
        total_l = jnp.sum(exp_l, -1, keepdims=True)
        hot = hot_ref[step]
        each = top + jnp.log(total_l) - jnp.sum(jnp.where(class_ok, logits, 0.0) * hot, -1, keepdims=True)
        loss = jnp.sum(jnp.where(small_ok, each, 0.0), 0, keepdims=True) * 0.25
        live = live_ref[0, step]
        rho = live_ref[1, step]
        loss_tile = live * loss
        d_logits = jnp.where(small_ok, (exp_l / total_l - hot) * 0.25, 0.0).astype(BF16)
        d_head = tn(d_logits, pooled)
        head_g[...] = d_head
        d_pooled = nn(d_logits, head[...])
        d_average = norm_grad(d_pooled, gain3, normed3, inverse3)
        d_token = d_average * (1.0 / seq)
        d_mlp = d_token.astype(BF16)
        dact[...] = nn(d_mlp, w2t[...])
        for r in range(4):
            scal[r] = jnp.broadcast_to(d_token[r : r + 1, :], (8, width))
        vec_g[...] = jnp.zeros_like(vec_g)
        vec_g[4:5, :] = jnp.sum(d_pooled * normed3, 0, keepdims=True)
        vec_g[5:6, :] = jnp.sum(d_pooled, 0, keepdims=True)
        vec_g[8:9, :] = jnp.sum(d_average, 0, keepdims=True)
        low_at = pl.ds(pl.multiple_of(step * SMALL, SMALL), SMALL)
        low_d[low_at, :] = d_mlp
        low_a[low_at, :] = act_sum
        gram_d = nt(d_mlp, d_mlp)
        gram_a = nt(act_hi, act_hi) + nt(act_hi, act_lo) + nt(act_lo, act_hi)
        own_squares = total(gram_d * gram_a)

        for n in range(4):
            scal[4 + n] = jnp.broadcast_to(dact[n : n + 1, :], (8, width))
        bsum[...] = jnp.zeros_like(bsum)
        vacc[...] = jnp.zeros_like(vacc)

        def upper_partial(n):
            at = pl.ds(pl.multiple_of(n * pad, 16), 2 * pad)
            rate = jnp.concatenate(
                [jnp.broadcast_to(scal[4 + n + i][0:1, :], (pad, width)) for i in range(2)], 0
            )
            g = (rate * slope[at, :]).astype(BF16)
            dpre[at, :] = g
            bsum[...] = bsum[...] + fold(g.astype(F32))
            return nt(g, w1[...])

        other = upper_partial(oth0)
        for k in (0, 1):
            s1[k] = other[k * pad : (k + 1) * pad].astype(BF16)
            to_mate(k).start()
        own = upper_partial(own0)
        for k in (0, 1):
            to_mate(k).wait_recv()
            part = own[k * pad : (k + 1) * pad] + r1[k].astype(F32)
            chip[k] = part
            s2[k] = part.astype(BF16)
            to_across(0, k).start()

        ssq[...] = jnp.zeros_like(ssq)
        w1_g = slope

        def weight_grad(left, right, out, which):
            def tile(j, carry):
                at = pl.ds(pl.multiple_of(j * LANE, LANE), LANE)
                g = tn(left[:, at], right[...])
                out[at, :] = g
                ssq[which] = ssq[which] + fold(g * g)
                return carry

            lax.fori_loop(0, width // LANE, tile, 0)

        def embedding_grad(k, left):
            def tile(j, carry):
                at = pl.ds(pl.multiple_of(j * LANE, LANE), LANE)
                g = tn(left[rows(own0 + k), at], xbuf[slot, rows(own0 + k), :])
                g = g + tn(left[rows(oth0 + k), at], xbuf[slot, rows(oth0 + k), :])
                if k == 1:
                    g = g + wet_g[at, :]
                    ssq[3] = ssq[3] + fold(g * g)
                wet_g[at, :] = g
                return carry

            lax.fori_loop(0, width // LANE, tile, 0)

        weight_grad(ubuf, dpre, w1_g, 0)

        for k in (0, 1):
            normed, inverse = normalise(h1own[k])
            h1own[k] = normed
            inverses[k] = inverse
            normed, inverse = normalise(h0[rows(own0 + k), :])
            h0[rows(own0 + k), :] = normed
            inverses[2 + k] = inverse

        def attention_partial(n):
            own_columns = jnp.concatenate(
                [
                    wot[:, pl.ds(pl.multiple_of(me * 128, 128), 128)],
                    wot[:, pl.ds(pl.multiple_of(4 * 128 + (me // 2) * 128, 128), 128)],
                ],
                1,
            )
            wide = nn(datt[rows(n), :], own_columns)
            thirds = jnp.where(core == 1, swap(wide[:, 128:]), wide[:, 128:])
            thirds = jnp.where(low_half((pad, 128)), thirds, 0.0)
            d_ctx = jnp.concatenate([wide[:, :128], thirds], 1).astype(BF16)
            projected = qkv[rows(n), :]
            q, k, v = projected[:, :LANE], projected[:, LANE : 2 * LANE], projected[:, 2 * LANE :]
            d_q = jnp.zeros((pad, LANE), F32)
            d_k = jnp.zeros((pad, LANE), F32)
            d_v = jnp.zeros((pad, LANE), F32)
            for h in range(3):
                part = of_head(d_ctx, h)
                p = prob[n * 3 + h]
                again = p.astype(F32)
                d_p = nt(part, v)
                inner = d_p - jnp.sum(d_p * again, -1, keepdims=True)
                d_s = (again * inner).astype(BF16)
                d_v = d_v + tn(p, part)
                d_q = d_q + nn(d_s, of_head(k, h))
                d_k = d_k + tn(d_s, of_head(q, h))
            d_all = jnp.concatenate([d_q * scale, d_k * scale, d_v], 1).astype(BF16)
            qkv[rows(n), :] = d_all
            return nt(d_all, wqkv[...])

        for k in (0, 1):
            to_across(0, k).wait_recv()
            d_upper = chip[k] + r2[k].astype(F32)
            normed = h1own[k]
            d_state = norm_grad(d_upper, gain2, normed, inverses[k]) + scal[own0 + k][0:1, :]
            d_state = jnp.where(token, d_state, 0.0)
            h1own[k] = d_state
            datt[rows(own0 + k), :] = d_state.astype(BF16)
            gradient_to_mate(datt, 0, own0 + k, k).start()
            vacc[0] = vacc[0] + fold(d_upper * normed)
            vacc[1] = vacc[1] + fold(d_upper)
            vacc[2] = vacc[2] + fold(d_state)
            own = attention_partial(own0 + k)
            remote(
                datt.at[sent_rows(oth0 + k)], datt.at[sent_rows(oth0 + k)], das.at[k], dar.at[k], mate
            ).wait_recv()
            other = attention_partial(oth0 + k)
            to_mate(k).wait_send()
            s1[k] = other.astype(BF16)
            to_mate(k).start()
            to_mate(k).wait_recv()
            own = own + r1[k].astype(F32)
            chip[k] = own
            to_across(0, k).wait_send()
            s2[k] = own.astype(BF16)
            to_across(1, k).start()

        weight_grad(datt, oall, wot_g, 1)
        weight_grad(abuf, qkv, wqkv_g, 2)

        d_emb = ubuf
        for k in (0, 1):
            to_across(1, k).wait_recv()
            d_normed = chip[k] + r2[2 + k].astype(F32)
            normed = h0[rows(own0 + k), :]
            d_state = h1own[k] + norm_grad(d_normed, gain1, normed, inverses[2 + k])
            d_emb[rows(own0 + k), :] = d_state.astype(BF16)
            gradient_to_mate(d_emb, 1, own0 + k, k).start()
            vacc[3] = vacc[3] + fold(d_normed * normed)
            vacc[4] = vacc[4] + fold(d_normed)
            vacc[5] = vacc[5] + fold(jnp.where(row_id >= 1, d_state, 0.0))
            if k == 0:
                pos_g[...] = d_state
            else:
                pos_g[...] = pos_g[...] + d_state
                pos_to_mate().start()
                vec_to_mate().start()
            remote(
                d_emb.at[sent_rows(oth0 + k)], d_emb.at[sent_rows(oth0 + k)],
                das.at[2 + k], dar.at[2 + k], mate,
            ).wait_recv()
            embedding_grad(k, d_emb)
        pos_to_mate().wait()
        vec_to_mate().wait()
        pos_g[...] = pos_g[...] + pos_r[...]
        sums = [jnp.sum(vacc[r] + vec_r[r], 0, keepdims=True) for r in range(6)]
        vec_g[0:1, :] = sums[3]
        vec_g[1:2, :] = sums[4]
        vec_g[2:3, :] = sums[0]
        vec_g[3:4, :] = sums[1]
        vec_g[6:7, :] = sums[5]
        vec_g[7:8, :] = sums[2]
        d_bias = jnp.sum(bsum[...], 0, keepdims=True)
        shared = (
            total(ssq[1] + ssq[3] + fold(pos_g[...] * pos_g[...]) + fold(head_g[...] * head_g[...]))
            + total(vec_g[...] * vec_g[...])
        )
        own_squares = own_squares + total(ssq[0] + ssq[2]) + total(d_bias * d_bias)
        for message in range(6):
            o_to_mate(message).wait_send()
            o_across(message).wait_send()
            o_forward(message).wait_send()
        for k in (0, 1):
            to_mate(k).wait_send()
            to_across(1, k).wait_send()
            gradient_to_mate(datt, 0, own0 + k, k).wait_send()
            gradient_to_mate(d_emb, 1, own0 + k, k).wait_send()
        for shift in (1, 2, 3):
            spread(mx_s, mx_r, mxs, mxr, shift).wait_send()
        first_lane = lax.broadcasted_iota(jnp.int32, (8, 128), 1) < 64
        nx_s[...] = jnp.where(first_lane, own_squares + 0.25 * shared, loss_tile)
        for shift in (1, 2, 3):
            spread(nx_s, nx_r, nxs, nxr, shift).start()
        nx_r[me] = nx_s[...]

        load(2).start()

        @pl.when(step == steps - 1)
        def _():
            for which in (0, 1, 3, 4):
                load(which).start()

        for shift in (1, 2, 3):
            remote(
                nx_s, nx_r.at[lax.rem(me + 4 - shift, 4)], nxs.at[shift - 1], nxr.at[shift - 1], mate
            ).wait_recv()
        norm = jnp.sqrt((nx_r[0] + nx_r[1] + nx_r[2] + nx_r[3]))
        factor = live * (CLIP_LIMIT / jnp.maximum(norm, CLIP_LIMIT))
        norm_out[step] = live * norm
        loss_out[...] = loss_out[...] + nx_r[0]
        for shift in (1, 2, 3):
            spread(nx_s, nx_r, nxs, nxr, shift).wait_send()
        fac = factor[0:1, 0:1]

        low_row = lax.broadcasted_iota(jnp.int32, low_b.shape, 0) // SMALL
        low_b[...] = jnp.where(low_row == step, fac, rho * low_b[...])
        low_w[...] = low_w[...] + live * low_b[...]
        factors = (LOCAL_RATE * low_w[:, 0:1]) * low_a[...]
        low_hi, low_lo = split_two(factors)
        pair = jnp.concatenate([low_hi, low_lo], 0)
        load(2).wait()

        def low_rank(j, carry):
            at = pl.ds(pl.multiple_of(j * LANE, LANE), LANE)
            moved = tn(jnp.concatenate([low_d[:, at], low_d[:, at]], 0), pair)
            w2t[at, :] = (w2t[at, :].astype(F32) - moved).astype(BF16)
            return carry

        lax.fori_loop(0, width // LANE, low_rank, 0)

        def small_update(full, mom, grad):
            mom[...] = rho * mom[...] + fac * grad
            full[...] = full[...] - (live * LOCAL_RATE) * mom[...]

        small_update(pos_f, pos_m, pos_g[...])
        small_update(vec_f, vec_m, vec_g[...])
        small_update(bias_f, bias_m, jnp.broadcast_to(d_bias, (8, width)))
        small_update(head_f, head_m, head_g[...])
        table = (
            (wqkv, wqkv_f, wqkv_m, wqkv_g),
            (w1, w1_f, w1_m, w1_g),
            (wot, wot_f, wot_m, wot_g),
            (wet, wet_f, wet_m, wet_g),
        )

        @pl.when(step < steps - 1)
        def _():
            head[...] = head_f[...].astype(BF16)

            def update(j, carry):
                at = pl.ds(pl.multiple_of(j * 16, 16), 16)
                for low, full, mom, grad in table:
                    m = rho * mom[at, :] + fac * grad[at, :]
                    mom[at, :] = m
                    w = full[at, :] - (live * LOCAL_RATE) * m
                    full[at, :] = w
                    low[at, :] = w.astype(BF16)
                return carry

            lax.fori_loop(0, width // 16, update, 0)

        @pl.when(step == steps - 1)
        def _():
            share = live_ref[2, 0]
            for which in (0, 1, 3, 4):
                load(which).wait()

            def finish(j, carry):
                at = pl.ds(pl.multiple_of(j * 16, 16), 16)

                def ended(full, mom, grad, lanes):
                    m = rho * mom[at, lanes] + fac * grad[at, lanes]
                    return full[at, lanes] - (live * LOCAL_RATE) * m

                for low, full, mom, grad in (table[1], table[3]):
                    w = ended(full, mom, grad, slice(None))
                    low[at, :] = (share * (low[at, :].astype(F32) - w)).astype(BF16)
                three = tiles(ended(wqkv_f, wqkv_m, wqkv_g, slice(None)))
                _, full, mom, grad = table[2]
                wo_first = ended(full, mom, grad, pl.ds(pl.multiple_of(me * 128, 128), 128))
                wo_last = ended(
                    full, mom, grad, pl.ds(pl.multiple_of(4 * 128 + (me // 2) * 128, 128), 128)
                )
                wo_last = jnp.where(core == 1, swap(wo_last), wo_last)
                packed = join(
                    pack_two(three[0:2], three[2:4]) + pack_two(three[4:6], [wo_first, wo_last])
                )
                raw[at, :] = (share * (raw[at, :].astype(F32) - packed)).astype(BF16)
                return carry

            lax.fori_loop(0, width // 16, finish, 0)
            h0[0:REST, :] = jnp.transpose(rest[...].astype(F32))
            for ref, low_row, count in ((pos_f, 0, pad), (vec_f, vec_at, SMALL), (head_f, head_at, n_head)):
                place = pl.ds(low_row, count)
                h0[place, :] = share * (h0[place, :] - ref[...])
            rest[...] = jnp.transpose(h0[0:REST, :]).astype(BF16)
            outs = (
                (w1, main_out.at[:, 0:width]),
                (raw, main_out.at[:, width : 2 * width]),
                (wet, table_out.at[:, 0:width]),
                (rest, table_out.at[:, width : width + REST]),
            )
            copies = [
                pltpu.make_async_copy(src, dst, osem.at[i]) for i, (src, dst) in enumerate(outs)
            ]
            for copy in copies:
                copy.start()
            dbias_out[...] = share * (bias_in[...] - bias_f[...])
            low_d_out[...] = low_d[...]
            low_a_out[...] = share * factors
            for copy in copies:
                copy.wait()

        return carry

    lax.fori_loop(0, steps, one_step, 0)


def local_training(live, patches, hot, main, wo, table, bias, pad, seq, classes):
    steps = patches.shape[0]
    width = main.shape[0]
    n_all = 4 * pad
    n_head = hot.shape[2]
    n_low = steps * SMALL
    vmem = pltpu.VMEM
    dma = pltpu.SemaphoreType.DMA
    anywhere = pl.BlockSpec(memory_space=pl.ANY)
    inside = pl.BlockSpec(memory_space=pltpu.VMEM)
    square = (width, width)
    out_shape = (
        jax.ShapeDtypeStruct((width, 2 * width), BF16),
        jax.ShapeDtypeStruct(table.shape, BF16),
        jax.ShapeDtypeStruct((8, width), F32),
        jax.ShapeDtypeStruct((n_low, width), BF16),
        jax.ShapeDtypeStruct((n_low, width), F32),
        jax.ShapeDtypeStruct((8, 128), F32),
        jax.ShapeDtypeStruct((steps, 8, 128), F32),
    )
    scratch = [
        vmem(square, BF16), vmem(square, BF16), vmem(square, BF16), vmem(square, BF16),
        vmem(square, BF16), vmem((n_head, width), BF16),
    ]
    for _ in range(2):
        scratch += [
            vmem(square, F32), vmem(square, F32), vmem(square, F32), vmem(square, F32),
            vmem((pad, width), F32), vmem((n_head, width), F32), vmem((SMALL, width), F32),
            vmem((8, width), F32),
        ]
    scratch += [
        vmem(square, F32), vmem(square, F32), vmem(square, F32), vmem((pad, width), F32),
        vmem((n_head, width), F32), vmem((SMALL, width), F32),
        vmem((2, n_all, width), BF16), vmem((n_all, width), F32), vmem((n_all, width), F32),
        vmem((12, pad, pad), BF16), vmem((n_all, width), BF16), vmem((n_all, width), BF16),
        vmem((n_all, width), BF16), vmem((2, pad, 4 * 128), BF16), vmem((n_all, width), BF16),
        vmem((n_all, width), BF16), vmem((3, pad, width), F32), vmem((n_all, width), BF16),
        vmem((2, pad, width), F32), vmem((4, pad, 1), F32),
        vmem((4, 8, width), F32), vmem((4, 8, width), F32), vmem((SMALL, width), F32),
        vmem((8, width), F32), vmem((6, 8, width), F32), vmem((4, 8, width), F32),
        vmem((n_low, width), BF16), vmem((n_low, width), F32), vmem((n_low, 128), F32),
        vmem((n_low, 128), F32), vmem((8, 8, width), F32),
        vmem((2, pad, width), BF16), vmem((2, pad, width), BF16), vmem((2, pad, width), BF16),
        vmem((4, pad, width), BF16), vmem((8, width), F32), vmem((4, 8, width), F32),
        vmem((8, 128), F32), vmem((4, 8, 128), F32), vmem((pad, width), F32),
        vmem((6, 8, width), F32),
        dma((9,)), dma((2,)), dma((6,)), dma((6,)), dma((6,)), dma((6,)), dma((6,)), dma((6,)),
        dma((2,)), dma((2,)), dma((4,)), dma((4,)), dma((4,)), dma((4,)), dma((2,)), dma((2,)),
        dma((3,)), dma((3,)), dma((3,)), dma((3,)), dma((6,)),
    ]
    return pl.pallas_call(
        functools.partial(train_kernel, (steps, seq, pad, classes)),
        out_shape=out_shape,
        in_specs=[pl.BlockSpec(memory_space=pltpu.SMEM), anywhere, inside]
        + [anywhere] * 3 + [inside],
        out_specs=(anywhere,) * 2 + (inside,) * 5,
        scratch_shapes=scratch,
        compiler_params=pltpu.CompilerParams(
            collective_id=0, has_side_effects=True, vmem_limit_bytes=VMEM_LIMIT
        ),
        name="local_training",
    )(live, patches, hot, main, wo, table, bias)


def place_patches(chosen_ref, pool_ref, out_ref):
    seq_rows, width = pool_ref.shape[1], pool_ref.shape[2]
    pad = out_ref.shape[1]
    below = jnp.zeros((pad - 1 - seq_rows, width), F32)
    whole = jnp.concatenate([jnp.zeros((1, width), F32), pool_ref[0].astype(F32), below], 0)
    out_ref[0] = whole.astype(BF16)


def pick_patches(pool, chosen, pad):
    count = chosen.shape[0]
    _, patch_rows, width = pool.shape
    return pl.pallas_call(
        place_patches,
        out_shape=jax.ShapeDtypeStruct((count, pad, width), BF16),
        grid_spec=pltpu.PrefetchScalarGridSpec(
            num_scalar_prefetch=1,
            grid=(count,),
            in_specs=[pl.BlockSpec((1, patch_rows, width), lambda i, ids: (ids[i], 0, 0))],
            out_specs=pl.BlockSpec((1, pad, width), lambda i, ids: (i, 0, 0)),
        ),
        name="pick_patches",
    )(chosen, pool)


def ring_places(clients):
    depth = clients // 2
    client = lax.axis_index("client")
    member = lax.axis_index("tensor")
    core = lax.rem(member, 2)
    return (
        depth, client, client // 2, lax.rem(client, 2), member, core, member // 2,
        member + 1 - 2 * core, lax.rem(member + 2, 4),
    )


def send(src, dst, send_sem, recv_sem, client, member):
    return pltpu.make_async_remote_copy(
        src_ref=src, dst_ref=dst, send_sem=send_sem, recv_sem=recv_sem,
        device_id={"client": client, "tensor": member}, device_id_type=MESH,
    )


def span(start, size, unit):
    return pl.ds(pl.multiple_of(start, unit), size)


def gather_kernel(
    clients, main_ref, table_ref, chosen_ref, pool_ref, main_out, wo_out, table_out, x_out,
    pool_buf, x_buf, pool_sem, x_sem, up_s, up_r, down_s, down_r, y_s, y_r, mate_s, mate_r, x_s, x_r, on_s, on_r, own_sem, keep_sem,
):
    depth, client, z, y, member, core, chip_x, mate, across = ring_places(clients)
    block = main_ref.shape[0]
    half = block // 2
    columns = table_ref.shape[1] // 2
    peer = client + 1 - 2 * y

    wide = main_ref.shape[1]
    tail = wide - LANE

    def table_part(origin, who):
        return table_out.at[
            span(origin * block + (who // 2) * half, half, half),
            span(lax.rem(who, 2) * columns, columns, 128),
        ]

    def wo_part(origin, who):
        return wo_out.at[span(origin * block, block, block), span(who * LANE, LANE, LANE)]

    def shared(origin, who):
        return (wo_part(origin, who), table_part(origin, who))

    def main_part(origin, lanes):
        return main_out.at[span(origin * block, block, block), lanes]

    front, back = slice(0, 2 * wide // 3), slice(2 * wide // 3, wide)

    def landed(origin):
        return (main_part(origin, back), table_part(origin, member), main_part(origin, front))

    own_table = table_ref.at[span(chip_x * half, half, half), span(core * columns, columns, 128)]
    own_pieces = (main_ref.at[:, back], own_table, main_ref.at[:, front])

    def given(origin, mine):
        if mine:
            return (main_ref.at[:, tail:wide], own_table)
        return (main_part(origin, slice(tail, wide)), table_part(origin, member))

    def message(origin, mine, send_sem, recv_sem, index, to, part):
        sources = own_pieces if mine else landed(origin)
        return [
            send(src, dst, send_sem.at[p, index], recv_sem.at[p, index], to, member)
            for p, (src, dst) in enumerate(zip(sources, landed(origin)))
        ][part]

    first, second, every = slice(0, 2), slice(2, 3), slice(0, 3)

    def up(origin, i, part, mine=False):
        return message(origin, mine, up_s, up_r, i, client + 2, part)

    def down(origin, i, part, mine=False):
        return message(origin, mine, down_s, down_r, i, client - 2, part)

    def over(origin, part, mine=False):
        return message(origin, mine, y_s, y_r, origin // 2, peer, part)

    def give(origin, mine, send_sem, recv_sem, to):
        return [
            send(src, dst, send_sem.at[p, origin], recv_sem.at[p, origin], client, to)
            for p, (src, dst) in enumerate(zip(given(origin, mine), shared(origin, member)))
        ]

    def keep(origin, mine=False):
        return pltpu.make_async_copy(given(origin, mine)[0], wo_part(origin, member), keep_sem.at[origin])

    def share(origin, mine=False):
        return give(origin, mine, mate_s, mate_r, mate) + give(origin, mine, x_s, x_r, across)

    def from_across(origin):
        return [
            send(dst, dst, x_s.at[p, origin], x_r.at[p, origin], client, across)
            for p, dst in enumerate(shared(origin, across))
        ]

    def pass_on(origin):
        return [
            send(dst, dst, on_s.at[p, origin], on_r.at[p, origin], client, mate)
            for p, dst in enumerate(shared(origin, across))
        ]

    def start(copies):
        for copy in copies:
            copy.start()

    def arrived(copies):
        for copy in copies:
            copy.wait_recv()

    def sent(copies):
        for copy in copies:
            copy.wait_send()

    has_up, has_down = z < depth - 1, z > 0

    barrier = pltpu.get_barrier_semaphore()

    def hello(to_client, to_member):
        pl.semaphore_signal(
            barrier, inc=1, device_id={"client": to_client, "tensor": to_member}, device_id_type=MESH
        )

    hello(peer, member)
    for shift in (1, 2, 3):
        hello(client, lax.rem(member + shift, 4))
    for shift in range(1, depth):
        hello(2 * lax.rem(z + shift, depth) + y, member)
    pl.semaphore_wait(barrier, 3 + depth)

    for part in (first, second):
        start(over(client, part, True))

        @pl.when(has_up)
        def _():
            start(up(client, 0, part, True))

        @pl.when(has_down)
        def _():
            start(down(client, 0, part, True))

    start(share(client, True))
    keep(client, True).start()
    local = [
        pltpu.make_async_copy(src, dst, own_sem.at[p])
        for p, (src, dst) in enumerate(zip(own_pieces, landed(client)))
    ]
    start(local)

    images = chosen_ref.shape[0] // 8
    pool_size = pool_buf.shape[1] // 8
    patch_rows = pool_ref.shape[0] // pool_size
    pad = x_out.shape[1]

    def base(b):
        return lax.min(lax.max(8 * b - 1, 0), patch_rows - 8)

    deep = pool_buf.shape[0]

    def pool_load(b):
        k = lax.rem(b, deep)
        return pltpu.make_async_copy(
            pool_ref.at[span(base(b) * pool_size, 8 * pool_size, 32), :], pool_buf.at[k], pool_sem.at[k]
        )

    def x_store(b):
        k = lax.rem(b, deep)
        return pltpu.make_async_copy(x_buf.at[k], x_out.at[:, span(8 * b, 8, 8), :], x_sem.at[k])

    for b in range(deep - 1):
        pool_load(b).start()
    lane = lax.broadcasted_iota(jnp.int32, (8 * images, 8 * pool_size), 1)
    line_row = lax.rem(lax.broadcasted_iota(jnp.int32, (8 * images, 1), 0), 8)

    def pick(b, carry):
        k = lax.rem(b, deep)
        pool_load(b).wait()

        @pl.when(b < pad // 8 - (deep - 1))
        def _():
            pool_load(b + deep - 1).start()

        wanted = (8 * b - 1 + line_row - base(b)) * pool_size + chosen_ref[...]
        picked = nn((lane == wanted).astype(BF16), pool_buf[k]).astype(BF16)

        @pl.when(b >= deep)
        def _():
            x_store(b - deep).wait()

        x_buf[k] = picked.reshape(images, 8, picked.shape[1])
        x_store(b).start()
        return carry

    lax.fori_loop(0, pad // 8, pick, 0)
    for b in range(pad // 8 - deep, pad // 8):
        x_store(b).wait()

    def line(d, act):
        @pl.when(z >= d)
        def _():
            act(client - 2 * d, True)

        @pl.when(z < depth - d)
        def _():
            act(client + 2 * d, False)

    def across_line(d, act):
        if d == 0:
            act(peer, True)
            return

        @pl.when(z >= d)
        def _():
            act(peer - 2 * d, True)

        @pl.when(z < depth - d)
        def _():
            act(peer + 2 * d, False)

    def line_in(d, part):
        def act(origin, below):
            line_s, line_r = (up_s, up_r) if below else (down_s, down_r)
            arrived(message(origin, False, line_s, line_r, d - 1, peer, part))
            if d < depth - 1:

                @pl.when(has_up if below else has_down)
                def _():
                    start(up(origin, d, part) if below else down(origin, d, part))

            start(over(origin, part))
            if part is first:
                start(share(origin))
                keep(origin).start()

        return act

    def y_in(origin, below):
        arrived(over(origin, first))
        start(share(origin))
        keep(origin).start()

    def forward(origin, below=True):
        arrived(from_across(origin))
        start(pass_on(origin))

    for d in range(1, depth + 1):
        if d < depth:
            line(d, line_in(d, first))
        across_line(d - 1, y_in)
        if d < depth:
            line(d, line_in(d, second))
        if d == 1:
            forward(client)
        else:
            line(d - 1, forward)
            across_line(d - 2, forward)
    across_line(depth - 1, forward)
    for d in range(depth):
        across_line(d, lambda origin, below: arrived(over(origin, second)))

    for copy in local:
        copy.wait()
    for origin in range(clients):
        sent(share(origin))
        sent(pass_on(origin))
        keep(origin).wait()
        arrived([
            send(dst, dst, mate_s.at[p, origin], mate_r.at[p, origin], client, mate)
            for p, dst in enumerate(shared(origin, mate))
        ])
        arrived([
            send(dst, dst, on_s.at[p, origin], on_r.at[p, origin], client, mate)
            for p, dst in enumerate(shared(origin, lax.rem(mate + 2, 4)))
        ])
    for d in range(depth):
        sent(over(2 * d + y, every))

        @pl.when(has_up & (z >= d))
        def _():
            if d < depth - 1:
                sent(up(client - 2 * d, d, every))

        @pl.when(has_down & (z < depth - d))
        def _():
            if d < depth - 1:
                sent(down(client + 2 * d, d, every))


def gather_weights(clients, main, table, chosen, pool, pad):
    depth = clients // 2
    dma = pltpu.SemaphoreType.DMA
    anywhere = pl.BlockSpec(memory_space=pl.ANY)
    inside = pl.BlockSpec(memory_space=pltpu.VMEM)
    width = main.shape[0] * clients
    hops = depth - 1
    pool_size, patch_rows, features = pool.shape
    images = chosen.shape[0]
    rows = jnp.transpose(pool, (1, 0, 2)).reshape(patch_rows * pool_size, features)
    column = jnp.repeat(chosen, 8).reshape(8 * images, 1)
    return pl.pallas_call(
        functools.partial(gather_kernel, clients),
        out_shape=(
            jax.ShapeDtypeStruct((width, main.shape[1]), BF16),
            jax.ShapeDtypeStruct((width, 4 * LANE), BF16),
            jax.ShapeDtypeStruct((width, table.shape[1]), BF16),
            jax.ShapeDtypeStruct((images, pad, features), BF16),
        ),
        in_specs=[inside] * 3 + [anywhere],
        out_specs=(anywhere,) * 4,
        scratch_shapes=[
            pltpu.VMEM((6, 8 * pool_size, features), BF16), pltpu.VMEM((6, images, 8, features), BF16),
            dma((6,)), dma((6,)),
            dma((3, hops)), dma((3, hops)), dma((3, hops)), dma((3, hops)), dma((3, depth)),
            dma((3, depth)),
        ] + [dma((2, clients))] * 6 + [dma((3,)), dma((clients,))],
        compiler_params=pltpu.CompilerParams(collective_id=1, has_side_effects=True),
        name="gather_weights",
    )(main, table, column, rows)


def reduce_kernel(
    clients, main_in, table_in, low_in, tile_in, main_out, table_out, low_out, tile_out,
    own_main, own_table, y_main, y_table, zs_main, zs_table, zr_main, zr_table, whole, low_all, tile_all,
    own_sem, y_s, y_r, z_s, z_r, low_s, low_r, tile_s, tile_r, q_s, q_r,
):
    depth, client, z, y, member, core, chip_x, mate, across = ring_places(clients)
    block = own_main.shape[1]
    half, columns = own_table.shape[1], own_table.shape[2]
    peer = client + 1 - 2 * y
    cut = own_main.shape[2] // 2
    lanes = (None, slice(0, cut), slice(cut, 2 * cut))
    parts = (0, 1, 2)

    def source(owner, p):
        if p == 0:
            return table_in.at[
                span(owner * block + chip_x * half, half, half), span(core * columns, columns, 128)
            ]
        return main_in.at[span(owner * block, block, block), lanes[p]]

    def slot(table_ref, main_ref, i, p):
        return table_ref.at[i] if p == 0 else main_ref.at[i, :, lanes[p]]

    def own_load(level, p):
        return pltpu.make_async_copy(
            source(2 * level + y, p), slot(own_table, own_main, level, p), own_sem.at[p, level]
        )

    def over(level, p):
        return send(
            source(2 * level + 1 - y, p), slot(y_table, y_main, level, p),
            y_s.at[p, level], y_r.at[p, level], peer, member,
        )

    def onward(i, p):
        owner = 2 * lax.rem(z + 1 + i, depth) + y
        return send(
            slot(zs_table, zs_main, i, p), slot(zr_table, zr_main, i, p),
            z_s.at[p, i], z_r.at[p, i], owner, member,
        )

    def small(shift):
        to = lax.rem(client + shift, clients)
        return [
            send(low_in.at[to], low_all.at[client], low_s.at[shift - 1], low_r.at[shift - 1], to, member),
            send(tile_in, tile_all.at[client], tile_s.at[shift - 1], tile_r.at[shift - 1], to, member),
        ]

    def small_from(shift):
        origin = lax.rem(client + clients - shift, clients)
        return [
            send(low_in.at[origin], low_all.at[origin], low_s.at[shift - 1], low_r.at[shift - 1], origin, member),
            send(tile_in, tile_all.at[origin], tile_s.at[shift - 1], tile_r.at[shift - 1], origin, member),
        ]

    def quarter(who):
        return whole.at[span((who // 2) * half, half, half), span(lax.rem(who, 2) * columns, columns, 128)]

    def pass_quarter(who, index, to):
        return send(quarter(who), quarter(who), q_s.at[index], q_r.at[index], client, to)

    barrier = pltpu.get_barrier_semaphore()
    for shift in range(1, clients):
        pl.semaphore_signal(
            barrier, inc=1,
            device_id={"client": lax.rem(client + shift, clients), "tensor": member}, device_id_type=MESH,
        )
    for shift in (1, 2, 3):
        pl.semaphore_signal(
            barrier, inc=1,
            device_id={"client": client, "tensor": lax.rem(member + shift, 4)}, device_id_type=MESH,
        )
    order = [(i, 0) for i in range(depth)] + [(i, p) for i in range(depth) for p in (1, 2)]
    for i, p in order:
        own_load(lax.rem(z + 1 + i, depth), p).start()
    pl.semaphore_wait(barrier, clients - 1 + 3)
    for i, p in order:
        over(lax.rem(z + 1 + i, depth), p).start()
    for shift in range(1, clients):
        for copy in small(shift):
            copy.start()
    low_all[client] = low_in[client]
    tile_all[client] = tile_in[...]

    def pair_up(i, p):
        level = lax.rem(z + 1 + i, depth)
        own_load(level, p).wait()
        over(level, p).wait_recv()
        pair = (
            slot(own_table, own_main, level, p)[...].astype(F32)
            + slot(y_table, y_main, level, p)[...].astype(F32)
        )
        if i < depth - 1:
            slot(zs_table, zs_main, i, p)[...] = pair.astype(BF16)
            onward(i, p).start()
        elif p == 0:
            quarter(member)[...] = pair
        else:
            main_out[:, lanes[p]] = pair

    for i in range(depth):
        pair_up(i, 0)
    pair_up(0, 1)
    pair_up(0, 2)
    mine = quarter(member)
    for i in range(depth - 1):
        onward(i, 0).wait_recv()
        mine[...] = mine[...] + zr_table[i].astype(F32)
    to_others = [pass_quarter(member, 0, mate), pass_quarter(member, 1, across)]
    for copy in to_others:
        copy.start()
    for i in range(1, depth):
        pair_up(i, 1)
        pair_up(i, 2)
        if i == 1:
            pass_quarter(across, 1, across).wait_recv()
            second = pass_quarter(across, 2, mate)
            second.start()
    for shift in range(1, clients):
        for copy in small_from(shift):
            copy.wait_recv()
    low_out[...] = low_all[...]
    tile_out[...] = tile_all[...]
    pass_quarter(mate, 0, mate).wait_recv()
    pass_quarter(lax.rem(mate + 2, 4), 2, mate).wait_recv()
    table_out[...] = whole[...]
    for i in range(depth - 1):
        for p in (1, 2):
            onward(i, p).wait_recv()
            main_out[:, lanes[p]] = main_out[:, lanes[p]] + zr_main[i, :, lanes[p]].astype(F32)
    for copy in to_others + [second]:
        copy.wait_send()
    for shift in range(1, clients):
        for copy in small(shift):
            copy.wait_send()
    for i in range(depth):
        for p in parts:
            over(i, p).wait_send()
            if i < depth - 1:
                onward(i, p).wait_send()


def reduce_deltas(clients, main, table, low, tile):
    depth = clients // 2
    dma = pltpu.SemaphoreType.DMA
    vmem = pltpu.VMEM
    anywhere = pl.BlockSpec(memory_space=pl.ANY)
    inside = pl.BlockSpec(memory_space=pltpu.VMEM)
    block = main.shape[0] // clients
    half, columns = block // 2, table.shape[1] // 2
    wide = main.shape[1]
    hops = depth - 1
    return pl.pallas_call(
        functools.partial(reduce_kernel, clients),
        out_shape=(
            jax.ShapeDtypeStruct((block, wide), F32),
            jax.ShapeDtypeStruct((block, table.shape[1]), F32),
            jax.ShapeDtypeStruct(low.shape, BF16),
            jax.ShapeDtypeStruct((clients,) + tile.shape, F32),
        ),
        in_specs=[anywhere, anywhere, inside, inside],
        out_specs=(inside,) * 4,
        scratch_shapes=[
            vmem((depth, block, wide), BF16), vmem((depth, half, columns), BF16),
            vmem((depth, block, wide), BF16), vmem((depth, half, columns), BF16),
            vmem((hops, block, wide), BF16), vmem((hops, half, columns), BF16),
            vmem((hops, block, wide), BF16), vmem((hops, half, columns), BF16),
            vmem((block, table.shape[1]), F32), vmem(low.shape, BF16),
            vmem((clients,) + tile.shape, F32),
            dma((3, depth)), dma((3, depth)), dma((3, depth)), dma((3, hops)), dma((3, hops)),
            dma((clients - 1,)), dma((clients - 1,)), dma((clients - 1,)), dma((clients - 1,)),
            dma((3,)), dma((3,)),
        ],
        compiler_params=pltpu.CompilerParams(collective_id=2, has_side_effects=True),
        name="reduce_deltas",
    )(main, table, low, tile)


def adam(master, first, second, grad):
    first2 = BETA_ONE * first + (1.0 - BETA_ONE) * grad
    second2 = BETA_TWO * second + (1.0 - BETA_TWO) * grad * grad
    moved = (
        first2 / (1.0 - BETA_ONE**ROUND) / (jnp.sqrt(second2 / (1.0 - BETA_TWO**ROUND)) + ADAM_EPS)
    )
    fresh = master - SERVER_RATE * (moved + WEIGHT_DECAY * master)
    return (fresh, first2, second2, fresh.astype(jnp.bfloat16))


def on_device(
    pool, index, tau, counts, labels,
    in_bf, out_bf, table_bf, bias_bf,
    in_master, out_master, table_master, bias_master,
    in_first, out_first, table_first, bias_first,
    in_second, out_second, table_second, bias_second,
):
    clients = lax.axis_size("client")
    group = in_bf.shape[2]
    steps, images = index.shape[1], index.shape[2]
    patch_rows, features = pool.shape[1], pool.shape[2]
    seq = patch_rows + 1
    pad = (seq + 15) // 16 * 16
    own = in_bf.shape[1]
    width = own * clients
    rows_total = table_bf.shape[0]
    classes = rows_total - features - seq - 9
    head_rows = (classes + 127) // 128 * 128
    vec_at, head_at = pad, pad + SMALL

    in_rows = jnp.transpose(in_bf, (1, 0, 2))
    out_rows = jnp.transpose(out_bf, (2, 0, 1))
    wo_rows = out_rows[:, :1]
    main_own = jnp.concatenate(
        [in_rows[:, 3:], out_rows[:, 1:], in_rows[:, :3], wo_rows], 1
    ).reshape(own, 12 * group)
    empty = functools.partial(jnp.zeros, dtype=BF16)
    table_own = jnp.concatenate(
        [
            table_bf[: features + seq],
            empty((pad - seq, own)),
            table_bf[features + seq : features + seq + 9],
            empty((SMALL - 9, own)),
            table_bf[features + seq + 9 :],
            empty((REST - head_at - classes, own)),
        ],
        0,
    ).T
    direct = clients == 8
    if direct:
        main, wo_all, table, patches = gather_weights(
            clients, main_own, table_own, index[0].reshape(steps * images), pool, pad
        )
    else:
        main = lax.all_gather(main_own, "client", axis=0, tiled=True)
        table = lax.all_gather(table_own, "client", axis=0, tiled=True)
        wo_all = lax.all_gather(main[:, 12 * group - LANE :], "tensor", axis=1, tiled=True)
        patches = pick_patches(pool, index[0].reshape(steps * images), pad)
    bias = jnp.broadcast_to(bias_bf.astype(F32).reshape(1, 4 * group), (8, 4 * group))

    taken = tau[0]
    ladder = jnp.arange(steps, dtype=jnp.int32)
    live = (ladder < taken).astype(F32)
    factor_sum = jnp.sum(
        jnp.where(
            ladder < taken,
            (1.0 - MOMENTUM_RHO ** (ladder + 1).astype(F32)) / (1.0 - MOMENTUM_RHO),
            0.0,
        )
    )
    examples = counts[0].astype(F32)
    share = examples / factor_sum
    scalars = jnp.stack(
        [live, jnp.where(ladder < taken, MOMENTUM_RHO, 1.0), jnp.full((steps,), share)]
    )
    patches = patches.reshape(steps, images * pad, features)
    slots = jnp.arange(pool.shape[0], dtype=jnp.int32)
    picked = index[0][:, :, None] == slots[None, None, :]
    target = jnp.sum(picked.astype(jnp.int32) * labels[None, None, :], 2)
    hot = (target[:, :, None] == jnp.arange(head_rows, dtype=jnp.int32)).astype(F32)
    hot = jnp.pad(hot, ((0, 0), (0, SMALL - images), (0, 0)))

    d_main, d_table, d_bias, low_d, low_a, loss_sum, norms = local_training(
        scalars, patches, hot, main, wo_all, table, bias, pad, seq, classes
    )
    norms = norms[:, 0, 0]
    loss_sum = loss_sum[0, 64]
    used = steps * images

    def squeeze(value):
        return value.reshape(steps, SMALL, width)[:, :images].reshape(used, width)

    low_d, low_a = squeeze(low_d), squeeze(low_a).astype(BF16)
    own_scalars = jnp.stack([examples, examples * loss_sum / taken.astype(F32), examples * factor_sum])
    if direct:
        parts = jnp.pad(
            jnp.transpose(low_d.reshape(used, clients, own), (1, 0, 2)),
            ((0, 0), (0, 0), (0, 128 - own)),
        )
        low = jnp.concatenate([jnp.broadcast_to(low_a[None], (clients, used, width)), parts], 2)
        bias_rows = width // 128
        tile = jnp.concatenate(
            [
                d_bias[:1].reshape(bias_rows, 128),
                jnp.pad(own_scalars.reshape(1, 3), ((0, 7 - bias_rows), (0, 125))),
                jnp.zeros((1, 128), F32),
            ],
            0,
        )
        mine, table_sum, low_all, tile_all = reduce_deltas(clients, d_main, d_table, low, tile)
        all_a = low_all[:, :, :width].reshape(clients * used, width).astype(F32)
        part_d = low_all[:, :, width : width + own].reshape(clients * used, own).astype(F32)
        tile_sum = jnp.sum(tile_all, 0)
        bias_delta = tile_sum[:bias_rows].reshape(4, group)
        total_c, weighted_loss, weighted_factor = (tile_sum[bias_rows, i] for i in range(3))
    else:
        sums = lax.psum((own_scalars, d_bias[:1].reshape(4, group)), "client")
        total_c, weighted_loss, weighted_factor = (sums[0][i] for i in range(3))
        bias_delta = sums[1]
        mine = lax.psum_scatter(d_main, "client", scatter_dimension=0, tiled=True).astype(F32)
        first_member = lax.axis_index("tensor") == 0
        d_table = jnp.where(first_member, d_table, jnp.zeros_like(d_table))
        table_sum = lax.psum(
            lax.psum_scatter(d_table, "client", scatter_dimension=0, tiled=True).astype(F32), "tensor"
        )
        all_a = lax.all_gather(low_a, "client", axis=0, tiled=True).astype(F32)
        all_d = lax.all_gather(low_d, "client", axis=0, tiled=True)
        part_d = lax.dynamic_slice_in_dim(all_d, lax.axis_index("client") * own, own, 1).astype(F32)
    slabs = jnp.transpose(mine.reshape(own, 8, group), (1, 0, 2))
    in_delta = jnp.concatenate([slabs[4:7], slabs[:4]], 0)
    d_wo = slabs[7].T
    d_w2 = jnp.einsum("rc,rd->cd", all_a, part_d, precision=lax.Precision.HIGHEST)
    out_delta = jnp.concatenate([d_wo[None], d_w2.reshape(4, group, own)], 0)
    turned = table_sum.T
    table_delta = jnp.concatenate(
        [
            turned[: features + seq],
            turned[features + vec_at : features + vec_at + 9],
            turned[features + head_at : features + head_at + classes],
        ],
        0,
    )
    server_scale = weighted_factor / total_c / total_c
    masters = (in_master, out_master, table_master, bias_master)
    firsts = (in_first, out_first, table_first, bias_first)
    seconds = (in_second, out_second, table_second, bias_second)
    deltas = (in_delta, out_delta, table_delta, bias_delta)
    results = [
        adam(mst, fst, snd, server_scale * dlt)
        for mst, fst, snd, dlt in zip(masters, firsts, seconds, deltas)
    ]
    return (
        weighted_loss / total_c,
        norms[None],
        *[r[0] for r in results],
        *[r[1] for r in results],
        *[r[2] for r in results],
        *[r[3] for r in results],
    )


def solution(mesh):
    by_client = P("client", None, None)
    state = (P(None, "client", "tensor"), P(None, "tensor", "client"), P(None, "client"), P(None, "tensor"))
    in_specs = (by_client, by_client, P("client"), P("client"), P("client")) + state * 4
    out_specs = (P(), P("client", None)) + state * 4
    return jax.shard_map(
        on_device, mesh=mesh, in_specs=in_specs, out_specs=out_specs, check_vma=False
    )
```

```python
import functools

import jax
import jax.numpy as jnp
from jax import lax
from jax.experimental import pallas as pl
from jax.experimental.pallas import tpu as pltpu
from jax.sharding import PartitionSpec as P

HEAD_DIM = 64
ROUND = 5
EPS_NORM = 1e-06
MOMENTUM_RHO = 0.9
LOCAL_RATE = 0.05
CLIP_LIMIT = 1.0
BETA_ONE = 0.5
BETA_TWO = 0.7
ADAM_EPS = 1e-08
WEIGHT_DECAY = 0.05
SERVER_RATE = 0.05
SQRT_HALF = 0.7071067811865476
INV_ROOT_TAU = 0.3989422804014327
MESH = pl.DeviceIdType.MESH
F32 = jnp.float32
BF16 = jnp.bfloat16
NEG = -1e30
LANE = 256
SMALL = 16
REST = 512
VMEM_LIMIT = 67043328


def dot(left, right, dims):
    return lax.dot_general(left, right, (dims, ((), ())), preferred_element_type=F32)


def nn(left, right):
    return dot(left, right, ((1,), (0,)))


def nt(left, right):
    return dot(left, right, ((1,), (1,)))


def tn(left, right):
    return dot(left, right, ((0,), (0,)))


def fold(value):
    rows, width = value.shape
    return jnp.sum(value.reshape(rows // 8, 8, width), 0)


def total(value):
    return jnp.sum(jnp.sum(value, 1, keepdims=True), 0, keepdims=True)


def normalise(value):
    centre = value - jnp.mean(value, -1, keepdims=True)
    inverse = lax.rsqrt(jnp.mean(centre * centre, -1, keepdims=True) + EPS_NORM)
    return (centre * inverse, inverse)


def norm_grad(grad, gain, normed, inverse):
    scaled = grad * gain
    return inverse * (
        scaled
        - jnp.mean(scaled, -1, keepdims=True)
        - normed * jnp.mean(scaled * normed, -1, keepdims=True)
    )


def split_two(value):
    high = value.astype(BF16)
    return (high, (value - high.astype(F32)).astype(BF16))


def swap(tile):
    return pltpu.roll(tile, HEAD_DIM, 1)


def tiles(value):
    return [value[:, i : i + 128] for i in range(0, value.shape[1], 128)]


def low_half(shape):
    return lax.broadcasted_iota(jnp.int32, shape, 1) < HEAD_DIM


def pack_two(left, right):
    low = low_half(left[0].shape)
    return [
        left[0],
        jnp.where(low, left[1], swap(right[0])),
        jnp.where(low, swap(right[0]), swap(right[1])),
    ]


def unpack_two(packed):
    low = low_half(packed[0].shape)
    nothing = jnp.zeros_like(packed[0])
    middle, last = swap(packed[1]), swap(packed[2])
    return (
        [packed[0], jnp.where(low, packed[1], nothing)],
        [jnp.where(low, middle, last), jnp.where(low, last, nothing)],
    )


def train_kernel(
    sizes,
    tau_ref,
    count_ref,
    label_ref,
    index_ref,
    x_hbm,
    main_in,
    wo_in,
    table_in,
    bias_in,
    main_out,
    table_out,
    low_out,
    tile_out,
    norm_out,
    wqkv, w1, wot, w2t, wet, head,
    wqkv_f, w1_f, wot_f, wet_f, pos_f, head_f, vec_f, bias_f,
    wqkv_m, w1_m, wot_m, wet_m, pos_m, head_m, vec_m, bias_m,
    wqkv_g, wot_g, wet_g, pos_g, head_g, vec_g,
    xbuf, h0, slope, prob, abuf, qkv, oall, third, ubuf, dpre, h1own, datt, chip, inverses,
    hsum, asum, dact, bsum, vacc, ssq,
    low_d, low_a, low_b, low_w, scal, loss_all, factor_kept,
    s1, r1, s2, r2, mx_s, mx_r, nx_s, nx_r, pos_r, vec_r,
    wsem, xsem, o_ps, o_xs, o_fs, o_pr, o_xr, o_fr,
    a1s, a1r, a2s, a2r, das, dar, pvs, pvr, mxs, mxr, nxs, nxr, osem,
):
    steps, seq, pad, classes, clients = sizes
    width = 768
    kept = (seq + 7) // 8 * 8
    me = lax.axis_index("tensor")
    core = lax.rem(me, 2)
    mate = me + 1 - 2 * core
    across = lax.rem(me + 2, 4)
    own0 = 2 * core
    oth0 = 2 - 2 * core

    def rows(n):
        return pl.ds(pl.multiple_of(n * pad, 16), pad)

    def sent_rows(n):
        return pl.ds(pl.multiple_of(n * pad, 16), kept)

    def remote(src, dst, send, recv, device):
        return pltpu.make_async_remote_copy(
            src_ref=src, dst_ref=dst, send_sem=send, recv_sem=recv,
            device_id={"tensor": device}, device_id_type=MESH,
        )

    rest = dpre.at[0:width, 0:REST]
    square_rows = pl.ds(0, width)
    raw = abuf.at[square_rows, :]
    wo_raw = [ubuf.at[square_rows, pl.ds(g * LANE, LANE)] for g in range(3)] + [
        qkv.at[square_rows, pl.ds(0, LANE)]
    ]
    weights_in = [
        main_in.at[:, 2 * width : 3 * width],
        main_in.at[:, 0:width],
        main_in.at[:, width : 2 * width],
        table_in.at[:, 0:width],
        table_in.at[:, width : width + REST],
    ] + [wo_in.at[:, g * LANE : (g + 1) * LANE] for g in range(4)]
    weights = [raw, w1, w2t, wet, rest] + wo_raw

    def load(which):
        return pltpu.make_async_copy(weights_in[which], weights[which], wsem.at[which])

    def fetch(step, slot):
        return pltpu.make_async_copy(x_hbm.at[step], xbuf.at[slot], xsem.at[slot])

    barrier = pltpu.get_barrier_semaphore()
    fetch(0, 0).start()
    for which in range(9):
        load(which).start()
    for zero in (r1, r2, oall, third, datt):
        zero[...] = jnp.zeros_like(zero)
    for shift in (1, 2, 3):
        pl.semaphore_signal(
            barrier, inc=1, device_id={"tensor": lax.rem(me + shift, 4)}, device_id_type=MESH
        )
    bias_f[...] = bias_in[...]
    for zero in (pos_m, head_m, vec_m, bias_m, low_a, low_b, low_w, loss_all):
        zero[...] = jnp.zeros_like(zero)
    low_d[...] = jnp.zeros_like(low_d)
    for which in range(9):
        load(which).wait()
    n_head = head.shape[0]
    vec_at, head_at = seq, seq + 9
    h0[0:REST, :] = jnp.transpose(rest[...].astype(F32))
    pos_rows = lax.broadcasted_iota(jnp.int32, (pad, 1), 0) < seq
    vec_rows = lax.broadcasted_iota(jnp.int32, (SMALL, 1), 0) < 9
    pos_f[...] = jnp.where(pos_rows, h0[0:pad, :], 0.0)
    vec_f[...] = jnp.where(vec_rows, h0[vec_at : vec_at + SMALL, :], 0.0)
    start_head = h0[head_at : head_at + n_head, :]
    head_f[...] = start_head
    head[...] = start_head.astype(BF16)
    taken = tau_ref[0]

    def join(parts):
        return jnp.concatenate(parts, 1)

    def start_rows(j, carry):
        at = pl.ds(pl.multiple_of(j * 32, 32), 32)
        packed = tiles(raw[at, :].astype(F32))
        q, k = unpack_two(packed[:3])
        v, _ = unpack_two(packed[3:])
        all_three = join(q + k + v)
        wqkv_f[at, :] = all_three
        wqkv[at, :] = all_three.astype(BF16)
        pieces = [tiles(piece[at, :].astype(F32)) for piece in wo_raw]
        low = low_half((32, 128))
        first = [jnp.where(low, swap(p[0]), swap(p[1])) for p in pieces]
        last = [
            jnp.where(low, swap(pieces[g][1]), pieces[g + 1][1]) for g in (0, 2)
        ]
        wo_rows = join(first + last)
        wot_f[at, :] = wo_rows
        wot[at, :] = wo_rows.astype(BF16)
        for low_ref, full in ((w1, w1_f), (wet, wet_f)):
            full[at, :] = low_ref[at, :].astype(F32)
        for mom in (wqkv_m, w1_m, wot_m, wet_m):
            mom[at, :] = jnp.zeros((32, mom.shape[1]), F32)
        return carry

    lax.fori_loop(0, width // 32, start_rows, 0)
    pl.semaphore_wait(barrier, 3)

    row_id = lax.broadcasted_iota(jnp.int32, (pad, 1), 0)
    token = row_id < seq
    key_ok = lax.broadcasted_iota(jnp.int32, (1, pad), 1) < seq
    lane_head = lax.broadcasted_iota(jnp.int32, (1, LANE), 1) // HEAD_DIM
    small_ok = lax.broadcasted_iota(jnp.int32, (SMALL, 1), 0) < 4
    scale = HEAD_DIM ** (-0.5)

    def of_head(value, h):
        return jnp.where(lane_head == h, value, jnp.zeros_like(value))

    def o_part(message, group):
        lanes = pl.ds(pl.multiple_of(group * 128, 128), 128)
        pair, which = message // 3, message % 3
        if which == 2:
            return third.at[pair, 0:kept, lanes]
        return oall.at[pl.ds((2 * pair + which) * pad, kept), lanes]

    def o_to_mate(message):
        place = o_part(message, me)
        return remote(place, place, o_ps.at[message], o_pr.at[message], mate)

    def o_across(message):
        place = o_part(message, me)
        return remote(place, place, o_xs.at[message], o_xr.at[message], across)

    def o_forward(message):
        place = o_part(message, across)
        return remote(place, place, o_fs.at[message], o_fr.at[message], mate)

    def relay_o(message):
        place = o_part(message, across)
        remote(place, place, o_xs.at[message], o_xr.at[message], across).wait_recv()
        o_forward(message).start()

    def o_here(message):
        direct = o_part(message, mate)
        remote(direct, direct, o_ps.at[message], o_pr.at[message], mate).wait_recv()
        passed = o_part(message, lax.rem(mate + 2, 4))
        remote(passed, passed, o_fs.at[message], o_fr.at[message], mate).wait_recv()

    def to_mate(n):
        return remote(s1.at[n, 0:kept], r1.at[n, 0:kept], a1s.at[n], a1r.at[n], mate)

    def to_across(which, n):
        return remote(s2.at[n, 0:kept], r2.at[2 * which + n, 0:kept], a2s.at[2 * which + n], a2r.at[2 * which + n], across)

    def gradient_to_mate(buffer, which, image, k):
        return remote(
            buffer.at[sent_rows(image)], buffer.at[sent_rows(image)],
            das.at[2 * which + k], dar.at[2 * which + k], mate,
        )

    def pos_to_mate():
        return remote(pos_g, pos_r, pvs.at[0], pvr.at[0], mate)

    def vec_to_mate():
        return remote(vacc, vec_r, pvs.at[1], pvr.at[1], mate)

    def spread(src, dst, send, recv, shift):
        return remote(
            src, dst.at[me], send.at[shift - 1], recv.at[shift - 1], lax.rem(me + shift, 4)
        )

    def update_rows(entries, rho, live, fac):
        def update(j, carry):
            at = pl.ds(pl.multiple_of(j * 16, 16), 16)
            for low, full, mom, grad in entries:
                m = rho * mom[at, :] + fac * grad[at, :]
                mom[at, :] = m
                w = full[at, :] - (live * LOCAL_RATE) * m
                full[at, :] = w
                low[at, :] = w.astype(BF16)
            return carry

        lax.fori_loop(0, width // 16, update, 0)

    def one_step(step, carry):
        slot = lax.rem(step, 2)
        fetch(step, slot).wait()

        @pl.when(step < steps - 1)
        def _():
            fetch(step + 1, 1 - slot).start()

        gain1, shift1 = vec_f[0:1, :], vec_f[1:2, :]
        gain2, shift2 = vec_f[2:3, :], vec_f[3:4, :]
        gain3, shift3 = vec_f[4:5, :], vec_f[5:6, :]

        def attend(pair):
            two = slice(2 * pair * pad, 2 * (pair + 1) * pad)
            inside = (row_id >= 1) & token
            added = pos_f[...] + jnp.where(inside, vec_f[6:7, :], 0.0)
            state = nt(xbuf[slot, two, :], wet[...]) + jnp.concatenate([added, added], 0)
            h0[two, :] = state
            normed, _ = normalise(state)
            a = (normed * gain1 + shift1).astype(BF16)
            abuf[two, :] = a
            both = nn(a, wqkv[...]).astype(BF16)
            qkv[two, :] = both
            mine = pl.ds(pl.multiple_of(me * 128, 128), 128)
            thirds = []
            for i in range(2):
                projected = both[i * pad : (i + 1) * pad]
                q, k, v = projected[:, :LANE], projected[:, LANE : 2 * LANE], projected[:, 2 * LANE :]
                out = jnp.zeros((pad, LANE), F32)
                for h in range(3):
                    scores = jnp.where(key_ok, nt(of_head(q, h), k) * scale, NEG)
                    expd = jnp.exp(scores - jnp.max(scores, -1, keepdims=True))
                    p = (expd / jnp.sum(expd, -1, keepdims=True)).astype(BF16)
                    prob[(2 * pair + i) * 3 + h] = p
                    out = out + nn(p, of_head(v, h))
                oall[(2 * pair + i) * pad : (2 * pair + i + 1) * pad, mine] = out[:, :128].astype(BF16)
                thirds.append(out[:, 128:])
                o_to_mate(3 * pair + i).start()
                o_across(3 * pair + i).start()
            third[pair, :, mine] = (thirds[0] + swap(thirds[1])).astype(BF16)
            o_to_mate(3 * pair + 2).start()
            o_across(3 * pair + 2).start()

        attend(0)
        attend(1)

        @pl.when(step > 0)
        def _():
            was_live = jnp.where(step - 1 < taken, 1.0, 0.0)
            was_rho = jnp.where(step - 1 < taken, MOMENTUM_RHO, 1.0)
            was_fac = factor_kept[0:1, 0:1]
            update_rows(((w1, w1_f, w1_m, slope), (wot, wot_f, wot_m, wot_g)), was_rho, was_live, was_fac)
            head_m[...] = was_rho * head_m[...] + was_fac * head_g[...]
            head_f[...] = head_f[...] - (was_live * LOCAL_RATE) * head_m[...]
            head[...] = head_f[...].astype(BF16)
            moved_rows = (LOCAL_RATE * low_w[:, 0:1]) * low_a[...]
            low_hi, low_lo = split_two(moved_rows)
            pair_rows = jnp.concatenate([low_hi, low_lo], 0)
            load(2).wait()

            def low_rank(j, carry):
                at = pl.ds(pl.multiple_of(j * LANE, LANE), LANE)
                moved = tn(jnp.concatenate([low_d[:, at], low_d[:, at]], 0), pair_rows)
                w2t[at, :] = (w2t[at, :].astype(F32) - moved).astype(BF16)
                return carry

            lax.fori_loop(0, width // LANE, low_rank, 0)

        for message in range(3):
            relay_o(message)

        def feed(pair):
            for message in range(3):
                o_here(3 * pair + message)
            two = slice(2 * pair * pad, 2 * (pair + 1) * pad)
            side = tiles(third[pair].astype(F32))
            low = low_half((pad, 128))
            for i in range(2):
                for g in (0, 2):
                    if i == 0:
                        tile = jnp.where(low, side[g], swap(side[g + 1]))
                    else:
                        tile = jnp.where(low, swap(side[g]), side[g + 1])
                    at = 4 * 128 + g * HEAD_DIM
                    oall[(2 * pair + i) * pad : (2 * pair + i + 1) * pad, at : at + 128] = tile.astype(BF16)
            state = h0[two, :] + nt(oall[two, :], wot[...]) + vec_f[7:8, :]
            differs = (pair + core) - 2 * pair * core
            for i in range(2):
                part = state[i * pad : (i + 1) * pad]
                h1own[i * (1 - differs) + 2 * differs] = part
                hsum[2 * pair + i] = fold(jnp.where(token, part, 0.0))
            normed, _ = normalise(state)
            u = (normed * gain2 + shift2).astype(BF16)
            ubuf[two, :] = u
            if pair == 0:
                relay_o(3)
                relay_o(4)
            z = nn(u, w1[...]) + bias_f[0:1, :]
            cdf = 0.5 * (1.0 + lax.erf(z * SQRT_HALF))
            act = (z * cdf).astype(BF16).astype(F32)
            tail = cdf + z * jnp.exp(-0.5 * z * z) * INV_ROOT_TAU
            for i in range(2):
                part = slice(i * pad, (i + 1) * pad)
                asum[2 * pair + i] = fold(jnp.where(token, act[part], 0.0))
                slope[(2 * pair + i) * pad : (2 * pair + i + 1) * pad, :] = jnp.where(token, tail[part], 0.0)
            if pair == 0:
                relay_o(5)

        feed(0)
        feed(1)

        def stack(ref):
            parts = [jnp.sum(ref[n], 0, keepdims=True) for n in range(4)]
            return jnp.concatenate(parts + [jnp.zeros((SMALL - 4, width), F32)], 0)

        act_sum = stack(asum)
        act_hi, act_lo = split_two(act_sum)
        both = nt(jnp.concatenate([act_hi, act_lo], 0), w2t[...])
        mx_s[...] = both[:8] + both[SMALL : SMALL + 8]
        for shift in (1, 2, 3):
            spread(mx_s, mx_r, mxs, mxr, shift).start()
        mx_r[me] = mx_s[...]
        h_mean = stack(hsum) * (1.0 / seq)
        for shift in (1, 2, 3):
            remote(
                mx_s, mx_r.at[lax.rem(me + 4 - shift, 4)], mxs.at[shift - 1], mxr.at[shift - 1], mate
            ).wait_recv()
        mlp = jnp.concatenate(
            [mx_r[0] + mx_r[1] + mx_r[2] + mx_r[3], jnp.zeros((SMALL - 8, width), F32)], 0
        )
        average = h_mean + mlp * (1.0 / seq) + vec_f[8:9, :]
        normed3, inverse3 = normalise(average)
        pooled = (normed3 * gain3 + shift3).astype(BF16)
        logits = nt(pooled, head[...])
        class_ok = lax.broadcasted_iota(jnp.int32, (1, head.shape[0]), 1) < classes
        logits = jnp.where(class_ok, logits, NEG)
        top = jnp.max(logits, -1, keepdims=True)
        exp_l = jnp.exp(logits - top)
        total_l = jnp.sum(exp_l, -1, keepdims=True)
        hot_row = lax.broadcasted_iota(jnp.int32, (SMALL, n_head), 0)
        hot_lane = lax.broadcasted_iota(jnp.int32, (SMALL, n_head), 1)
        hot = jnp.zeros((SMALL, n_head), F32)
        for n in range(4):
            label = label_ref[index_ref[0, step, n]]
            hot = jnp.where((hot_row == n) & (hot_lane == label), 1.0, hot)
        each = top + jnp.log(total_l) - jnp.sum(jnp.where(class_ok, logits, 0.0) * hot, -1, keepdims=True)
        loss = jnp.sum(jnp.where(small_ok, each, 0.0), 0, keepdims=True) * 0.25
        live = jnp.where(step < taken, 1.0, 0.0)
        rho = jnp.where(step < taken, MOMENTUM_RHO, 1.0)
        loss_tile = live * loss
        d_logits = jnp.where(small_ok, (exp_l / total_l - hot) * 0.25, 0.0).astype(BF16)
        d_head = tn(d_logits, pooled)
        head_g[...] = d_head
        d_pooled = nn(d_logits, head[...])
        d_average = norm_grad(d_pooled, gain3, normed3, inverse3)
        d_token = d_average * (1.0 / seq)
        d_mlp = d_token.astype(BF16)
        dact[...] = nn(d_mlp, w2t[...])
        for r in range(4):
            scal[r] = jnp.broadcast_to(d_token[r : r + 1, :], (8, width))
        vec_g[...] = jnp.zeros_like(vec_g)
        vec_g[4:5, :] = jnp.sum(d_pooled * normed3, 0, keepdims=True)
        vec_g[5:6, :] = jnp.sum(d_pooled, 0, keepdims=True)
        vec_g[8:9, :] = jnp.sum(d_average, 0, keepdims=True)
        low_at = pl.ds(pl.multiple_of(step * SMALL, SMALL), SMALL)
        low_d[low_at, :] = d_mlp
        low_a[low_at, :] = act_sum
        gram_d = nt(d_mlp, d_mlp)
        gram_a = nt(act_hi, act_hi) + nt(act_hi, act_lo) + nt(act_lo, act_hi)
        own_squares = total(gram_d * gram_a)

        for n in range(4):
            scal[4 + n] = jnp.broadcast_to(dact[n : n + 1, :], (8, width))
        bsum[...] = jnp.zeros_like(bsum)
        vacc[...] = jnp.zeros_like(vacc)

        def upper_partial(n):
            at = pl.ds(pl.multiple_of(n * pad, 16), 2 * pad)
            rate = jnp.concatenate(
                [jnp.broadcast_to(scal[4 + n + i][0:1, :], (pad, width)) for i in range(2)], 0
            )
            g = (rate * slope[at, :]).astype(BF16)
            dpre[at, :] = g
            bsum[...] = bsum[...] + fold(g.astype(F32))
            return nt(g, w1[...])

        other = upper_partial(oth0)
        for k in (0, 1):
            s1[k] = other[k * pad : (k + 1) * pad].astype(BF16)
            to_mate(k).start()
        own = upper_partial(own0)
        for k in (0, 1):
            to_mate(k).wait_recv()
            part = own[k * pad : (k + 1) * pad] + r1[k].astype(F32)
            chip[k] = part
            s2[k] = part.astype(BF16)
            to_across(0, k).start()

        ssq[...] = jnp.zeros_like(ssq)
        w1_g = slope

        def weight_grad(left, right, out, which):
            def tile(j, carry):
                at = pl.ds(pl.multiple_of(j * LANE, LANE), LANE)
                g = tn(left[:, at], right[...])
                out[at, :] = g
                ssq[which] = ssq[which] + fold(g * g)
                return carry

            lax.fori_loop(0, width // LANE, tile, 0)

        def embedding_grad(k, left):
            def tile(j, carry):
                at = pl.ds(pl.multiple_of(j * LANE, LANE), LANE)
                g = tn(left[rows(own0 + k), at], xbuf[slot, rows(own0 + k), :])
                g = g + tn(left[rows(oth0 + k), at], xbuf[slot, rows(oth0 + k), :])
                if k == 1:
                    g = g + wet_g[at, :]
                    ssq[3] = ssq[3] + fold(g * g)
                wet_g[at, :] = g
                return carry

            lax.fori_loop(0, width // LANE, tile, 0)

        weight_grad(ubuf, dpre, w1_g, 0)

        for k in (0, 1):
            normed, inverse = normalise(h1own[k])
            h1own[k] = normed
            inverses[k] = inverse
            normed, inverse = normalise(h0[rows(own0 + k), :])
            h0[rows(own0 + k), :] = normed
            inverses[2 + k] = inverse

        def attention_partial(n):
            own_columns = jnp.concatenate(
                [
                    wot[:, pl.ds(pl.multiple_of(me * 128, 128), 128)],
                    wot[:, pl.ds(pl.multiple_of(4 * 128 + (me // 2) * 128, 128), 128)],
                ],
                1,
            )
            wide = nn(datt[rows(n), :], own_columns)
            thirds = jnp.where(core == 1, swap(wide[:, 128:]), wide[:, 128:])
            thirds = jnp.where(low_half((pad, 128)), thirds, 0.0)
            d_ctx = jnp.concatenate([wide[:, :128], thirds], 1).astype(BF16)
            projected = qkv[rows(n), :]
            q, k, v = projected[:, :LANE], projected[:, LANE : 2 * LANE], projected[:, 2 * LANE :]
            d_q = jnp.zeros((pad, LANE), F32)
            d_k = jnp.zeros((pad, LANE), F32)
            d_v = jnp.zeros((pad, LANE), F32)
            for h in range(3):
                part = of_head(d_ctx, h)
                p = prob[n * 3 + h]
                again = p.astype(F32)
                d_p = nt(part, v)
                inner = d_p - jnp.sum(d_p * again, -1, keepdims=True)
                d_s = (again * inner).astype(BF16)
                d_v = d_v + tn(p, part)
                d_q = d_q + nn(d_s, of_head(k, h))
                d_k = d_k + tn(d_s, of_head(q, h))
            d_all = jnp.concatenate([d_q * scale, d_k * scale, d_v], 1).astype(BF16)
            qkv[rows(n), :] = d_all
            return nt(d_all, wqkv[...])

        for k in (0, 1):
            to_across(0, k).wait_recv()
            d_upper = chip[k] + r2[k].astype(F32)
            normed = h1own[k]
            d_state = norm_grad(d_upper, gain2, normed, inverses[k]) + scal[own0 + k][0:1, :]
            d_state = jnp.where(token, d_state, 0.0)
            h1own[k] = d_state
            datt[rows(own0 + k), :] = d_state.astype(BF16)
            gradient_to_mate(datt, 0, own0 + k, k).start()
            vacc[0] = vacc[0] + fold(d_upper * normed)
            vacc[1] = vacc[1] + fold(d_upper)
            vacc[2] = vacc[2] + fold(d_state)
            own = attention_partial(own0 + k)
            remote(
                datt.at[sent_rows(oth0 + k)], datt.at[sent_rows(oth0 + k)], das.at[k], dar.at[k], mate
            ).wait_recv()
            other = attention_partial(oth0 + k)
            to_mate(k).wait_send()
            s1[k] = other.astype(BF16)
            to_mate(k).start()
            to_mate(k).wait_recv()
            own = own + r1[k].astype(F32)
            chip[k] = own
            to_across(0, k).wait_send()
            s2[k] = own.astype(BF16)
            to_across(1, k).start()

        weight_grad(datt, oall, wot_g, 1)
        weight_grad(abuf, qkv, wqkv_g, 2)

        d_emb = ubuf
        for k in (0, 1):
            to_across(1, k).wait_recv()
            d_normed = chip[k] + r2[2 + k].astype(F32)
            normed = h0[rows(own0 + k), :]
            d_state = h1own[k] + norm_grad(d_normed, gain1, normed, inverses[2 + k])
            d_emb[rows(own0 + k), :] = d_state.astype(BF16)
            gradient_to_mate(d_emb, 1, own0 + k, k).start()
            vacc[3] = vacc[3] + fold(d_normed * normed)
            vacc[4] = vacc[4] + fold(d_normed)
            vacc[5] = vacc[5] + fold(jnp.where(row_id >= 1, d_state, 0.0))
            if k == 0:
                pos_g[...] = d_state
            else:
                pos_g[...] = pos_g[...] + d_state
                pos_to_mate().start()
                vec_to_mate().start()
            remote(
                d_emb.at[sent_rows(oth0 + k)], d_emb.at[sent_rows(oth0 + k)],
                das.at[2 + k], dar.at[2 + k], mate,
            ).wait_recv()
            embedding_grad(k, d_emb)
        pos_to_mate().wait()
        vec_to_mate().wait()
        pos_g[...] = pos_g[...] + pos_r[...]
        sums = [jnp.sum(vacc[r] + vec_r[r], 0, keepdims=True) for r in range(6)]
        vec_g[0:1, :] = sums[3]
        vec_g[1:2, :] = sums[4]
        vec_g[2:3, :] = sums[0]
        vec_g[3:4, :] = sums[1]
        vec_g[6:7, :] = sums[5]
        vec_g[7:8, :] = sums[2]
        d_bias = jnp.sum(bsum[...], 0, keepdims=True)
        shared = (
            total(ssq[1] + ssq[3] + fold(pos_g[...] * pos_g[...]) + fold(head_g[...] * head_g[...]))
            + total(vec_g[...] * vec_g[...])
        )
        own_squares = own_squares + total(ssq[0] + ssq[2]) + total(d_bias * d_bias)
        for message in range(6):
            o_to_mate(message).wait_send()
            o_across(message).wait_send()
            o_forward(message).wait_send()
        for k in (0, 1):
            to_mate(k).wait_send()
            to_across(1, k).wait_send()
            gradient_to_mate(datt, 0, own0 + k, k).wait_send()
            gradient_to_mate(d_emb, 1, own0 + k, k).wait_send()
        for shift in (1, 2, 3):
            spread(mx_s, mx_r, mxs, mxr, shift).wait_send()
        first_lane = lax.broadcasted_iota(jnp.int32, (8, 128), 1) < 64
        nx_s[...] = jnp.where(first_lane, own_squares + 0.25 * shared, loss_tile)
        for shift in (1, 2, 3):
            spread(nx_s, nx_r, nxs, nxr, shift).start()
        nx_r[me] = nx_s[...]

        @pl.when(step == steps - 1)
        def _():
            for which in (0, 1, 3, 4):
                load(which).start()

        for shift in (1, 2, 3):
            remote(
                nx_s, nx_r.at[lax.rem(me + 4 - shift, 4)], nxs.at[shift - 1], nxr.at[shift - 1], mate
            ).wait_recv()
        norm = jnp.sqrt((nx_r[0] + nx_r[1] + nx_r[2] + nx_r[3]))
        factor = live * (CLIP_LIMIT / jnp.maximum(norm, CLIP_LIMIT))
        norm_out[step] = live * norm
        loss_all[...] = loss_all[...] + nx_r[0]
        for shift in (1, 2, 3):
            spread(nx_s, nx_r, nxs, nxr, shift).wait_send()
        fac = factor[0:1, 0:1]

        low_row = lax.broadcasted_iota(jnp.int32, low_b.shape, 0) // SMALL
        low_b[...] = jnp.where(low_row == step, fac, rho * low_b[...])
        low_w[...] = low_w[...] + live * low_b[...]
        factors = (LOCAL_RATE * low_w[:, 0:1]) * low_a[...]
        factor_kept[...] = factor

        def small_update(full, mom, grad):
            mom[...] = rho * mom[...] + fac * grad
            full[...] = full[...] - (live * LOCAL_RATE) * mom[...]

        small_update(pos_f, pos_m, pos_g[...])
        small_update(vec_f, vec_m, vec_g[...])
        small_update(bias_f, bias_m, jnp.broadcast_to(d_bias, (8, width)))
        table = (
            (wqkv, wqkv_f, wqkv_m, wqkv_g),
            (w1, w1_f, w1_m, w1_g),
            (wot, wot_f, wot_m, wot_g),
            (wet, wet_f, wet_m, wet_g),
        )

        @pl.when(step < steps - 1)
        def _():
            load(2).start()
            update_rows((table[0], table[3]), rho, live, fac)

        @pl.when(step == steps - 1)
        def _():
            examples = jnp.full((1, 1), count_ref[0].astype(F32))
            factor_sum = jnp.zeros((), F32)
            for k in range(steps):
                worth = (1.0 - MOMENTUM_RHO ** (k + 1)) / (1.0 - MOMENTUM_RHO)
                factor_sum = factor_sum + jnp.where(k < taken, worth, 0.0)
            factor_sum = jnp.full((1, 1), factor_sum)
            share = examples / factor_sum
            for which in (0, 1, 3, 4):
                load(which).wait()

            def finish(j, carry):
                at = pl.ds(pl.multiple_of(j * 16, 16), 16)

                def ended(full, mom, grad, lanes):
                    m = rho * mom[at, lanes] + fac * grad[at, lanes]
                    return full[at, lanes] - (live * LOCAL_RATE) * m

                for low, full, mom, grad in (table[1], table[3]):
                    w = ended(full, mom, grad, slice(None))
                    low[at, :] = (share * (low[at, :].astype(F32) - w)).astype(BF16)
                three = tiles(ended(wqkv_f, wqkv_m, wqkv_g, slice(None)))
                _, full, mom, grad = table[2]
                wo_first = ended(full, mom, grad, pl.ds(pl.multiple_of(me * 128, 128), 128))
                wo_last = ended(
                    full, mom, grad, pl.ds(pl.multiple_of(4 * 128 + (me // 2) * 128, 128), 128)
                )
                wo_last = jnp.where(core == 1, swap(wo_last), wo_last)
                packed = join(
                    pack_two(three[0:2], three[2:4]) + pack_two(three[4:6], [wo_first, wo_last])
                )
                raw[at, :] = (share * (raw[at, :].astype(F32) - packed)).astype(BF16)
                return carry

            lax.fori_loop(0, width // 16, finish, 0)
            small_update(head_f, head_m, head_g[...])
            h0[0:REST, :] = jnp.transpose(rest[...].astype(F32))
            for ref, begin, count in ((pos_f, 0, seq), (vec_f, vec_at, 9), (head_f, head_at, classes)):
                h0[begin : begin + count, :] = share * (h0[begin : begin + count, :] - ref[0:count, :])
            rest[...] = jnp.transpose(h0[0:REST, :]).astype(BF16)
            outs = (
                (w1, main_out.at[:, 0:width]),
                (raw, main_out.at[:, width : 2 * width]),
                (wet, table_out.at[:, 0:width]),
                (rest, table_out.at[:, width : width + REST]),
            )
            copies = [
                pltpu.make_async_copy(src, dst, osem.at[i]) for i, (src, dst) in enumerate(outs)
            ]
            for copy in copies:
                copy.start()
            d_bias_all = share * (bias_in[0:1, :] - bias_f[0:1, :])
            for r in range(width // 128):
                tile_out[r : r + 1, :] = d_bias_all[:, 128 * r : 128 * (r + 1)]
            lane = lax.broadcasted_iota(jnp.int32, (1, 128), 1)
            loss_sum = loss_all[0:1, 64:65]
            mean_loss = examples * loss_sum / jnp.full((1, 1), taken.astype(F32))
            scalars = jnp.where(lane == 0, examples, jnp.where(lane == 1, mean_loss, examples * factor_sum))
            tile_out[width // 128 : width // 128 + 1, :] = jnp.where(lane < 3, scalars, 0.0)
            tile_out[width // 128 + 1 :, :] = jnp.zeros((7 - width // 128, 128), F32)
            used = 4 * steps
            wanted_row = lax.broadcasted_iota(jnp.int32, (used, steps * SMALL), 0)
            wanted_row = (wanted_row // 4) * SMALL + lax.rem(wanted_row, 4)
            picker = (lax.broadcasted_iota(jnp.int32, (used, steps * SMALL), 1) == wanted_row).astype(BF16)
            low_left = nn(picker, (share * factors).astype(BF16)).astype(BF16)
            low_right = nn(picker, low_d[...])
            part = width // clients
            kept_lanes = lax.broadcasted_iota(jnp.int32, (used, 128), 1) < part
            for j in range(clients):
                low_out[j, :, 0:width] = low_left
                turned = pltpu.roll(low_right, (width - part * j) % width, 1) if j else low_right
                low_out[j, :, width : width + 128] = jnp.where(kept_lanes, turned[:, :128], 0.0).astype(BF16)
            for copy in copies:
                copy.wait()

        return carry

    lax.fori_loop(0, steps, one_step, 0)


def local_training(tau, counts, labels, index, patches, main, wo, table, bias, clients, pad, seq, classes):
    steps = patches.shape[0]
    width = main.shape[0]
    n_all = 4 * pad
    n_head = (classes + 127) // 128 * 128
    n_low = steps * SMALL
    vmem = pltpu.VMEM
    dma = pltpu.SemaphoreType.DMA
    anywhere = pl.BlockSpec(memory_space=pl.ANY)
    inside = pl.BlockSpec(memory_space=pltpu.VMEM)
    square = (width, width)
    out_shape = (
        jax.ShapeDtypeStruct((width, 2 * width), BF16),
        jax.ShapeDtypeStruct(table.shape, BF16),
        jax.ShapeDtypeStruct((clients, 4 * steps, width + 128), BF16),
        jax.ShapeDtypeStruct((8, 128), F32),
        jax.ShapeDtypeStruct((steps, 8, 128), F32),
    )
    scratch = [
        vmem(square, BF16), vmem(square, BF16), vmem(square, BF16), vmem(square, BF16),
        vmem(square, BF16), vmem((n_head, width), BF16),
    ]
    for _ in range(2):
        scratch += [
            vmem(square, F32), vmem(square, F32), vmem(square, F32), vmem(square, F32),
            vmem((pad, width), F32), vmem((n_head, width), F32), vmem((SMALL, width), F32),
            vmem((8, width), F32),
        ]
    scratch += [
        vmem(square, F32), vmem(square, F32), vmem(square, F32), vmem((pad, width), F32),
        vmem((n_head, width), F32), vmem((SMALL, width), F32),
        vmem((2, n_all, width), BF16), vmem((n_all, width), F32), vmem((n_all, width), F32),
        vmem((12, pad, pad), BF16), vmem((n_all, width), BF16), vmem((n_all, width), BF16),
        vmem((n_all, width), BF16), vmem((2, pad, 4 * 128), BF16), vmem((n_all, width), BF16),
        vmem((n_all, width), BF16), vmem((3, pad, width), F32), vmem((n_all, width), BF16),
        vmem((2, pad, width), F32), vmem((4, pad, 1), F32),
        vmem((4, 8, width), F32), vmem((4, 8, width), F32), vmem((SMALL, width), F32),
        vmem((8, width), F32), vmem((6, 8, width), F32), vmem((4, 8, width), F32),
        vmem((n_low, width), BF16), vmem((n_low, width), F32), vmem((n_low, 128), F32),
        vmem((n_low, 128), F32), vmem((8, 8, width), F32), vmem((8, 128), F32), vmem((8, 128), F32),
        vmem((2, pad, width), BF16), vmem((2, pad, width), BF16), vmem((2, pad, width), BF16),
        vmem((4, pad, width), BF16), vmem((8, width), F32), vmem((4, 8, width), F32),
        vmem((8, 128), F32), vmem((4, 8, 128), F32), vmem((pad, width), F32),
        vmem((6, 8, width), F32),
        dma((9,)), dma((2,)), dma((6,)), dma((6,)), dma((6,)), dma((6,)), dma((6,)), dma((6,)),
        dma((2,)), dma((2,)), dma((4,)), dma((4,)), dma((4,)), dma((4,)), dma((2,)), dma((2,)),
        dma((3,)), dma((3,)), dma((3,)), dma((3,)), dma((6,)),
    ]
    return pl.pallas_call(
        functools.partial(train_kernel, (steps, seq, pad, classes, clients)),
        out_shape=out_shape,
        in_specs=[pl.BlockSpec(memory_space=pltpu.SMEM)] * 4 + [anywhere] * 4 + [inside],
        out_specs=(anywhere,) * 2 + (inside,) * 3,
        scratch_shapes=scratch,
        compiler_params=pltpu.CompilerParams(
            collective_id=0, has_side_effects=True, vmem_limit_bytes=VMEM_LIMIT
        ),
        name="local_training",
    )(tau, counts, labels, index, patches, main, wo, table, bias)


def place_patches(chosen_ref, pool_ref, out_ref):
    seq_rows, width = pool_ref.shape[1], pool_ref.shape[2]
    pad = out_ref.shape[1]
    below = jnp.zeros((pad - 1 - seq_rows, width), F32)
    whole = jnp.concatenate([jnp.zeros((1, width), F32), pool_ref[0].astype(F32), below], 0)
    out_ref[0] = whole.astype(BF16)


def pick_patches(pool, chosen, pad):
    count = chosen.shape[0]
    _, patch_rows, width = pool.shape
    return pl.pallas_call(
        place_patches,
        out_shape=jax.ShapeDtypeStruct((count, pad, width), BF16),
        grid_spec=pltpu.PrefetchScalarGridSpec(
            num_scalar_prefetch=1,
            grid=(count,),
            in_specs=[pl.BlockSpec((1, patch_rows, width), lambda i, ids: (ids[i], 0, 0))],
            out_specs=pl.BlockSpec((1, pad, width), lambda i, ids: (i, 0, 0)),
        ),
        name="pick_patches",
    )(chosen, pool)


def ring_places(clients):
    depth = clients // 2
    client = lax.axis_index("client")
    member = lax.axis_index("tensor")
    core = lax.rem(member, 2)
    return (
        depth, client, client // 2, lax.rem(client, 2), member, core, member // 2,
        member + 1 - 2 * core, lax.rem(member + 2, 4),
    )


def send(src, dst, send_sem, recv_sem, client, member):
    return pltpu.make_async_remote_copy(
        src_ref=src, dst_ref=dst, send_sem=send_sem, recv_sem=recv_sem,
        device_id={"client": client, "tensor": member}, device_id_type=MESH,
    )


def span(start, size, unit):
    return pl.ds(pl.multiple_of(start, unit), size)


def gather_kernel(
    clients, index_ref, in_ref, out_ref, table_in, pool_ref, main_out, wo_out, table_out, x_out,
    main_ref, table_ref, wide_in, wide_out, pool_buf, x_buf, pool_sem, x_sem, up_s, up_r, down_s, down_r, y_s, y_r, mate_s, mate_r, x_s, x_r, on_s, on_r, own_sem, keep_sem,
):
    depth, client, z, y, member, core, chip_x, mate, across = ring_places(clients)
    block = main_ref.shape[0]
    half = block // 2
    columns = table_ref.shape[1] // 2
    peer = client + 1 - 2 * y

    wide = main_ref.shape[1]
    tail = wide - LANE

    def table_part(origin, who):
        return table_out.at[
            span(origin * block + (who // 2) * half, half, half),
            span(lax.rem(who, 2) * columns, columns, 128),
        ]

    def wo_part(origin, who):
        return wo_out.at[span(origin * block, block, block), span(who * LANE, LANE, LANE)]

    def shared(origin, who):
        return (wo_part(origin, who), table_part(origin, who))

    def main_part(origin, lanes):
        return main_out.at[span(origin * block, block, block), lanes]

    front, back = slice(0, 2 * wide // 3), slice(2 * wide // 3, wide)

    def landed(origin):
        return (main_part(origin, back), table_part(origin, member), main_part(origin, front))

    own_table = table_ref.at[span(chip_x * half, half, half), span(core * columns, columns, 128)]
    own_pieces = (main_ref.at[:, back], own_table, main_ref.at[:, front])

    def given(origin, mine):
        if mine:
            return (main_ref.at[:, tail:wide], own_table)
        return (main_part(origin, slice(tail, wide)), table_part(origin, member))

    def message(origin, mine, send_sem, recv_sem, index, to, part):
        sources = own_pieces if mine else landed(origin)
        return [
            send(src, dst, send_sem.at[p, index], recv_sem.at[p, index], to, member)
            for p, (src, dst) in enumerate(zip(sources, landed(origin)))
        ][part]

    first, second, every = slice(0, 2), slice(2, 3), slice(0, 3)

    def up(origin, i, part, mine=False):
        return message(origin, mine, up_s, up_r, i, client + 2, part)

    def down(origin, i, part, mine=False):
        return message(origin, mine, down_s, down_r, i, client - 2, part)

    def over(origin, part, mine=False):
        return message(origin, mine, y_s, y_r, origin // 2, peer, part)

    def give(origin, mine, send_sem, recv_sem, to):
        return [
            send(src, dst, send_sem.at[p, origin], recv_sem.at[p, origin], client, to)
            for p, (src, dst) in enumerate(zip(given(origin, mine), shared(origin, member)))
        ]

    def keep(origin, mine=False):
        return pltpu.make_async_copy(given(origin, mine)[0], wo_part(origin, member), keep_sem.at[origin])

    def share(origin, mine=False):
        return give(origin, mine, mate_s, mate_r, mate) + give(origin, mine, x_s, x_r, across)

    def from_across(origin):
        return [
            send(dst, dst, x_s.at[p, origin], x_r.at[p, origin], client, across)
            for p, dst in enumerate(shared(origin, across))
        ]

    def pass_on(origin):
        return [
            send(dst, dst, on_s.at[p, origin], on_r.at[p, origin], client, mate)
            for p, dst in enumerate(shared(origin, across))
        ]

    def start(copies):
        for copy in copies:
            copy.start()

    def arrived(copies):
        for copy in copies:
            copy.wait_recv()

    def sent(copies):
        for copy in copies:
            copy.wait_send()

    has_up, has_down = z < depth - 1, z > 0

    barrier = pltpu.get_barrier_semaphore()

    def hello(to_client, to_member):
        pl.semaphore_signal(
            barrier, inc=1, device_id={"client": to_client, "tensor": to_member}, device_id_type=MESH
        )

    wide_in[...] = jnp.zeros_like(wide_in)
    wide_out[...] = jnp.zeros_like(wide_out)
    table_ref[...] = jnp.zeros_like(table_ref)
    table_ref[:, 0 : table_in.shape[1]] = table_in[...]

    def in_slab(i):
        wide_in[i, :, 0 : in_ref.shape[2]] = in_ref[i].astype(F32)
        return tiles(wide_in[i])

    def out_slab(i):
        wide_out[i, 0 : out_ref.shape[1], 0:block] = out_ref[i].astype(F32)
        return tiles(jnp.transpose(wide_out[i])[:block])

    ordered = [in_slab(i) for i in (3, 4, 5, 6)] + [out_slab(i) for i in (1, 2, 3, 4)]
    ordered += [in_slab(i) for i in (0, 1, 2)] + [out_slab(0)]
    for i in range(0, 12, 2):
        packed = jnp.concatenate(pack_two(ordered[i], ordered[i + 1]), 1)
        main_ref[:, 192 * i : 192 * (i + 2)] = packed.astype(BF16)

    hello(peer, member)
    for shift in (1, 2, 3):
        hello(client, lax.rem(member + shift, 4))
    for shift in range(1, depth):
        hello(2 * lax.rem(z + shift, depth) + y, member)
    pl.semaphore_wait(barrier, 3 + depth)

    for part in (first, second):
        start(over(client, part, True))

        @pl.when(has_up)
        def _():
            start(up(client, 0, part, True))

        @pl.when(has_down)
        def _():
            start(down(client, 0, part, True))

    start(share(client, True))
    keep(client, True).start()
    local = [
        pltpu.make_async_copy(src, dst, own_sem.at[p])
        for p, (src, dst) in enumerate(zip(own_pieces, landed(client)))
    ]
    start(local)

    _, steps, each = index_ref.shape
    images = steps * each
    pool_size = pool_buf.shape[1] // 8
    patch_rows = pool_ref.shape[0] // pool_size
    pad = x_out.shape[1]

    def base(b):
        return lax.min(lax.max(8 * b - 1, 0), patch_rows - 8)

    deep = pool_buf.shape[0]

    def pool_load(b):
        k = lax.rem(b, deep)
        return pltpu.make_async_copy(
            pool_ref.at[span(base(b) * pool_size, 8 * pool_size, 32), :], pool_buf.at[k], pool_sem.at[k]
        )

    def x_store(b):
        k = lax.rem(b, deep)
        return pltpu.make_async_copy(x_buf.at[k], x_out.at[:, span(8 * b, 8, 8), :], x_sem.at[k])

    for b in range(deep - 1):
        pool_load(b).start()
    lane = lax.broadcasted_iota(jnp.int32, (8 * images, 8 * pool_size), 1)
    select_row = lax.broadcasted_iota(jnp.int32, (8 * images, 1), 0)
    line_row = lax.rem(select_row, 8)
    chosen = jnp.zeros((8 * images, 1), jnp.int32)
    for i in range(images):
        chosen = jnp.where(select_row // 8 == i, index_ref[0, i // each, i % each], chosen)

    def pick(b, carry):
        k = lax.rem(b, deep)
        pool_load(b).wait()

        @pl.when(b < pad // 8 - (deep - 1))
        def _():
            pool_load(b + deep - 1).start()

        wanted = (8 * b - 1 + line_row - base(b)) * pool_size + chosen
        picked = nn((lane == wanted).astype(BF16), pool_buf[k]).astype(BF16)

        @pl.when(b >= deep)
        def _():
            x_store(b - deep).wait()

        x_buf[k] = picked.reshape(images, 8, picked.shape[1])
        x_store(b).start()
        return carry

    lax.fori_loop(0, pad // 8, pick, 0)
    for b in range(pad // 8 - deep, pad // 8):
        x_store(b).wait()

    def line(d, act):
        @pl.when(z >= d)
        def _():
            act(client - 2 * d, True)

        @pl.when(z < depth - d)
        def _():
            act(client + 2 * d, False)

    def across_line(d, act):
        if d == 0:
            act(peer, True)
            return

        @pl.when(z >= d)
        def _():
            act(peer - 2 * d, True)

        @pl.when(z < depth - d)
        def _():
            act(peer + 2 * d, False)

    def line_in(d, part):
        def act(origin, below):
            line_s, line_r = (up_s, up_r) if below else (down_s, down_r)
            arrived(message(origin, False, line_s, line_r, d - 1, peer, part))
            if d < depth - 1:

                @pl.when(has_up if below else has_down)
                def _():
                    start(up(origin, d, part) if below else down(origin, d, part))

            start(over(origin, part))
            if part is first:
                start(share(origin))
                keep(origin).start()

        return act

    def y_in(origin, below):
        arrived(over(origin, first))
        start(share(origin))
        keep(origin).start()

    def forward(origin, below=True):
        arrived(from_across(origin))
        start(pass_on(origin))

    for d in range(1, depth + 1):
        if d < depth:
            line(d, line_in(d, first))
        across_line(d - 1, y_in)
        if d < depth:
            line(d, line_in(d, second))
        if d == 1:
            forward(client)
        else:
            line(d - 1, forward)
            across_line(d - 2, forward)
    across_line(depth - 1, forward)
    for d in range(depth):
        across_line(d, lambda origin, below: arrived(over(origin, second)))

    for copy in local:
        copy.wait()
    for origin in range(clients):
        sent(share(origin))
        sent(pass_on(origin))
        keep(origin).wait()
        arrived([
            send(dst, dst, mate_s.at[p, origin], mate_r.at[p, origin], client, mate)
            for p, dst in enumerate(shared(origin, mate))
        ])
        arrived([
            send(dst, dst, on_s.at[p, origin], on_r.at[p, origin], client, mate)
            for p, dst in enumerate(shared(origin, lax.rem(mate + 2, 4)))
        ])
    for d in range(depth):
        sent(over(2 * d + y, every))

        @pl.when(has_up & (z >= d))
        def _():
            if d < depth - 1:
                sent(up(client - 2 * d, d, every))

        @pl.when(has_down & (z < depth - d))
        def _():
            if d < depth - 1:
                sent(down(client + 2 * d, d, every))


def gather_weights(clients, index, in_bf, out_bf, table_t, pool, pad):
    depth = clients // 2
    dma = pltpu.SemaphoreType.DMA
    anywhere = pl.BlockSpec(memory_space=pl.ANY)
    inside = pl.BlockSpec(memory_space=pltpu.VMEM)
    slabs, own, group = in_bf.shape
    width = own * clients
    packed = (slabs + out_bf.shape[0]) * group
    table_lanes = width + REST
    hops = depth - 1
    pool_size, patch_rows, features = pool.shape
    images = index.shape[1] * index.shape[2]
    rows = jnp.transpose(pool, (1, 0, 2)).reshape(patch_rows * pool_size, features)
    return pl.pallas_call(
        functools.partial(gather_kernel, clients),
        out_shape=(
            jax.ShapeDtypeStruct((width, packed), BF16),
            jax.ShapeDtypeStruct((width, 4 * LANE), BF16),
            jax.ShapeDtypeStruct((width, table_lanes), BF16),
            jax.ShapeDtypeStruct((images, pad, features), BF16),
        ),
        in_specs=[pl.BlockSpec(memory_space=pltpu.SMEM)] + [inside] * 3 + [anywhere],
        out_specs=(anywhere,) * 4,
        scratch_shapes=[
            pltpu.VMEM((own, packed), BF16), pltpu.VMEM((own, table_lanes), BF16),
            pltpu.VMEM((slabs, own, LANE), F32), pltpu.VMEM((out_bf.shape[0], LANE, 128), F32),
            pltpu.VMEM((6, 8 * pool_size, features), BF16), pltpu.VMEM((6, images, 8, features), BF16),
            dma((6,)), dma((6,)),
            dma((3, hops)), dma((3, hops)), dma((3, hops)), dma((3, hops)), dma((3, depth)),
            dma((3, depth)),
        ] + [dma((2, clients))] * 6 + [dma((3,)), dma((clients,))],
        compiler_params=pltpu.CompilerParams(collective_id=1, has_side_effects=True),
        name="gather_weights",
    )(index, in_bf, out_bf, table_t, rows)


def reduce_kernel(
    clients, main_in, table_in, low_in, tile_in, main_out, table_out, low_out, tile_out,
    own_main, own_table, y_main, y_table, zs_main, zs_table, zr_main, zr_table, whole, low_all, tile_all,
    own_sem, y_s, y_r, z_s, z_r, low_s, low_r, tile_s, tile_r, q_s, q_r,
):
    depth, client, z, y, member, core, chip_x, mate, across = ring_places(clients)
    block = own_main.shape[1]
    half, columns = own_table.shape[1], own_table.shape[2]
    peer = client + 1 - 2 * y
    cut = own_main.shape[2] // 2
    lanes = (None, slice(0, cut), slice(cut, 2 * cut))
    parts = (0, 1, 2)

    def source(owner, p):
        if p == 0:
            return table_in.at[
                span(owner * block + chip_x * half, half, half), span(core * columns, columns, 128)
            ]
        return main_in.at[span(owner * block, block, block), lanes[p]]

    def slot(table_ref, main_ref, i, p):
        return table_ref.at[i] if p == 0 else main_ref.at[i, :, lanes[p]]

    def own_load(level, p):
        return pltpu.make_async_copy(
            source(2 * level + y, p), slot(own_table, own_main, level, p), own_sem.at[p, level]
        )

    def over(level, p):
        return send(
            source(2 * level + 1 - y, p), slot(y_table, y_main, level, p),
            y_s.at[p, level], y_r.at[p, level], peer, member,
        )

    def onward(i, p):
        owner = 2 * lax.rem(z + 1 + i, depth) + y
        return send(
            slot(zs_table, zs_main, i, p), slot(zr_table, zr_main, i, p),
            z_s.at[p, i], z_r.at[p, i], owner, member,
        )

    def small(shift):
        to = lax.rem(client + shift, clients)
        return [
            send(low_in.at[to], low_all.at[client], low_s.at[shift - 1], low_r.at[shift - 1], to, member),
            send(tile_in, tile_all.at[client], tile_s.at[shift - 1], tile_r.at[shift - 1], to, member),
        ]

    def small_from(shift):
        origin = lax.rem(client + clients - shift, clients)
        return [
            send(low_in.at[origin], low_all.at[origin], low_s.at[shift - 1], low_r.at[shift - 1], origin, member),
            send(tile_in, tile_all.at[origin], tile_s.at[shift - 1], tile_r.at[shift - 1], origin, member),
        ]

    def quarter(who):
        return whole.at[span((who // 2) * half, half, half), span(lax.rem(who, 2) * columns, columns, 128)]

    def pass_quarter(who, index, to):
        return send(quarter(who), quarter(who), q_s.at[index], q_r.at[index], client, to)

    barrier = pltpu.get_barrier_semaphore()
    for shift in range(1, clients):
        pl.semaphore_signal(
            barrier, inc=1,
            device_id={"client": lax.rem(client + shift, clients), "tensor": member}, device_id_type=MESH,
        )
    for shift in (1, 2, 3):
        pl.semaphore_signal(
            barrier, inc=1,
            device_id={"client": client, "tensor": lax.rem(member + shift, 4)}, device_id_type=MESH,
        )
    order = [(i, 0) for i in range(depth)] + [(i, p) for i in range(depth) for p in (1, 2)]
    for i, p in order:
        own_load(lax.rem(z + 1 + i, depth), p).start()
    pl.semaphore_wait(barrier, clients - 1 + 3)
    for i, p in order:
        over(lax.rem(z + 1 + i, depth), p).start()
    for shift in range(1, clients):
        for copy in small(shift):
            copy.start()
    low_all[client] = low_in[client]
    tile_all[client] = tile_in[...]

    def pair_up(i, p):
        level = lax.rem(z + 1 + i, depth)
        own_load(level, p).wait()
        over(level, p).wait_recv()
        pair = (
            slot(own_table, own_main, level, p)[...].astype(F32)
            + slot(y_table, y_main, level, p)[...].astype(F32)
        )
        if i < depth - 1:
            slot(zs_table, zs_main, i, p)[...] = pair.astype(BF16)
            onward(i, p).start()
        elif p == 0:
            quarter(member)[...] = pair
        else:
            main_out[:, lanes[p]] = pair

    for i in range(depth):
        pair_up(i, 0)
    pair_up(0, 1)
    pair_up(0, 2)
    mine = quarter(member)
    for i in range(depth - 1):
        onward(i, 0).wait_recv()
        mine[...] = mine[...] + zr_table[i].astype(F32)
    to_others = [pass_quarter(member, 0, mate), pass_quarter(member, 1, across)]
    for copy in to_others:
        copy.start()
    for i in range(1, depth):
        pair_up(i, 1)
        pair_up(i, 2)
        if i == 1:
            pass_quarter(across, 1, across).wait_recv()
            second = pass_quarter(across, 2, mate)
            second.start()
    for shift in range(1, clients):
        for copy in small_from(shift):
            copy.wait_recv()
    low_out[...] = low_all[...]
    tile_out[...] = tile_all[...]
    pass_quarter(mate, 0, mate).wait_recv()
    pass_quarter(lax.rem(mate + 2, 4), 2, mate).wait_recv()
    table_out[...] = whole[...]
    for i in range(depth - 1):
        for p in (1, 2):
            onward(i, p).wait_recv()
            main_out[:, lanes[p]] = main_out[:, lanes[p]] + zr_main[i, :, lanes[p]].astype(F32)
    for copy in to_others + [second]:
        copy.wait_send()
    for shift in range(1, clients):
        for copy in small(shift):
            copy.wait_send()
    for i in range(depth):
        for p in parts:
            over(i, p).wait_send()
            if i < depth - 1:
                onward(i, p).wait_send()


def reduce_deltas(clients, main, table, low, tile):
    depth = clients // 2
    dma = pltpu.SemaphoreType.DMA
    vmem = pltpu.VMEM
    anywhere = pl.BlockSpec(memory_space=pl.ANY)
    inside = pl.BlockSpec(memory_space=pltpu.VMEM)
    block = main.shape[0] // clients
    half, columns = block // 2, table.shape[1] // 2
    wide = main.shape[1]
    hops = depth - 1
    return pl.pallas_call(
        functools.partial(reduce_kernel, clients),
        out_shape=(
            jax.ShapeDtypeStruct((block, wide), F32),
            jax.ShapeDtypeStruct((block, table.shape[1]), F32),
            jax.ShapeDtypeStruct(low.shape, BF16),
            jax.ShapeDtypeStruct((clients,) + tile.shape, F32),
        ),
        in_specs=[anywhere, anywhere, inside, inside],
        out_specs=(inside,) * 4,
        scratch_shapes=[
            vmem((depth, block, wide), BF16), vmem((depth, half, columns), BF16),
            vmem((depth, block, wide), BF16), vmem((depth, half, columns), BF16),
            vmem((hops, block, wide), BF16), vmem((hops, half, columns), BF16),
            vmem((hops, block, wide), BF16), vmem((hops, half, columns), BF16),
            vmem((block, table.shape[1]), F32), vmem(low.shape, BF16),
            vmem((clients,) + tile.shape, F32),
            dma((3, depth)), dma((3, depth)), dma((3, depth)), dma((3, hops)), dma((3, hops)),
            dma((clients - 1,)), dma((clients - 1,)), dma((clients - 1,)), dma((clients - 1,)),
            dma((3,)), dma((3,)),
        ],
        compiler_params=pltpu.CompilerParams(collective_id=2, has_side_effects=True),
        name="reduce_deltas",
    )(main, table, low, tile)


def adam(master, first, second, grad):
    first2 = BETA_ONE * first + (1.0 - BETA_ONE) * grad
    second2 = BETA_TWO * second + (1.0 - BETA_TWO) * grad * grad
    moved = (
        first2 / (1.0 - BETA_ONE**ROUND) / (jnp.sqrt(second2 / (1.0 - BETA_TWO**ROUND)) + ADAM_EPS)
    )
    fresh = master - SERVER_RATE * (moved + WEIGHT_DECAY * master)
    return (fresh, first2, second2, fresh.astype(jnp.bfloat16))


def server_kernel(main_ref, table_ref, low_ref, tile_ref, norm_ref, *refs):
    masters, firsts, seconds = refs[0:4], refs[4:8], refs[8:12]
    loss_out, norms_out = refs[12:14]
    outs = [refs[14 + i : 30 : 4] for i in range(4)]
    own, group = masters[0].shape[1:]
    tile = jnp.sum(tile_ref[...], 0)
    row = main_ref.shape[1] // 256
    examples, weighted_loss, weighted_factor = (tile[row : row + 1, i : i + 1] for i in range(3))
    scale = weighted_factor / examples / examples
    loss_out[...] = weighted_loss / examples
    lane = lax.broadcasted_iota(jnp.int32, (1, 128), 1)
    norms = jnp.zeros((1, 128), F32)
    for i in range(norm_ref.shape[0]):
        norms = jnp.where(lane == i, norm_ref[i, 0:1, 0:1], norms)
    norms_out[...] = norms[:, 0 : norm_ref.shape[0]]

    def apply(which, at, delta):
        results = adam(
            masters[which][at], firsts[which][at], seconds[which][at], scale * delta
        )
        for ref, value in zip(outs[which], results):
            ref[at] = value

    def slab(pair):
        return jnp.concatenate(pair, 1)

    every = slice(None)
    packed = tiles(main_ref[...])
    slabs = []
    for i in range(0, len(packed), 3):
        slabs += [slab(pair) for pair in unpack_two(packed[i : i + 3])]
    for i, which in enumerate((3, 4, 5, 6, 0, 1, 2)):
        apply(0, (which, every, every), slabs[i][:, :group])
    wo_rows = jnp.concatenate([slabs[7], jnp.zeros((128 - own, LANE), F32)], 0)
    apply(1, (0, every, every), jnp.transpose(wo_rows)[:group, :own])
    width = low_ref.shape[2] - 128
    messages = low_ref[...].reshape(low_ref.shape[0] * low_ref.shape[1], low_ref.shape[2])
    moved = tn(messages[:, :width], messages[:, width:])
    for i in range(4):
        apply(1, (i + 1, every, every), moved[i * group : (i + 1) * group, :own])
    apply(2, (every, every), table_ref[:, 0 : masters[2].shape[1]])
    bias = [tile[i : i + 1, :] for i in range(row)]
    rows = []
    for i in range(0, row, 3):
        rows += [slab(pair) for pair in unpack_two(bias[i : i + 3])]
    for i in range(4):
        apply(3, (slice(i, i + 1), every), rows[i][:, :group])


def server_update(main, table, low, tile, norms, state):
    inside = pl.BlockSpec(memory_space=pltpu.VMEM)
    shapes = [value.shape for value in state[:4]]
    out_shape = [jax.ShapeDtypeStruct((1, 1), F32), jax.ShapeDtypeStruct((1, norms.shape[0]), F32)]
    for kind in (F32, F32, F32, BF16):
        out_shape += [jax.ShapeDtypeStruct(shape, kind) for shape in shapes]
    return pl.pallas_call(
        server_kernel,
        out_shape=tuple(out_shape),
        in_specs=[inside] * (5 + len(state)),
        out_specs=(inside,) * len(out_shape),
        compiler_params=pltpu.CompilerParams(vmem_limit_bytes=VMEM_LIMIT),
        name="server_update",
    )(main, table, low, tile, norms, *state)


def on_device(
    pool, index, tau, counts, labels,
    in_bf, out_bf, table_bf, bias_bf,
    in_master, out_master, table_master, bias_master,
    in_first, out_first, table_first, bias_first,
    in_second, out_second, table_second, bias_second,
):
    clients = lax.axis_size("client")
    group = in_bf.shape[2]
    steps, images = index.shape[1], index.shape[2]
    patch_rows, features = pool.shape[1], pool.shape[2]
    seq = patch_rows + 1
    pad = (seq + 15) // 16 * 16
    own = in_bf.shape[1]
    rows_total = table_bf.shape[0]
    classes = rows_total - features - seq - 9
    table_t = table_bf.T
    direct = clients == 8
    if direct:
        main, wo_all, table, patches = gather_weights(
            clients, index, in_bf, out_bf, table_t, pool, pad
        )
    else:
        in_rows = jnp.transpose(in_bf, (1, 0, 2))
        out_rows = jnp.transpose(out_bf, (2, 0, 1))
        main_own = jnp.concatenate(
            [in_rows[:, 3:], out_rows[:, 1:], in_rows[:, :3], out_rows[:, :1]], 1
        ).reshape(own, 12 * group)
        table_own = jnp.pad(table_t, ((0, 0), (0, features + REST - rows_total)))
        main = lax.all_gather(main_own, "client", axis=0, tiled=True)
        table = lax.all_gather(table_own, "client", axis=0, tiled=True)
        wo_all = lax.all_gather(main[:, 12 * group - LANE :], "tensor", axis=1, tiled=True)
        patches = pick_patches(pool, index[0].reshape(steps * images), pad)
    bias = jnp.broadcast_to(bias_bf.astype(F32).reshape(1, 4 * group), (8, 4 * group))
    patches = patches.reshape(steps, images * pad, features)
    d_main, d_table, low, tile, norms = local_training(
        tau, counts, labels, index, patches, main, wo_all, table, bias, clients, pad, seq, classes
    )
    if direct:
        main_sum, table_sum, low_all, tile_all = reduce_deltas(clients, d_main, d_table, low, tile)
    else:
        tile_all = lax.psum(tile, "client")[None]
        main_sum = lax.psum_scatter(d_main, "client", scatter_dimension=0, tiled=True).astype(F32)
        first_member = lax.axis_index("tensor") == 0
        d_table = jnp.where(first_member, d_table, jnp.zeros_like(d_table))
        table_sum = lax.psum(
            lax.psum_scatter(d_table, "client", scatter_dimension=0, tiled=True).astype(F32), "tensor"
        )
        low_all = lax.all_to_all(low, "client", split_axis=0, concat_axis=0, tiled=True)
    state = (
        in_master, out_master, table_master.T, bias_master,
        in_first, out_first, table_first.T, bias_first,
        in_second, out_second, table_second.T, bias_second,
    )
    loss, norms, *fresh = server_update(main_sum, table_sum, low_all, tile_all, norms, state)
    fresh[2::4] = [value.T for value in fresh[2::4]]
    return (loss.reshape(()), norms, *fresh)


def solution(mesh):
    by_client = P("client", None, None)
    state = (P(None, "client", "tensor"), P(None, "tensor", "client"), P(None, "client"), P(None, "tensor"))
    in_specs = (by_client, by_client, P("client"), P("client"), P("client")) + state * 4
    out_specs = (P(), P("client", None)) + state * 4
    return jax.shard_map(
        on_device, mesh=mesh, in_specs=in_specs, out_specs=out_specs, check_vma=False
    )
```

```python
import functools

import jax
import jax.numpy as jnp
from jax import lax
from jax.experimental import pallas as pl
from jax.experimental.pallas import tpu as pltpu
from jax.sharding import PartitionSpec as P

HEAD_DIM = 64
ROUND = 5
EPS_NORM = 1e-06
MOMENTUM_RHO = 0.9
LOCAL_RATE = 0.05
CLIP_LIMIT = 1.0
BETA_ONE = 0.5
BETA_TWO = 0.7
ADAM_EPS = 1e-08
WEIGHT_DECAY = 0.05
SERVER_RATE = 0.05
SQRT_HALF = 0.7071067811865476
INV_ROOT_TAU = 0.3989422804014327
MESH = pl.DeviceIdType.MESH
F32 = jnp.float32
BF16 = jnp.bfloat16
NEG = -1e30
LANE = 256
SMALL = 16
REST = 512
VMEM_LIMIT = 67043328


def dot(left, right, dims):
    return lax.dot_general(left, right, (dims, ((), ())), preferred_element_type=F32)


def nn(left, right):
    return dot(left, right, ((1,), (0,)))


def nt(left, right):
    return dot(left, right, ((1,), (1,)))


def tn(left, right):
    return dot(left, right, ((0,), (0,)))


def fold(value):
    rows, width = value.shape
    return jnp.sum(value.reshape(rows // 8, 8, width), 0)


def total(value):
    return jnp.sum(jnp.sum(value, 1, keepdims=True), 0, keepdims=True)


def normalise(value):
    centre = value - jnp.mean(value, -1, keepdims=True)
    inverse = lax.rsqrt(jnp.mean(centre * centre, -1, keepdims=True) + EPS_NORM)
    return (centre * inverse, inverse)


def norm_grad(grad, gain, normed, inverse):
    scaled = grad * gain
    return inverse * (
        scaled
        - jnp.mean(scaled, -1, keepdims=True)
        - normed * jnp.mean(scaled * normed, -1, keepdims=True)
    )


def split_two(value):
    high = value.astype(BF16)
    return (high, (value - high.astype(F32)).astype(BF16))


def swap(tile):
    return pltpu.roll(tile, HEAD_DIM, 1)


def tiles(value):
    return [value[:, i : i + 128] for i in range(0, value.shape[1], 128)]


def low_half(shape):
    return lax.broadcasted_iota(jnp.int32, shape, 1) < HEAD_DIM


def pack_two(left, right):
    low = low_half(left[0].shape)
    return [
        left[0],
        jnp.where(low, left[1], swap(right[0])),
        jnp.where(low, swap(right[0]), swap(right[1])),
    ]


def unpack_two(packed):
    low = low_half(packed[0].shape)
    nothing = jnp.zeros_like(packed[0])
    middle, last = swap(packed[1]), swap(packed[2])
    return (
        [packed[0], jnp.where(low, packed[1], nothing)],
        [jnp.where(low, middle, last), jnp.where(low, last, nothing)],
    )


def train_kernel(
    sizes,
    tau_ref,
    count_ref,
    label_ref,
    index_ref,
    x_hbm,
    main_in,
    wo_in,
    table_in,
    bias_in,
    main_out,
    table_out,
    low_out,
    tile_out,
    norm_out,
    wqkv, w1, wot, w2t, wet, head,
    wqkv_f, w1_f, wot_f, wet_f, pos_f, head_f, vec_f, bias_f,
    wqkv_m, w1_m, wot_m, wet_m, pos_m, head_m, vec_m, bias_m,
    wqkv_g, wot_g, wet_g, pos_g, head_g, vec_g,
    xbuf, h0, slope, prob, abuf, qkv, oall, third, ubuf, dpre, h1own, datt, chip, inverses,
    hsum, asum, dact, bsum, vacc, ssq,
    low_d, low_a, low_b, low_w, scal, loss_all, factor_kept,
    s1, r1, s2, r2, mx_s, mx_r, nx_s, nx_r, pos_r, vec_r,
    wsem, xsem, o_ps, o_xs, o_fs, o_pr, o_xr, o_fr,
    a1s, a1r, a2s, a2r, das, dar, pvs, pvr, mxs, mxr, nxs, nxr, osem,
):
    steps, seq, pad, classes, clients = sizes
    width = 768
    kept = (seq + 7) // 8 * 8
    me = lax.axis_index("tensor")
    core = lax.rem(me, 2)
    mate = me + 1 - 2 * core
    across = lax.rem(me + 2, 4)
    own0 = 2 * core
    oth0 = 2 - 2 * core

    def rows(n):
        return pl.ds(pl.multiple_of(n * pad, 16), pad)

    def sent_rows(n):
        return pl.ds(pl.multiple_of(n * pad, 16), kept)

    def remote(src, dst, send, recv, device):
        return pltpu.make_async_remote_copy(
            src_ref=src, dst_ref=dst, send_sem=send, recv_sem=recv,
            device_id={"tensor": device}, device_id_type=MESH,
        )

    rest = dpre.at[0:width, 0:REST]
    square_rows = pl.ds(0, width)
    raw = abuf.at[square_rows, :]
    wo_raw = [ubuf.at[square_rows, pl.ds(g * LANE, LANE)] for g in range(3)] + [
        qkv.at[square_rows, pl.ds(0, LANE)]
    ]
    weights_in = [
        main_in.at[:, 2 * width : 3 * width],
        main_in.at[:, 0:width],
        main_in.at[:, width : 2 * width],
        table_in.at[:, 0:width],
        table_in.at[:, width : width + REST],
    ] + [wo_in.at[:, g * LANE : (g + 1) * LANE] for g in range(4)]
    weights = [raw, w1, w2t, wet, rest] + wo_raw

    def load(which):
        return pltpu.make_async_copy(weights_in[which], weights[which], wsem.at[which])

    def fetch(step, slot):
        return pltpu.make_async_copy(x_hbm.at[step], xbuf.at[slot], xsem.at[slot])

    barrier = pltpu.get_barrier_semaphore()
    fetch(0, 0).start()
    for which in range(9):
        load(which).start()
    for zero in (r1, r2, oall, third, datt):
        zero[...] = jnp.zeros_like(zero)
    for shift in (1, 2, 3):
        pl.semaphore_signal(
            barrier, inc=1, device_id={"tensor": lax.rem(me + shift, 4)}, device_id_type=MESH
        )
    bias_f[...] = bias_in[...]
    for zero in (pos_m, head_m, vec_m, bias_m, low_a, low_b, low_w, loss_all):
        zero[...] = jnp.zeros_like(zero)
    low_d[...] = jnp.zeros_like(low_d)
    for which in (0, 3, 4, 5, 6, 7, 8):
        load(which).wait()
    n_head = head.shape[0]
    vec_at, head_at = seq, seq + 9
    h0[0:REST, :] = jnp.transpose(rest[...].astype(F32))
    pos_rows = lax.broadcasted_iota(jnp.int32, (pad, 1), 0) < seq
    vec_rows = lax.broadcasted_iota(jnp.int32, (SMALL, 1), 0) < 9
    pos_f[...] = jnp.where(pos_rows, h0[0:pad, :], 0.0)
    vec_f[...] = jnp.where(vec_rows, h0[vec_at : vec_at + SMALL, :], 0.0)
    start_head = h0[head_at : head_at + n_head, :]
    head_f[...] = start_head
    head[...] = start_head.astype(BF16)
    taken = tau_ref[0]

    def join(parts):
        return jnp.concatenate(parts, 1)

    def start_rows(j, carry):
        at = pl.ds(pl.multiple_of(j * 64, 64), 64)
        packed = tiles(raw[at, :].astype(F32))
        q, k = unpack_two(packed[:3])
        v, _ = unpack_two(packed[3:])
        wqkv[at, :] = join(q + k + v).astype(BF16)
        pieces = [tiles(piece[at, :].astype(F32)) for piece in wo_raw]
        low = low_half((64, 128))
        first = [jnp.where(low, swap(p[0]), swap(p[1])) for p in pieces]
        last = [
            jnp.where(low, swap(pieces[g][1]), pieces[g + 1][1]) for g in (0, 2)
        ]
        wot[at, :] = join(first + last).astype(BF16)
        return carry

    lax.fori_loop(0, width // 64, start_rows, 0)
    pl.semaphore_wait(barrier, 3)

    row_id = lax.broadcasted_iota(jnp.int32, (pad, 1), 0)
    token = row_id < seq
    key_ok = lax.broadcasted_iota(jnp.int32, (1, pad), 1) < seq
    lane_head = lax.broadcasted_iota(jnp.int32, (1, LANE), 1) // HEAD_DIM
    small_ok = lax.broadcasted_iota(jnp.int32, (SMALL, 1), 0) < 4
    scale = HEAD_DIM ** (-0.5)

    def of_head(value, h):
        return jnp.where(lane_head == h, value, jnp.zeros_like(value))

    def o_part(message, group):
        lanes = pl.ds(pl.multiple_of(group * 128, 128), 128)
        pair, which = message // 3, message % 3
        if which == 2:
            return third.at[pair, 0:kept, lanes]
        return oall.at[pl.ds((2 * pair + which) * pad, kept), lanes]

    def o_to_mate(message):
        place = o_part(message, me)
        return remote(place, place, o_ps.at[message], o_pr.at[message], mate)

    def o_across(message):
        place = o_part(message, me)
        return remote(place, place, o_xs.at[message], o_xr.at[message], across)

    def o_forward(message):
        place = o_part(message, across)
        return remote(place, place, o_fs.at[message], o_fr.at[message], mate)

    def relay_o(message):
        place = o_part(message, across)
        remote(place, place, o_xs.at[message], o_xr.at[message], across).wait_recv()
        o_forward(message).start()

    def o_here(message):
        direct = o_part(message, mate)
        remote(direct, direct, o_ps.at[message], o_pr.at[message], mate).wait_recv()
        passed = o_part(message, lax.rem(mate + 2, 4))
        remote(passed, passed, o_fs.at[message], o_fr.at[message], mate).wait_recv()

    def to_mate(n):
        return remote(s1.at[n, 0:kept], r1.at[n, 0:kept], a1s.at[n], a1r.at[n], mate)

    def to_across(which, n):
        return remote(s2.at[n, 0:kept], r2.at[2 * which + n, 0:kept], a2s.at[2 * which + n], a2r.at[2 * which + n], across)

    def gradient_to_mate(buffer, which, image, k):
        return remote(
            buffer.at[sent_rows(image)], buffer.at[sent_rows(image)],
            das.at[2 * which + k], dar.at[2 * which + k], mate,
        )

    def pos_to_mate():
        return remote(pos_g, pos_r, pvs.at[0], pvr.at[0], mate)

    def vec_to_mate():
        return remote(vacc, vec_r, pvs.at[1], pvr.at[1], mate)

    def spread(src, dst, send, recv, shift):
        return remote(
            src, dst.at[me], send.at[shift - 1], recv.at[shift - 1], lax.rem(me + shift, 4)
        )

    def update_rows(entries, rho, live, fac):
        def update(j, carry):
            at = pl.ds(pl.multiple_of(j * 64, 64), 64)
            for low, full, mom, grad in entries:
                m = rho * mom[at, :] + fac * grad[at, :]
                mom[at, :] = m
                w = full[at, :] - (live * LOCAL_RATE) * m
                full[at, :] = w
                low[at, :] = w.astype(BF16)
            return carry

        lax.fori_loop(0, width // 64, update, 0)

    def one_step(step, carry):
        slot = lax.rem(step, 2)
        fetch(step, slot).wait()

        @pl.when(step < steps - 1)
        def _():
            fetch(step + 1, 1 - slot).start()

        gain1, shift1 = vec_f[0:1, :], vec_f[1:2, :]
        gain2, shift2 = vec_f[2:3, :], vec_f[3:4, :]
        gain3, shift3 = vec_f[4:5, :], vec_f[5:6, :]

        def attend(pair):
            two = slice(2 * pair * pad, 2 * (pair + 1) * pad)
            inside = (row_id >= 1) & token
            added = pos_f[...] + jnp.where(inside, vec_f[6:7, :], 0.0)
            state = nt(xbuf[slot, two, :], wet[...]) + jnp.concatenate([added, added], 0)
            h0[two, :] = state
            normed, _ = normalise(state)
            a = (normed * gain1 + shift1).astype(BF16)
            abuf[two, :] = a
            both = nn(a, wqkv[...]).astype(BF16)
            qkv[two, :] = both
            mine = pl.ds(pl.multiple_of(me * 128, 128), 128)
            thirds = []
            for i in range(2):
                projected = both[i * pad : (i + 1) * pad]
                q, k, v = projected[:, :LANE], projected[:, LANE : 2 * LANE], projected[:, 2 * LANE :]
                out = jnp.zeros((pad, LANE), F32)
                for h in range(3):
                    scores = jnp.where(key_ok, nt(of_head(q, h), k) * scale, NEG)
                    expd = jnp.exp(scores - jnp.max(scores, -1, keepdims=True))
                    p = (expd / jnp.sum(expd, -1, keepdims=True)).astype(BF16)
                    prob[(2 * pair + i) * 3 + h] = p
                    out = out + nn(p, of_head(v, h))
                oall[(2 * pair + i) * pad : (2 * pair + i + 1) * pad, mine] = out[:, :128].astype(BF16)
                thirds.append(out[:, 128:])
                o_to_mate(3 * pair + i).start()
                o_across(3 * pair + i).start()
            third[pair, :, mine] = (thirds[0] + swap(thirds[1])).astype(BF16)
            o_to_mate(3 * pair + 2).start()
            o_across(3 * pair + 2).start()

        attend(0)
        attend(1)

        @pl.when(step == 0)
        def _():
            load(1).wait()
            load(2).wait()

            def begin(j, carry):
                at = pl.ds(pl.multiple_of(j * 32, 32), 32)
                for low_ref, full, mom in (
                    (wqkv, wqkv_f, wqkv_m), (w1, w1_f, w1_m), (wot, wot_f, wot_m), (wet, wet_f, wet_m)
                ):
                    full[at, :] = low_ref[at, :].astype(F32)
                    mom[at, :] = jnp.zeros((32, width), F32)
                return carry

            lax.fori_loop(0, width // 32, begin, 0)

        @pl.when(step > 0)
        def _():
            was_live = jnp.where(step - 1 < taken, 1.0, 0.0)
            was_rho = jnp.where(step - 1 < taken, MOMENTUM_RHO, 1.0)
            was_fac = factor_kept[0:1, 0:1]
            update_rows(((w1, w1_f, w1_m, slope), (wot, wot_f, wot_m, wot_g)), was_rho, was_live, was_fac)
            head_m[...] = was_rho * head_m[...] + was_fac * head_g[...]
            head_f[...] = head_f[...] - (was_live * LOCAL_RATE) * head_m[...]
            head[...] = head_f[...].astype(BF16)
            moved_rows = (LOCAL_RATE * low_w[:, 0:1]) * low_a[...]
            low_hi, low_lo = split_two(moved_rows)
            pair_rows = jnp.concatenate([low_hi, low_lo], 0)
            load(2).wait()

            def low_rank(j, carry):
                at = pl.ds(pl.multiple_of(j * LANE, LANE), LANE)
                moved = tn(jnp.concatenate([low_d[:, at], low_d[:, at]], 0), pair_rows)
                w2t[at, :] = (w2t[at, :].astype(F32) - moved).astype(BF16)
                return carry

            lax.fori_loop(0, width // LANE, low_rank, 0)

        for message in range(3):
            relay_o(message)

        def feed(pair):
            for message in range(3):
                o_here(3 * pair + message)
            two = slice(2 * pair * pad, 2 * (pair + 1) * pad)
            side = tiles(third[pair].astype(F32))
            low = low_half((pad, 128))
            for i in range(2):
                for g in (0, 2):
                    if i == 0:
                        tile = jnp.where(low, side[g], swap(side[g + 1]))
                    else:
                        tile = jnp.where(low, swap(side[g]), side[g + 1])
                    at = 4 * 128 + g * HEAD_DIM
                    oall[(2 * pair + i) * pad : (2 * pair + i + 1) * pad, at : at + 128] = tile.astype(BF16)
            state = h0[two, :] + nt(oall[two, :], wot[...]) + vec_f[7:8, :]
            differs = (pair + core) - 2 * pair * core
            for i in range(2):
                part = state[i * pad : (i + 1) * pad]
                h1own[i * (1 - differs) + 2 * differs] = part
                hsum[2 * pair + i] = fold(jnp.where(token, part, 0.0))
            normed, _ = normalise(state)
            u = (normed * gain2 + shift2).astype(BF16)
            ubuf[two, :] = u
            if pair == 0:
                relay_o(3)
                relay_o(4)
            z = nn(u, w1[...]) + bias_f[0:1, :]
            cdf = 0.5 * (1.0 + lax.erf(z * SQRT_HALF))
            act = (z * cdf).astype(BF16).astype(F32)
            tail = cdf + z * jnp.exp(-0.5 * z * z) * INV_ROOT_TAU
            for i in range(2):
                part = slice(i * pad, (i + 1) * pad)
                asum[2 * pair + i] = fold(jnp.where(token, act[part], 0.0))
                slope[(2 * pair + i) * pad : (2 * pair + i + 1) * pad, :] = jnp.where(token, tail[part], 0.0)
            if pair == 0:
                relay_o(5)

        feed(0)
        feed(1)

        def stack(ref):
            parts = [jnp.sum(ref[n], 0, keepdims=True) for n in range(4)]
            return jnp.concatenate(parts + [jnp.zeros((SMALL - 4, width), F32)], 0)

        act_sum = stack(asum)
        act_hi, act_lo = split_two(act_sum)
        both = nt(jnp.concatenate([act_hi, act_lo], 0), w2t[...])
        mx_s[...] = both[:8] + both[SMALL : SMALL + 8]
        for shift in (1, 2, 3):
            spread(mx_s, mx_r, mxs, mxr, shift).start()
        mx_r[me] = mx_s[...]
        h_mean = stack(hsum) * (1.0 / seq)
        for shift in (1, 2, 3):
            remote(
                mx_s, mx_r.at[lax.rem(me + 4 - shift, 4)], mxs.at[shift - 1], mxr.at[shift - 1], mate
            ).wait_recv()
        mlp = jnp.concatenate(
            [mx_r[0] + mx_r[1] + mx_r[2] + mx_r[3], jnp.zeros((SMALL - 8, width), F32)], 0
        )
        average = h_mean + mlp * (1.0 / seq) + vec_f[8:9, :]
        normed3, inverse3 = normalise(average)
        pooled = (normed3 * gain3 + shift3).astype(BF16)
        logits = nt(pooled, head[...])
        class_ok = lax.broadcasted_iota(jnp.int32, (1, head.shape[0]), 1) < classes
        logits = jnp.where(class_ok, logits, NEG)
        top = jnp.max(logits, -1, keepdims=True)
        exp_l = jnp.exp(logits - top)
        total_l = jnp.sum(exp_l, -1, keepdims=True)
        hot_row = lax.broadcasted_iota(jnp.int32, (SMALL, n_head), 0)
        hot_lane = lax.broadcasted_iota(jnp.int32, (SMALL, n_head), 1)
        hot = jnp.zeros((SMALL, n_head), F32)
        for n in range(4):
            label = label_ref[index_ref[0, step, n]]
            hot = jnp.where((hot_row == n) & (hot_lane == label), 1.0, hot)
        each = top + jnp.log(total_l) - jnp.sum(jnp.where(class_ok, logits, 0.0) * hot, -1, keepdims=True)
        loss = jnp.sum(jnp.where(small_ok, each, 0.0), 0, keepdims=True) * 0.25
        live = jnp.where(step < taken, 1.0, 0.0)
        rho = jnp.where(step < taken, MOMENTUM_RHO, 1.0)
        loss_tile = live * loss
        d_logits = jnp.where(small_ok, (exp_l / total_l - hot) * 0.25, 0.0).astype(BF16)
        d_head = tn(d_logits, pooled)
        head_g[...] = d_head
        d_pooled = nn(d_logits, head[...])
        d_average = norm_grad(d_pooled, gain3, normed3, inverse3)
        d_token = d_average * (1.0 / seq)
        d_mlp = d_token.astype(BF16)
        dact[...] = nn(d_mlp, w2t[...])
        for r in range(4):
            scal[r] = jnp.broadcast_to(d_token[r : r + 1, :], (8, width))
        vec_g[...] = jnp.zeros_like(vec_g)
        vec_g[4:5, :] = jnp.sum(d_pooled * normed3, 0, keepdims=True)
        vec_g[5:6, :] = jnp.sum(d_pooled, 0, keepdims=True)
        vec_g[8:9, :] = jnp.sum(d_average, 0, keepdims=True)
        low_at = pl.ds(pl.multiple_of(step * SMALL, SMALL), SMALL)
        low_d[low_at, :] = d_mlp
        low_a[low_at, :] = act_sum
        gram_d = nt(d_mlp, d_mlp)
        gram_a = nt(act_hi, act_hi) + nt(act_hi, act_lo) + nt(act_lo, act_hi)
        own_squares = total(gram_d * gram_a)

        for n in range(4):
            scal[4 + n] = jnp.broadcast_to(dact[n : n + 1, :], (8, width))
        bsum[...] = jnp.zeros_like(bsum)
        vacc[...] = jnp.zeros_like(vacc)

        def upper_partial(n):
            at = pl.ds(pl.multiple_of(n * pad, 16), 2 * pad)
            rate = jnp.concatenate(
                [jnp.broadcast_to(scal[4 + n + i][0:1, :], (pad, width)) for i in range(2)], 0
            )
            g = (rate * slope[at, :]).astype(BF16)
            dpre[at, :] = g
            bsum[...] = bsum[...] + fold(g.astype(F32))
            return nt(g, w1[...])

        other = upper_partial(oth0)
        for k in (0, 1):
            s1[k] = other[k * pad : (k + 1) * pad].astype(BF16)
            to_mate(k).start()
        own = upper_partial(own0)
        for k in (0, 1):
            to_mate(k).wait_recv()
            part = own[k * pad : (k + 1) * pad] + r1[k].astype(F32)
            chip[k] = part
            s2[k] = part.astype(BF16)
            to_across(0, k).start()

        ssq[...] = jnp.zeros_like(ssq)
        w1_g = slope

        def weight_grad(left, right, out, which):
            def tile(j, carry):
                at = pl.ds(pl.multiple_of(j * LANE, LANE), LANE)
                g = tn(left[:, at], right[...])
                out[at, :] = g
                ssq[which] = ssq[which] + fold(g * g)
                return carry

            lax.fori_loop(0, width // LANE, tile, 0)

        def embedding_grad(k, left):
            def tile(j, carry):
                at = pl.ds(pl.multiple_of(j * LANE, LANE), LANE)
                g = tn(left[rows(own0 + k), at], xbuf[slot, rows(own0 + k), :])
                g = g + tn(left[rows(oth0 + k), at], xbuf[slot, rows(oth0 + k), :])
                if k == 1:
                    g = g + wet_g[at, :]
                    ssq[3] = ssq[3] + fold(g * g)
                wet_g[at, :] = g
                return carry

            lax.fori_loop(0, width // LANE, tile, 0)

        weight_grad(ubuf, dpre, w1_g, 0)

        for k in (0, 1):
            normed, inverse = normalise(h1own[k])
            h1own[k] = normed
            inverses[k] = inverse
            normed, inverse = normalise(h0[rows(own0 + k), :])
            h0[rows(own0 + k), :] = normed
            inverses[2 + k] = inverse

        def attention_partial(n):
            own_columns = jnp.concatenate(
                [
                    wot[:, pl.ds(pl.multiple_of(me * 128, 128), 128)],
                    wot[:, pl.ds(pl.multiple_of(4 * 128 + (me // 2) * 128, 128), 128)],
                ],
                1,
            )
            wide = nn(datt[rows(n), :], own_columns)
            thirds = jnp.where(core == 1, swap(wide[:, 128:]), wide[:, 128:])
            thirds = jnp.where(low_half((pad, 128)), thirds, 0.0)
            d_ctx = jnp.concatenate([wide[:, :128], thirds], 1).astype(BF16)
            projected = qkv[rows(n), :]
            q, k, v = projected[:, :LANE], projected[:, LANE : 2 * LANE], projected[:, 2 * LANE :]
            d_q = jnp.zeros((pad, LANE), F32)
            d_k = jnp.zeros((pad, LANE), F32)
            d_v = jnp.zeros((pad, LANE), F32)
            for h in range(3):
                part = of_head(d_ctx, h)
                p = prob[n * 3 + h]
                again = p.astype(F32)
                d_p = nt(part, v)
                inner = d_p - jnp.sum(d_p * again, -1, keepdims=True)
                d_s = (again * inner).astype(BF16)
                d_v = d_v + tn(p, part)
                d_q = d_q + nn(d_s, of_head(k, h))
                d_k = d_k + tn(d_s, of_head(q, h))
            d_all = jnp.concatenate([d_q * scale, d_k * scale, d_v], 1).astype(BF16)
            qkv[rows(n), :] = d_all
            return nt(d_all, wqkv[...])

        for k in (0, 1):
            to_across(0, k).wait_recv()
            d_upper = chip[k] + r2[k].astype(F32)
            normed = h1own[k]
            d_state = norm_grad(d_upper, gain2, normed, inverses[k]) + scal[own0 + k][0:1, :]
            d_state = jnp.where(token, d_state, 0.0)
            h1own[k] = d_state
            datt[rows(own0 + k), :] = d_state.astype(BF16)
            gradient_to_mate(datt, 0, own0 + k, k).start()
            vacc[0] = vacc[0] + fold(d_upper * normed)
            vacc[1] = vacc[1] + fold(d_upper)
            vacc[2] = vacc[2] + fold(d_state)
            own = attention_partial(own0 + k)
            remote(
                datt.at[sent_rows(oth0 + k)], datt.at[sent_rows(oth0 + k)], das.at[k], dar.at[k], mate
            ).wait_recv()
            other = attention_partial(oth0 + k)
            to_mate(k).wait_send()
            s1[k] = other.astype(BF16)
            to_mate(k).start()
            to_mate(k).wait_recv()
            own = own + r1[k].astype(F32)
            chip[k] = own
            to_across(0, k).wait_send()
            s2[k] = own.astype(BF16)
            to_across(1, k).start()

        weight_grad(datt, oall, wot_g, 1)
        weight_grad(abuf, qkv, wqkv_g, 2)

        d_emb = ubuf
        for k in (0, 1):
            to_across(1, k).wait_recv()
            d_normed = chip[k] + r2[2 + k].astype(F32)
            normed = h0[rows(own0 + k), :]
            d_state = h1own[k] + norm_grad(d_normed, gain1, normed, inverses[2 + k])
            d_emb[rows(own0 + k), :] = d_state.astype(BF16)
            gradient_to_mate(d_emb, 1, own0 + k, k).start()
            vacc[3] = vacc[3] + fold(d_normed * normed)
            vacc[4] = vacc[4] + fold(d_normed)
            vacc[5] = vacc[5] + fold(jnp.where(row_id >= 1, d_state, 0.0))
            if k == 0:
                pos_g[...] = d_state
            else:
                pos_g[...] = pos_g[...] + d_state
                pos_to_mate().start()
                vec_to_mate().start()
            remote(
                d_emb.at[sent_rows(oth0 + k)], d_emb.at[sent_rows(oth0 + k)],
                das.at[2 + k], dar.at[2 + k], mate,
            ).wait_recv()
            embedding_grad(k, d_emb)
        pos_to_mate().wait()
        vec_to_mate().wait()
        pos_g[...] = pos_g[...] + pos_r[...]
        sums = [jnp.sum(vacc[r] + vec_r[r], 0, keepdims=True) for r in range(6)]
        vec_g[0:1, :] = sums[3]
        vec_g[1:2, :] = sums[4]
        vec_g[2:3, :] = sums[0]
        vec_g[3:4, :] = sums[1]
        vec_g[6:7, :] = sums[5]
        vec_g[7:8, :] = sums[2]
        d_bias = jnp.sum(bsum[...], 0, keepdims=True)
        shared = (
            total(ssq[1] + ssq[3] + fold(pos_g[...] * pos_g[...]) + fold(head_g[...] * head_g[...]))
            + total(vec_g[...] * vec_g[...])
        )
        own_squares = own_squares + total(ssq[0] + ssq[2]) + total(d_bias * d_bias)
        for message in range(6):
            o_to_mate(message).wait_send()
            o_across(message).wait_send()
            o_forward(message).wait_send()
        for k in (0, 1):
            to_mate(k).wait_send()
            to_across(1, k).wait_send()
            gradient_to_mate(datt, 0, own0 + k, k).wait_send()
            gradient_to_mate(d_emb, 1, own0 + k, k).wait_send()
        for shift in (1, 2, 3):
            spread(mx_s, mx_r, mxs, mxr, shift).wait_send()
        first_lane = lax.broadcasted_iota(jnp.int32, (8, 128), 1) < 64
        nx_s[...] = jnp.where(first_lane, own_squares + 0.25 * shared, loss_tile)
        for shift in (1, 2, 3):
            spread(nx_s, nx_r, nxs, nxr, shift).start()
        nx_r[me] = nx_s[...]

        @pl.when(step == steps - 1)
        def _():
            for which in (0, 1, 3, 4):
                load(which).start()

        for shift in (1, 2, 3):
            remote(
                nx_s, nx_r.at[lax.rem(me + 4 - shift, 4)], nxs.at[shift - 1], nxr.at[shift - 1], mate
            ).wait_recv()
        norm = jnp.sqrt((nx_r[0] + nx_r[1] + nx_r[2] + nx_r[3]))
        factor = live * (CLIP_LIMIT / jnp.maximum(norm, CLIP_LIMIT))
        norm_out[step] = live * norm
        loss_all[...] = loss_all[...] + nx_r[0]
        for shift in (1, 2, 3):
            spread(nx_s, nx_r, nxs, nxr, shift).wait_send()
        fac = factor[0:1, 0:1]

        low_row = lax.broadcasted_iota(jnp.int32, low_b.shape, 0) // SMALL
        low_b[...] = jnp.where(low_row == step, fac, rho * low_b[...])
        low_w[...] = low_w[...] + live * low_b[...]
        factors = (LOCAL_RATE * low_w[:, 0:1]) * low_a[...]
        factor_kept[...] = factor

        def small_update(full, mom, grad):
            mom[...] = rho * mom[...] + fac * grad
            full[...] = full[...] - (live * LOCAL_RATE) * mom[...]

        small_update(pos_f, pos_m, pos_g[...])
        small_update(vec_f, vec_m, vec_g[...])
        small_update(bias_f, bias_m, jnp.broadcast_to(d_bias, (8, width)))
        table = (
            (wqkv, wqkv_f, wqkv_m, wqkv_g),
            (w1, w1_f, w1_m, w1_g),
            (wot, wot_f, wot_m, wot_g),
            (wet, wet_f, wet_m, wet_g),
        )

        @pl.when(step < steps - 1)
        def _():
            load(2).start()
            update_rows((table[0], table[3]), rho, live, fac)

        @pl.when(step == steps - 1)
        def _():
            examples = jnp.full((1, 1), count_ref[0].astype(F32))
            factor_sum = jnp.zeros((), F32)
            for k in range(steps):
                worth = (1.0 - MOMENTUM_RHO ** (k + 1)) / (1.0 - MOMENTUM_RHO)
                factor_sum = factor_sum + jnp.where(k < taken, worth, 0.0)
            factor_sum = jnp.full((1, 1), factor_sum)
            share = examples / factor_sum
            for which in (0, 1, 3, 4):
                load(which).wait()

            def ended(at, full, mom, grad, lanes):
                m = rho * mom[at, lanes] + fac * grad[at, lanes]
                return full[at, lanes] - (live * LOCAL_RATE) * m

            outs = (
                (w1, main_out.at[:, 0:width]),
                (wet, table_out.at[:, 0:width]),
                (raw, main_out.at[:, width : 2 * width]),
                (rest, table_out.at[:, width : width + REST]),
            )
            copies = [
                pltpu.make_async_copy(src, dst, osem.at[i]) for i, (src, dst) in enumerate(outs)
            ]
            for i, (low, full, mom, grad) in enumerate((table[1], table[3])):

                def finish_square(j, carry):
                    at = pl.ds(pl.multiple_of(j * 64, 64), 64)
                    w = ended(at, full, mom, grad, slice(None))
                    low[at, :] = (share * (low[at, :].astype(F32) - w)).astype(BF16)
                    return carry

                lax.fori_loop(0, width // 64, finish_square, 0)
                copies[i].start()

            def finish(j, carry):
                at = pl.ds(pl.multiple_of(j * 64, 64), 64)
                three = tiles(ended(at, wqkv_f, wqkv_m, wqkv_g, slice(None)))
                _, full, mom, grad = table[2]
                wo_first = ended(at, full, mom, grad, pl.ds(pl.multiple_of(me * 128, 128), 128))
                wo_last = ended(
                    at, full, mom, grad, pl.ds(pl.multiple_of(4 * 128 + (me // 2) * 128, 128), 128)
                )
                wo_last = jnp.where(core == 1, swap(wo_last), wo_last)
                packed = join(
                    pack_two(three[0:2], three[2:4]) + pack_two(three[4:6], [wo_first, wo_last])
                )
                raw[at, :] = (share * (raw[at, :].astype(F32) - packed)).astype(BF16)
                return carry

            lax.fori_loop(0, width // 64, finish, 0)
            copies[2].start()
            small_update(head_f, head_m, head_g[...])
            h0[0:REST, :] = jnp.transpose(rest[...].astype(F32))
            for ref, begin, count in ((pos_f, 0, seq), (vec_f, vec_at, 9), (head_f, head_at, classes)):
                h0[begin : begin + count, :] = share * (h0[begin : begin + count, :] - ref[0:count, :])
            rest[...] = jnp.transpose(h0[0:REST, :]).astype(BF16)
            copies[3].start()
            d_bias_all = share * (bias_in[0:1, :] - bias_f[0:1, :])
            for r in range(width // 128):
                tile_out[r : r + 1, :] = d_bias_all[:, 128 * r : 128 * (r + 1)]
            lane = lax.broadcasted_iota(jnp.int32, (1, 128), 1)
            loss_sum = loss_all[0:1, 64:65]
            mean_loss = examples * loss_sum / jnp.full((1, 1), taken.astype(F32))
            scalars = jnp.where(lane == 0, examples, jnp.where(lane == 1, mean_loss, examples * factor_sum))
            tile_out[width // 128 : width // 128 + 1, :] = jnp.where(lane < 3, scalars, 0.0)
            tile_out[width // 128 + 1 :, :] = jnp.zeros((7 - width // 128, 128), F32)
            used = 4 * steps
            wanted_row = lax.broadcasted_iota(jnp.int32, (used, steps * SMALL), 0)
            wanted_row = (wanted_row // 4) * SMALL + lax.rem(wanted_row, 4)
            picker = (lax.broadcasted_iota(jnp.int32, (used, steps * SMALL), 1) == wanted_row).astype(BF16)
            low_left = nn(picker, (share * factors).astype(BF16)).astype(BF16)
            low_right = nn(picker, low_d[...])
            part = width // clients
            kept_lanes = lax.broadcasted_iota(jnp.int32, (used, 128), 1) < part
            for j in range(clients):
                low_out[j, :, 0:width] = low_left
                turned = pltpu.roll(low_right, (width - part * j) % width, 1) if j else low_right
                low_out[j, :, width : width + 128] = jnp.where(kept_lanes, turned[:, :128], 0.0).astype(BF16)
            for copy in copies:
                copy.wait()

        return carry

    lax.fori_loop(0, steps, one_step, 0)


def local_training(tau, counts, labels, index, patches, main, wo, table, bias, clients, pad, seq, classes):
    steps = patches.shape[0]
    width = main.shape[0]
    n_all = 4 * pad
    n_head = (classes + 127) // 128 * 128
    n_low = steps * SMALL
    vmem = pltpu.VMEM
    dma = pltpu.SemaphoreType.DMA
    anywhere = pl.BlockSpec(memory_space=pl.ANY)
    inside = pl.BlockSpec(memory_space=pltpu.VMEM)
    square = (width, width)
    out_shape = (
        jax.ShapeDtypeStruct((width, 2 * width), BF16),
        jax.ShapeDtypeStruct(table.shape, BF16),
        jax.ShapeDtypeStruct((clients, 4 * steps, width + 128), BF16),
        jax.ShapeDtypeStruct((8, 128), F32),
        jax.ShapeDtypeStruct((steps, 8, 128), F32),
    )
    scratch = [
        vmem(square, BF16), vmem(square, BF16), vmem(square, BF16), vmem(square, BF16),
        vmem(square, BF16), vmem((n_head, width), BF16),
    ]
    for _ in range(2):
        scratch += [
            vmem(square, F32), vmem(square, F32), vmem(square, F32), vmem(square, F32),
            vmem((pad, width), F32), vmem((n_head, width), F32), vmem((SMALL, width), F32),
            vmem((8, width), F32),
        ]
    scratch += [
        vmem(square, F32), vmem(square, F32), vmem(square, F32), vmem((pad, width), F32),
        vmem((n_head, width), F32), vmem((SMALL, width), F32),
        vmem((2, n_all, width), BF16), vmem((n_all, width), F32), vmem((n_all, width), F32),
        vmem((12, pad, pad), BF16), vmem((n_all, width), BF16), vmem((n_all, width), BF16),
        vmem((n_all, width), BF16), vmem((2, pad, 4 * 128), BF16), vmem((n_all, width), BF16),
        vmem((n_all, width), BF16), vmem((3, pad, width), F32), vmem((n_all, width), BF16),
        vmem((2, pad, width), F32), vmem((4, pad, 1), F32),
        vmem((4, 8, width), F32), vmem((4, 8, width), F32), vmem((SMALL, width), F32),
        vmem((8, width), F32), vmem((6, 8, width), F32), vmem((4, 8, width), F32),
        vmem((n_low, width), BF16), vmem((n_low, width), F32), vmem((n_low, 128), F32),
        vmem((n_low, 128), F32), vmem((8, 8, width), F32), vmem((8, 128), F32), vmem((8, 128), F32),
        vmem((2, pad, width), BF16), vmem((2, pad, width), BF16), vmem((2, pad, width), BF16),
        vmem((4, pad, width), BF16), vmem((8, width), F32), vmem((4, 8, width), F32),
        vmem((8, 128), F32), vmem((4, 8, 128), F32), vmem((pad, width), F32),
        vmem((6, 8, width), F32),
        dma((9,)), dma((2,)), dma((6,)), dma((6,)), dma((6,)), dma((6,)), dma((6,)), dma((6,)),
        dma((2,)), dma((2,)), dma((4,)), dma((4,)), dma((4,)), dma((4,)), dma((2,)), dma((2,)),
        dma((3,)), dma((3,)), dma((3,)), dma((3,)), dma((6,)),
    ]
    return pl.pallas_call(
        functools.partial(train_kernel, (steps, seq, pad, classes, clients)),
        out_shape=out_shape,
        in_specs=[pl.BlockSpec(memory_space=pltpu.SMEM)] * 4 + [anywhere] * 4 + [inside],
        out_specs=(anywhere,) * 2 + (inside,) * 3,
        scratch_shapes=scratch,
        compiler_params=pltpu.CompilerParams(
            collective_id=0, has_side_effects=True, vmem_limit_bytes=VMEM_LIMIT
        ),
        name="local_training",
    )(tau, counts, labels, index, patches, main, wo, table, bias)


def place_patches(chosen_ref, pool_ref, out_ref):
    seq_rows, width = pool_ref.shape[1], pool_ref.shape[2]
    pad = out_ref.shape[1]
    below = jnp.zeros((pad - 1 - seq_rows, width), F32)
    whole = jnp.concatenate([jnp.zeros((1, width), F32), pool_ref[0].astype(F32), below], 0)
    out_ref[0] = whole.astype(BF16)


def pick_patches(pool, chosen, pad):
    count = chosen.shape[0]
    _, patch_rows, width = pool.shape
    return pl.pallas_call(
        place_patches,
        out_shape=jax.ShapeDtypeStruct((count, pad, width), BF16),
        grid_spec=pltpu.PrefetchScalarGridSpec(
            num_scalar_prefetch=1,
            grid=(count,),
            in_specs=[pl.BlockSpec((1, patch_rows, width), lambda i, ids: (ids[i], 0, 0))],
            out_specs=pl.BlockSpec((1, pad, width), lambda i, ids: (i, 0, 0)),
        ),
        name="pick_patches",
    )(chosen, pool)


def ring_places(clients):
    depth = clients // 2
    client = lax.axis_index("client")
    member = lax.axis_index("tensor")
    core = lax.rem(member, 2)
    return (
        depth, client, client // 2, lax.rem(client, 2), member, core, member // 2,
        member + 1 - 2 * core, lax.rem(member + 2, 4),
    )


def send(src, dst, send_sem, recv_sem, client, member):
    return pltpu.make_async_remote_copy(
        src_ref=src, dst_ref=dst, send_sem=send_sem, recv_sem=recv_sem,
        device_id={"client": client, "tensor": member}, device_id_type=MESH,
    )


def span(start, size, unit):
    return pl.ds(pl.multiple_of(start, unit), size)


def gather_kernel(
    clients, index_ref, in_ref, out_ref, table_in, pool_ref, main_out, wo_out, table_out, x_out,
    main_ref, table_ref, wide_in, wide_out, pool_buf, x_buf, pool_sem, x_sem, up_s, up_r, down_s, down_r, y_s, y_r, mate_s, mate_r, x_s, x_r, on_s, on_r, own_sem, keep_sem,
):
    depth, client, z, y, member, core, chip_x, mate, across = ring_places(clients)
    block = main_ref.shape[0]
    half = block // 2
    columns = table_ref.shape[1] // 2
    peer = client + 1 - 2 * y

    wide = main_ref.shape[1]
    tail = wide - LANE

    def table_part(origin, who):
        return table_out.at[
            span(origin * block + (who // 2) * half, half, half),
            span(lax.rem(who, 2) * columns, columns, 128),
        ]

    def wo_part(origin, who):
        return wo_out.at[span(origin * block, block, block), span(who * LANE, LANE, LANE)]

    def shared(origin, who):
        return (wo_part(origin, who), table_part(origin, who))

    def main_part(origin, lanes):
        return main_out.at[span(origin * block, block, block), lanes]

    early, front, back = slice(0, wide // 6), slice(wide // 6, 2 * wide // 3), slice(2 * wide // 3, wide)

    def beside(origin):
        return origin + 1 - 2 * lax.rem(origin, 2)

    def landed(origin):
        return (
            main_part(origin, back), table_part(origin, member), main_part(origin, front),
            main_part(origin, early), main_part(beside(origin), early),
        )

    own_table = table_ref.at[span(chip_x * half, half, half), span(core * columns, columns, 128)]
    own_pieces = (
        main_ref.at[:, back], own_table, main_ref.at[:, front], main_ref.at[:, early],
        main_part(peer, early),
    )

    def given(origin, mine):
        if mine:
            return (main_ref.at[:, tail:wide], own_table)
        return (main_part(origin, slice(tail, wide)), table_part(origin, member))

    def message(origin, mine, send_sem, recv_sem, index, to, part):
        sources = own_pieces if mine else landed(origin)
        return [
            send(src, dst, send_sem.at[p, index], recv_sem.at[p, index], to, member)
            for p, (src, dst) in enumerate(zip(sources, landed(origin)))
        ][part]

    first, second, third, over_all, crossing = slice(0, 2), slice(2, 4), slice(4, 5), slice(0, 3), slice(3, 4)
    over_second = slice(2, 3)

    def up(origin, i, part, mine=False):
        return message(origin, mine, up_s, up_r, i, client + 2, part)

    def down(origin, i, part, mine=False):
        return message(origin, mine, down_s, down_r, i, client - 2, part)

    def over(origin, part, mine=False):
        return message(origin, mine, y_s, y_r, origin // 2, peer, part)

    def give(origin, mine, send_sem, recv_sem, to):
        return [
            send(src, dst, send_sem.at[p, origin], recv_sem.at[p, origin], client, to)
            for p, (src, dst) in enumerate(zip(given(origin, mine), shared(origin, member)))
        ]

    def keep(origin, mine=False):
        return pltpu.make_async_copy(given(origin, mine)[0], wo_part(origin, member), keep_sem.at[origin])

    def share(origin, mine=False):
        return give(origin, mine, mate_s, mate_r, mate) + give(origin, mine, x_s, x_r, across)

    def from_across(origin):
        return [
            send(dst, dst, x_s.at[p, origin], x_r.at[p, origin], client, across)
            for p, dst in enumerate(shared(origin, across))
        ]

    def pass_on(origin):
        return [
            send(dst, dst, on_s.at[p, origin], on_r.at[p, origin], client, mate)
            for p, dst in enumerate(shared(origin, across))
        ]

    def start(copies):
        for copy in copies:
            copy.start()

    def arrived(copies):
        for copy in copies:
            copy.wait_recv()

    def sent(copies):
        for copy in copies:
            copy.wait_send()

    has_up, has_down = z < depth - 1, z > 0

    barrier = pltpu.get_barrier_semaphore()

    def hello(to_client, to_member):
        pl.semaphore_signal(
            barrier, inc=1, device_id={"client": to_client, "tensor": to_member}, device_id_type=MESH
        )

    wide_in[...] = jnp.zeros_like(wide_in)
    wide_out[...] = jnp.zeros_like(wide_out)
    table_ref[...] = jnp.zeros_like(table_ref)
    table_ref[:, 0 : table_in.shape[1]] = table_in[...]

    def in_slab(i):
        wide_in[i, :, 0 : in_ref.shape[2]] = in_ref[i].astype(F32)
        return tiles(wide_in[i])

    def out_slab(i):
        wide_out[i, 0 : out_ref.shape[1], 0:block] = out_ref[i].astype(F32)
        return tiles(jnp.transpose(wide_out[i])[:block])

    ordered = [in_slab(i) for i in (3, 4, 5, 6)] + [out_slab(i) for i in (1, 2, 3, 4)]
    ordered += [in_slab(i) for i in (0, 1, 2)] + [out_slab(0)]
    for i in range(0, 12, 2):
        packed = jnp.concatenate(pack_two(ordered[i], ordered[i + 1]), 1)
        main_ref[:, 192 * i : 192 * (i + 2)] = packed.astype(BF16)

    hello(peer, member)
    for shift in (1, 2, 3):
        hello(client, lax.rem(member + shift, 4))
    for shift in range(1, depth):
        hello(2 * lax.rem(z + shift, depth) + y, member)
    pl.semaphore_wait(barrier, 3 + depth)

    def line_start(part):
        @pl.when(has_up)
        def _():
            start(up(client, 0, part, True))

        @pl.when(has_down)
        def _():
            start(down(client, 0, part, True))

    start(over(client, crossing, True))
    start(over(client, first, True))
    line_start(first)
    start(over(client, over_second, True))
    line_start(second)
    start(share(client, True))
    keep(client, True).start()
    local = [
        pltpu.make_async_copy(src, dst, own_sem.at[p])
        for p, (src, dst) in enumerate(zip(own_pieces[:4], landed(client)))
    ]
    start(local)

    _, steps, each = index_ref.shape
    images = steps * each
    pool_size = pool_buf.shape[1] // 8
    patch_rows = pool_ref.shape[0] // pool_size
    pad = x_out.shape[1]

    def base(b):
        return lax.min(lax.max(8 * b - 1, 0), patch_rows - 8)

    deep = pool_buf.shape[0]

    def pool_load(b):
        k = lax.rem(b, deep)
        return pltpu.make_async_copy(
            pool_ref.at[span(base(b) * pool_size, 8 * pool_size, 32), :], pool_buf.at[k], pool_sem.at[k]
        )

    def x_store(b):
        k = lax.rem(b, deep)
        return pltpu.make_async_copy(x_buf.at[k], x_out.at[:, span(8 * b, 8, 8), :], x_sem.at[k])

    for b in range(deep - 1):
        pool_load(b).start()
    lane = lax.broadcasted_iota(jnp.int32, (8 * images, 8 * pool_size), 1)
    select_row = lax.broadcasted_iota(jnp.int32, (8 * images, 1), 0)
    line_row = lax.rem(select_row, 8)
    chosen = jnp.zeros((8 * images, 1), jnp.int32)
    for i in range(images):
        chosen = jnp.where(select_row // 8 == i, index_ref[0, i // each, i % each], chosen)

    def pick(b, carry):
        k = lax.rem(b, deep)
        pool_load(b).wait()

        @pl.when(b < pad // 8 - (deep - 1))
        def _():
            pool_load(b + deep - 1).start()

        wanted = (8 * b - 1 + line_row - base(b)) * pool_size + chosen
        picked = nn((lane == wanted).astype(BF16), pool_buf[k]).astype(BF16)

        @pl.when(b >= deep)
        def _():
            x_store(b - deep).wait()

        x_buf[k] = picked.reshape(images, 8, picked.shape[1])
        x_store(b).start()
        return carry

    lax.fori_loop(0, pad // 8, pick, 0)
    for b in range(pad // 8 - deep, pad // 8):
        x_store(b).wait()

    def line(d, act):
        @pl.when(z >= d)
        def _():
            act(client - 2 * d, True)

        @pl.when(z < depth - d)
        def _():
            act(client + 2 * d, False)

    def across_line(d, act):
        if d == 0:
            act(peer, True)
            return

        @pl.when(z >= d)
        def _():
            act(peer - 2 * d, True)

        @pl.when(z < depth - d)
        def _():
            act(peer + 2 * d, False)

    def line_in(d, part):
        def act(origin, below):
            line_s, line_r = (up_s, up_r) if below else (down_s, down_r)
            arrived(message(origin, False, line_s, line_r, d - 1, peer, part))
            if d < depth - 1:

                @pl.when(has_up if below else has_down)
                def _():
                    start(up(origin, d, part) if below else down(origin, d, part))

            if part is not third:
                start(over(origin, first if part is first else over_second))
            if part is first:
                start(share(origin))
                keep(origin).start()

        return act

    def y_in(origin, below):
        arrived(over(origin, first))
        start(share(origin))
        keep(origin).start()

    def forward(origin, below=True):
        arrived(from_across(origin))
        start(pass_on(origin))

    arrived(over(peer, crossing))
    line_start(third)
    for d in range(1, depth + 1):
        if d < depth:
            line(d, line_in(d, first))
        across_line(d - 1, y_in)
        if d < depth:
            line(d, line_in(d, second))
            line(d, line_in(d, third))
        if d == 1:
            forward(client)
        else:
            line(d - 1, forward)
            across_line(d - 2, forward)
    across_line(depth - 1, forward)
    for d in range(depth):
        across_line(d, lambda origin, below: arrived(over(origin, over_second)))

    for copy in local:
        copy.wait()
    for origin in range(clients):
        sent(share(origin))
        sent(pass_on(origin))
        keep(origin).wait()
        arrived([
            send(dst, dst, mate_s.at[p, origin], mate_r.at[p, origin], client, mate)
            for p, dst in enumerate(shared(origin, mate))
        ])
        arrived([
            send(dst, dst, on_s.at[p, origin], on_r.at[p, origin], client, mate)
            for p, dst in enumerate(shared(origin, lax.rem(mate + 2, 4)))
        ])
    sent(over(client, crossing))
    for d in range(depth):
        sent(over(2 * d + y, over_all))

        @pl.when(has_up & (z >= d))
        def _():
            if d < depth - 1:
                sent(up(client - 2 * d, d, slice(0, 5)))

        @pl.when(has_down & (z < depth - d))
        def _():
            if d < depth - 1:
                sent(down(client + 2 * d, d, slice(0, 5)))


def gather_weights(clients, index, in_bf, out_bf, table_t, pool, pad):
    depth = clients // 2
    dma = pltpu.SemaphoreType.DMA
    anywhere = pl.BlockSpec(memory_space=pl.ANY)
    inside = pl.BlockSpec(memory_space=pltpu.VMEM)
    slabs, own, group = in_bf.shape
    width = own * clients
    packed = (slabs + out_bf.shape[0]) * group
    table_lanes = width + REST
    hops = depth - 1
    pool_size, patch_rows, features = pool.shape
    images = index.shape[1] * index.shape[2]
    rows = jnp.transpose(pool, (1, 0, 2)).reshape(patch_rows * pool_size, features)
    return pl.pallas_call(
        functools.partial(gather_kernel, clients),
        out_shape=(
            jax.ShapeDtypeStruct((width, packed), BF16),
            jax.ShapeDtypeStruct((width, 4 * LANE), BF16),
            jax.ShapeDtypeStruct((width, table_lanes), BF16),
            jax.ShapeDtypeStruct((images, pad, features), BF16),
        ),
        in_specs=[pl.BlockSpec(memory_space=pltpu.SMEM)] + [inside] * 3 + [anywhere],
        out_specs=(anywhere,) * 4,
        scratch_shapes=[
            pltpu.VMEM((own, packed), BF16), pltpu.VMEM((own, table_lanes), BF16),
            pltpu.VMEM((slabs, own, LANE), F32), pltpu.VMEM((out_bf.shape[0], LANE, 128), F32),
            pltpu.VMEM((6, 8 * pool_size, features), BF16), pltpu.VMEM((6, images, 8, features), BF16),
            dma((6,)), dma((6,)),
            dma((5, hops)), dma((5, hops)), dma((5, hops)), dma((5, hops)), dma((4, depth)),
            dma((4, depth)),
        ] + [dma((2, clients))] * 6 + [dma((4,)), dma((clients,))],
        compiler_params=pltpu.CompilerParams(collective_id=1, has_side_effects=True),
        name="gather_weights",
    )(index, in_bf, out_bf, table_t, rows)


def reduce_kernel(
    clients, main_in, table_in, low_in, tile_in, main_out, table_out, low_out, tile_out,
    own_main, own_table, y_main, y_table, zs_main, zs_table, zr_main, zr_table, whole, low_all, tile_all,
    own_sem, y_s, y_r, z_s, z_r, low_s, low_r, tile_s, tile_r, q_s, q_r, keep_sem,
):
    depth, client, z, y, member, core, chip_x, mate, across = ring_places(clients)
    block = own_main.shape[1]
    half, columns = own_table.shape[1], own_table.shape[2]
    peer = client + 1 - 2 * y
    cut = own_main.shape[2] // 2
    lanes = (None, slice(0, cut), slice(cut, 2 * cut))
    parts = (0, 1, 2)

    def source(owner, p):
        if p == 0:
            return table_in.at[
                span(owner * block + chip_x * half, half, half), span(core * columns, columns, 128)
            ]
        return main_in.at[span(owner * block, block, block), lanes[p]]

    def slot(table_ref, main_ref, i, p):
        return table_ref.at[i] if p == 0 else main_ref.at[i, :, lanes[p]]

    def own_load(level, p):
        return pltpu.make_async_copy(
            source(2 * level + y, p), slot(own_table, own_main, level, p), own_sem.at[p, level]
        )

    def over(level, p):
        return send(
            source(2 * level + 1 - y, p), slot(y_table, y_main, level, p),
            y_s.at[p, level], y_r.at[p, level], peer, member,
        )

    def onward(i, p):
        owner = 2 * lax.rem(z + 1 + i, depth) + y
        return send(
            slot(zs_table, zs_main, i, p), slot(zr_table, zr_main, i, p),
            z_s.at[p, i], z_r.at[p, i], owner, member,
        )

    def small(shift):
        to = lax.rem(client + shift, clients)
        return [
            send(low_in.at[to], low_all.at[client], low_s.at[shift - 1], low_r.at[shift - 1], to, member),
            send(tile_in, tile_all.at[client], tile_s.at[shift - 1], tile_r.at[shift - 1], to, member),
        ]

    def small_from(shift):
        origin = lax.rem(client + clients - shift, clients)
        return [
            send(low_in.at[origin], low_all.at[origin], low_s.at[shift - 1], low_r.at[shift - 1], origin, member),
            send(tile_in, tile_all.at[origin], tile_s.at[shift - 1], tile_r.at[shift - 1], origin, member),
        ]

    def quarter(who):
        return whole.at[span((who // 2) * half, half, half), span(lax.rem(who, 2) * columns, columns, 128)]

    def pass_quarter(who, index, to):
        return send(quarter(who), quarter(who), q_s.at[index], q_r.at[index], client, to)

    barrier = pltpu.get_barrier_semaphore()
    for shift in range(1, clients):
        pl.semaphore_signal(
            barrier, inc=1,
            device_id={"client": lax.rem(client + shift, clients), "tensor": member}, device_id_type=MESH,
        )
    for shift in (1, 2, 3):
        pl.semaphore_signal(
            barrier, inc=1,
            device_id={"client": client, "tensor": lax.rem(member + shift, 4)}, device_id_type=MESH,
        )
    order = [(i, 0) for i in range(depth)] + [(i, p) for i in range(depth) for p in (1, 2)]
    for i, p in order:
        own_load(lax.rem(z + 1 + i, depth), p).start()
    own_small = [
        pltpu.make_async_copy(low_in.at[client], low_all.at[client], keep_sem.at[0]),
        pltpu.make_async_copy(tile_in, tile_all.at[client], keep_sem.at[1]),
    ]
    for copy in own_small:
        copy.start()
    pl.semaphore_wait(barrier, clients - 1 + 3)
    for i, p in order:
        over(lax.rem(z + 1 + i, depth), p).start()
    for shift in range(1, clients):
        for copy in small(shift):
            copy.start()

    def pair_up(i, p):
        level = lax.rem(z + 1 + i, depth)
        own_load(level, p).wait()
        over(level, p).wait_recv()
        pair = (
            slot(own_table, own_main, level, p)[...].astype(F32)
            + slot(y_table, y_main, level, p)[...].astype(F32)
        )
        if i < depth - 1:
            slot(zs_table, zs_main, i, p)[...] = pair.astype(BF16)
            onward(i, p).start()
        elif p == 0:
            quarter(member)[...] = pair
        else:
            main_out[:, lanes[p]] = pair

    for i in range(depth):
        pair_up(i, 0)
    pair_up(0, 1)
    pair_up(0, 2)
    mine = quarter(member)
    for i in range(depth - 1):
        onward(i, 0).wait_recv()
        mine[...] = mine[...] + zr_table[i].astype(F32)
    to_others = [pass_quarter(member, 0, mate), pass_quarter(member, 1, across)]
    for copy in to_others:
        copy.start()
    for i in range(1, depth):
        pair_up(i, 1)
        pair_up(i, 2)
        if i == 1:
            pass_quarter(across, 1, across).wait_recv()
            second = pass_quarter(across, 2, mate)
            second.start()
    for shift in range(1, clients):
        for copy in small_from(shift):
            copy.wait_recv()
    for copy in own_small:
        copy.wait()
    low_out[...] = low_all[...]
    tile_out[...] = tile_all[...]
    pass_quarter(mate, 0, mate).wait_recv()
    pass_quarter(lax.rem(mate + 2, 4), 2, mate).wait_recv()
    table_out[...] = whole[...]
    for i in range(depth - 1):
        for p in (1, 2):
            onward(i, p).wait_recv()
            main_out[:, lanes[p]] = main_out[:, lanes[p]] + zr_main[i, :, lanes[p]].astype(F32)
    for copy in to_others + [second]:
        copy.wait_send()
    for shift in range(1, clients):
        for copy in small(shift):
            copy.wait_send()
    for i in range(depth):
        for p in parts:
            over(i, p).wait_send()
            if i < depth - 1:
                onward(i, p).wait_send()


def reduce_deltas(clients, main, table, low, tile):
    depth = clients // 2
    dma = pltpu.SemaphoreType.DMA
    vmem = pltpu.VMEM
    anywhere = pl.BlockSpec(memory_space=pl.ANY)
    inside = pl.BlockSpec(memory_space=pltpu.VMEM)
    block = main.shape[0] // clients
    half, columns = block // 2, table.shape[1] // 2
    wide = main.shape[1]
    hops = depth - 1
    return pl.pallas_call(
        functools.partial(reduce_kernel, clients),
        out_shape=(
            jax.ShapeDtypeStruct((block, wide), F32),
            jax.ShapeDtypeStruct((block, table.shape[1]), F32),
            jax.ShapeDtypeStruct(low.shape, BF16),
            jax.ShapeDtypeStruct((clients,) + tile.shape, F32),
        ),
        in_specs=[anywhere] * 4,
        out_specs=(inside,) * 4,
        scratch_shapes=[
            vmem((depth, block, wide), BF16), vmem((depth, half, columns), BF16),
            vmem((depth, block, wide), BF16), vmem((depth, half, columns), BF16),
            vmem((hops, block, wide), BF16), vmem((hops, half, columns), BF16),
            vmem((hops, block, wide), BF16), vmem((hops, half, columns), BF16),
            vmem((block, table.shape[1]), F32), vmem(low.shape, BF16),
            vmem((clients,) + tile.shape, F32),
            dma((3, depth)), dma((3, depth)), dma((3, depth)), dma((3, hops)), dma((3, hops)),
            dma((clients - 1,)), dma((clients - 1,)), dma((clients - 1,)), dma((clients - 1,)),
            dma((3,)), dma((3,)), dma((2,)),
        ],
        compiler_params=pltpu.CompilerParams(
            collective_id=2, has_side_effects=True, vmem_limit_bytes=52 << 20
        ),
        name="reduce_deltas",
    )(main, table, low, tile)


def adam(master, first, second, grad):
    first2 = BETA_ONE * first + (1.0 - BETA_ONE) * grad
    second2 = BETA_TWO * second + (1.0 - BETA_TWO) * grad * grad
    moved = (
        first2 / (1.0 - BETA_ONE**ROUND) / (jnp.sqrt(second2 / (1.0 - BETA_TWO**ROUND)) + ADAM_EPS)
    )
    fresh = master - SERVER_RATE * (moved + WEIGHT_DECAY * master)
    return (fresh, first2, second2, fresh.astype(jnp.bfloat16))


def server_kernel(main_ref, table_ref, low_ref, tile_ref, norm_ref, *refs):
    masters, firsts, seconds = refs[0:4], refs[4:8], refs[8:12]
    loss_out, norms_out = refs[12:14]
    outs = [refs[14 + i : 30 : 4] for i in range(4)]
    own, group = masters[0].shape[1:]
    tile = jnp.sum(tile_ref[...], 0)
    row = main_ref.shape[1] // 256
    examples, weighted_loss, weighted_factor = (tile[row : row + 1, i : i + 1] for i in range(3))
    scale = weighted_factor / examples / examples
    loss_out[...] = weighted_loss / examples
    lane = lax.broadcasted_iota(jnp.int32, (1, 128), 1)
    norms = jnp.zeros((1, 128), F32)
    for i in range(norm_ref.shape[0]):
        norms = jnp.where(lane == i, norm_ref[i, 0:1, 0:1], norms)
    norms_out[...] = norms[:, 0 : norm_ref.shape[0]]

    def apply(which, at, delta):
        results = adam(
            masters[which][at], firsts[which][at], seconds[which][at], scale * delta
        )
        for ref, value in zip(outs[which], results):
            ref[at] = value

    def slab(pair):
        return jnp.concatenate(pair, 1)

    every = slice(None)
    packed = tiles(main_ref[...])
    slabs = []
    for i in range(0, len(packed), 3):
        slabs += [slab(pair) for pair in unpack_two(packed[i : i + 3])]
    for i, which in enumerate((3, 4, 5, 6, 0, 1, 2)):
        apply(0, (which, every, every), slabs[i][:, :group])
    wo_rows = jnp.concatenate([slabs[7], jnp.zeros((128 - own, LANE), F32)], 0)
    apply(1, (0, every, every), jnp.transpose(wo_rows)[:group, :own])
    width = low_ref.shape[2] - 128
    messages = low_ref[...].reshape(low_ref.shape[0] * low_ref.shape[1], low_ref.shape[2])
    moved = tn(messages[:, :width], messages[:, width:])
    for i in range(4):
        apply(1, (i + 1, every, every), moved[i * group : (i + 1) * group, :own])
    apply(2, (every, every), table_ref[:, 0 : masters[2].shape[1]])
    bias = [tile[i : i + 1, :] for i in range(row)]
    rows = []
    for i in range(0, row, 3):
        rows += [slab(pair) for pair in unpack_two(bias[i : i + 3])]
    for i in range(4):
        apply(3, (slice(i, i + 1), every), rows[i][:, :group])


def server_update(main, table, low, tile, norms, state):
    inside = pl.BlockSpec(memory_space=pltpu.VMEM)
    shapes = [value.shape for value in state[:4]]
    out_shape = [jax.ShapeDtypeStruct((1, 1), F32), jax.ShapeDtypeStruct((1, norms.shape[0]), F32)]
    for kind in (F32, F32, F32, BF16):
        out_shape += [jax.ShapeDtypeStruct(shape, kind) for shape in shapes]
    return pl.pallas_call(
        server_kernel,
        out_shape=tuple(out_shape),
        in_specs=[inside] * (5 + len(state)),
        out_specs=(inside,) * len(out_shape),
        compiler_params=pltpu.CompilerParams(vmem_limit_bytes=24 << 20),
        name="server_update",
    )(main, table, low, tile, norms, *state)


def on_device(
    pool, index, tau, counts, labels,
    in_bf, out_bf, table_bf, bias_bf,
    in_master, out_master, table_master, bias_master,
    in_first, out_first, table_first, bias_first,
    in_second, out_second, table_second, bias_second,
):
    clients = lax.axis_size("client")
    group = in_bf.shape[2]
    steps, images = index.shape[1], index.shape[2]
    patch_rows, features = pool.shape[1], pool.shape[2]
    seq = patch_rows + 1
    pad = (seq + 15) // 16 * 16
    own = in_bf.shape[1]
    rows_total = table_bf.shape[0]
    classes = rows_total - features - seq - 9
    table_t = table_bf.T
    direct = clients == 8
    if direct:
        main, wo_all, table, patches = gather_weights(
            clients, index, in_bf, out_bf, table_t, pool, pad
        )
    else:
        in_rows = jnp.transpose(in_bf, (1, 0, 2))
        out_rows = jnp.transpose(out_bf, (2, 0, 1))
        main_own = jnp.concatenate(
            [in_rows[:, 3:], out_rows[:, 1:], in_rows[:, :3], out_rows[:, :1]], 1
        ).reshape(own, 12 * group)
        table_own = jnp.pad(table_t, ((0, 0), (0, features + REST - rows_total)))
        main = lax.all_gather(main_own, "client", axis=0, tiled=True)
        table = lax.all_gather(table_own, "client", axis=0, tiled=True)
        wo_all = lax.all_gather(main[:, 12 * group - LANE :], "tensor", axis=1, tiled=True)
        patches = pick_patches(pool, index[0].reshape(steps * images), pad)
    bias = jnp.broadcast_to(bias_bf.astype(F32).reshape(1, 4 * group), (8, 4 * group))
    patches = patches.reshape(steps, images * pad, features)
    d_main, d_table, low, tile, norms = local_training(
        tau, counts, labels, index, patches, main, wo_all, table, bias, clients, pad, seq, classes
    )
    if direct:
        main_sum, table_sum, low_all, tile_all = reduce_deltas(clients, d_main, d_table, low, tile)
    else:
        tile_all = lax.psum(tile, "client")[None]
        main_sum = lax.psum_scatter(d_main, "client", scatter_dimension=0, tiled=True).astype(F32)
        first_member = lax.axis_index("tensor") == 0
        d_table = jnp.where(first_member, d_table, jnp.zeros_like(d_table))
        table_sum = lax.psum(
            lax.psum_scatter(d_table, "client", scatter_dimension=0, tiled=True).astype(F32), "tensor"
        )
        low_all = lax.all_to_all(low, "client", split_axis=0, concat_axis=0, tiled=True)
    state = (
        in_master, out_master, table_master.T, bias_master,
        in_first, out_first, table_first.T, bias_first,
        in_second, out_second, table_second.T, bias_second,
    )
    loss, norms, *fresh = server_update(main_sum, table_sum, low_all, tile_all, norms, state)
    fresh[2::4] = [value.T for value in fresh[2::4]]
    return (loss.reshape(()), norms, *fresh)


def solution(mesh):
    by_client = P("client", None, None)
    state = (P(None, "client", "tensor"), P(None, "tensor", "client"), P(None, "client"), P(None, "tensor"))
    in_specs = (by_client, by_client, P("client"), P("client"), P("client")) + state * 4
    out_specs = (P(), P("client", None)) + state * 4
    return jax.shard_map(
        on_device, mesh=mesh, in_specs=in_specs, out_specs=out_specs, check_vma=False
    )
```

```python
import functools

import jax
import jax.numpy as jnp
from jax import lax
from jax.experimental import pallas as pl
from jax.experimental.pallas import tpu as pltpu
from jax.sharding import PartitionSpec as P

HEAD_DIM = 64
ROUND = 5
EPS_NORM = 1e-06
MOMENTUM_RHO = 0.9
LOCAL_RATE = 0.05
CLIP_LIMIT = 1.0
BETA_ONE = 0.5
BETA_TWO = 0.7
ADAM_EPS = 1e-08
WEIGHT_DECAY = 0.05
SERVER_RATE = 0.05
SQRT_HALF = 0.7071067811865476
INV_ROOT_TAU = 0.3989422804014327
MESH = pl.DeviceIdType.MESH
F32 = jnp.float32
BF16 = jnp.bfloat16
NEG = -1e30
LANE = 256
SMALL = 16
REST = 512
VMEM_LIMIT = 67043328


def dot(left, right, dims):
    return lax.dot_general(left, right, (dims, ((), ())), preferred_element_type=F32)


def nn(left, right):
    return dot(left, right, ((1,), (0,)))


def nt(left, right):
    return dot(left, right, ((1,), (1,)))


def tn(left, right):
    return dot(left, right, ((0,), (0,)))


def fold(value):
    rows, width = value.shape
    return jnp.sum(value.reshape(rows // 8, 8, width), 0)


def total(value):
    return jnp.sum(jnp.sum(value, 1, keepdims=True), 0, keepdims=True)


def normalise(value):
    centre = value - jnp.mean(value, -1, keepdims=True)
    inverse = lax.rsqrt(jnp.mean(centre * centre, -1, keepdims=True) + EPS_NORM)
    return (centre * inverse, inverse)


def norm_grad(grad, gain, normed, inverse):
    scaled = grad * gain
    return inverse * (
        scaled
        - jnp.mean(scaled, -1, keepdims=True)
        - normed * jnp.mean(scaled * normed, -1, keepdims=True)
    )


def split_two(value):
    high = value.astype(BF16)
    return (high, (value - high.astype(F32)).astype(BF16))


def swap(tile):
    return pltpu.roll(tile, HEAD_DIM, 1)


def tiles(value):
    return [value[:, i : i + 128] for i in range(0, value.shape[1], 128)]


def low_half(shape):
    return lax.broadcasted_iota(jnp.int32, shape, 1) < HEAD_DIM


def pack_two(left, right):
    low = low_half(left[0].shape)
    return [
        left[0],
        jnp.where(low, left[1], swap(right[0])),
        jnp.where(low, swap(right[0]), swap(right[1])),
    ]


def unpack_two(packed):
    low = low_half(packed[0].shape)
    nothing = jnp.zeros_like(packed[0])
    middle, last = swap(packed[1]), swap(packed[2])
    return (
        [packed[0], jnp.where(low, packed[1], nothing)],
        [jnp.where(low, middle, last), jnp.where(low, last, nothing)],
    )


def train_kernel(
    sizes,
    tau_ref,
    count_ref,
    label_ref,
    index_ref,
    x_hbm,
    main_in,
    wo_in,
    table_in,
    bias_in,
    main_out,
    table_out,
    low_out,
    tile_out,
    norm_out,
    wqkv, w1, wot, w2t, wet, head,
    wqkv_f, w1_f, wot_f, wet_f, pos_f, head_f, vec_f, bias_f,
    wqkv_m, w1_m, wot_m, wet_m, pos_m, head_m, vec_m, bias_m,
    wqkv_g, wot_g, wet_g, pos_g, head_g, vec_g,
    xbuf, h0, slope, prob, abuf, qkv, oall, third, ubuf, dpre, h1own, datt, chip, inverses,
    hsum, asum, dact, bsum, vacc, ssq,
    low_d, low_a, low_b, low_w, scal, loss_all, factor_kept, bias_wide, bias_start,
    s1, r1, s2, r2, mx_s, mx_r, nx_s, nx_r, pos_r, vec_r,
    wsem, xsem, o_ps, o_xs, o_fs, o_pr, o_xr, o_fr,
    a1s, a1r, a2s, a2r, das, dar, pvs, pvr, mxs, mxr, nxs, nxr, osem,
):
    steps, seq, pad, classes, clients = sizes
    width = 768
    kept = (seq + 7) // 8 * 8
    me = lax.axis_index("tensor")
    core = lax.rem(me, 2)
    mate = me + 1 - 2 * core
    across = lax.rem(me + 2, 4)
    own0 = 2 * core
    oth0 = 2 - 2 * core

    def rows(n):
        return pl.ds(pl.multiple_of(n * pad, 16), pad)

    def sent_rows(n):
        return pl.ds(pl.multiple_of(n * pad, 16), kept)

    def remote(src, dst, send, recv, device):
        return pltpu.make_async_remote_copy(
            src_ref=src, dst_ref=dst, send_sem=send, recv_sem=recv,
            device_id={"tensor": device}, device_id_type=MESH,
        )

    rest = dpre.at[0:width, 0:REST]
    square_rows = pl.ds(0, width)
    raw = abuf.at[square_rows, :]
    wo_raw = [ubuf.at[square_rows, pl.ds(g * LANE, LANE)] for g in range(3)] + [
        qkv.at[square_rows, pl.ds(0, LANE)]
    ]
    weights_in = [
        main_in.at[:, 2 * width : 3 * width],
        main_in.at[:, 0:width],
        main_in.at[:, width : 2 * width],
        table_in.at[:, 0:width],
        table_in.at[:, width : width + REST],
    ] + [wo_in.at[:, g * LANE : (g + 1) * LANE] for g in range(4)]
    weights = [raw, w1, w2t, wet, rest] + wo_raw

    def load(which):
        return pltpu.make_async_copy(weights_in[which], weights[which], wsem.at[which])

    def fetch(step, slot):
        return pltpu.make_async_copy(x_hbm.at[step], xbuf.at[slot], xsem.at[slot])

    barrier = pltpu.get_barrier_semaphore()
    fetch(0, 0).start()
    for which in range(9):
        load(which).start()
    for zero in (r1, r2, oall, third, datt):
        zero[...] = jnp.zeros_like(zero)
    for shift in (1, 2, 3):
        pl.semaphore_signal(
            barrier, inc=1, device_id={"tensor": lax.rem(me + shift, 4)}, device_id_type=MESH
        )
    bias_wide[...] = jnp.zeros_like(bias_wide)
    bias_wide[0 : bias_in.shape[0], 0 : bias_in.shape[1]] = bias_in[...].astype(F32)
    slabs = [tiles(bias_wide[r : r + 1, :]) for r in range(4)]
    first_bias = jnp.concatenate(pack_two(slabs[0], slabs[1]) + pack_two(slabs[2], slabs[3]), 1)
    bias_start[...] = jnp.broadcast_to(first_bias, (8, width))
    bias_f[...] = bias_start[...]
    for zero in (pos_m, head_m, vec_m, bias_m, low_a, low_b, low_w, loss_all):
        zero[...] = jnp.zeros_like(zero)
    low_d[...] = jnp.zeros_like(low_d)
    for which in (0, 3, 4, 5, 6, 7, 8):
        load(which).wait()
    n_head = head.shape[0]
    vec_at, head_at = seq, seq + 9
    h0[0:REST, :] = jnp.transpose(rest[...].astype(F32))
    pos_rows = lax.broadcasted_iota(jnp.int32, (pad, 1), 0) < seq
    vec_rows = lax.broadcasted_iota(jnp.int32, (SMALL, 1), 0) < 9
    pos_f[...] = jnp.where(pos_rows, h0[0:pad, :], 0.0)
    vec_f[...] = jnp.where(vec_rows, h0[vec_at : vec_at + SMALL, :], 0.0)
    start_head = h0[head_at : head_at + n_head, :]
    head_f[...] = start_head
    head[...] = start_head.astype(BF16)
    taken = tau_ref[0]

    def join(parts):
        return jnp.concatenate(parts, 1)

    def start_rows(j, carry):
        at = pl.ds(pl.multiple_of(j * 64, 64), 64)
        packed = tiles(raw[at, :].astype(F32))
        q, k = unpack_two(packed[:3])
        v, _ = unpack_two(packed[3:])
        wqkv[at, :] = join(q + k + v).astype(BF16)
        pieces = [tiles(piece[at, :].astype(F32)) for piece in wo_raw]
        low = low_half((64, 128))
        first = [jnp.where(low, swap(p[0]), swap(p[1])) for p in pieces]
        last = [
            jnp.where(low, swap(pieces[g][1]), pieces[g + 1][1]) for g in (0, 2)
        ]
        wot[at, :] = join(first + last).astype(BF16)
        return carry

    lax.fori_loop(0, width // 64, start_rows, 0)
    pl.semaphore_wait(barrier, 3)

    row_id = lax.broadcasted_iota(jnp.int32, (pad, 1), 0)
    token = row_id < seq
    key_ok = lax.broadcasted_iota(jnp.int32, (1, pad), 1) < seq
    lane_head = lax.broadcasted_iota(jnp.int32, (1, LANE), 1) // HEAD_DIM
    small_ok = lax.broadcasted_iota(jnp.int32, (SMALL, 1), 0) < 4
    scale = HEAD_DIM ** (-0.5)

    def of_head(value, h):
        return jnp.where(lane_head == h, value, jnp.zeros_like(value))

    def o_part(message, group):
        lanes = pl.ds(pl.multiple_of(group * 128, 128), 128)
        pair, which = message // 3, message % 3
        if which == 2:
            return third.at[pair, 0:kept, lanes]
        return oall.at[pl.ds((2 * pair + which) * pad, kept), lanes]

    def o_to_mate(message):
        place = o_part(message, me)
        return remote(place, place, o_ps.at[message], o_pr.at[message], mate)

    def o_across(message):
        place = o_part(message, me)
        return remote(place, place, o_xs.at[message], o_xr.at[message], across)

    def o_forward(message):
        place = o_part(message, across)
        return remote(place, place, o_fs.at[message], o_fr.at[message], mate)

    def relay_o(message):
        place = o_part(message, across)
        remote(place, place, o_xs.at[message], o_xr.at[message], across).wait_recv()
        o_forward(message).start()

    def o_here(message):
        direct = o_part(message, mate)
        remote(direct, direct, o_ps.at[message], o_pr.at[message], mate).wait_recv()
        passed = o_part(message, lax.rem(mate + 2, 4))
        remote(passed, passed, o_fs.at[message], o_fr.at[message], mate).wait_recv()

    def to_mate(n):
        return remote(s1.at[n, 0:kept], r1.at[n, 0:kept], a1s.at[n], a1r.at[n], mate)

    def to_across(which, n):
        return remote(s2.at[n, 0:kept], r2.at[2 * which + n, 0:kept], a2s.at[2 * which + n], a2r.at[2 * which + n], across)

    def gradient_to_mate(buffer, which, image, k):
        return remote(
            buffer.at[sent_rows(image)], buffer.at[sent_rows(image)],
            das.at[2 * which + k], dar.at[2 * which + k], mate,
        )

    def pos_to_mate():
        return remote(pos_g, pos_r, pvs.at[0], pvr.at[0], mate)

    def vec_to_mate():
        return remote(vacc, vec_r, pvs.at[1], pvr.at[1], mate)

    def spread(src, dst, send, recv, shift):
        return remote(
            src, dst.at[me], send.at[shift - 1], recv.at[shift - 1], lax.rem(me + shift, 4)
        )

    def update_rows(entries, rho, live, fac):
        def update(j, carry):
            at = pl.ds(pl.multiple_of(j * 64, 64), 64)
            for low, full, mom, grad in entries:
                m = rho * mom[at, :] + fac * grad[at, :]
                mom[at, :] = m
                w = full[at, :] - (live * LOCAL_RATE) * m
                full[at, :] = w
                low[at, :] = w.astype(BF16)
            return carry

        lax.fori_loop(0, width // 64, update, 0)

    def one_step(step, carry):
        slot = lax.rem(step, 2)
        fetch(step, slot).wait()

        @pl.when(step < steps - 1)
        def _():
            fetch(step + 1, 1 - slot).start()

        gain1, shift1 = vec_f[0:1, :], vec_f[1:2, :]
        gain2, shift2 = vec_f[2:3, :], vec_f[3:4, :]
        gain3, shift3 = vec_f[4:5, :], vec_f[5:6, :]

        def attend(pair):
            two = slice(2 * pair * pad, 2 * (pair + 1) * pad)
            inside = (row_id >= 1) & token
            added = pos_f[...] + jnp.where(inside, vec_f[6:7, :], 0.0)
            state = nt(xbuf[slot, two, :], wet[...]) + jnp.concatenate([added, added], 0)
            h0[two, :] = state
            normed, _ = normalise(state)
            a = (normed * gain1 + shift1).astype(BF16)
            abuf[two, :] = a
            both = nn(a, wqkv[...]).astype(BF16)
            qkv[two, :] = both
            mine = pl.ds(pl.multiple_of(me * 128, 128), 128)
            thirds = []
            for i in range(2):
                projected = both[i * pad : (i + 1) * pad]
                q, k, v = projected[:, :LANE], projected[:, LANE : 2 * LANE], projected[:, 2 * LANE :]
                out = jnp.zeros((pad, LANE), F32)
                for h in range(3):
                    scores = jnp.where(key_ok, nt(of_head(q, h), k) * scale, NEG)
                    expd = jnp.exp(scores - jnp.max(scores, -1, keepdims=True))
                    p = (expd / jnp.sum(expd, -1, keepdims=True)).astype(BF16)
                    prob[(2 * pair + i) * 3 + h] = p
                    out = out + nn(p, of_head(v, h))
                oall[(2 * pair + i) * pad : (2 * pair + i + 1) * pad, mine] = out[:, :128].astype(BF16)
                thirds.append(out[:, 128:])
                o_to_mate(3 * pair + i).start()
                o_across(3 * pair + i).start()
            third[pair, :, mine] = (thirds[0] + swap(thirds[1])).astype(BF16)
            o_to_mate(3 * pair + 2).start()
            o_across(3 * pair + 2).start()

        attend(0)
        attend(1)

        @pl.when(step == 0)
        def _():
            load(1).wait()
            load(2).wait()

            def begin(j, carry):
                at = pl.ds(pl.multiple_of(j * 32, 32), 32)
                for low_ref, full, mom in (
                    (wqkv, wqkv_f, wqkv_m), (w1, w1_f, w1_m), (wot, wot_f, wot_m), (wet, wet_f, wet_m)
                ):
                    full[at, :] = low_ref[at, :].astype(F32)
                    mom[at, :] = jnp.zeros((32, width), F32)
                return carry

            lax.fori_loop(0, width // 32, begin, 0)

        @pl.when(step > 0)
        def _():
            was_live = jnp.where(step - 1 < taken, 1.0, 0.0)
            was_rho = jnp.where(step - 1 < taken, MOMENTUM_RHO, 1.0)
            was_fac = factor_kept[0:1, 0:1]
            update_rows(((w1, w1_f, w1_m, slope), (wot, wot_f, wot_m, wot_g)), was_rho, was_live, was_fac)
            head_m[...] = was_rho * head_m[...] + was_fac * head_g[...]
            head_f[...] = head_f[...] - (was_live * LOCAL_RATE) * head_m[...]
            head[...] = head_f[...].astype(BF16)
            moved_rows = (LOCAL_RATE * low_w[:, 0:1]) * low_a[...]
            low_hi, low_lo = split_two(moved_rows)
            pair_rows = jnp.concatenate([low_hi, low_lo], 0)
            load(2).wait()

            def low_rank(j, carry):
                at = pl.ds(pl.multiple_of(j * LANE, LANE), LANE)
                moved = tn(jnp.concatenate([low_d[:, at], low_d[:, at]], 0), pair_rows)
                w2t[at, :] = (w2t[at, :].astype(F32) - moved).astype(BF16)
                return carry

            lax.fori_loop(0, width // LANE, low_rank, 0)

        for message in range(3):
            relay_o(message)

        def feed(pair):
            for message in range(3):
                o_here(3 * pair + message)
            two = slice(2 * pair * pad, 2 * (pair + 1) * pad)
            side = tiles(third[pair].astype(F32))
            low = low_half((pad, 128))
            for i in range(2):
                for g in (0, 2):
                    if i == 0:
                        tile = jnp.where(low, side[g], swap(side[g + 1]))
                    else:
                        tile = jnp.where(low, swap(side[g]), side[g + 1])
                    at = 4 * 128 + g * HEAD_DIM
                    oall[(2 * pair + i) * pad : (2 * pair + i + 1) * pad, at : at + 128] = tile.astype(BF16)
            state = h0[two, :] + nt(oall[two, :], wot[...]) + vec_f[7:8, :]
            differs = (pair + core) - 2 * pair * core
            for i in range(2):
                part = state[i * pad : (i + 1) * pad]
                h1own[i * (1 - differs) + 2 * differs] = part
                hsum[2 * pair + i] = fold(jnp.where(token, part, 0.0))
            normed, _ = normalise(state)
            u = (normed * gain2 + shift2).astype(BF16)
            ubuf[two, :] = u
            if pair == 0:
                relay_o(3)
                relay_o(4)
            z = nn(u, w1[...]) + bias_f[0:1, :]
            cdf = 0.5 * (1.0 + lax.erf(z * SQRT_HALF))
            act = (z * cdf).astype(BF16).astype(F32)
            tail = cdf + z * jnp.exp(-0.5 * z * z) * INV_ROOT_TAU
            for i in range(2):
                part = slice(i * pad, (i + 1) * pad)
                asum[2 * pair + i] = fold(jnp.where(token, act[part], 0.0))
                slope[(2 * pair + i) * pad : (2 * pair + i + 1) * pad, :] = jnp.where(token, tail[part], 0.0)
            if pair == 0:
                relay_o(5)

        feed(0)
        feed(1)

        def stack(ref):
            parts = [jnp.sum(ref[n], 0, keepdims=True) for n in range(4)]
            return jnp.concatenate(parts + [jnp.zeros((SMALL - 4, width), F32)], 0)

        act_sum = stack(asum)
        act_hi, act_lo = split_two(act_sum)
        both = nt(jnp.concatenate([act_hi, act_lo], 0), w2t[...])
        mx_s[...] = both[:8] + both[SMALL : SMALL + 8]
        for shift in (1, 2, 3):
            spread(mx_s, mx_r, mxs, mxr, shift).start()
        mx_r[me] = mx_s[...]
        h_mean = stack(hsum) * (1.0 / seq)
        for shift in (1, 2, 3):
            remote(
                mx_s, mx_r.at[lax.rem(me + 4 - shift, 4)], mxs.at[shift - 1], mxr.at[shift - 1], mate
            ).wait_recv()
        mlp = jnp.concatenate(
            [mx_r[0] + mx_r[1] + mx_r[2] + mx_r[3], jnp.zeros((SMALL - 8, width), F32)], 0
        )
        average = h_mean + mlp * (1.0 / seq) + vec_f[8:9, :]
        normed3, inverse3 = normalise(average)
        pooled = (normed3 * gain3 + shift3).astype(BF16)
        logits = nt(pooled, head[...])
        class_ok = lax.broadcasted_iota(jnp.int32, (1, head.shape[0]), 1) < classes
        logits = jnp.where(class_ok, logits, NEG)
        top = jnp.max(logits, -1, keepdims=True)
        exp_l = jnp.exp(logits - top)
        total_l = jnp.sum(exp_l, -1, keepdims=True)
        hot_row = lax.broadcasted_iota(jnp.int32, (SMALL, n_head), 0)
        hot_lane = lax.broadcasted_iota(jnp.int32, (SMALL, n_head), 1)
        hot = jnp.zeros((SMALL, n_head), F32)
        for n in range(4):
            label = label_ref[index_ref[0, step, n]]
            hot = jnp.where((hot_row == n) & (hot_lane == label), 1.0, hot)
        each = top + jnp.log(total_l) - jnp.sum(jnp.where(class_ok, logits, 0.0) * hot, -1, keepdims=True)
        loss = jnp.sum(jnp.where(small_ok, each, 0.0), 0, keepdims=True) * 0.25
        live = jnp.where(step < taken, 1.0, 0.0)
        rho = jnp.where(step < taken, MOMENTUM_RHO, 1.0)
        loss_tile = live * loss
        d_logits = jnp.where(small_ok, (exp_l / total_l - hot) * 0.25, 0.0).astype(BF16)
        d_head = tn(d_logits, pooled)
        head_g[...] = d_head
        d_pooled = nn(d_logits, head[...])
        d_average = norm_grad(d_pooled, gain3, normed3, inverse3)
        d_token = d_average * (1.0 / seq)
        d_mlp = d_token.astype(BF16)
        dact[...] = nn(d_mlp, w2t[...])
        for r in range(4):
            scal[r] = jnp.broadcast_to(d_token[r : r + 1, :], (8, width))
        vec_g[...] = jnp.zeros_like(vec_g)
        vec_g[4:5, :] = jnp.sum(d_pooled * normed3, 0, keepdims=True)
        vec_g[5:6, :] = jnp.sum(d_pooled, 0, keepdims=True)
        vec_g[8:9, :] = jnp.sum(d_average, 0, keepdims=True)
        low_at = pl.ds(pl.multiple_of(step * SMALL, SMALL), SMALL)
        low_d[low_at, :] = d_mlp
        low_a[low_at, :] = act_sum
        gram_d = nt(d_mlp, d_mlp)
        gram_a = nt(act_hi, act_hi) + nt(act_hi, act_lo) + nt(act_lo, act_hi)
        own_squares = total(gram_d * gram_a)

        for n in range(4):
            scal[4 + n] = jnp.broadcast_to(dact[n : n + 1, :], (8, width))
        bsum[...] = jnp.zeros_like(bsum)
        vacc[...] = jnp.zeros_like(vacc)

        def upper_partial(n):
            at = pl.ds(pl.multiple_of(n * pad, 16), 2 * pad)
            rate = jnp.concatenate(
                [jnp.broadcast_to(scal[4 + n + i][0:1, :], (pad, width)) for i in range(2)], 0
            )
            g = (rate * slope[at, :]).astype(BF16)
            dpre[at, :] = g
            bsum[...] = bsum[...] + fold(g.astype(F32))
            return nt(g, w1[...])

        other = upper_partial(oth0)
        for k in (0, 1):
            s1[k] = other[k * pad : (k + 1) * pad].astype(BF16)
            to_mate(k).start()
        own = upper_partial(own0)
        for k in (0, 1):
            to_mate(k).wait_recv()
            part = own[k * pad : (k + 1) * pad] + r1[k].astype(F32)
            chip[k] = part
            s2[k] = part.astype(BF16)
            to_across(0, k).start()

        ssq[...] = jnp.zeros_like(ssq)
        w1_g = slope

        def weight_grad(left, right, out, which):
            def tile(j, carry):
                at = pl.ds(pl.multiple_of(j * LANE, LANE), LANE)
                g = tn(left[:, at], right[...])
                out[at, :] = g
                ssq[which] = ssq[which] + fold(g * g)
                return carry

            lax.fori_loop(0, width // LANE, tile, 0)

        def embedding_grad(k, left):
            def tile(j, carry):
                at = pl.ds(pl.multiple_of(j * LANE, LANE), LANE)
                g = tn(left[rows(own0 + k), at], xbuf[slot, rows(own0 + k), :])
                g = g + tn(left[rows(oth0 + k), at], xbuf[slot, rows(oth0 + k), :])
                if k == 1:
                    g = g + wet_g[at, :]
                    ssq[3] = ssq[3] + fold(g * g)
                wet_g[at, :] = g
                return carry

            lax.fori_loop(0, width // LANE, tile, 0)

        weight_grad(ubuf, dpre, w1_g, 0)

        for k in (0, 1):
            normed, inverse = normalise(h1own[k])
            h1own[k] = normed
            inverses[k] = inverse
            normed, inverse = normalise(h0[rows(own0 + k), :])
            h0[rows(own0 + k), :] = normed
            inverses[2 + k] = inverse

        def attention_partial(n):
            own_columns = jnp.concatenate(
                [
                    wot[:, pl.ds(pl.multiple_of(me * 128, 128), 128)],
                    wot[:, pl.ds(pl.multiple_of(4 * 128 + (me // 2) * 128, 128), 128)],
                ],
                1,
            )
            wide = nn(datt[rows(n), :], own_columns)
            thirds = jnp.where(core == 1, swap(wide[:, 128:]), wide[:, 128:])
            thirds = jnp.where(low_half((pad, 128)), thirds, 0.0)
            d_ctx = jnp.concatenate([wide[:, :128], thirds], 1).astype(BF16)
            projected = qkv[rows(n), :]
            q, k, v = projected[:, :LANE], projected[:, LANE : 2 * LANE], projected[:, 2 * LANE :]
            d_q = jnp.zeros((pad, LANE), F32)
            d_k = jnp.zeros((pad, LANE), F32)
            d_v = jnp.zeros((pad, LANE), F32)
            for h in range(3):
                part = of_head(d_ctx, h)
                p = prob[n * 3 + h]
                again = p.astype(F32)
                d_p = nt(part, v)
                inner = d_p - jnp.sum(d_p * again, -1, keepdims=True)
                d_s = (again * inner).astype(BF16)
                d_v = d_v + tn(p, part)
                d_q = d_q + nn(d_s, of_head(k, h))
                d_k = d_k + tn(d_s, of_head(q, h))
            d_all = jnp.concatenate([d_q * scale, d_k * scale, d_v], 1).astype(BF16)
            qkv[rows(n), :] = d_all
            return nt(d_all, wqkv[...])

        for k in (0, 1):
            to_across(0, k).wait_recv()
            d_upper = chip[k] + r2[k].astype(F32)
            normed = h1own[k]
            d_state = norm_grad(d_upper, gain2, normed, inverses[k]) + scal[own0 + k][0:1, :]
            d_state = jnp.where(token, d_state, 0.0)
            h1own[k] = d_state
            datt[rows(own0 + k), :] = d_state.astype(BF16)
            gradient_to_mate(datt, 0, own0 + k, k).start()
            vacc[0] = vacc[0] + fold(d_upper * normed)
            vacc[1] = vacc[1] + fold(d_upper)
            vacc[2] = vacc[2] + fold(d_state)
            own = attention_partial(own0 + k)
            remote(
                datt.at[sent_rows(oth0 + k)], datt.at[sent_rows(oth0 + k)], das.at[k], dar.at[k], mate
            ).wait_recv()
            other = attention_partial(oth0 + k)
            to_mate(k).wait_send()
            s1[k] = other.astype(BF16)
            to_mate(k).start()
            to_mate(k).wait_recv()
            own = own + r1[k].astype(F32)
            chip[k] = own
            to_across(0, k).wait_send()
            s2[k] = own.astype(BF16)
            to_across(1, k).start()

        weight_grad(datt, oall, wot_g, 1)
        weight_grad(abuf, qkv, wqkv_g, 2)

        d_emb = ubuf
        for k in (0, 1):
            to_across(1, k).wait_recv()
            d_normed = chip[k] + r2[2 + k].astype(F32)
            normed = h0[rows(own0 + k), :]
            d_state = h1own[k] + norm_grad(d_normed, gain1, normed, inverses[2 + k])
            d_emb[rows(own0 + k), :] = d_state.astype(BF16)
            gradient_to_mate(d_emb, 1, own0 + k, k).start()
            vacc[3] = vacc[3] + fold(d_normed * normed)
            vacc[4] = vacc[4] + fold(d_normed)
            vacc[5] = vacc[5] + fold(jnp.where(row_id >= 1, d_state, 0.0))
            if k == 0:
                pos_g[...] = d_state
            else:
                pos_g[...] = pos_g[...] + d_state
                pos_to_mate().start()
                vec_to_mate().start()
            remote(
                d_emb.at[sent_rows(oth0 + k)], d_emb.at[sent_rows(oth0 + k)],
                das.at[2 + k], dar.at[2 + k], mate,
            ).wait_recv()
            embedding_grad(k, d_emb)
        pos_to_mate().wait()
        vec_to_mate().wait()
        pos_g[...] = pos_g[...] + pos_r[...]
        sums = [jnp.sum(vacc[r] + vec_r[r], 0, keepdims=True) for r in range(6)]
        vec_g[0:1, :] = sums[3]
        vec_g[1:2, :] = sums[4]
        vec_g[2:3, :] = sums[0]
        vec_g[3:4, :] = sums[1]
        vec_g[6:7, :] = sums[5]
        vec_g[7:8, :] = sums[2]
        d_bias = jnp.sum(bsum[...], 0, keepdims=True)
        shared = (
            total(ssq[1] + ssq[3] + fold(pos_g[...] * pos_g[...]) + fold(head_g[...] * head_g[...]))
            + total(vec_g[...] * vec_g[...])
        )
        own_squares = own_squares + total(ssq[0] + ssq[2]) + total(d_bias * d_bias)
        for message in range(6):
            o_to_mate(message).wait_send()
            o_across(message).wait_send()
            o_forward(message).wait_send()
        for k in (0, 1):
            to_mate(k).wait_send()
            to_across(1, k).wait_send()
            gradient_to_mate(datt, 0, own0 + k, k).wait_send()
            gradient_to_mate(d_emb, 1, own0 + k, k).wait_send()
        for shift in (1, 2, 3):
            spread(mx_s, mx_r, mxs, mxr, shift).wait_send()
        first_lane = lax.broadcasted_iota(jnp.int32, (8, 128), 1) < 64
        nx_s[...] = jnp.where(first_lane, own_squares + 0.25 * shared, loss_tile)
        for shift in (1, 2, 3):
            spread(nx_s, nx_r, nxs, nxr, shift).start()
        nx_r[me] = nx_s[...]

        @pl.when(step == steps - 1)
        def _():
            for which in (0, 1, 3, 4):
                load(which).start()

        for shift in (1, 2, 3):
            remote(
                nx_s, nx_r.at[lax.rem(me + 4 - shift, 4)], nxs.at[shift - 1], nxr.at[shift - 1], mate
            ).wait_recv()
        norm = jnp.sqrt((nx_r[0] + nx_r[1] + nx_r[2] + nx_r[3]))
        factor = live * (CLIP_LIMIT / jnp.maximum(norm, CLIP_LIMIT))
        norm_out[step] = live * norm
        loss_all[...] = loss_all[...] + nx_r[0]
        for shift in (1, 2, 3):
            spread(nx_s, nx_r, nxs, nxr, shift).wait_send()
        fac = factor[0:1, 0:1]

        low_row = lax.broadcasted_iota(jnp.int32, low_b.shape, 0) // SMALL
        low_b[...] = jnp.where(low_row == step, fac, rho * low_b[...])
        low_w[...] = low_w[...] + live * low_b[...]
        factors = (LOCAL_RATE * low_w[:, 0:1]) * low_a[...]
        factor_kept[...] = factor

        def small_update(full, mom, grad):
            mom[...] = rho * mom[...] + fac * grad
            full[...] = full[...] - (live * LOCAL_RATE) * mom[...]

        small_update(pos_f, pos_m, pos_g[...])
        small_update(vec_f, vec_m, vec_g[...])
        small_update(bias_f, bias_m, jnp.broadcast_to(d_bias, (8, width)))
        table = (
            (wqkv, wqkv_f, wqkv_m, wqkv_g),
            (w1, w1_f, w1_m, w1_g),
            (wot, wot_f, wot_m, wot_g),
            (wet, wet_f, wet_m, wet_g),
        )

        @pl.when(step < steps - 1)
        def _():
            load(2).start()
            update_rows((table[0], table[3]), rho, live, fac)

        @pl.when(step == steps - 1)
        def _():
            examples = jnp.full((1, 1), count_ref[0].astype(F32))
            factor_sum = jnp.zeros((), F32)
            for k in range(steps):
                worth = (1.0 - MOMENTUM_RHO ** (k + 1)) / (1.0 - MOMENTUM_RHO)
                factor_sum = factor_sum + jnp.where(k < taken, worth, 0.0)
            factor_sum = jnp.full((1, 1), factor_sum)
            share = examples / factor_sum
            for which in (0, 1, 3, 4):
                load(which).wait()

            def ended(at, full, mom, grad, lanes):
                m = rho * mom[at, lanes] + fac * grad[at, lanes]
                return full[at, lanes] - (live * LOCAL_RATE) * m

            outs = (
                (w1, main_out.at[:, 0:width]),
                (wet, table_out.at[:, 0:width]),
                (raw, main_out.at[:, width : 2 * width]),
                (rest, table_out.at[:, width : width + REST]),
            )
            copies = [
                pltpu.make_async_copy(src, dst, osem.at[i]) for i, (src, dst) in enumerate(outs)
            ]
            for i, (low, full, mom, grad) in enumerate((table[1], table[3])):

                def finish_square(j, carry):
                    at = pl.ds(pl.multiple_of(j * 64, 64), 64)
                    w = ended(at, full, mom, grad, slice(None))
                    low[at, :] = (share * (low[at, :].astype(F32) - w)).astype(BF16)
                    return carry

                lax.fori_loop(0, width // 64, finish_square, 0)
                copies[i].start()

            def finish(j, carry):
                at = pl.ds(pl.multiple_of(j * 64, 64), 64)
                three = tiles(ended(at, wqkv_f, wqkv_m, wqkv_g, slice(None)))
                _, full, mom, grad = table[2]
                wo_first = ended(at, full, mom, grad, pl.ds(pl.multiple_of(me * 128, 128), 128))
                wo_last = ended(
                    at, full, mom, grad, pl.ds(pl.multiple_of(4 * 128 + (me // 2) * 128, 128), 128)
                )
                wo_last = jnp.where(core == 1, swap(wo_last), wo_last)
                packed = join(
                    pack_two(three[0:2], three[2:4]) + pack_two(three[4:6], [wo_first, wo_last])
                )
                raw[at, :] = (share * (raw[at, :].astype(F32) - packed)).astype(BF16)
                return carry

            lax.fori_loop(0, width // 64, finish, 0)
            copies[2].start()
            small_update(head_f, head_m, head_g[...])
            h0[0:REST, :] = jnp.transpose(rest[...].astype(F32))
            for ref, begin, count in ((pos_f, 0, seq), (vec_f, vec_at, 9), (head_f, head_at, classes)):
                h0[begin : begin + count, :] = share * (h0[begin : begin + count, :] - ref[0:count, :])
            rest[...] = jnp.transpose(h0[0:REST, :]).astype(BF16)
            copies[3].start()
            d_bias_all = share * (bias_start[0:1, :] - bias_f[0:1, :])
            for r in range(width // 128):
                tile_out[r : r + 1, :] = d_bias_all[:, 128 * r : 128 * (r + 1)]
            lane = lax.broadcasted_iota(jnp.int32, (1, 128), 1)
            loss_sum = loss_all[0:1, 64:65]
            mean_loss = examples * loss_sum / jnp.full((1, 1), taken.astype(F32))
            scalars = jnp.where(lane == 0, examples, jnp.where(lane == 1, mean_loss, examples * factor_sum))
            tile_out[width // 128 : width // 128 + 1, :] = jnp.where(lane < 3, scalars, 0.0)
            tile_out[width // 128 + 1 :, :] = jnp.zeros((7 - width // 128, 128), F32)
            used = 4 * steps
            wanted_row = lax.broadcasted_iota(jnp.int32, (used, steps * SMALL), 0)
            wanted_row = (wanted_row // 4) * SMALL + lax.rem(wanted_row, 4)
            picker = (lax.broadcasted_iota(jnp.int32, (used, steps * SMALL), 1) == wanted_row).astype(BF16)
            low_left = nn(picker, (share * factors).astype(BF16)).astype(BF16)
            low_right = nn(picker, low_d[...])
            part = width // clients
            kept_lanes = lax.broadcasted_iota(jnp.int32, (used, 128), 1) < part
            for j in range(clients):
                low_out[j, :, 0:width] = low_left
                turned = pltpu.roll(low_right, (width - part * j) % width, 1) if j else low_right
                low_out[j, :, width : width + 128] = jnp.where(kept_lanes, turned[:, :128], 0.0).astype(BF16)
            for copy in copies:
                copy.wait()

        return carry

    lax.fori_loop(0, steps, one_step, 0)


def local_training(tau, counts, labels, index, patches, main, wo, table, bias, clients, pad, seq, classes):
    steps = patches.shape[0]
    width = main.shape[0]
    n_all = 4 * pad
    n_head = (classes + 127) // 128 * 128
    n_low = steps * SMALL
    vmem = pltpu.VMEM
    dma = pltpu.SemaphoreType.DMA
    anywhere = pl.BlockSpec(memory_space=pl.ANY)
    inside = pl.BlockSpec(memory_space=pltpu.VMEM)
    square = (width, width)
    out_shape = (
        jax.ShapeDtypeStruct((width, 2 * width), BF16),
        jax.ShapeDtypeStruct(table.shape, BF16),
        jax.ShapeDtypeStruct((clients, 4 * steps, width + 128), BF16),
        jax.ShapeDtypeStruct((8, 128), F32),
        jax.ShapeDtypeStruct((steps, 8, 128), F32),
    )
    scratch = [
        vmem(square, BF16), vmem(square, BF16), vmem(square, BF16), vmem(square, BF16),
        vmem(square, BF16), vmem((n_head, width), BF16),
    ]
    for _ in range(2):
        scratch += [
            vmem(square, F32), vmem(square, F32), vmem(square, F32), vmem(square, F32),
            vmem((pad, width), F32), vmem((n_head, width), F32), vmem((SMALL, width), F32),
            vmem((8, width), F32),
        ]
    scratch += [
        vmem(square, F32), vmem(square, F32), vmem(square, F32), vmem((pad, width), F32),
        vmem((n_head, width), F32), vmem((SMALL, width), F32),
        vmem((2, n_all, width), BF16), vmem((n_all, width), F32), vmem((n_all, width), F32),
        vmem((12, pad, pad), BF16), vmem((n_all, width), BF16), vmem((n_all, width), BF16),
        vmem((n_all, width), BF16), vmem((2, pad, 4 * 128), BF16), vmem((n_all, width), BF16),
        vmem((n_all, width), BF16), vmem((3, pad, width), F32), vmem((n_all, width), BF16),
        vmem((2, pad, width), F32), vmem((4, pad, 1), F32),
        vmem((4, 8, width), F32), vmem((4, 8, width), F32), vmem((SMALL, width), F32),
        vmem((8, width), F32), vmem((6, 8, width), F32), vmem((4, 8, width), F32),
        vmem((n_low, width), BF16), vmem((n_low, width), F32), vmem((n_low, 128), F32),
        vmem((n_low, 128), F32), vmem((8, 8, width), F32), vmem((8, 128), F32), vmem((8, 128), F32),
        vmem((8, LANE), F32), vmem((8, width), F32),
        vmem((2, pad, width), BF16), vmem((2, pad, width), BF16), vmem((2, pad, width), BF16),
        vmem((4, pad, width), BF16), vmem((8, width), F32), vmem((4, 8, width), F32),
        vmem((8, 128), F32), vmem((4, 8, 128), F32), vmem((pad, width), F32),
        vmem((6, 8, width), F32),
        dma((9,)), dma((2,)), dma((6,)), dma((6,)), dma((6,)), dma((6,)), dma((6,)), dma((6,)),
        dma((2,)), dma((2,)), dma((4,)), dma((4,)), dma((4,)), dma((4,)), dma((2,)), dma((2,)),
        dma((3,)), dma((3,)), dma((3,)), dma((3,)), dma((6,)),
    ]
    return pl.pallas_call(
        functools.partial(train_kernel, (steps, seq, pad, classes, clients)),
        out_shape=out_shape,
        in_specs=[pl.BlockSpec(memory_space=pltpu.SMEM)] * 4 + [anywhere] * 4 + [inside],
        out_specs=(anywhere,) * 2 + (inside,) * 3,
        scratch_shapes=scratch,
        compiler_params=pltpu.CompilerParams(
            collective_id=0, has_side_effects=True, vmem_limit_bytes=VMEM_LIMIT
        ),
        name="local_training",
    )(tau, counts, labels, index, patches, main, wo, table, bias)


def place_patches(chosen_ref, pool_ref, out_ref):
    seq_rows, width = pool_ref.shape[1], pool_ref.shape[2]
    pad = out_ref.shape[1]
    below = jnp.zeros((pad - 1 - seq_rows, width), F32)
    whole = jnp.concatenate([jnp.zeros((1, width), F32), pool_ref[0].astype(F32), below], 0)
    out_ref[0] = whole.astype(BF16)


def pick_patches(pool, chosen, pad):
    count = chosen.shape[0]
    _, patch_rows, width = pool.shape
    return pl.pallas_call(
        place_patches,
        out_shape=jax.ShapeDtypeStruct((count, pad, width), BF16),
        grid_spec=pltpu.PrefetchScalarGridSpec(
            num_scalar_prefetch=1,
            grid=(count,),
            in_specs=[pl.BlockSpec((1, patch_rows, width), lambda i, ids: (ids[i], 0, 0))],
            out_specs=pl.BlockSpec((1, pad, width), lambda i, ids: (i, 0, 0)),
        ),
        name="pick_patches",
    )(chosen, pool)


def ring_places(clients):
    depth = clients // 2
    client = lax.axis_index("client")
    member = lax.axis_index("tensor")
    core = lax.rem(member, 2)
    return (
        depth, client, client // 2, lax.rem(client, 2), member, core, member // 2,
        member + 1 - 2 * core, lax.rem(member + 2, 4),
    )


def send(src, dst, send_sem, recv_sem, client, member):
    return pltpu.make_async_remote_copy(
        src_ref=src, dst_ref=dst, send_sem=send_sem, recv_sem=recv_sem,
        device_id={"client": client, "tensor": member}, device_id_type=MESH,
    )


def span(start, size, unit):
    return pl.ds(pl.multiple_of(start, unit), size)


def gather_kernel(
    clients, index_ref, in_ref, out_ref, table_in, pool_ref, main_out, wo_out, table_out, x_out,
    main_ref, table_ref, wide_in, wide_out, pool_buf, x_buf, pool_sem, x_sem, up_s, up_r, down_s, down_r, y_s, y_r, mate_s, mate_r, x_s, x_r, on_s, on_r, own_sem, keep_sem,
):
    depth, client, z, y, member, core, chip_x, mate, across = ring_places(clients)
    block = main_ref.shape[0]
    half = block // 2
    columns = table_ref.shape[1] // 2
    peer = client + 1 - 2 * y

    wide = main_ref.shape[1]
    tail = wide - LANE

    def table_part(origin, who):
        return table_out.at[
            span(origin * block + (who // 2) * half, half, half),
            span(lax.rem(who, 2) * columns, columns, 128),
        ]

    def wo_part(origin, who):
        return wo_out.at[span(origin * block, block, block), span(who * LANE, LANE, LANE)]

    def shared(origin, who):
        return (wo_part(origin, who), table_part(origin, who))

    def main_part(origin, lanes):
        return main_out.at[span(origin * block, block, block), lanes]

    early, front, back = slice(0, wide // 6), slice(wide // 6, 2 * wide // 3), slice(2 * wide // 3, wide)

    def beside(origin):
        return origin + 1 - 2 * lax.rem(origin, 2)

    def landed(origin):
        return (
            main_part(origin, back), table_part(origin, member), main_part(origin, front),
            main_part(origin, early), main_part(beside(origin), early),
        )

    own_table = table_ref.at[span(chip_x * half, half, half), span(core * columns, columns, 128)]
    own_pieces = (
        main_ref.at[:, back], own_table, main_ref.at[:, front], main_ref.at[:, early],
        main_part(peer, early),
    )

    def given(origin, mine):
        if mine:
            return (main_ref.at[:, tail:wide], own_table)
        return (main_part(origin, slice(tail, wide)), table_part(origin, member))

    def message(origin, mine, send_sem, recv_sem, index, to, part):
        sources = own_pieces if mine else landed(origin)
        return [
            send(src, dst, send_sem.at[p, index], recv_sem.at[p, index], to, member)
            for p, (src, dst) in enumerate(zip(sources, landed(origin)))
        ][part]

    first, second, third, over_all, crossing = slice(0, 2), slice(2, 3), slice(3, 5), slice(0, 3), slice(3, 4)

    def up(origin, i, part, mine=False):
        return message(origin, mine, up_s, up_r, i, client + 2, part)

    def down(origin, i, part, mine=False):
        return message(origin, mine, down_s, down_r, i, client - 2, part)

    def over(origin, part, mine=False):
        return message(origin, mine, y_s, y_r, origin // 2, peer, part)

    def give(origin, mine, send_sem, recv_sem, to):
        return [
            send(src, dst, send_sem.at[p, origin], recv_sem.at[p, origin], client, to)
            for p, (src, dst) in enumerate(zip(given(origin, mine), shared(origin, member)))
        ]

    def keep(origin, mine=False):
        return pltpu.make_async_copy(given(origin, mine)[0], wo_part(origin, member), keep_sem.at[origin])

    def share(origin, mine=False):
        return give(origin, mine, mate_s, mate_r, mate) + give(origin, mine, x_s, x_r, across)

    def from_across(origin):
        return [
            send(dst, dst, x_s.at[p, origin], x_r.at[p, origin], client, across)
            for p, dst in enumerate(shared(origin, across))
        ]

    def pass_on(origin):
        return [
            send(dst, dst, on_s.at[p, origin], on_r.at[p, origin], client, mate)
            for p, dst in enumerate(shared(origin, across))
        ]

    def start(copies):
        for copy in copies:
            copy.start()

    def arrived(copies):
        for copy in copies:
            copy.wait_recv()

    def sent(copies):
        for copy in copies:
            copy.wait_send()

    has_up, has_down = z < depth - 1, z > 0

    barrier = pltpu.get_barrier_semaphore()

    def hello(to_client, to_member):
        pl.semaphore_signal(
            barrier, inc=1, device_id={"client": to_client, "tensor": to_member}, device_id_type=MESH
        )

    hello(peer, member)
    for shift in (1, 2, 3):
        hello(client, lax.rem(member + shift, 4))
    for shift in range(1, depth):
        hello(2 * lax.rem(z + shift, depth) + y, member)
    wide_in[...] = jnp.zeros_like(wide_in)
    wide_out[...] = jnp.zeros_like(wide_out)
    table_ref[...] = jnp.zeros_like(table_ref)
    table_ref[:, 0 : table_in.shape[1]] = table_in[...]

    def in_slab(i):
        wide_in[i, :, 0 : in_ref.shape[2]] = in_ref[i].astype(F32)
        return tiles(wide_in[i])

    def out_slab(i):
        wide_out[i, 0 : out_ref.shape[1], 0:block] = out_ref[i].astype(F32)
        return tiles(jnp.transpose(wide_out[i])[:block])

    ordered = [in_slab(i) for i in (3, 4, 5, 6)] + [out_slab(i) for i in (1, 2, 3, 4)]
    ordered += [in_slab(i) for i in (0, 1, 2)] + [out_slab(0)]
    for i in range(0, 12, 2):
        packed = jnp.concatenate(pack_two(ordered[i], ordered[i + 1]), 1)
        main_ref[:, 192 * i : 192 * (i + 2)] = packed.astype(BF16)

    pl.semaphore_wait(barrier, 3 + depth)

    def line_start(part):
        @pl.when(has_up)
        def _():
            start(up(client, 0, part, True))

        @pl.when(has_down)
        def _():
            start(down(client, 0, part, True))

    start(over(client, crossing, True))
    start(over(client, first, True))
    line_start(first)
    start(over(client, second, True))
    line_start(second)
    start(share(client, True))
    keep(client, True).start()
    local = [
        pltpu.make_async_copy(src, dst, own_sem.at[p])
        for p, (src, dst) in enumerate(zip(own_pieces[:4], landed(client)))
    ]
    start(local)

    _, steps, each = index_ref.shape
    images = steps * each
    pool_size = pool_buf.shape[1] // 8
    patch_rows = pool_ref.shape[0] // pool_size
    pad = x_out.shape[1]

    def base(b):
        return lax.min(lax.max(8 * b - 1, 0), patch_rows - 8)

    deep = pool_buf.shape[0]

    def pool_load(b):
        k = lax.rem(b, deep)
        return pltpu.make_async_copy(
            pool_ref.at[span(base(b) * pool_size, 8 * pool_size, 32), :], pool_buf.at[k], pool_sem.at[k]
        )

    def x_store(b):
        k = lax.rem(b, deep)
        return pltpu.make_async_copy(x_buf.at[k], x_out.at[:, span(8 * b, 8, 8), :], x_sem.at[k])

    for b in range(deep - 1):
        pool_load(b).start()
    lane = lax.broadcasted_iota(jnp.int32, (8 * images, 8 * pool_size), 1)
    select_row = lax.broadcasted_iota(jnp.int32, (8 * images, 1), 0)
    line_row = lax.rem(select_row, 8)
    chosen = jnp.zeros((8 * images, 1), jnp.int32)
    for i in range(images):
        chosen = jnp.where(select_row // 8 == i, index_ref[0, i // each, i % each], chosen)

    def pick(b, carry):
        k = lax.rem(b, deep)
        pool_load(b).wait()

        @pl.when(b < pad // 8 - (deep - 1))
        def _():
            pool_load(b + deep - 1).start()

        wanted = (8 * b - 1 + line_row - base(b)) * pool_size + chosen
        picked = nn((lane == wanted).astype(BF16), pool_buf[k]).astype(BF16)

        @pl.when(b >= deep)
        def _():
            x_store(b - deep).wait()

        x_buf[k] = picked.reshape(images, 8, picked.shape[1])
        x_store(b).start()
        return carry

    lax.fori_loop(0, pad // 16, pick, 0)

    def line(d, act):
        @pl.when(z >= d)
        def _():
            act(client - 2 * d, True)

        @pl.when(z < depth - d)
        def _():
            act(client + 2 * d, False)

    def across_line(d, act):
        if d == 0:
            act(peer, True)
            return

        @pl.when(z >= d)
        def _():
            act(peer - 2 * d, True)

        @pl.when(z < depth - d)
        def _():
            act(peer + 2 * d, False)

    def line_in(d, part):
        def act(origin, below):
            line_s, line_r = (up_s, up_r) if below else (down_s, down_r)
            arrived(message(origin, False, line_s, line_r, d - 1, peer, part))
            if d < depth - 1:

                @pl.when(has_up if below else has_down)
                def _():
                    start(up(origin, d, part) if below else down(origin, d, part))

            if part is not third:
                start(over(origin, part))
            if part is first:
                start(share(origin))
                keep(origin).start()

        return act

    def y_in(origin, below):
        arrived(over(origin, first))
        start(share(origin))
        keep(origin).start()

    def forward(origin, below=True):
        arrived(from_across(origin))
        start(pass_on(origin))

    for d in range(1, depth + 1):
        if d < depth:
            line(d, line_in(d, first))
        across_line(d - 1, y_in)
        if d < depth:
            line(d, line_in(d, second))
        if d == 1:
            arrived(over(peer, crossing))
            line_start(third)
        else:
            line(d - 1, line_in(d - 1, third))
        if d == 1:
            lax.fori_loop(pad // 16, pad // 8, pick, 0)
            for b in range(pad // 8 - deep, pad // 8):
                x_store(b).wait()
            forward(client)
        else:
            line(d - 1, forward)
            across_line(d - 2, forward)
    across_line(depth - 1, forward)
    for d in range(depth):
        across_line(d, lambda origin, below: arrived(over(origin, second)))

    for copy in local:
        copy.wait()
    for origin in range(clients):
        sent(share(origin))
        sent(pass_on(origin))
        keep(origin).wait()
        arrived([
            send(dst, dst, mate_s.at[p, origin], mate_r.at[p, origin], client, mate)
            for p, dst in enumerate(shared(origin, mate))
        ])
        arrived([
            send(dst, dst, on_s.at[p, origin], on_r.at[p, origin], client, mate)
            for p, dst in enumerate(shared(origin, lax.rem(mate + 2, 4)))
        ])
    sent(over(client, crossing))
    for d in range(depth):
        sent(over(2 * d + y, over_all))

        @pl.when(has_up & (z >= d))
        def _():
            if d < depth - 1:
                sent(up(client - 2 * d, d, slice(0, 5)))

        @pl.when(has_down & (z < depth - d))
        def _():
            if d < depth - 1:
                sent(down(client + 2 * d, d, slice(0, 5)))


def gather_weights(clients, index, in_bf, out_bf, table_t, pool, pad):
    depth = clients // 2
    dma = pltpu.SemaphoreType.DMA
    anywhere = pl.BlockSpec(memory_space=pl.ANY)
    inside = pl.BlockSpec(memory_space=pltpu.VMEM)
    slabs, own, group = in_bf.shape
    width = own * clients
    packed = (slabs + out_bf.shape[0]) * group
    table_lanes = width + REST
    hops = depth - 1
    pool_size, patch_rows, features = pool.shape
    images = index.shape[1] * index.shape[2]
    rows = jnp.transpose(pool, (1, 0, 2)).reshape(patch_rows * pool_size, features)
    return pl.pallas_call(
        functools.partial(gather_kernel, clients),
        out_shape=(
            jax.ShapeDtypeStruct((width, packed), BF16),
            jax.ShapeDtypeStruct((width, 4 * LANE), BF16),
            jax.ShapeDtypeStruct((width, table_lanes), BF16),
            jax.ShapeDtypeStruct((images, pad, features), BF16),
        ),
        in_specs=[pl.BlockSpec(memory_space=pltpu.SMEM)] + [inside] * 3 + [anywhere],
        out_specs=(anywhere,) * 4,
        scratch_shapes=[
            pltpu.VMEM((own, packed), BF16), pltpu.VMEM((own, table_lanes), BF16),
            pltpu.VMEM((slabs, own, LANE), F32), pltpu.VMEM((out_bf.shape[0], LANE, 128), F32),
            pltpu.VMEM((6, 8 * pool_size, features), BF16), pltpu.VMEM((6, images, 8, features), BF16),
            dma((6,)), dma((6,)),
            dma((5, hops)), dma((5, hops)), dma((5, hops)), dma((5, hops)), dma((4, depth)),
            dma((4, depth)),
        ] + [dma((2, clients))] * 6 + [dma((4,)), dma((clients,))],
        compiler_params=pltpu.CompilerParams(collective_id=1, has_side_effects=True),
        name="gather_weights",
    )(index, in_bf, out_bf, table_t, rows)


def reduce_kernel(
    clients, main_in, table_in, low_in, tile_in, main_out, table_out, low_out, tile_out,
    own_main, own_table, y_main, y_table, zs_main, zs_table, zr_main, zr_table, rl_main, rl_table,
    whole, low_all, tile_all, own_sem, y_s, y_r, z_s, z_r, rl_s, rl_r, low_s, low_r, tile_s, tile_r, q_s, q_r, keep_sem,
):
    depth, client, z, y, member, core, chip_x, mate, across = ring_places(clients)
    block = own_main.shape[1]
    half, columns = own_table.shape[1], own_table.shape[2]
    peer = client + 1 - 2 * y
    cut = own_main.shape[2] // 2
    lanes = (None, slice(0, cut), slice(cut, 2 * cut))
    parts = (0, 1, 2)

    def source(owner, p):
        if p == 0:
            return table_in.at[
                span(owner * block + chip_x * half, half, half), span(core * columns, columns, 128)
            ]
        return main_in.at[span(owner * block, block, block), lanes[p]]

    def slot(table_ref, main_ref, i, p):
        return table_ref.at[i] if p == 0 else main_ref.at[i, :, lanes[p]]

    def own_load(level, p):
        return pltpu.make_async_copy(
            source(2 * level + y, p), slot(own_table, own_main, level, p), own_sem.at[p, level]
        )

    def over(level, p):
        return send(
            source(2 * level + 1 - y, p), slot(y_table, y_main, level, p),
            y_s.at[p, level], y_r.at[p, level], peer, member,
        )

    side = z // 2
    outer = z == 3 * side
    near = z + 1 - 2 * lax.rem(z, 2)
    levels = (3 * (1 - side), 2 - side, near, z)

    def relay(i, p):
        return send(
            slot(zs_table, zs_main, i, p), slot(rl_table, rl_main, i, p),
            rl_s.at[p, i], rl_r.at[p, i], 2 * near + y, member,
        )

    def onward(i, p):
        last = i // 2
        return send(
            slot(zs_table, zs_main, i, p), slot(zr_table, zr_main, last, p),
            z_s.at[p, i], z_r.at[p, last], 2 * levels[i] + y, member,
        )

    def came(last, p):
        return send(
            slot(zs_table, zs_main, 0, p), slot(zr_table, zr_main, last, p),
            z_s.at[p, 0], z_r.at[p, last], peer, member,
        )

    def small(shift):
        to = lax.rem(client + shift, clients)
        return [
            send(low_in.at[to], low_all.at[client], low_s.at[shift - 1], low_r.at[shift - 1], to, member),
            send(tile_in, tile_all.at[client], tile_s.at[shift - 1], tile_r.at[shift - 1], to, member),
        ]

    def small_from(shift):
        origin = lax.rem(client + clients - shift, clients)
        return [
            send(low_in.at[origin], low_all.at[origin], low_s.at[shift - 1], low_r.at[shift - 1], origin, member),
            send(tile_in, tile_all.at[origin], tile_s.at[shift - 1], tile_r.at[shift - 1], origin, member),
        ]

    def quarter(who):
        return whole.at[span((who // 2) * half, half, half), span(lax.rem(who, 2) * columns, columns, 128)]

    def pass_quarter(who, index, to):
        return send(quarter(who), quarter(who), q_s.at[index], q_r.at[index], client, to)

    barrier = pltpu.get_barrier_semaphore()
    for shift in range(1, clients):
        pl.semaphore_signal(
            barrier, inc=1,
            device_id={"client": lax.rem(client + shift, clients), "tensor": member}, device_id_type=MESH,
        )
    for shift in (1, 2, 3):
        pl.semaphore_signal(
            barrier, inc=1,
            device_id={"client": client, "tensor": lax.rem(member + shift, 4)}, device_id_type=MESH,
        )
    order = [(0, 1), (0, 2)] + [(i, 0) for i in range(depth)]
    order += [(i, p) for i in range(1, depth) for p in (1, 2)]
    for i, p in order:
        own_load(levels[i], p).start()
    own_small = [
        pltpu.make_async_copy(low_in.at[client], low_all.at[client], keep_sem.at[0]),
        pltpu.make_async_copy(tile_in, tile_all.at[client], keep_sem.at[1]),
    ]
    for copy in own_small:
        copy.start()
    pl.semaphore_wait(barrier, clients - 1 + 3)
    for i, p in order:
        over(levels[i], p).start()
    for shift in range(1, clients):
        for copy in small(shift):
            copy.start()

    def pair_up(i, p):
        level = levels[i]
        own_load(level, p).wait()
        over(level, p).wait_recv()
        pair = (
            slot(own_table, own_main, level, p)[...].astype(F32)
            + slot(y_table, y_main, level, p)[...].astype(F32)
        )
        if i == 3:
            if p == 0:
                quarter(member)[...] = pair
            else:
                main_out[:, lanes[p]] = pair
            return
        if i == 2:
            slot(zs_table, zs_main, i, p)[...] = pair.astype(BF16)
            onward(i, p).start()
            return

        @pl.when(outer)
        def _():
            slot(zs_table, zs_main, i, p)[...] = pair.astype(BF16)
            relay(i, p).start()

        @pl.when(z != 3 * side)
        def _():
            relay(i, p).wait_recv()
            both = pair + slot(rl_table, rl_main, i, p)[...].astype(F32)
            slot(zs_table, zs_main, i, p)[...] = both.astype(BF16)
            onward(i, p).start()

    pair_up(0, 1)
    pair_up(0, 2)
    for i in range(depth):
        pair_up(i, 0)
    pair_up(1, 1)
    pair_up(1, 2)
    mine = quarter(member)
    for last in (0, 1):
        came(last, 0).wait_recv()
        mine[...] = mine[...] + zr_table[last].astype(F32)
    to_others = [pass_quarter(member, 0, mate), pass_quarter(member, 1, across)]
    for copy in to_others:
        copy.start()
    pair_up(2, 1)
    pair_up(2, 2)
    pass_quarter(across, 1, across).wait_recv()
    second = pass_quarter(across, 2, mate)
    second.start()
    pair_up(3, 1)
    pair_up(3, 2)
    for shift in range(1, clients):
        for copy in small_from(shift):
            copy.wait_recv()
    for copy in own_small:
        copy.wait()
    low_out[...] = low_all[...]
    tile_out[...] = tile_all[...]
    pass_quarter(mate, 0, mate).wait_recv()
    pass_quarter(lax.rem(mate + 2, 4), 2, mate).wait_recv()
    table_out[...] = whole[...]
    for last in (1, 0):
        for p in (1, 2):
            came(last, p).wait_recv()
            main_out[:, lanes[p]] = main_out[:, lanes[p]] + zr_main[last, :, lanes[p]].astype(F32)
    for copy in to_others + [second]:
        copy.wait_send()
    for shift in range(1, clients):
        for copy in small(shift):
            copy.wait_send()
    for i in range(depth):
        for p in parts:
            over(i, p).wait_send()
    for p in parts:
        onward(2, p).wait_send()

    @pl.when(outer)
    def _():
        for i in (0, 1):
            for p in parts:
                relay(i, p).wait_send()

    @pl.when(z != 3 * side)
    def _():
        for i in (0, 1):
            for p in parts:
                onward(i, p).wait_send()


def reduce_deltas(clients, main, table, low, tile):
    depth = clients // 2
    dma = pltpu.SemaphoreType.DMA
    vmem = pltpu.VMEM
    anywhere = pl.BlockSpec(memory_space=pl.ANY)
    inside = pl.BlockSpec(memory_space=pltpu.VMEM)
    block = main.shape[0] // clients
    half, columns = block // 2, table.shape[1] // 2
    wide = main.shape[1]
    hops = depth - 1
    return pl.pallas_call(
        functools.partial(reduce_kernel, clients),
        out_shape=(
            jax.ShapeDtypeStruct((block, wide), F32),
            jax.ShapeDtypeStruct((block, table.shape[1]), F32),
            jax.ShapeDtypeStruct(low.shape, BF16),
            jax.ShapeDtypeStruct((clients,) + tile.shape, F32),
        ),
        in_specs=[anywhere] * 4,
        out_specs=(inside,) * 4,
        scratch_shapes=[
            vmem((depth, block, wide), BF16), vmem((depth, half, columns), BF16),
            vmem((depth, block, wide), BF16), vmem((depth, half, columns), BF16),
            vmem((hops, block, wide), BF16), vmem((hops, half, columns), BF16),
            vmem((2, block, wide), BF16), vmem((2, half, columns), BF16),
            vmem((2, block, wide), BF16), vmem((2, half, columns), BF16),
            vmem((block, table.shape[1]), F32), vmem(low.shape, BF16),
            vmem((clients,) + tile.shape, F32),
            dma((3, depth)), dma((3, depth)), dma((3, depth)), dma((3, hops)), dma((3, 2)),
            dma((3, 2)), dma((3, 2)),
            dma((clients - 1,)), dma((clients - 1,)), dma((clients - 1,)), dma((clients - 1,)),
            dma((3,)), dma((3,)), dma((2,)),
        ],
        compiler_params=pltpu.CompilerParams(
            collective_id=2, has_side_effects=True, vmem_limit_bytes=52 << 20
        ),
        name="reduce_deltas",
    )(main, table, low, tile)


def adam(master, first, second, grad):
    first2 = BETA_ONE * first + (1.0 - BETA_ONE) * grad
    second2 = BETA_TWO * second + (1.0 - BETA_TWO) * grad * grad
    moved = (
        first2 / (1.0 - BETA_ONE**ROUND) / (jnp.sqrt(second2 / (1.0 - BETA_TWO**ROUND)) + ADAM_EPS)
    )
    fresh = master - SERVER_RATE * (moved + WEIGHT_DECAY * master)
    return (fresh, first2, second2, fresh.astype(jnp.bfloat16))


def server_kernel(main_ref, table_ref, low_ref, tile_ref, norm_ref, *refs):
    masters, firsts, seconds = refs[0:4], refs[4:8], refs[8:12]
    loss_out, norms_out = refs[12:14]
    outs = [refs[14 + i : 30 : 4] for i in range(4)]
    own, group = masters[0].shape[1:]
    tile = jnp.sum(tile_ref[...], 0)
    row = main_ref.shape[1] // 256
    examples, weighted_loss, weighted_factor = (tile[row : row + 1, i : i + 1] for i in range(3))
    scale = weighted_factor / examples / examples
    loss_out[...] = weighted_loss / examples
    lane = lax.broadcasted_iota(jnp.int32, (1, 128), 1)
    norms = jnp.zeros((1, 128), F32)
    for i in range(norm_ref.shape[0]):
        norms = jnp.where(lane == i, norm_ref[i, 0:1, 0:1], norms)
    norms_out[...] = norms[:, 0 : norm_ref.shape[0]]

    def apply(which, at, delta):
        results = adam(
            masters[which][at], firsts[which][at], seconds[which][at], scale * delta
        )
        for ref, value in zip(outs[which], results):
            ref[at] = value

    def slab(pair):
        return jnp.concatenate(pair, 1)

    every = slice(None)
    packed = tiles(main_ref[...])
    slabs = []
    for i in range(0, len(packed), 3):
        slabs += [slab(pair) for pair in unpack_two(packed[i : i + 3])]
    for i, which in enumerate((3, 4, 5, 6, 0, 1, 2)):
        apply(0, (which, every, every), slabs[i][:, :group])
    wo_rows = jnp.concatenate([slabs[7], jnp.zeros((128 - own, LANE), F32)], 0)
    apply(1, (0, every, every), jnp.transpose(wo_rows)[:group, :own])
    width = low_ref.shape[2] - 128
    messages = low_ref[...].reshape(low_ref.shape[0] * low_ref.shape[1], low_ref.shape[2])
    moved = tn(messages[:, :width], messages[:, width:])
    for i in range(4):
        apply(1, (i + 1, every, every), moved[i * group : (i + 1) * group, :own])
    apply(2, (every, every), table_ref[:, 0 : masters[2].shape[1]])
    bias = [tile[i : i + 1, :] for i in range(row)]
    rows = []
    for i in range(0, row, 3):
        rows += [slab(pair) for pair in unpack_two(bias[i : i + 3])]
    for i in range(4):
        apply(3, (slice(i, i + 1), every), rows[i][:, :group])


def server_update(main, table, low, tile, norms, state):
    inside = pl.BlockSpec(memory_space=pltpu.VMEM)
    shapes = [value.shape for value in state[:4]]
    out_shape = [jax.ShapeDtypeStruct((1, 1), F32), jax.ShapeDtypeStruct((1, norms.shape[0]), F32)]
    for kind in (F32, F32, F32, BF16):
        out_shape += [jax.ShapeDtypeStruct(shape, kind) for shape in shapes]
    return pl.pallas_call(
        server_kernel,
        out_shape=tuple(out_shape),
        in_specs=[inside] * (5 + len(state)),
        out_specs=(inside,) * len(out_shape),
        compiler_params=pltpu.CompilerParams(vmem_limit_bytes=24 << 20),
        name="server_update",
    )(main, table, low, tile, norms, *state)


def on_device(
    pool, index, tau, counts, labels,
    in_bf, out_bf, table_bf, bias_bf,
    in_master, out_master, table_master, bias_master,
    in_first, out_first, table_first, bias_first,
    in_second, out_second, table_second, bias_second,
):
    clients = lax.axis_size("client")
    group = in_bf.shape[2]
    steps, images = index.shape[1], index.shape[2]
    patch_rows, features = pool.shape[1], pool.shape[2]
    seq = patch_rows + 1
    pad = (seq + 15) // 16 * 16
    own = in_bf.shape[1]
    rows_total = table_bf.shape[0]
    classes = rows_total - features - seq - 9
    table_t = table_bf.T
    direct = clients == 8
    if direct:
        main, wo_all, table, patches = gather_weights(
            clients, index, in_bf, out_bf, table_t, pool, pad
        )
    else:
        in_rows = jnp.transpose(in_bf, (1, 0, 2))
        out_rows = jnp.transpose(out_bf, (2, 0, 1))
        main_own = jnp.concatenate(
            [in_rows[:, 3:], out_rows[:, 1:], in_rows[:, :3], out_rows[:, :1]], 1
        ).reshape(own, 12 * group)
        table_own = jnp.pad(table_t, ((0, 0), (0, features + REST - rows_total)))
        main = lax.all_gather(main_own, "client", axis=0, tiled=True)
        table = lax.all_gather(table_own, "client", axis=0, tiled=True)
        wo_all = lax.all_gather(main[:, 12 * group - LANE :], "tensor", axis=1, tiled=True)
        patches = pick_patches(pool, index[0].reshape(steps * images), pad)
    patches = patches.reshape(steps, images * pad, features)
    d_main, d_table, low, tile, norms = local_training(
        tau, counts, labels, index, patches, main, wo_all, table, bias_bf, clients, pad, seq, classes
    )
    if direct:
        main_sum, table_sum, low_all, tile_all = reduce_deltas(clients, d_main, d_table, low, tile)
    else:
        tile_all = lax.psum(tile, "client")[None]
        main_sum = lax.psum_scatter(d_main, "client", scatter_dimension=0, tiled=True).astype(F32)
        first_member = lax.axis_index("tensor") == 0
        d_table = jnp.where(first_member, d_table, jnp.zeros_like(d_table))
        table_sum = lax.psum(
            lax.psum_scatter(d_table, "client", scatter_dimension=0, tiled=True).astype(F32), "tensor"
        )
        low_all = lax.all_to_all(low, "client", split_axis=0, concat_axis=0, tiled=True)
    state = (
        in_master, out_master, table_master.T, bias_master,
        in_first, out_first, table_first.T, bias_first,
        in_second, out_second, table_second.T, bias_second,
    )
    loss, norms, *fresh = server_update(main_sum, table_sum, low_all, tile_all, norms, state)
    fresh[2::4] = [value.T for value in fresh[2::4]]
    return (loss.reshape(()), norms, *fresh)


def solution(mesh):
    by_client = P("client", None, None)
    state = (P(None, "client", "tensor"), P(None, "tensor", "client"), P(None, "client"), P(None, "tensor"))
    in_specs = (by_client, by_client, P("client"), P("client"), P("client")) + state * 4
    out_specs = (P(), P("client", None)) + state * 4
    return jax.shard_map(
        on_device, mesh=mesh, in_specs=in_specs, out_specs=out_specs, check_vma=False
    )
```

```python
import functools

import jax
import jax.numpy as jnp
from jax import lax
from jax.experimental import pallas as pl
from jax.experimental.pallas import tpu as pltpu
from jax.sharding import PartitionSpec as P

HEAD_DIM = 64
ROUND = 5
EPS_NORM = 1e-06
MOMENTUM_RHO = 0.9
LOCAL_RATE = 0.05
CLIP_LIMIT = 1.0
BETA_ONE = 0.5
BETA_TWO = 0.7
ADAM_EPS = 1e-08
WEIGHT_DECAY = 0.05
SERVER_RATE = 0.05
SQRT_HALF = 0.7071067811865476
INV_ROOT_TAU = 0.3989422804014327
MESH = pl.DeviceIdType.MESH
F32 = jnp.float32
BF16 = jnp.bfloat16
NEG = -1e30
LANE = 256
SMALL = 16
REST = 512
VMEM_LIMIT = 67043328


def dot(left, right, dims):
    return lax.dot_general(left, right, (dims, ((), ())), preferred_element_type=F32)


def nn(left, right):
    return dot(left, right, ((1,), (0,)))


def nt(left, right):
    return dot(left, right, ((1,), (1,)))


def tn(left, right):
    return dot(left, right, ((0,), (0,)))


def fold(value):
    rows, width = value.shape
    return jnp.sum(value.reshape(rows // 8, 8, width), 0)


def total(value):
    return jnp.sum(jnp.sum(value, 1, keepdims=True), 0, keepdims=True)


def normalise(value):
    centre = value - jnp.mean(value, -1, keepdims=True)
    inverse = lax.rsqrt(jnp.mean(centre * centre, -1, keepdims=True) + EPS_NORM)
    return (centre * inverse, inverse)


def norm_grad(grad, gain, normed, inverse):
    scaled = grad * gain
    return inverse * (
        scaled
        - jnp.mean(scaled, -1, keepdims=True)
        - normed * jnp.mean(scaled * normed, -1, keepdims=True)
    )


def split_two(value):
    high = value.astype(BF16)
    return (high, (value - high.astype(F32)).astype(BF16))


def swap(tile):
    return pltpu.roll(tile, HEAD_DIM, 1)


def tiles(value):
    return [value[:, i : i + 128] for i in range(0, value.shape[1], 128)]


def low_half(shape):
    return lax.broadcasted_iota(jnp.int32, shape, 1) < HEAD_DIM


def pack_two(left, right):
    low = low_half(left[0].shape)
    return [
        left[0],
        jnp.where(low, left[1], swap(right[0])),
        jnp.where(low, swap(right[0]), swap(right[1])),
    ]


def unpack_two(packed):
    low = low_half(packed[0].shape)
    nothing = jnp.zeros_like(packed[0])
    middle, last = swap(packed[1]), swap(packed[2])
    return (
        [packed[0], jnp.where(low, packed[1], nothing)],
        [jnp.where(low, middle, last), jnp.where(low, last, nothing)],
    )


def train_kernel(
    sizes,
    tau_ref,
    count_ref,
    label_ref,
    index_ref,
    x_hbm,
    main_in,
    wo_in,
    table_in,
    bias_in,
    main_out,
    table_out,
    low_out,
    tile_out,
    norm_out,
    wqkv, w1, wot, w2t, wet, head,
    wqkv_f, w1_f, wot_f, wet_f, pos_f, head_f, vec_f, bias_f,
    wqkv_m, w1_m, wot_m, wet_m, pos_m, head_m, vec_m, bias_m,
    wqkv_g, wot_g, wet_g, pos_g, head_g, vec_g,
    xbuf, h0, slope, prob, abuf, qkv, oall, third, ubuf, dpre, h1own, datt, chip, inverses,
    hsum, asum, dact, bsum, vacc, ssq,
    low_d, low_a, low_b, low_w, scal, loss_all, factor_kept, bias_wide, bias_start,
    s1, r1, s2, r2, mx_s, mx_r, nx_s, nx_r, pos_r, vec_r,
    wsem, xsem, o_ps, o_xs, o_fs, o_pr, o_xr, o_fr,
    a1s, a1r, a2s, a2r, das, dar, pvs, pvr, mxs, mxr, nxs, nxr, osem,
):
    steps, seq, pad, classes, clients = sizes
    width = 768
    kept = (seq + 7) // 8 * 8
    me = lax.axis_index("tensor")
    core = lax.rem(me, 2)
    mate = me + 1 - 2 * core
    across = lax.rem(me + 2, 4)
    own0 = 2 * core
    oth0 = 2 - 2 * core

    def rows(n):
        return pl.ds(pl.multiple_of(n * pad, 16), pad)

    def sent_rows(n):
        return pl.ds(pl.multiple_of(n * pad, 16), kept)

    def remote(src, dst, send, recv, device):
        return pltpu.make_async_remote_copy(
            src_ref=src, dst_ref=dst, send_sem=send, recv_sem=recv,
            device_id={"tensor": device}, device_id_type=MESH,
        )

    rest = dpre.at[0:width, 0:REST]
    square_rows = pl.ds(0, width)
    raw = abuf.at[square_rows, :]
    wo_raw = [ubuf.at[square_rows, pl.ds(g * LANE, LANE)] for g in range(3)] + [
        qkv.at[square_rows, pl.ds(0, LANE)]
    ]
    weights_in = [
        main_in.at[:, 2 * width : 3 * width],
        main_in.at[:, 0:width],
        main_in.at[:, width : 2 * width],
        table_in.at[:, 0:width],
        table_in.at[:, width : width + REST],
    ] + [wo_in.at[:, g * LANE : (g + 1) * LANE] for g in range(4)]
    weights = [raw, w1, w2t, wet, rest] + wo_raw

    def load(which):
        return pltpu.make_async_copy(weights_in[which], weights[which], wsem.at[which])

    def fetch(step, slot):
        return pltpu.make_async_copy(x_hbm.at[step], xbuf.at[slot], xsem.at[slot])

    barrier = pltpu.get_barrier_semaphore()
    fetch(0, 0).start()
    for which in range(9):
        load(which).start()
    for zero in (r1, r2, oall, third, datt):
        zero[...] = jnp.zeros_like(zero)
    for shift in (1, 2, 3):
        pl.semaphore_signal(
            barrier, inc=1, device_id={"tensor": lax.rem(me + shift, 4)}, device_id_type=MESH
        )
    bias_wide[...] = jnp.zeros_like(bias_wide)
    bias_wide[0 : bias_in.shape[0], 0 : bias_in.shape[1]] = bias_in[...].astype(F32)
    slabs = [tiles(bias_wide[r : r + 1, :]) for r in range(4)]
    first_bias = jnp.concatenate(pack_two(slabs[0], slabs[1]) + pack_two(slabs[2], slabs[3]), 1)
    bias_start[...] = jnp.broadcast_to(first_bias, (8, width))
    bias_f[...] = bias_start[...]
    for zero in (pos_m, head_m, vec_m, bias_m, low_a, low_b, low_w, loss_all):
        zero[...] = jnp.zeros_like(zero)
    low_d[...] = jnp.zeros_like(low_d)
    for which in (0, 3, 4, 5, 6, 7, 8):
        load(which).wait()
    n_head = head.shape[0]
    vec_at, head_at = seq, seq + 9
    h0[0:REST, :] = jnp.transpose(rest[...].astype(F32))
    pos_rows = lax.broadcasted_iota(jnp.int32, (pad, 1), 0) < seq
    vec_rows = lax.broadcasted_iota(jnp.int32, (SMALL, 1), 0) < 9
    pos_f[...] = jnp.where(pos_rows, h0[0:pad, :], 0.0)
    vec_f[...] = jnp.where(vec_rows, h0[vec_at : vec_at + SMALL, :], 0.0)
    start_head = h0[head_at : head_at + n_head, :]
    head_f[...] = start_head
    head[...] = start_head.astype(BF16)
    taken = tau_ref[0]

    def join(parts):
        return jnp.concatenate(parts, 1)

    def start_rows(j, carry):
        at = pl.ds(pl.multiple_of(j * 64, 64), 64)
        packed = tiles(raw[at, :].astype(F32))
        q, k = unpack_two(packed[:3])
        v, _ = unpack_two(packed[3:])
        wqkv[at, :] = join(q + k + v).astype(BF16)
        pieces = [tiles(piece[at, :].astype(F32)) for piece in wo_raw]
        low = low_half((64, 128))
        first = [jnp.where(low, swap(p[0]), swap(p[1])) for p in pieces]
        last = [
            jnp.where(low, swap(pieces[g][1]), pieces[g + 1][1]) for g in (0, 2)
        ]
        wot[at, :] = join(first + last).astype(BF16)
        return carry

    lax.fori_loop(0, width // 64, start_rows, 0)
    pl.semaphore_wait(barrier, 3)

    row_id = lax.broadcasted_iota(jnp.int32, (pad, 1), 0)
    token = row_id < seq
    key_ok = lax.broadcasted_iota(jnp.int32, (1, pad), 1) < seq
    lane_head = lax.broadcasted_iota(jnp.int32, (1, LANE), 1) // HEAD_DIM
    small_ok = lax.broadcasted_iota(jnp.int32, (SMALL, 1), 0) < 4
    scale = HEAD_DIM ** (-0.5)

    def of_head(value, h):
        return jnp.where(lane_head == h, value, jnp.zeros_like(value))

    def o_part(message, group):
        lanes = pl.ds(pl.multiple_of(group * 128, 128), 128)
        pair, which = message // 3, message % 3
        if which == 2:
            return third.at[pair, 0:kept, lanes]
        return oall.at[pl.ds((2 * pair + which) * pad, kept), lanes]

    def o_to_mate(message):
        place = o_part(message, me)
        return remote(place, place, o_ps.at[message], o_pr.at[message], mate)

    def o_across(message):
        place = o_part(message, me)
        return remote(place, place, o_xs.at[message], o_xr.at[message], across)

    def o_forward(message):
        place = o_part(message, across)
        return remote(place, place, o_fs.at[message], o_fr.at[message], mate)

    def relay_o(message):
        place = o_part(message, across)
        remote(place, place, o_xs.at[message], o_xr.at[message], across).wait_recv()
        o_forward(message).start()

    def o_here(message):
        direct = o_part(message, mate)
        remote(direct, direct, o_ps.at[message], o_pr.at[message], mate).wait_recv()
        passed = o_part(message, lax.rem(mate + 2, 4))
        remote(passed, passed, o_fs.at[message], o_fr.at[message], mate).wait_recv()

    def to_mate(n):
        return remote(s1.at[n, 0:kept], r1.at[n, 0:kept], a1s.at[n], a1r.at[n], mate)

    def to_across(which, n):
        return remote(s2.at[n, 0:kept], r2.at[2 * which + n, 0:kept], a2s.at[2 * which + n], a2r.at[2 * which + n], across)

    def gradient_to_mate(buffer, which, image, k):
        return remote(
            buffer.at[sent_rows(image)], buffer.at[sent_rows(image)],
            das.at[2 * which + k], dar.at[2 * which + k], mate,
        )

    def pos_to_mate():
        return remote(pos_g, pos_r, pvs.at[0], pvr.at[0], mate)

    def vec_to_mate():
        return remote(vacc, vec_r, pvs.at[1], pvr.at[1], mate)

    def spread(src, dst, send, recv, shift):
        return remote(
            src, dst.at[me], send.at[shift - 1], recv.at[shift - 1], lax.rem(me + shift, 4)
        )

    def update_rows(entries, rho, live, fac):
        def update(j, carry):
            at = pl.ds(pl.multiple_of(j * 64, 64), 64)
            for low, full, mom, grad in entries:
                m = rho * mom[at, :] + fac * grad[at, :]
                mom[at, :] = m
                w = full[at, :] - (live * LOCAL_RATE) * m
                full[at, :] = w
                low[at, :] = w.astype(BF16)
            return carry

        lax.fori_loop(0, width // 64, update, 0)

    def one_step(step, carry):
        slot = lax.rem(step, 2)
        fetch(step, slot).wait()

        @pl.when(step < steps - 1)
        def _():
            fetch(step + 1, 1 - slot).start()

        gain1, shift1 = vec_f[0:1, :], vec_f[1:2, :]
        gain2, shift2 = vec_f[2:3, :], vec_f[3:4, :]
        gain3, shift3 = vec_f[4:5, :], vec_f[5:6, :]

        def attend(pair):
            two = slice(2 * pair * pad, 2 * (pair + 1) * pad)
            inside = (row_id >= 1) & token
            added = pos_f[...] + jnp.where(inside, vec_f[6:7, :], 0.0)
            state = nt(xbuf[slot, two, :], wet[...]) + jnp.concatenate([added, added], 0)
            h0[two, :] = state
            normed, _ = normalise(state)
            a = (normed * gain1 + shift1).astype(BF16)
            abuf[two, :] = a
            both = nn(a, wqkv[...]).astype(BF16)
            qkv[two, :] = both
            mine = pl.ds(pl.multiple_of(me * 128, 128), 128)
            thirds = []
            for i in range(2):
                projected = both[i * pad : (i + 1) * pad]
                q, k, v = projected[:, :LANE], projected[:, LANE : 2 * LANE], projected[:, 2 * LANE :]
                out = jnp.zeros((pad, LANE), F32)
                for h in range(3):
                    scores = jnp.where(key_ok, nt(of_head(q, h), k) * scale, NEG)
                    expd = jnp.exp(scores - jnp.max(scores, -1, keepdims=True))
                    p = (expd * (1.0 / jnp.sum(expd, -1, keepdims=True))).astype(BF16)
                    prob[(2 * pair + i) * 3 + h] = p
                    out = out + nn(p, of_head(v, h))
                oall[(2 * pair + i) * pad : (2 * pair + i + 1) * pad, mine] = out[:, :128].astype(BF16)
                thirds.append(out[:, 128:])
                o_to_mate(3 * pair + i).start()
                o_across(3 * pair + i).start()
            third[pair, :, mine] = (thirds[0] + swap(thirds[1])).astype(BF16)
            o_to_mate(3 * pair + 2).start()
            o_across(3 * pair + 2).start()

        attend(0)
        attend(1)

        @pl.when(step == 0)
        def _():
            load(1).wait()
            load(2).wait()

            def begin(j, carry):
                at = pl.ds(pl.multiple_of(j * 32, 32), 32)
                for low_ref, full, mom in (
                    (wqkv, wqkv_f, wqkv_m), (w1, w1_f, w1_m), (wot, wot_f, wot_m), (wet, wet_f, wet_m)
                ):
                    full[at, :] = low_ref[at, :].astype(F32)
                    mom[at, :] = jnp.zeros((32, width), F32)
                return carry

            lax.fori_loop(0, width // 32, begin, 0)

        @pl.when(step > 0)
        def _():
            was_live = jnp.where(step - 1 < taken, 1.0, 0.0)
            was_rho = jnp.where(step - 1 < taken, MOMENTUM_RHO, 1.0)
            was_fac = factor_kept[0:1, 0:1]
            update_rows(((w1, w1_f, w1_m, slope), (wot, wot_f, wot_m, wot_g)), was_rho, was_live, was_fac)
            head_m[...] = was_rho * head_m[...] + was_fac * head_g[...]
            head_f[...] = head_f[...] - (was_live * LOCAL_RATE) * head_m[...]
            head[...] = head_f[...].astype(BF16)
            moved_rows = (LOCAL_RATE * low_w[:, 0:1]) * low_a[...]
            low_hi, low_lo = split_two(moved_rows)
            pair_rows = jnp.concatenate([low_hi, low_lo], 0)
            load(2).wait()

            def low_rank(j, carry):
                at = pl.ds(pl.multiple_of(j * LANE, LANE), LANE)
                moved = tn(jnp.concatenate([low_d[:, at], low_d[:, at]], 0), pair_rows)
                w2t[at, :] = (w2t[at, :].astype(F32) - moved).astype(BF16)
                return carry

            lax.fori_loop(0, width // LANE, low_rank, 0)

        for message in range(3):
            relay_o(message)

        def feed(pair):
            for message in range(3):
                o_here(3 * pair + message)
            two = slice(2 * pair * pad, 2 * (pair + 1) * pad)
            side = tiles(third[pair].astype(F32))
            low = low_half((pad, 128))
            for i in range(2):
                for g in (0, 2):
                    if i == 0:
                        tile = jnp.where(low, side[g], swap(side[g + 1]))
                    else:
                        tile = jnp.where(low, swap(side[g]), side[g + 1])
                    at = 4 * 128 + g * HEAD_DIM
                    oall[(2 * pair + i) * pad : (2 * pair + i + 1) * pad, at : at + 128] = tile.astype(BF16)
            state = h0[two, :] + nt(oall[two, :], wot[...]) + vec_f[7:8, :]
            differs = (pair + core) - 2 * pair * core
            for i in range(2):
                part = state[i * pad : (i + 1) * pad]
                h1own[i * (1 - differs) + 2 * differs] = part
                hsum[2 * pair + i] = fold(jnp.where(token, part, 0.0))
            normed, _ = normalise(state)
            u = (normed * gain2 + shift2).astype(BF16)
            ubuf[two, :] = u
            if pair == 0:
                relay_o(3)
                relay_o(4)
            z = nn(u, w1[...]) + bias_f[0:1, :]
            cdf = 0.5 * (1.0 + lax.erf(z * SQRT_HALF))
            act = (z * cdf).astype(BF16).astype(F32)
            tail = cdf + z * jnp.exp(-0.5 * z * z) * INV_ROOT_TAU
            for i in range(2):
                part = slice(i * pad, (i + 1) * pad)
                asum[2 * pair + i] = fold(jnp.where(token, act[part], 0.0))
                slope[(2 * pair + i) * pad : (2 * pair + i + 1) * pad, :] = jnp.where(token, tail[part], 0.0)
            if pair == 0:
                relay_o(5)

        feed(0)
        feed(1)

        def stack(ref):
            parts = [jnp.sum(ref[n], 0, keepdims=True) for n in range(4)]
            return jnp.concatenate(parts + [jnp.zeros((SMALL - 4, width), F32)], 0)

        act_sum = stack(asum)
        act_hi, act_lo = split_two(act_sum)
        both = nt(jnp.concatenate([act_hi, act_lo], 0), w2t[...])
        folded = both[:4] + both[SMALL : SMALL + 4]
        mx_s[...] = jnp.concatenate([folded[:, : width // 2], folded[:, width // 2 :]], 0)
        for shift in (1, 2, 3):
            spread(mx_s, mx_r, mxs, mxr, shift).start()
        mx_r[me] = mx_s[...]
        h_mean = stack(hsum) * (1.0 / seq)
        for shift in (1, 2, 3):
            remote(
                mx_s, mx_r.at[lax.rem(me + 4 - shift, 4)], mxs.at[shift - 1], mxr.at[shift - 1], mate
            ).wait_recv()
        halves = mx_r[0] + mx_r[1] + mx_r[2] + mx_r[3]
        mlp = jnp.concatenate(
            [jnp.concatenate([halves[:4], halves[4:]], 1), jnp.zeros((SMALL - 4, width), F32)], 0
        )
        average = h_mean + mlp * (1.0 / seq) + vec_f[8:9, :]
        normed3, inverse3 = normalise(average)
        pooled = (normed3 * gain3 + shift3).astype(BF16)
        logits = nt(pooled, head[...])
        class_ok = lax.broadcasted_iota(jnp.int32, (1, head.shape[0]), 1) < classes
        logits = jnp.where(class_ok, logits, NEG)
        top = jnp.max(logits, -1, keepdims=True)
        exp_l = jnp.exp(logits - top)
        total_l = jnp.sum(exp_l, -1, keepdims=True)
        hot_row = lax.broadcasted_iota(jnp.int32, (SMALL, n_head), 0)
        hot_lane = lax.broadcasted_iota(jnp.int32, (SMALL, n_head), 1)
        hot = jnp.zeros((SMALL, n_head), F32)
        for n in range(4):
            label = label_ref[index_ref[0, step, n]]
            hot = jnp.where((hot_row == n) & (hot_lane == label), 1.0, hot)
        each = top + jnp.log(total_l) - jnp.sum(jnp.where(class_ok, logits, 0.0) * hot, -1, keepdims=True)
        loss = jnp.sum(jnp.where(small_ok, each, 0.0), 0, keepdims=True) * 0.25
        live = jnp.where(step < taken, 1.0, 0.0)
        rho = jnp.where(step < taken, MOMENTUM_RHO, 1.0)
        loss_tile = live * loss
        d_logits = jnp.where(small_ok, (exp_l / total_l - hot) * 0.25, 0.0).astype(BF16)
        d_head = tn(d_logits, pooled)
        head_g[...] = d_head
        d_pooled = nn(d_logits, head[...])
        d_average = norm_grad(d_pooled, gain3, normed3, inverse3)
        d_token = d_average * (1.0 / seq)
        d_mlp = d_token.astype(BF16)
        dact[...] = nn(d_mlp, w2t[...])
        for r in range(4):
            scal[r] = jnp.broadcast_to(d_token[r : r + 1, :], (8, width))
        vec_g[...] = jnp.zeros_like(vec_g)
        vec_g[4:5, :] = jnp.sum(d_pooled * normed3, 0, keepdims=True)
        vec_g[5:6, :] = jnp.sum(d_pooled, 0, keepdims=True)
        vec_g[8:9, :] = jnp.sum(d_average, 0, keepdims=True)
        low_at = pl.ds(pl.multiple_of(step * SMALL, SMALL), SMALL)
        low_d[low_at, :] = d_mlp
        low_a[low_at, :] = act_sum
        gram_d = nt(d_mlp, d_mlp)
        gram_a = nt(act_hi, act_hi) + nt(act_hi, act_lo) + nt(act_lo, act_hi)
        own_squares = total(gram_d * gram_a)

        for n in range(4):
            scal[4 + n] = jnp.broadcast_to(dact[n : n + 1, :], (8, width))
        bsum[...] = jnp.zeros_like(bsum)
        vacc[...] = jnp.zeros_like(vacc)

        def upper_partial(n):
            at = pl.ds(pl.multiple_of(n * pad, 16), 2 * pad)
            rate = jnp.concatenate(
                [jnp.broadcast_to(scal[4 + n + i][0:1, :], (pad, width)) for i in range(2)], 0
            )
            g = (rate * slope[at, :]).astype(BF16)
            dpre[at, :] = g
            bsum[...] = bsum[...] + fold(g.astype(F32))
            return nt(g, w1[...])

        other = upper_partial(oth0)
        for k in (0, 1):
            s1[k] = other[k * pad : (k + 1) * pad].astype(BF16)
            to_mate(k).start()
        own = upper_partial(own0)
        for k in (0, 1):
            to_mate(k).wait_recv()
            part = own[k * pad : (k + 1) * pad] + r1[k].astype(F32)
            chip[k] = part
            s2[k] = part.astype(BF16)
            to_across(0, k).start()

        ssq[...] = jnp.zeros_like(ssq)
        w1_g = slope

        def weight_grad(left, right, out, which):
            def tile(j, carry):
                at = pl.ds(pl.multiple_of(j * LANE, LANE), LANE)
                g = tn(left[:, at], right[...])
                out[at, :] = g
                ssq[which] = ssq[which] + fold(g * g)
                return carry

            lax.fori_loop(0, width // LANE, tile, 0)

        def embedding_grad(image, left, adds, last):
            def tile(j, carry):
                at = pl.ds(pl.multiple_of(j * LANE, LANE), LANE)
                g = tn(left[rows(image), at], xbuf[slot, rows(image), :])
                if adds:
                    g = g + wet_g[at, :]
                if last:
                    ssq[3] = ssq[3] + fold(g * g)
                wet_g[at, :] = g
                return carry

            lax.fori_loop(0, width // LANE, tile, 0)

        weight_grad(ubuf, dpre, w1_g, 0)

        for k in (0, 1):
            normed, inverse = normalise(h1own[k])
            h1own[k] = normed
            inverses[k] = inverse
            normed, inverse = normalise(h0[rows(own0 + k), :])
            h0[rows(own0 + k), :] = normed
            inverses[2 + k] = inverse

        def attention_partial(n):
            own_columns = jnp.concatenate(
                [
                    wot[:, pl.ds(pl.multiple_of(me * 128, 128), 128)],
                    wot[:, pl.ds(pl.multiple_of(4 * 128 + (me // 2) * 128, 128), 128)],
                ],
                1,
            )
            wide = nn(datt[rows(n), :], own_columns)
            thirds = jnp.where(core == 1, swap(wide[:, 128:]), wide[:, 128:])
            thirds = jnp.where(low_half((pad, 128)), thirds, 0.0)
            d_ctx = jnp.concatenate([wide[:, :128], thirds], 1).astype(BF16)
            projected = qkv[rows(n), :]
            q, k, v = projected[:, :LANE], projected[:, LANE : 2 * LANE], projected[:, 2 * LANE :]
            d_q = jnp.zeros((pad, LANE), F32)
            d_k = jnp.zeros((pad, LANE), F32)
            d_v = jnp.zeros((pad, LANE), F32)
            for h in range(3):
                part = of_head(d_ctx, h)
                p = prob[n * 3 + h]
                again = p.astype(F32)
                d_p = nt(part, v)
                inner = d_p - jnp.sum(d_p * again, -1, keepdims=True)
                d_s = (again * inner).astype(BF16)
                d_v = d_v + tn(p, part)
                d_q = d_q + nn(d_s, of_head(k, h))
                d_k = d_k + tn(d_s, of_head(q, h))
            d_all = jnp.concatenate([d_q * scale, d_k * scale, d_v], 1).astype(BF16)
            qkv[rows(n), :] = d_all
            return nt(d_all, wqkv[...])

        for k in (0, 1):
            to_across(0, k).wait_recv()
            d_upper = chip[k] + r2[k].astype(F32)
            normed = h1own[k]
            d_state = norm_grad(d_upper, gain2, normed, inverses[k]) + scal[own0 + k][0:1, :]
            d_state = jnp.where(token, d_state, 0.0)
            h1own[k] = d_state
            datt[rows(own0 + k), :] = d_state.astype(BF16)
            gradient_to_mate(datt, 0, own0 + k, k).start()
            vacc[0] = vacc[0] + fold(d_upper * normed)
            vacc[1] = vacc[1] + fold(d_upper)
            vacc[2] = vacc[2] + fold(d_state)
            own = attention_partial(own0 + k)
            remote(
                datt.at[sent_rows(oth0 + k)], datt.at[sent_rows(oth0 + k)], das.at[k], dar.at[k], mate
            ).wait_recv()
            other = attention_partial(oth0 + k)
            to_mate(k).wait_send()
            s1[k] = other.astype(BF16)
            to_mate(k).start()
            to_mate(k).wait_recv()
            own = own + r1[k].astype(F32)
            chip[k] = own
            to_across(0, k).wait_send()
            s2[k] = own.astype(BF16)
            to_across(1, k).start()

        weight_grad(datt, oall, wot_g, 1)
        weight_grad(abuf, qkv, wqkv_g, 2)

        d_bias = jnp.sum(bsum[...], 0, keepdims=True)
        own_squares = own_squares + total(ssq[0] + ssq[2]) + total(d_bias * d_bias)
        shared = total(ssq[1] + fold(head_g[...] * head_g[...]))

        d_emb = ubuf
        for k in (0, 1):
            to_across(1, k).wait_recv()
            d_normed = chip[k] + r2[2 + k].astype(F32)
            normed = h0[rows(own0 + k), :]
            d_state = h1own[k] + norm_grad(d_normed, gain1, normed, inverses[2 + k])
            d_emb[rows(own0 + k), :] = d_state.astype(BF16)
            gradient_to_mate(d_emb, 1, own0 + k, k).start()
            vacc[3] = vacc[3] + fold(d_normed * normed)
            vacc[4] = vacc[4] + fold(d_normed)
            vacc[5] = vacc[5] + fold(jnp.where(row_id >= 1, d_state, 0.0))
            if k == 0:
                pos_g[...] = d_state
            else:
                pos_g[...] = pos_g[...] + d_state
                pos_to_mate().start()
                vec_to_mate().start()
            embedding_grad(own0 + k, d_emb, k == 1, False)
            remote(
                d_emb.at[sent_rows(oth0 + k)], d_emb.at[sent_rows(oth0 + k)],
                das.at[2 + k], dar.at[2 + k], mate,
            ).wait_recv()
            embedding_grad(oth0 + k, d_emb, True, k == 1)
        pos_to_mate().wait()
        vec_to_mate().wait()
        pos_g[...] = pos_g[...] + pos_r[...]
        sums = [jnp.sum(vacc[r] + vec_r[r], 0, keepdims=True) for r in range(6)]
        vec_g[0:1, :] = sums[3]
        vec_g[1:2, :] = sums[4]
        vec_g[2:3, :] = sums[0]
        vec_g[3:4, :] = sums[1]
        vec_g[6:7, :] = sums[5]
        vec_g[7:8, :] = sums[2]
        shared = (
            shared
            + total(ssq[3] + fold(pos_g[...] * pos_g[...]))
            + total(vec_g[...] * vec_g[...])
        )
        for message in range(6):
            o_to_mate(message).wait_send()
            o_across(message).wait_send()
            o_forward(message).wait_send()
        for k in (0, 1):
            to_mate(k).wait_send()
            to_across(1, k).wait_send()
            gradient_to_mate(datt, 0, own0 + k, k).wait_send()
            gradient_to_mate(d_emb, 1, own0 + k, k).wait_send()
        for shift in (1, 2, 3):
            spread(mx_s, mx_r, mxs, mxr, shift).wait_send()
        first_lane = lax.broadcasted_iota(jnp.int32, (8, 128), 1) < 64
        nx_s[...] = jnp.where(first_lane, own_squares + 0.25 * shared, loss_tile)
        for shift in (1, 2, 3):
            spread(nx_s, nx_r, nxs, nxr, shift).start()
        nx_r[me] = nx_s[...]

        @pl.when(step == steps - 1)
        def _():
            for which in (0, 1, 3, 4):
                load(which).start()

        for shift in (1, 2, 3):
            remote(
                nx_s, nx_r.at[lax.rem(me + 4 - shift, 4)], nxs.at[shift - 1], nxr.at[shift - 1], mate
            ).wait_recv()
        norm = jnp.sqrt((nx_r[0] + nx_r[1] + nx_r[2] + nx_r[3]))
        factor = live * (CLIP_LIMIT / jnp.maximum(norm, CLIP_LIMIT))
        norm_out[step] = live * norm
        loss_all[...] = loss_all[...] + nx_r[0]
        for shift in (1, 2, 3):
            spread(nx_s, nx_r, nxs, nxr, shift).wait_send()
        fac = factor[0:1, 0:1]

        low_row = lax.broadcasted_iota(jnp.int32, low_b.shape, 0) // SMALL
        low_b[...] = jnp.where(low_row == step, fac, rho * low_b[...])
        low_w[...] = low_w[...] + live * low_b[...]
        factors = (LOCAL_RATE * low_w[:, 0:1]) * low_a[...]
        factor_kept[...] = factor

        def small_update(full, mom, grad):
            mom[...] = rho * mom[...] + fac * grad
            full[...] = full[...] - (live * LOCAL_RATE) * mom[...]

        small_update(pos_f, pos_m, pos_g[...])
        small_update(vec_f, vec_m, vec_g[...])
        small_update(bias_f, bias_m, jnp.broadcast_to(d_bias, (8, width)))
        table = (
            (wqkv, wqkv_f, wqkv_m, wqkv_g),
            (w1, w1_f, w1_m, w1_g),
            (wot, wot_f, wot_m, wot_g),
            (wet, wet_f, wet_m, wet_g),
        )

        @pl.when(step < steps - 1)
        def _():
            load(2).start()
            update_rows((table[0], table[3]), rho, live, fac)

        @pl.when(step == steps - 1)
        def _():
            examples = jnp.full((1, 1), count_ref[0].astype(F32))
            factor_sum = jnp.zeros((), F32)
            for k in range(steps):
                worth = (1.0 - MOMENTUM_RHO ** (k + 1)) / (1.0 - MOMENTUM_RHO)
                factor_sum = factor_sum + jnp.where(k < taken, worth, 0.0)
            factor_sum = jnp.full((1, 1), factor_sum)
            share = examples / factor_sum
            for which in (0, 1, 3, 4):
                load(which).wait()

            def ended(at, full, mom, grad, lanes):
                m = rho * mom[at, lanes] + fac * grad[at, lanes]
                return full[at, lanes] - (live * LOCAL_RATE) * m

            outs = (
                (w1, main_out.at[:, 0:width]),
                (wet, table_out.at[:, 0:width]),
                (raw, main_out.at[:, width : 2 * width]),
                (rest, table_out.at[:, width : width + REST]),
            )
            copies = [
                pltpu.make_async_copy(src, dst, osem.at[i]) for i, (src, dst) in enumerate(outs)
            ]
            for i, (low, full, mom, grad) in enumerate((table[1], table[3])):

                def finish_square(j, carry):
                    at = pl.ds(pl.multiple_of(j * 64, 64), 64)
                    w = ended(at, full, mom, grad, slice(None))
                    low[at, :] = (share * (low[at, :].astype(F32) - w)).astype(BF16)
                    return carry

                lax.fori_loop(0, width // 64, finish_square, 0)
                copies[i].start()

            def finish(j, carry):
                at = pl.ds(pl.multiple_of(j * 64, 64), 64)
                three = tiles(ended(at, wqkv_f, wqkv_m, wqkv_g, slice(None)))
                _, full, mom, grad = table[2]
                wo_first = ended(at, full, mom, grad, pl.ds(pl.multiple_of(me * 128, 128), 128))
                wo_last = ended(
                    at, full, mom, grad, pl.ds(pl.multiple_of(4 * 128 + (me // 2) * 128, 128), 128)
                )
                wo_last = jnp.where(core == 1, swap(wo_last), wo_last)
                packed = join(
                    pack_two(three[0:2], three[2:4]) + pack_two(three[4:6], [wo_first, wo_last])
                )
                raw[at, :] = (share * (raw[at, :].astype(F32) - packed)).astype(BF16)
                return carry

            lax.fori_loop(0, width // 64, finish, 0)
            copies[2].start()
            small_update(head_f, head_m, head_g[...])
            h0[0:REST, :] = jnp.transpose(rest[...].astype(F32))
            for ref, begin, count in ((pos_f, 0, seq), (vec_f, vec_at, 9), (head_f, head_at, classes)):
                h0[begin : begin + count, :] = share * (h0[begin : begin + count, :] - ref[0:count, :])
            rest[...] = jnp.transpose(h0[0:REST, :]).astype(BF16)
            copies[3].start()
            d_bias_all = share * (bias_start[0:1, :] - bias_f[0:1, :])
            for r in range(width // 128):
                tile_out[r : r + 1, :] = d_bias_all[:, 128 * r : 128 * (r + 1)]
            lane = lax.broadcasted_iota(jnp.int32, (1, 128), 1)
            loss_sum = loss_all[0:1, 64:65]
            mean_loss = examples * loss_sum / jnp.full((1, 1), taken.astype(F32))
            scalars = jnp.where(lane == 0, examples, jnp.where(lane == 1, mean_loss, examples * factor_sum))
            tile_out[width // 128 : width // 128 + 1, :] = jnp.where(lane < 3, scalars, 0.0)
            tile_out[width // 128 + 1 :, :] = jnp.zeros((7 - width // 128, 128), F32)
            used = 4 * steps
            wanted_row = lax.broadcasted_iota(jnp.int32, (used, steps * SMALL), 0)
            wanted_row = (wanted_row // 4) * SMALL + lax.rem(wanted_row, 4)
            picker = (lax.broadcasted_iota(jnp.int32, (used, steps * SMALL), 1) == wanted_row).astype(BF16)
            low_left = nn(picker, (share * factors).astype(BF16)).astype(BF16)
            low_right = nn(picker, low_d[...])
            part = width // clients
            kept_lanes = lax.broadcasted_iota(jnp.int32, (used, 128), 1) < part
            for j in range(clients):
                low_out[j, :, 0:width] = low_left
                turned = pltpu.roll(low_right, (width - part * j) % width, 1) if j else low_right
                low_out[j, :, width : width + 128] = jnp.where(kept_lanes, turned[:, :128], 0.0).astype(BF16)
            for copy in copies:
                copy.wait()

        return carry

    lax.fori_loop(0, steps, one_step, 0)


def local_training(tau, counts, labels, index, patches, main, wo, table, bias, clients, pad, seq, classes):
    steps = patches.shape[0]
    width = main.shape[0]
    n_all = 4 * pad
    n_head = (classes + 127) // 128 * 128
    n_low = steps * SMALL
    vmem = pltpu.VMEM
    dma = pltpu.SemaphoreType.DMA
    anywhere = pl.BlockSpec(memory_space=pl.ANY)
    inside = pl.BlockSpec(memory_space=pltpu.VMEM)
    square = (width, width)
    out_shape = (
        jax.ShapeDtypeStruct((width, 2 * width), BF16),
        jax.ShapeDtypeStruct(table.shape, BF16),
        jax.ShapeDtypeStruct((clients, 4 * steps, width + 128), BF16),
        jax.ShapeDtypeStruct((8, 128), F32),
        jax.ShapeDtypeStruct((steps, 8, 128), F32),
    )
    scratch = [
        vmem(square, BF16), vmem(square, BF16), vmem(square, BF16), vmem(square, BF16),
        vmem(square, BF16), vmem((n_head, width), BF16),
    ]
    for _ in range(2):
        scratch += [
            vmem(square, F32), vmem(square, F32), vmem(square, F32), vmem(square, F32),
            vmem((pad, width), F32), vmem((n_head, width), F32), vmem((SMALL, width), F32),
            vmem((8, width), F32),
        ]
    scratch += [
        vmem(square, F32), vmem(square, F32), vmem(square, F32), vmem((pad, width), F32),
        vmem((n_head, width), F32), vmem((SMALL, width), F32),
        vmem((2, n_all, width), BF16), vmem((n_all, width), F32), vmem((n_all, width), F32),
        vmem((12, pad, pad), BF16), vmem((n_all, width), BF16), vmem((n_all, width), BF16),
        vmem((n_all, width), BF16), vmem((2, pad, 4 * 128), BF16), vmem((n_all, width), BF16),
        vmem((n_all, width), BF16), vmem((3, pad, width), F32), vmem((n_all, width), BF16),
        vmem((2, pad, width), F32), vmem((4, pad, 1), F32),
        vmem((4, 8, width), F32), vmem((4, 8, width), F32), vmem((SMALL, width), F32),
        vmem((8, width), F32), vmem((6, 8, width), F32), vmem((4, 8, width), F32),
        vmem((n_low, width), BF16), vmem((n_low, width), F32), vmem((n_low, 128), F32),
        vmem((n_low, 128), F32), vmem((8, 8, width), F32), vmem((8, 128), F32), vmem((8, 128), F32),
        vmem((8, LANE), F32), vmem((8, width), F32),
        vmem((2, pad, width), BF16), vmem((2, pad, width), BF16), vmem((2, pad, width), BF16),
        vmem((4, pad, width), BF16), vmem((8, width // 2), F32), vmem((4, 8, width // 2), F32),
        vmem((8, 128), F32), vmem((4, 8, 128), F32), vmem((pad, width), F32),
        vmem((6, 8, width), F32),
        dma((9,)), dma((2,)), dma((6,)), dma((6,)), dma((6,)), dma((6,)), dma((6,)), dma((6,)),
        dma((2,)), dma((2,)), dma((4,)), dma((4,)), dma((4,)), dma((4,)), dma((2,)), dma((2,)),
        dma((3,)), dma((3,)), dma((3,)), dma((3,)), dma((6,)),
    ]
    return pl.pallas_call(
        functools.partial(train_kernel, (steps, seq, pad, classes, clients)),
        out_shape=out_shape,
        in_specs=[pl.BlockSpec(memory_space=pltpu.SMEM)] * 4 + [anywhere] * 4 + [inside],
        out_specs=(anywhere,) * 2 + (inside,) * 3,
        scratch_shapes=scratch,
        compiler_params=pltpu.CompilerParams(
            collective_id=0, has_side_effects=True, vmem_limit_bytes=VMEM_LIMIT
        ),
        name="local_training",
    )(tau, counts, labels, index, patches, main, wo, table, bias)


def place_patches(chosen_ref, pool_ref, out_ref):
    seq_rows, width = pool_ref.shape[1], pool_ref.shape[2]
    pad = out_ref.shape[1]
    below = jnp.zeros((pad - 1 - seq_rows, width), F32)
    whole = jnp.concatenate([jnp.zeros((1, width), F32), pool_ref[0].astype(F32), below], 0)
    out_ref[0] = whole.astype(BF16)


def pick_patches(pool, chosen, pad):
    count = chosen.shape[0]
    _, patch_rows, width = pool.shape
    return pl.pallas_call(
        place_patches,
        out_shape=jax.ShapeDtypeStruct((count, pad, width), BF16),
        grid_spec=pltpu.PrefetchScalarGridSpec(
            num_scalar_prefetch=1,
            grid=(count,),
            in_specs=[pl.BlockSpec((1, patch_rows, width), lambda i, ids: (ids[i], 0, 0))],
            out_specs=pl.BlockSpec((1, pad, width), lambda i, ids: (i, 0, 0)),
        ),
        name="pick_patches",
    )(chosen, pool)


def ring_places(clients):
    depth = clients // 2
    client = lax.axis_index("client")
    member = lax.axis_index("tensor")
    core = lax.rem(member, 2)
    return (
        depth, client, client // 2, lax.rem(client, 2), member, core, member // 2,
        member + 1 - 2 * core, lax.rem(member + 2, 4),
    )


def send(src, dst, send_sem, recv_sem, client, member):
    return pltpu.make_async_remote_copy(
        src_ref=src, dst_ref=dst, send_sem=send_sem, recv_sem=recv_sem,
        device_id={"client": client, "tensor": member}, device_id_type=MESH,
    )


def span(start, size, unit):
    return pl.ds(pl.multiple_of(start, unit), size)


def gather_kernel(
    clients, index_ref, in_ref, out_ref, table_in, pool_ref, main_out, wo_out, table_out, x_out,
    main_ref, table_ref, wide_in, wide_out, pool_buf, x_buf, pool_sem, x_sem, up_s, up_r, down_s, down_r, y_s, y_r, mate_s, mate_r, x_s, x_r, on_s, on_r, own_sem, keep_sem,
):
    depth, client, z, y, member, core, chip_x, mate, across = ring_places(clients)
    block = main_ref.shape[0]
    half = block // 2
    columns = table_ref.shape[1] // 2
    peer = client + 1 - 2 * y

    wide = main_ref.shape[1]
    tail = wide - LANE

    def table_part(origin, who):
        return table_out.at[
            span(origin * block + (who // 2) * half, half, half),
            span(lax.rem(who, 2) * columns, columns, 128),
        ]

    def wo_part(origin, who):
        return wo_out.at[span(origin * block, block, block), span(who * LANE, LANE, LANE)]

    def shared(origin, who):
        return (wo_part(origin, who), table_part(origin, who))

    def main_part(origin, lanes):
        return main_out.at[span(origin * block, block, block), lanes]

    early, front, back = slice(0, wide // 6), slice(wide // 6, 2 * wide // 3), slice(2 * wide // 3, wide)

    def beside(origin):
        return origin + 1 - 2 * lax.rem(origin, 2)

    def landed(origin):
        return (
            main_part(origin, back), table_part(origin, member), main_part(origin, front),
            main_part(origin, early), main_part(beside(origin), early),
        )

    own_table = table_ref.at[span(chip_x * half, half, half), span(core * columns, columns, 128)]
    own_pieces = (
        main_ref.at[:, back], own_table, main_ref.at[:, front], main_ref.at[:, early],
        main_part(peer, early),
    )

    def given(origin, mine):
        if mine:
            return (main_ref.at[:, tail:wide], own_table)
        return (main_part(origin, slice(tail, wide)), table_part(origin, member))

    def message(origin, mine, send_sem, recv_sem, index, to, part):
        sources = own_pieces if mine else landed(origin)
        return [
            send(src, dst, send_sem.at[p, index], recv_sem.at[p, index], to, member)
            for p, (src, dst) in enumerate(zip(sources, landed(origin)))
        ][part]

    first, second, third, over_all, crossing = slice(0, 2), slice(2, 3), slice(3, 5), slice(0, 3), slice(3, 4)

    def up(origin, i, part, mine=False):
        return message(origin, mine, up_s, up_r, i, client + 2, part)

    def down(origin, i, part, mine=False):
        return message(origin, mine, down_s, down_r, i, client - 2, part)

    def over(origin, part, mine=False):
        return message(origin, mine, y_s, y_r, origin // 2, peer, part)

    def give(origin, mine, send_sem, recv_sem, to):
        return [
            send(src, dst, send_sem.at[p, origin], recv_sem.at[p, origin], client, to)
            for p, (src, dst) in enumerate(zip(given(origin, mine), shared(origin, member)))
        ]

    def keep(origin, mine=False):
        return pltpu.make_async_copy(given(origin, mine)[0], wo_part(origin, member), keep_sem.at[origin])

    def share(origin, mine=False):
        return give(origin, mine, mate_s, mate_r, mate) + give(origin, mine, x_s, x_r, across)

    def from_across(origin):
        return [
            send(dst, dst, x_s.at[p, origin], x_r.at[p, origin], client, across)
            for p, dst in enumerate(shared(origin, across))
        ]

    def pass_on(origin):
        return [
            send(dst, dst, on_s.at[p, origin], on_r.at[p, origin], client, mate)
            for p, dst in enumerate(shared(origin, across))
        ]

    def start(copies):
        for copy in copies:
            copy.start()

    def arrived(copies):
        for copy in copies:
            copy.wait_recv()

    def sent(copies):
        for copy in copies:
            copy.wait_send()

    has_up, has_down = z < depth - 1, z > 0

    barrier = pltpu.get_barrier_semaphore()

    def hello(to_client, to_member):
        pl.semaphore_signal(
            barrier, inc=1, device_id={"client": to_client, "tensor": to_member}, device_id_type=MESH
        )

    hello(peer, member)
    for shift in (1, 2, 3):
        hello(client, lax.rem(member + shift, 4))
    for shift in range(1, depth):
        hello(2 * lax.rem(z + shift, depth) + y, member)
    wide_in[...] = jnp.zeros_like(wide_in)
    wide_out[...] = jnp.zeros_like(wide_out)
    table_ref[...] = jnp.zeros_like(table_ref)
    table_ref[:, 0 : table_in.shape[1]] = table_in[...]

    def in_slab(i):
        wide_in[i, :, 0 : in_ref.shape[2]] = in_ref[i].astype(F32)
        return tiles(wide_in[i])

    def out_slab(i):
        wide_out[i, 0 : out_ref.shape[1], 0:block] = out_ref[i].astype(F32)
        return tiles(jnp.transpose(wide_out[i])[:block])

    ordered = [in_slab(i) for i in (3, 4, 5, 6)] + [out_slab(i) for i in (1, 2, 3, 4)]
    ordered += [in_slab(i) for i in (0, 1, 2)] + [out_slab(0)]
    for i in range(0, 12, 2):
        packed = jnp.concatenate(pack_two(ordered[i], ordered[i + 1]), 1)
        main_ref[:, 192 * i : 192 * (i + 2)] = packed.astype(BF16)

    pl.semaphore_wait(barrier, 3 + depth)

    def line_start(part):
        @pl.when(has_up)
        def _():
            start(up(client, 0, part, True))

        @pl.when(has_down)
        def _():
            start(down(client, 0, part, True))

    start(over(client, crossing, True))
    start(over(client, first, True))
    line_start(first)
    start(over(client, second, True))
    line_start(second)
    start(share(client, True))
    keep(client, True).start()
    local = [
        pltpu.make_async_copy(src, dst, own_sem.at[p])
        for p, (src, dst) in enumerate(zip(own_pieces[:4], landed(client)))
    ]
    start(local)

    _, steps, each = index_ref.shape
    images = steps * each
    pool_size = pool_buf.shape[1] // 8
    patch_rows = pool_ref.shape[0] // pool_size
    pad = x_out.shape[1]

    def base(b):
        return lax.min(lax.max(8 * b - 1, 0), patch_rows - 8)

    deep = pool_buf.shape[0]

    def pool_load(b):
        k = lax.rem(b, deep)
        return pltpu.make_async_copy(
            pool_ref.at[span(base(b) * pool_size, 8 * pool_size, 32), :], pool_buf.at[k], pool_sem.at[k]
        )

    def x_store(b):
        k = lax.rem(b, deep)
        return pltpu.make_async_copy(x_buf.at[k], x_out.at[:, span(8 * b, 8, 8), :], x_sem.at[k])

    for b in range(deep - 1):
        pool_load(b).start()
    lane = lax.broadcasted_iota(jnp.int32, (8 * images, 8 * pool_size), 1)
    select_row = lax.broadcasted_iota(jnp.int32, (8 * images, 1), 0)
    line_row = lax.rem(select_row, 8)
    chosen = jnp.zeros((8 * images, 1), jnp.int32)
    for i in range(images):
        chosen = jnp.where(select_row // 8 == i, index_ref[0, i // each, i % each], chosen)

    def pick(b, carry):
        k = lax.rem(b, deep)
        pool_load(b).wait()

        @pl.when(b < pad // 8 - (deep - 1))
        def _():
            pool_load(b + deep - 1).start()

        wanted = (8 * b - 1 + line_row - base(b)) * pool_size + chosen
        picked = nn((lane == wanted).astype(BF16), pool_buf[k]).astype(BF16)

        @pl.when(b >= deep)
        def _():
            x_store(b - deep).wait()

        x_buf[k] = picked.reshape(images, 8, picked.shape[1])
        x_store(b).start()
        return carry

    lax.fori_loop(0, pad // 16, pick, 0)

    def line(d, act):
        @pl.when(z >= d)
        def _():
            act(client - 2 * d, True)

        @pl.when(z < depth - d)
        def _():
            act(client + 2 * d, False)

    def across_line(d, act):
        if d == 0:
            act(peer, True)
            return

        @pl.when(z >= d)
        def _():
            act(peer - 2 * d, True)

        @pl.when(z < depth - d)
        def _():
            act(peer + 2 * d, False)

    def line_in(d, part):
        def act(origin, below):
            line_s, line_r = (up_s, up_r) if below else (down_s, down_r)
            arrived(message(origin, False, line_s, line_r, d - 1, peer, part))
            if d < depth - 1:

                @pl.when(has_up if below else has_down)
                def _():
                    start(up(origin, d, part) if below else down(origin, d, part))

            if part is not third:
                start(over(origin, part))
            if part is first:
                start(share(origin))
                keep(origin).start()

        return act

    def y_in(origin, below):
        arrived(over(origin, first))
        start(share(origin))
        keep(origin).start()

    def forward(origin, below=True):
        arrived(from_across(origin))
        start(pass_on(origin))

    for d in range(1, depth + 1):
        if d < depth:
            line(d, line_in(d, first))
        across_line(d - 1, y_in)
        if d < depth:
            line(d, line_in(d, second))
        if d == 1:
            arrived(over(peer, crossing))
            line_start(third)
        else:
            line(d - 1, line_in(d - 1, third))
        if d == 1:
            lax.fori_loop(pad // 16, pad // 8, pick, 0)
            for b in range(pad // 8 - deep, pad // 8):
                x_store(b).wait()
            forward(client)
        else:
            line(d - 1, forward)
            across_line(d - 2, forward)
    across_line(depth - 1, forward)
    for d in range(depth):
        across_line(d, lambda origin, below: arrived(over(origin, second)))

    for copy in local:
        copy.wait()
    for origin in range(clients):
        sent(share(origin))
        sent(pass_on(origin))
        keep(origin).wait()
        arrived([
            send(dst, dst, mate_s.at[p, origin], mate_r.at[p, origin], client, mate)
            for p, dst in enumerate(shared(origin, mate))
        ])
        arrived([
            send(dst, dst, on_s.at[p, origin], on_r.at[p, origin], client, mate)
            for p, dst in enumerate(shared(origin, lax.rem(mate + 2, 4)))
        ])
    sent(over(client, crossing))
    for d in range(depth):
        sent(over(2 * d + y, over_all))

        @pl.when(has_up & (z >= d))
        def _():
            if d < depth - 1:
                sent(up(client - 2 * d, d, slice(0, 5)))

        @pl.when(has_down & (z < depth - d))
        def _():
            if d < depth - 1:
                sent(down(client + 2 * d, d, slice(0, 5)))


def gather_weights(clients, index, in_bf, out_bf, table_t, pool, pad):
    depth = clients // 2
    dma = pltpu.SemaphoreType.DMA
    anywhere = pl.BlockSpec(memory_space=pl.ANY)
    inside = pl.BlockSpec(memory_space=pltpu.VMEM)
    slabs, own, group = in_bf.shape
    width = own * clients
    packed = (slabs + out_bf.shape[0]) * group
    table_lanes = width + REST
    hops = depth - 1
    pool_size, patch_rows, features = pool.shape
    images = index.shape[1] * index.shape[2]
    rows = jnp.transpose(pool, (1, 0, 2)).reshape(patch_rows * pool_size, features)
    return pl.pallas_call(
        functools.partial(gather_kernel, clients),
        out_shape=(
            jax.ShapeDtypeStruct((width, packed), BF16),
            jax.ShapeDtypeStruct((width, 4 * LANE), BF16),
            jax.ShapeDtypeStruct((width, table_lanes), BF16),
            jax.ShapeDtypeStruct((images, pad, features), BF16),
        ),
        in_specs=[pl.BlockSpec(memory_space=pltpu.SMEM)] + [inside] * 3 + [anywhere],
        out_specs=(anywhere,) * 4,
        scratch_shapes=[
            pltpu.VMEM((own, packed), BF16), pltpu.VMEM((own, table_lanes), BF16),
            pltpu.VMEM((slabs, own, LANE), F32), pltpu.VMEM((out_bf.shape[0], LANE, 128), F32),
            pltpu.VMEM((6, 8 * pool_size, features), BF16), pltpu.VMEM((6, images, 8, features), BF16),
            dma((6,)), dma((6,)),
            dma((5, hops)), dma((5, hops)), dma((5, hops)), dma((5, hops)), dma((4, depth)),
            dma((4, depth)),
        ] + [dma((2, clients))] * 6 + [dma((4,)), dma((clients,))],
        compiler_params=pltpu.CompilerParams(collective_id=1, has_side_effects=True),
        name="gather_weights",
    )(index, in_bf, out_bf, table_t, rows)


def reduce_kernel(
    clients, main_in, table_in, low_in, tile_in, main_out, table_out, low_out, tile_out,
    own_main, own_table, y_main, y_table, zs_main, zs_table, zr_main, zr_table, rl_main, rl_table,
    whole, low_all, tile_all, own_sem, y_s, y_r, z_s, z_r, rl_s, rl_r, low_s, low_r, tile_s, tile_r, q_s, q_r, keep_sem,
):
    depth, client, z, y, member, core, chip_x, mate, across = ring_places(clients)
    block = own_main.shape[1]
    half, columns = own_table.shape[1], own_table.shape[2]
    peer = client + 1 - 2 * y
    cut = own_main.shape[2] // 2
    lanes = (None, slice(0, cut), slice(cut, 2 * cut))
    parts = (0, 1, 2)

    def source(owner, p):
        if p == 0:
            return table_in.at[
                span(owner * block + chip_x * half, half, half), span(core * columns, columns, 128)
            ]
        return main_in.at[span(owner * block, block, block), lanes[p]]

    def slot(table_ref, main_ref, i, p):
        return table_ref.at[i] if p == 0 else main_ref.at[i, :, lanes[p]]

    def own_load(level, p):
        return pltpu.make_async_copy(
            source(2 * level + y, p), slot(own_table, own_main, level, p), own_sem.at[p, level]
        )

    def over(level, p):
        return send(
            source(2 * level + 1 - y, p), slot(y_table, y_main, level, p),
            y_s.at[p, level], y_r.at[p, level], peer, member,
        )

    side = z // 2
    outer = z == 3 * side
    near = z + 1 - 2 * lax.rem(z, 2)
    levels = (3 * (1 - side), 2 - side, near, z)

    def relay(i, p):
        return send(
            slot(zs_table, zs_main, i, p), slot(rl_table, rl_main, i, p),
            rl_s.at[p, i], rl_r.at[p, i], 2 * near + y, member,
        )

    def onward(i, p):
        last = i // 2
        return send(
            slot(zs_table, zs_main, i, p), slot(zr_table, zr_main, last, p),
            z_s.at[p, i], z_r.at[p, last], 2 * levels[i] + y, member,
        )

    def came(last, p):
        return send(
            slot(zs_table, zs_main, 0, p), slot(zr_table, zr_main, last, p),
            z_s.at[p, 0], z_r.at[p, last], peer, member,
        )

    def small(shift):
        to = lax.rem(client + shift, clients)
        return [
            send(low_in.at[to], low_all.at[client], low_s.at[shift - 1], low_r.at[shift - 1], to, member),
            send(tile_in, tile_all.at[client], tile_s.at[shift - 1], tile_r.at[shift - 1], to, member),
        ]

    def small_from(shift):
        origin = lax.rem(client + clients - shift, clients)
        return [
            send(low_in.at[origin], low_all.at[origin], low_s.at[shift - 1], low_r.at[shift - 1], origin, member),
            send(tile_in, tile_all.at[origin], tile_s.at[shift - 1], tile_r.at[shift - 1], origin, member),
        ]

    def quarter(who):
        return whole.at[span((who // 2) * half, half, half), span(lax.rem(who, 2) * columns, columns, 128)]

    def pass_quarter(who, index, to):
        return send(quarter(who), quarter(who), q_s.at[index], q_r.at[index], client, to)

    barrier = pltpu.get_barrier_semaphore()
    for shift in range(1, clients):
        pl.semaphore_signal(
            barrier, inc=1,
            device_id={"client": lax.rem(client + shift, clients), "tensor": member}, device_id_type=MESH,
        )
    for shift in (1, 2, 3):
        pl.semaphore_signal(
            barrier, inc=1,
            device_id={"client": client, "tensor": lax.rem(member + shift, 4)}, device_id_type=MESH,
        )
    order = [(0, 1), (0, 2)] + [(i, 0) for i in range(depth)]
    order += [(i, p) for i in range(1, depth) for p in (1, 2)]
    for i, p in order:
        own_load(levels[i], p).start()
    own_small = [
        pltpu.make_async_copy(low_in.at[client], low_all.at[client], keep_sem.at[0]),
        pltpu.make_async_copy(tile_in, tile_all.at[client], keep_sem.at[1]),
    ]
    for copy in own_small:
        copy.start()
    pl.semaphore_wait(barrier, clients - 1 + 3)
    for i, p in order:
        over(levels[i], p).start()
    for shift in range(1, clients):
        for copy in small(shift):
            copy.start()

    def pair_up(i, p):
        level = levels[i]
        own_load(level, p).wait()
        over(level, p).wait_recv()
        pair = (
            slot(own_table, own_main, level, p)[...].astype(F32)
            + slot(y_table, y_main, level, p)[...].astype(F32)
        )
        if i == 3:
            if p == 0:
                quarter(member)[...] = pair
            else:
                main_out[:, lanes[p]] = pair
            return
        if i == 2:
            slot(zs_table, zs_main, i, p)[...] = pair.astype(BF16)
            onward(i, p).start()
            return

        @pl.when(outer)
        def _():
            slot(zs_table, zs_main, i, p)[...] = pair.astype(BF16)
            relay(i, p).start()

        @pl.when(z != 3 * side)
        def _():
            relay(i, p).wait_recv()
            both = pair + slot(rl_table, rl_main, i, p)[...].astype(F32)
            slot(zs_table, zs_main, i, p)[...] = both.astype(BF16)
            onward(i, p).start()

    pair_up(0, 1)
    pair_up(0, 2)
    for i in range(depth):
        pair_up(i, 0)
    pair_up(1, 1)
    pair_up(1, 2)
    mine = quarter(member)
    for last in (0, 1):
        came(last, 0).wait_recv()
        mine[...] = mine[...] + zr_table[last].astype(F32)
    to_others = [pass_quarter(member, 0, mate), pass_quarter(member, 1, across)]
    for copy in to_others:
        copy.start()
    pair_up(2, 1)
    pair_up(2, 2)
    pass_quarter(across, 1, across).wait_recv()
    second = pass_quarter(across, 2, mate)
    second.start()
    pair_up(3, 1)
    pair_up(3, 2)
    for shift in range(1, clients):
        for copy in small_from(shift):
            copy.wait_recv()
    for copy in own_small:
        copy.wait()
    low_out[...] = low_all[...]
    tile_out[...] = tile_all[...]
    pass_quarter(mate, 0, mate).wait_recv()
    pass_quarter(lax.rem(mate + 2, 4), 2, mate).wait_recv()
    table_out[...] = whole[...]
    for last in (1, 0):
        for p in (1, 2):
            came(last, p).wait_recv()
            main_out[:, lanes[p]] = main_out[:, lanes[p]] + zr_main[last, :, lanes[p]].astype(F32)
    for copy in to_others + [second]:
        copy.wait_send()
    for shift in range(1, clients):
        for copy in small(shift):
            copy.wait_send()
    for i in range(depth):
        for p in parts:
            over(i, p).wait_send()
    for p in parts:
        onward(2, p).wait_send()

    @pl.when(outer)
    def _():
        for i in (0, 1):
            for p in parts:
                relay(i, p).wait_send()

    @pl.when(z != 3 * side)
    def _():
        for i in (0, 1):
            for p in parts:
                onward(i, p).wait_send()


def reduce_deltas(clients, main, table, low, tile):
    depth = clients // 2
    dma = pltpu.SemaphoreType.DMA
    vmem = pltpu.VMEM
    anywhere = pl.BlockSpec(memory_space=pl.ANY)
    inside = pl.BlockSpec(memory_space=pltpu.VMEM)
    block = main.shape[0] // clients
    half, columns = block // 2, table.shape[1] // 2
    wide = main.shape[1]
    hops = depth - 1
    return pl.pallas_call(
        functools.partial(reduce_kernel, clients),
        out_shape=(
            jax.ShapeDtypeStruct((block, wide), F32),
            jax.ShapeDtypeStruct((block, table.shape[1]), F32),
            jax.ShapeDtypeStruct(low.shape, BF16),
            jax.ShapeDtypeStruct((clients,) + tile.shape, F32),
        ),
        in_specs=[anywhere] * 4,
        out_specs=(inside,) * 4,
        scratch_shapes=[
            vmem((depth, block, wide), BF16), vmem((depth, half, columns), BF16),
            vmem((depth, block, wide), BF16), vmem((depth, half, columns), BF16),
            vmem((hops, block, wide), BF16), vmem((hops, half, columns), BF16),
            vmem((2, block, wide), BF16), vmem((2, half, columns), BF16),
            vmem((2, block, wide), BF16), vmem((2, half, columns), BF16),
            vmem((block, table.shape[1]), F32), vmem(low.shape, BF16),
            vmem((clients,) + tile.shape, F32),
            dma((3, depth)), dma((3, depth)), dma((3, depth)), dma((3, hops)), dma((3, 2)),
            dma((3, 2)), dma((3, 2)),
            dma((clients - 1,)), dma((clients - 1,)), dma((clients - 1,)), dma((clients - 1,)),
            dma((3,)), dma((3,)), dma((2,)),
        ],
        compiler_params=pltpu.CompilerParams(
            collective_id=2, has_side_effects=True, vmem_limit_bytes=52 << 20
        ),
        name="reduce_deltas",
    )(main, table, low, tile)


def adam(master, first, second, grad):
    first2 = BETA_ONE * first + (1.0 - BETA_ONE) * grad
    second2 = BETA_TWO * second + (1.0 - BETA_TWO) * grad * grad
    moved = (
        first2 / (1.0 - BETA_ONE**ROUND) / (jnp.sqrt(second2 / (1.0 - BETA_TWO**ROUND)) + ADAM_EPS)
    )
    fresh = master - SERVER_RATE * (moved + WEIGHT_DECAY * master)
    return (fresh, first2, second2, fresh.astype(jnp.bfloat16))


def server_kernel(main_ref, table_ref, low_ref, tile_ref, norm_ref, *refs):
    masters, firsts, seconds = refs[0:4], refs[4:8], refs[8:12]
    loss_out, norms_out = refs[12:14]
    outs = [refs[14 + i : 30 : 4] for i in range(4)]
    own, group = masters[0].shape[1:]
    tile = jnp.sum(tile_ref[...], 0)
    row = main_ref.shape[1] // 256
    examples, weighted_loss, weighted_factor = (tile[row : row + 1, i : i + 1] for i in range(3))
    scale = weighted_factor / examples / examples
    loss_out[...] = weighted_loss / examples
    lane = lax.broadcasted_iota(jnp.int32, (1, 128), 1)
    norms = jnp.zeros((1, 128), F32)
    for i in range(norm_ref.shape[0]):
        norms = jnp.where(lane == i, norm_ref[i, 0:1, 0:1], norms)
    norms_out[...] = norms[:, 0 : norm_ref.shape[0]]

    def apply(which, at, delta):
        results = adam(
            masters[which][at], firsts[which][at], seconds[which][at], scale * delta
        )
        for ref, value in zip(outs[which], results):
            ref[at] = value

    def slab(pair):
        return jnp.concatenate(pair, 1)

    every = slice(None)
    packed = tiles(main_ref[...])
    slabs = []
    for i in range(0, len(packed), 3):
        slabs += [slab(pair) for pair in unpack_two(packed[i : i + 3])]
    for i, which in enumerate((3, 4, 5, 6, 0, 1, 2)):
        apply(0, (which, every, every), slabs[i][:, :group])
    wo_rows = jnp.concatenate([slabs[7], jnp.zeros((128 - own, LANE), F32)], 0)
    apply(1, (0, every, every), jnp.transpose(wo_rows)[:group, :own])
    width = low_ref.shape[2] - 128
    messages = low_ref[...].reshape(low_ref.shape[0] * low_ref.shape[1], low_ref.shape[2])
    moved = tn(messages[:, :width], messages[:, width:])
    for i in range(4):
        apply(1, (i + 1, every, every), moved[i * group : (i + 1) * group, :own])
    apply(2, (every, every), table_ref[:, 0 : masters[2].shape[1]])
    bias = [tile[i : i + 1, :] for i in range(row)]
    rows = []
    for i in range(0, row, 3):
        rows += [slab(pair) for pair in unpack_two(bias[i : i + 3])]
    for i in range(4):
        apply(3, (slice(i, i + 1), every), rows[i][:, :group])


def server_update(main, table, low, tile, norms, state):
    inside = pl.BlockSpec(memory_space=pltpu.VMEM)
    shapes = [value.shape for value in state[:4]]
    out_shape = [jax.ShapeDtypeStruct((1, 1), F32), jax.ShapeDtypeStruct((1, norms.shape[0]), F32)]
    for kind in (F32, F32, F32, BF16):
        out_shape += [jax.ShapeDtypeStruct(shape, kind) for shape in shapes]
    return pl.pallas_call(
        server_kernel,
        out_shape=tuple(out_shape),
        in_specs=[inside] * (5 + len(state)),
        out_specs=(inside,) * len(out_shape),
        compiler_params=pltpu.CompilerParams(vmem_limit_bytes=24 << 20),
        name="server_update",
    )(main, table, low, tile, norms, *state)


def on_device(
    pool, index, tau, counts, labels,
    in_bf, out_bf, table_bf, bias_bf,
    in_master, out_master, table_master, bias_master,
    in_first, out_first, table_first, bias_first,
    in_second, out_second, table_second, bias_second,
):
    clients = lax.axis_size("client")
    group = in_bf.shape[2]
    steps, images = index.shape[1], index.shape[2]
    patch_rows, features = pool.shape[1], pool.shape[2]
    seq = patch_rows + 1
    pad = (seq + 15) // 16 * 16
    own = in_bf.shape[1]
    rows_total = table_bf.shape[0]
    classes = rows_total - features - seq - 9
    table_t = table_bf.T
    direct = clients == 8
    if direct:
        main, wo_all, table, patches = gather_weights(
            clients, index, in_bf, out_bf, table_t, pool, pad
        )
    else:
        in_rows = jnp.transpose(in_bf, (1, 0, 2))
        out_rows = jnp.transpose(out_bf, (2, 0, 1))
        main_own = jnp.concatenate(
            [in_rows[:, 3:], out_rows[:, 1:], in_rows[:, :3], out_rows[:, :1]], 1
        ).reshape(own, 12 * group)
        table_own = jnp.pad(table_t, ((0, 0), (0, features + REST - rows_total)))
        main = lax.all_gather(main_own, "client", axis=0, tiled=True)
        table = lax.all_gather(table_own, "client", axis=0, tiled=True)
        wo_all = lax.all_gather(main[:, 12 * group - LANE :], "tensor", axis=1, tiled=True)
        patches = pick_patches(pool, index[0].reshape(steps * images), pad)
    patches = patches.reshape(steps, images * pad, features)
    d_main, d_table, low, tile, norms = local_training(
        tau, counts, labels, index, patches, main, wo_all, table, bias_bf, clients, pad, seq, classes
    )
    if direct:
        main_sum, table_sum, low_all, tile_all = reduce_deltas(clients, d_main, d_table, low, tile)
    else:
        tile_all = lax.psum(tile, "client")[None]
        main_sum = lax.psum_scatter(d_main, "client", scatter_dimension=0, tiled=True).astype(F32)
        first_member = lax.axis_index("tensor") == 0
        d_table = jnp.where(first_member, d_table, jnp.zeros_like(d_table))
        table_sum = lax.psum(
            lax.psum_scatter(d_table, "client", scatter_dimension=0, tiled=True).astype(F32), "tensor"
        )
        low_all = lax.all_to_all(low, "client", split_axis=0, concat_axis=0, tiled=True)
    state = (
        in_master, out_master, table_master.T, bias_master,
        in_first, out_first, table_first.T, bias_first,
        in_second, out_second, table_second.T, bias_second,
    )
    loss, norms, *fresh = server_update(main_sum, table_sum, low_all, tile_all, norms, state)
    fresh[2::4] = [value.T for value in fresh[2::4]]
    return (loss.reshape(()), norms, *fresh)


def solution(mesh):
    by_client = P("client", None, None)
    state = (P(None, "client", "tensor"), P(None, "tensor", "client"), P(None, "client"), P(None, "tensor"))
    in_specs = (by_client, by_client, P("client"), P("client"), P("client")) + state * 4
    out_specs = (P(), P("client", None)) + state * 4
    return jax.shard_map(
        on_device, mesh=mesh, in_specs=in_specs, out_specs=out_specs, check_vma=False
    )
```

```python
import functools

import jax
import jax.numpy as jnp
from jax import lax
from jax.experimental import pallas as pl
from jax.experimental.pallas import tpu as pltpu
from jax.sharding import PartitionSpec as P

HEAD_DIM = 64
ROUND = 5
EPS_NORM = 1e-06
MOMENTUM_RHO = 0.9
LOCAL_RATE = 0.05
CLIP_LIMIT = 1.0
BETA_ONE = 0.5
BETA_TWO = 0.7
ADAM_EPS = 1e-08
WEIGHT_DECAY = 0.05
SERVER_RATE = 0.05
SQRT_HALF = 0.7071067811865476
INV_ROOT_TAU = 0.3989422804014327
MESH = pl.DeviceIdType.MESH
F32 = jnp.float32
BF16 = jnp.bfloat16
NEG = -1e30
LANE = 256
SMALL = 16
REST = 512
VMEM_LIMIT = 67043328


def dot(left, right, dims):
    return lax.dot_general(left, right, (dims, ((), ())), preferred_element_type=F32)


def nn(left, right):
    return dot(left, right, ((1,), (0,)))


def nt(left, right):
    return dot(left, right, ((1,), (1,)))


def tn(left, right):
    return dot(left, right, ((0,), (0,)))


def fold(value):
    rows, width = value.shape
    return jnp.sum(value.reshape(rows // 8, 8, width), 0)


def total(value):
    return jnp.sum(jnp.sum(value, 1, keepdims=True), 0, keepdims=True)


def normalise(value):
    centre = value - jnp.mean(value, -1, keepdims=True)
    inverse = lax.rsqrt(jnp.mean(centre * centre, -1, keepdims=True) + EPS_NORM)
    return (centre * inverse, inverse)


def norm_grad(grad, gain, normed, inverse):
    scaled = grad * gain
    return inverse * (
        scaled
        - jnp.mean(scaled, -1, keepdims=True)
        - normed * jnp.mean(scaled * normed, -1, keepdims=True)
    )


def split_two(value):
    high = value.astype(BF16)
    return (high, (value - high.astype(F32)).astype(BF16))


def swap(tile):
    return pltpu.roll(tile, HEAD_DIM, 1)


def tiles(value):
    return [value[:, i : i + 128] for i in range(0, value.shape[1], 128)]


def low_half(shape):
    return lax.broadcasted_iota(jnp.int32, shape, 1) < HEAD_DIM


def pack_two(left, right):
    low = low_half(left[0].shape)
    return [
        left[0],
        jnp.where(low, left[1], swap(right[0])),
        jnp.where(low, swap(right[0]), swap(right[1])),
    ]


def unpack_two(packed):
    low = low_half(packed[0].shape)
    nothing = jnp.zeros_like(packed[0])
    middle, last = swap(packed[1]), swap(packed[2])
    return (
        [packed[0], jnp.where(low, packed[1], nothing)],
        [jnp.where(low, middle, last), jnp.where(low, last, nothing)],
    )


def train_kernel(
    sizes,
    tau_ref,
    count_ref,
    label_ref,
    index_ref,
    x_hbm,
    main_in,
    wo_in,
    table_in,
    bias_in,
    main_out,
    table_out,
    low_out,
    tile_out,
    norm_out,
    wqkv, w1, wot, w2t, wet, head,
    wqkv_f, w1_f, wot_f, wet_f, pos_f, head_f, vec_f, bias_f,
    wqkv_m, w1_m, wot_m, wet_m, pos_m, head_m, vec_m, bias_m,
    wqkv_g, wot_g, wet_g, pos_g, head_g, vec_g,
    xbuf, h0, slope, prob, abuf, qkv, oall, third, ubuf, dpre, h1own, datt, chip, inverses,
    hsum, asum, dact, bsum, vacc, ssq,
    low_d, low_a, low_b, low_w, scal, loss_all, factor_kept, bias_wide, bias_start,
    s1, r1, s2, r2, mx_s, mx_r, nx_s, nx_r, pos_r, vec_r,
    wsem, xsem, o_ps, o_xs, o_fs, o_pr, o_xr, o_fr,
    a1s, a1r, a2s, a2r, das, dar, pvs, pvr, mxs, mxr, nxs, nxr, osem,
):
    steps, seq, pad, classes, clients = sizes
    width = 768
    kept = (seq + 7) // 8 * 8
    me = lax.axis_index("tensor")
    core = lax.rem(me, 2)
    mate = me + 1 - 2 * core
    across = lax.rem(me + 2, 4)
    own0 = 2 * core
    oth0 = 2 - 2 * core

    def rows(n):
        return pl.ds(pl.multiple_of(n * pad, 16), pad)

    def sent_rows(n):
        return pl.ds(pl.multiple_of(n * pad, 16), kept)

    def remote(src, dst, send, recv, device):
        return pltpu.make_async_remote_copy(
            src_ref=src, dst_ref=dst, send_sem=send, recv_sem=recv,
            device_id={"tensor": device}, device_id_type=MESH,
        )

    rest = dpre.at[0:width, 0:REST]
    square_rows = pl.ds(0, width)
    raw = abuf.at[square_rows, :]
    wo_raw = [ubuf.at[square_rows, pl.ds(g * LANE, LANE)] for g in range(3)] + [
        qkv.at[square_rows, pl.ds(0, LANE)]
    ]
    weights_in = [
        main_in.at[:, 2 * width : 3 * width],
        main_in.at[:, 0:width],
        main_in.at[:, width : 2 * width],
        table_in.at[:, 0:width],
        table_in.at[:, width : width + REST],
    ] + [wo_in.at[:, g * LANE : (g + 1) * LANE] for g in range(4)]
    weights = [raw, w1, w2t, wet, rest] + wo_raw

    def load(which):
        return pltpu.make_async_copy(weights_in[which], weights[which], wsem.at[which])

    def fetch(step, slot):
        return pltpu.make_async_copy(x_hbm.at[step], xbuf.at[slot], xsem.at[slot])

    barrier = pltpu.get_barrier_semaphore()
    fetch(0, 0).start()
    for which in range(9):
        load(which).start()
    for zero in (r1, r2, oall, third, datt):
        zero[...] = jnp.zeros_like(zero)
    for shift in (1, 2, 3):
        pl.semaphore_signal(
            barrier, inc=1, device_id={"tensor": lax.rem(me + shift, 4)}, device_id_type=MESH
        )
    bias_wide[...] = jnp.zeros_like(bias_wide)
    bias_wide[0 : bias_in.shape[0], 0 : bias_in.shape[1]] = bias_in[...].astype(F32)
    slabs = [tiles(bias_wide[r : r + 1, :]) for r in range(4)]
    first_bias = jnp.concatenate(pack_two(slabs[0], slabs[1]) + pack_two(slabs[2], slabs[3]), 1)
    bias_start[...] = jnp.broadcast_to(first_bias, (8, width))
    bias_f[...] = bias_start[...]
    for zero in (pos_m, head_m, vec_m, bias_m, low_a, low_b, low_w, loss_all):
        zero[...] = jnp.zeros_like(zero)
    low_d[...] = jnp.zeros_like(low_d)
    for which in (0, 3, 4, 5, 6, 7, 8):
        load(which).wait()
    n_head = head.shape[0]
    vec_at, head_at = seq, seq + 9
    h0[0:REST, :] = jnp.transpose(rest[...].astype(F32))
    pos_rows = lax.broadcasted_iota(jnp.int32, (pad, 1), 0) < seq
    vec_rows = lax.broadcasted_iota(jnp.int32, (SMALL, 1), 0) < 9
    pos_f[...] = jnp.where(pos_rows, h0[0:pad, :], 0.0)
    vec_f[...] = jnp.where(vec_rows, h0[vec_at : vec_at + SMALL, :], 0.0)
    start_head = h0[head_at : head_at + n_head, :]
    head_f[...] = start_head
    head[...] = start_head.astype(BF16)
    taken = tau_ref[0]

    def join(parts):
        return jnp.concatenate(parts, 1)

    def start_rows(j, carry):
        at = pl.ds(pl.multiple_of(j * 64, 64), 64)
        packed = tiles(raw[at, :].astype(F32))
        q, k = unpack_two(packed[:3])
        v, _ = unpack_two(packed[3:])
        wqkv[at, :] = join(q + k + v).astype(BF16)
        pieces = [tiles(piece[at, :].astype(F32)) for piece in wo_raw]
        low = low_half((64, 128))
        first = [jnp.where(low, swap(p[0]), swap(p[1])) for p in pieces]
        last = [
            jnp.where(low, swap(pieces[g][1]), pieces[g + 1][1]) for g in (0, 2)
        ]
        wot[at, :] = join(first + last).astype(BF16)
        return carry

    lax.fori_loop(0, width // 64, start_rows, 0)
    pl.semaphore_wait(barrier, 3)

    row_id = lax.broadcasted_iota(jnp.int32, (pad, 1), 0)
    token = row_id < seq
    key_ok = lax.broadcasted_iota(jnp.int32, (1, pad), 1) < seq
    lane_head = lax.broadcasted_iota(jnp.int32, (1, LANE), 1) // HEAD_DIM
    small_ok = lax.broadcasted_iota(jnp.int32, (SMALL, 1), 0) < 4
    scale = HEAD_DIM ** (-0.5)

    def of_head(value, h):
        return jnp.where(lane_head == h, value, jnp.zeros_like(value))

    def o_part(message, group):
        lanes = pl.ds(pl.multiple_of(group * 128, 128), 128)
        pair, which = message // 3, message % 3
        if which == 2:
            return third.at[pair, 0:kept, lanes]
        return oall.at[pl.ds((2 * pair + which) * pad, kept), lanes]

    def o_to_mate(message):
        place = o_part(message, me)
        return remote(place, place, o_ps.at[message], o_pr.at[message], mate)

    def o_across(message):
        place = o_part(message, me)
        return remote(place, place, o_xs.at[message], o_xr.at[message], across)

    def o_forward(message):
        place = o_part(message, across)
        return remote(place, place, o_fs.at[message], o_fr.at[message], mate)

    def relay_o(message):
        place = o_part(message, across)
        remote(place, place, o_xs.at[message], o_xr.at[message], across).wait_recv()
        o_forward(message).start()

    def o_here(message):
        direct = o_part(message, mate)
        remote(direct, direct, o_ps.at[message], o_pr.at[message], mate).wait_recv()
        passed = o_part(message, lax.rem(mate + 2, 4))
        remote(passed, passed, o_fs.at[message], o_fr.at[message], mate).wait_recv()

    def to_mate(n):
        return remote(s1.at[n, 0:kept], r1.at[n, 0:kept], a1s.at[n], a1r.at[n], mate)

    def to_across(which, n):
        return remote(s2.at[n, 0:kept], r2.at[2 * which + n, 0:kept], a2s.at[2 * which + n], a2r.at[2 * which + n], across)

    def gradient_to_mate(buffer, which, image, k):
        return remote(
            buffer.at[sent_rows(image)], buffer.at[sent_rows(image)],
            das.at[2 * which + k], dar.at[2 * which + k], mate,
        )

    def pos_to_mate():
        return remote(pos_g, pos_r, pvs.at[0], pvr.at[0], mate)

    def vec_to_mate():
        return remote(vacc, vec_r, pvs.at[1], pvr.at[1], mate)

    def spread(src, dst, send, recv, shift):
        return remote(
            src, dst.at[me], send.at[shift - 1], recv.at[shift - 1], lax.rem(me + shift, 4)
        )

    def update_rows(entries, rho, live, fac):
        def update(j, carry):
            at = pl.ds(pl.multiple_of(j * 64, 64), 64)
            for low, full, mom, grad in entries:
                m = rho * mom[at, :] + fac * grad[at, :]
                mom[at, :] = m
                w = full[at, :] - (live * LOCAL_RATE) * m
                full[at, :] = w
                low[at, :] = w.astype(BF16)
            return carry

        lax.fori_loop(0, width // 64, update, 0)

    def one_step(step, carry):
        slot = lax.rem(step, 2)
        fetch(step, slot).wait()

        @pl.when(step < steps - 1)
        def _():
            fetch(step + 1, 1 - slot).start()

        gain1, shift1 = vec_f[0:1, :], vec_f[1:2, :]
        gain2, shift2 = vec_f[2:3, :], vec_f[3:4, :]
        gain3, shift3 = vec_f[4:5, :], vec_f[5:6, :]

        def attend(pair):
            two = slice(2 * pair * pad, 2 * (pair + 1) * pad)
            inside = (row_id >= 1) & token
            added = pos_f[...] + jnp.where(inside, vec_f[6:7, :], 0.0)
            state = nt(xbuf[slot, two, :], wet[...]) + jnp.concatenate([added, added], 0)
            h0[two, :] = state
            normed, _ = normalise(state)
            a = (normed * gain1 + shift1).astype(BF16)
            abuf[two, :] = a
            both = nn(a, wqkv[...]).astype(BF16)
            qkv[two, :] = both
            mine = pl.ds(pl.multiple_of(me * 128, 128), 128)
            thirds = []
            for i in range(2):
                projected = both[i * pad : (i + 1) * pad]
                q, k, v = projected[:, :LANE], projected[:, LANE : 2 * LANE], projected[:, 2 * LANE :]
                out = jnp.zeros((pad, LANE), F32)
                for h in range(3):
                    scores = jnp.where(key_ok, nt(of_head(q, h), k) * scale, NEG)
                    expd = jnp.exp(scores - jnp.max(scores, -1, keepdims=True))
                    p = (expd * (1.0 / jnp.sum(expd, -1, keepdims=True))).astype(BF16)
                    prob[(2 * pair + i) * 3 + h] = p
                    out = out + nn(p, of_head(v, h))
                oall[(2 * pair + i) * pad : (2 * pair + i + 1) * pad, mine] = out[:, :128].astype(BF16)
                thirds.append(out[:, 128:])
                o_to_mate(3 * pair + i).start()
                o_across(3 * pair + i).start()
            third[pair, :, mine] = (thirds[0] + swap(thirds[1])).astype(BF16)
            o_to_mate(3 * pair + 2).start()
            o_across(3 * pair + 2).start()

        attend(0)
        attend(1)

        @pl.when(step == 0)
        def _():
            load(1).wait()
            load(2).wait()

            def begin(j, carry):
                at = pl.ds(pl.multiple_of(j * 32, 32), 32)
                for low_ref, full, mom in (
                    (wqkv, wqkv_f, wqkv_m), (w1, w1_f, w1_m), (wot, wot_f, wot_m), (wet, wet_f, wet_m)
                ):
                    full[at, :] = low_ref[at, :].astype(F32)
                    mom[at, :] = jnp.zeros((32, width), F32)
                return carry

            lax.fori_loop(0, width // 32, begin, 0)

        @pl.when(step > 0)
        def _():
            was_live = jnp.where(step - 1 < taken, 1.0, 0.0)
            was_rho = jnp.where(step - 1 < taken, MOMENTUM_RHO, 1.0)
            was_fac = factor_kept[0:1, 0:1]
            update_rows(((w1, w1_f, w1_m, slope), (wot, wot_f, wot_m, wot_g)), was_rho, was_live, was_fac)
            head_m[...] = was_rho * head_m[...] + was_fac * head_g[...]
            head_f[...] = head_f[...] - (was_live * LOCAL_RATE) * head_m[...]
            head[...] = head_f[...].astype(BF16)
            moved_rows = (LOCAL_RATE * low_w[:, 0:1]) * low_a[...]
            low_hi, low_lo = split_two(moved_rows)
            pair_rows = jnp.concatenate([low_hi, low_lo], 0)
            load(2).wait()

            def low_rank(j, carry):
                at = pl.ds(pl.multiple_of(j * LANE, LANE), LANE)
                moved = tn(jnp.concatenate([low_d[:, at], low_d[:, at]], 0), pair_rows)
                w2t[at, :] = (w2t[at, :].astype(F32) - moved).astype(BF16)
                return carry

            lax.fori_loop(0, width // LANE, low_rank, 0)

        for message in range(3):
            relay_o(message)

        def feed(pair):
            for message in range(3):
                o_here(3 * pair + message)
            two = slice(2 * pair * pad, 2 * (pair + 1) * pad)
            side = tiles(third[pair].astype(F32))
            low = low_half((pad, 128))
            for i in range(2):
                for g in (0, 2):
                    if i == 0:
                        tile = jnp.where(low, side[g], swap(side[g + 1]))
                    else:
                        tile = jnp.where(low, swap(side[g]), side[g + 1])
                    at = 4 * 128 + g * HEAD_DIM
                    oall[(2 * pair + i) * pad : (2 * pair + i + 1) * pad, at : at + 128] = tile.astype(BF16)
            state = h0[two, :] + nt(oall[two, :], wot[...]) + vec_f[7:8, :]
            differs = (pair + core) - 2 * pair * core
            for i in range(2):
                part = state[i * pad : (i + 1) * pad]
                h1own[i * (1 - differs) + 2 * differs] = part
                hsum[2 * pair + i] = fold(jnp.where(token, part, 0.0))
            normed, _ = normalise(state)
            u = (normed * gain2 + shift2).astype(BF16)
            ubuf[two, :] = u
            if pair == 0:
                relay_o(3)
                relay_o(4)
            z = nn(u, w1[...]) + bias_f[0:1, :]
            cdf = 0.5 * (1.0 + lax.erf(z * SQRT_HALF))
            act = (z * cdf).astype(BF16).astype(F32)
            tail = cdf + z * jnp.exp(-0.5 * z * z) * INV_ROOT_TAU
            for i in range(2):
                part = slice(i * pad, (i + 1) * pad)
                asum[2 * pair + i] = fold(jnp.where(token, act[part], 0.0))
                slope[(2 * pair + i) * pad : (2 * pair + i + 1) * pad, :] = jnp.where(token, tail[part], 0.0)
            if pair == 0:
                relay_o(5)

        feed(0)
        feed(1)

        def stack(ref):
            parts = [jnp.sum(ref[n], 0, keepdims=True) for n in range(4)]
            return jnp.concatenate(parts + [jnp.zeros((SMALL - 4, width), F32)], 0)

        act_sum = stack(asum)
        act_hi, act_lo = split_two(act_sum)
        both = nt(jnp.concatenate([act_hi, act_lo], 0), w2t[...])
        folded = both[:4] + both[SMALL : SMALL + 4]
        mx_s[...] = jnp.concatenate([folded[:, : width // 2], folded[:, width // 2 :]], 0)
        for shift in (1, 2, 3):
            spread(mx_s, mx_r, mxs, mxr, shift).start()
        mx_r[me] = mx_s[...]
        h_mean = stack(hsum) * (1.0 / seq)
        for shift in (1, 2, 3):
            remote(
                mx_s, mx_r.at[lax.rem(me + 4 - shift, 4)], mxs.at[shift - 1], mxr.at[shift - 1], mate
            ).wait_recv()
        halves = mx_r[0] + mx_r[1] + mx_r[2] + mx_r[3]
        mlp = jnp.concatenate(
            [jnp.concatenate([halves[:4], halves[4:]], 1), jnp.zeros((SMALL - 4, width), F32)], 0
        )
        average = h_mean + mlp * (1.0 / seq) + vec_f[8:9, :]
        normed3, inverse3 = normalise(average)
        pooled = (normed3 * gain3 + shift3).astype(BF16)
        logits = nt(pooled, head[...])
        class_ok = lax.broadcasted_iota(jnp.int32, (1, head.shape[0]), 1) < classes
        logits = jnp.where(class_ok, logits, NEG)
        top = jnp.max(logits, -1, keepdims=True)
        exp_l = jnp.exp(logits - top)
        total_l = jnp.sum(exp_l, -1, keepdims=True)
        hot_row = lax.broadcasted_iota(jnp.int32, (SMALL, n_head), 0)
        hot_lane = lax.broadcasted_iota(jnp.int32, (SMALL, n_head), 1)
        hot = jnp.zeros((SMALL, n_head), F32)
        for n in range(4):
            label = label_ref[index_ref[0, step, n]]
            hot = jnp.where((hot_row == n) & (hot_lane == label), 1.0, hot)
        each = top + jnp.log(total_l) - jnp.sum(jnp.where(class_ok, logits, 0.0) * hot, -1, keepdims=True)
        loss = jnp.sum(jnp.where(small_ok, each, 0.0), 0, keepdims=True) * 0.25
        live = jnp.where(step < taken, 1.0, 0.0)
        rho = jnp.where(step < taken, MOMENTUM_RHO, 1.0)
        loss_tile = live * loss
        d_logits = jnp.where(small_ok, (exp_l / total_l - hot) * 0.25, 0.0).astype(BF16)
        d_head = tn(d_logits, pooled)
        head_g[...] = d_head
        d_pooled = nn(d_logits, head[...])
        d_average = norm_grad(d_pooled, gain3, normed3, inverse3)
        d_token = d_average * (1.0 / seq)
        d_mlp = d_token.astype(BF16)
        dact[...] = nn(d_mlp, w2t[...])
        for r in range(4):
            scal[r] = jnp.broadcast_to(d_token[r : r + 1, :], (8, width))
        vec_g[...] = jnp.zeros_like(vec_g)
        vec_g[4:5, :] = jnp.sum(d_pooled * normed3, 0, keepdims=True)
        vec_g[5:6, :] = jnp.sum(d_pooled, 0, keepdims=True)
        vec_g[8:9, :] = jnp.sum(d_average, 0, keepdims=True)
        low_at = pl.ds(pl.multiple_of(step * SMALL, SMALL), SMALL)
        low_d[low_at, :] = d_mlp
        low_a[low_at, :] = act_sum
        gram_d = nt(d_mlp, d_mlp)
        gram_a = nt(act_hi, act_hi) + nt(act_hi, act_lo) + nt(act_lo, act_hi)
        own_squares = total(gram_d * gram_a)

        for n in range(4):
            scal[4 + n] = jnp.broadcast_to(dact[n : n + 1, :], (8, width))
        bsum[...] = jnp.zeros_like(bsum)
        vacc[...] = jnp.zeros_like(vacc)

        def upper_partial(n):
            at = pl.ds(pl.multiple_of(n * pad, 16), 2 * pad)
            rate = jnp.concatenate(
                [jnp.broadcast_to(scal[4 + n + i][0:1, :], (pad, width)) for i in range(2)], 0
            )
            g = (rate * slope[at, :]).astype(BF16)
            dpre[at, :] = g
            bsum[...] = bsum[...] + fold(g.astype(F32))
            return nt(g, w1[...])

        other = upper_partial(oth0)
        for k in (0, 1):
            s1[k] = other[k * pad : (k + 1) * pad].astype(BF16)
            to_mate(k).start()
        own = upper_partial(own0)
        for k in (0, 1):
            to_mate(k).wait_recv()
            part = own[k * pad : (k + 1) * pad] + r1[k].astype(F32)
            chip[k] = part
            s2[k] = part.astype(BF16)
            to_across(0, k).start()

        ssq[...] = jnp.zeros_like(ssq)
        w1_g = slope

        def weight_grad(left, right, out, which):
            def tile(j, carry):
                at = pl.ds(pl.multiple_of(j * LANE, LANE), LANE)
                g = tn(left[:, at], right[...])
                out[at, :] = g
                ssq[which] = ssq[which] + fold(g * g)
                return carry

            lax.fori_loop(0, width // LANE, tile, 0)

        def embedding_grad(image, left, adds, last):
            def tile(j, carry):
                at = pl.ds(pl.multiple_of(j * LANE, LANE), LANE)
                g = tn(left[rows(image), at], xbuf[slot, rows(image), :])
                if adds:
                    g = g + wet_g[at, :]
                if last:
                    ssq[3] = ssq[3] + fold(g * g)
                wet_g[at, :] = g
                return carry

            lax.fori_loop(0, width // LANE, tile, 0)

        weight_grad(ubuf, dpre, w1_g, 0)

        for k in (0, 1):
            normed, inverse = normalise(h1own[k])
            h1own[k] = normed
            inverses[k] = inverse
            normed, inverse = normalise(h0[rows(own0 + k), :])
            h0[rows(own0 + k), :] = normed
            inverses[2 + k] = inverse

        def attention_partial(n):
            own_columns = jnp.concatenate(
                [
                    wot[:, pl.ds(pl.multiple_of(me * 128, 128), 128)],
                    wot[:, pl.ds(pl.multiple_of(4 * 128 + (me // 2) * 128, 128), 128)],
                ],
                1,
            )
            wide = nn(datt[rows(n), :], own_columns)
            thirds = jnp.where(core == 1, swap(wide[:, 128:]), wide[:, 128:])
            thirds = jnp.where(low_half((pad, 128)), thirds, 0.0)
            d_ctx = jnp.concatenate([wide[:, :128], thirds], 1).astype(BF16)
            projected = qkv[rows(n), :]
            q, k, v = projected[:, :LANE], projected[:, LANE : 2 * LANE], projected[:, 2 * LANE :]
            d_q = jnp.zeros((pad, LANE), F32)
            d_k = jnp.zeros((pad, LANE), F32)
            d_v = jnp.zeros((pad, LANE), F32)
            for h in range(3):
                part = of_head(d_ctx, h)
                p = prob[n * 3 + h]
                again = p.astype(F32)
                d_p = nt(part, v)
                inner = d_p - jnp.sum(d_p * again, -1, keepdims=True)
                d_s = (again * inner).astype(BF16)
                d_v = d_v + tn(p, part)
                d_q = d_q + nn(d_s, of_head(k, h))
                d_k = d_k + tn(d_s, of_head(q, h))
            d_all = jnp.concatenate([d_q * scale, d_k * scale, d_v], 1).astype(BF16)
            qkv[rows(n), :] = d_all
            return nt(d_all, wqkv[...])

        for k in (0, 1):
            to_across(0, k).wait_recv()
            d_upper = chip[k] + r2[k].astype(F32)
            normed = h1own[k]
            d_state = norm_grad(d_upper, gain2, normed, inverses[k]) + scal[own0 + k][0:1, :]
            d_state = jnp.where(token, d_state, 0.0)
            h1own[k] = d_state
            datt[rows(own0 + k), :] = d_state.astype(BF16)
            gradient_to_mate(datt, 0, own0 + k, k).start()
            vacc[0] = vacc[0] + fold(d_upper * normed)
            vacc[1] = vacc[1] + fold(d_upper)
            vacc[2] = vacc[2] + fold(d_state)
            own = attention_partial(own0 + k)
            remote(
                datt.at[sent_rows(oth0 + k)], datt.at[sent_rows(oth0 + k)], das.at[k], dar.at[k], mate
            ).wait_recv()
            other = attention_partial(oth0 + k)
            to_mate(k).wait_send()
            s1[k] = other.astype(BF16)
            to_mate(k).start()
            to_mate(k).wait_recv()
            own = own + r1[k].astype(F32)
            chip[k] = own
            to_across(0, k).wait_send()
            s2[k] = own.astype(BF16)
            to_across(1, k).start()

        weight_grad(datt, oall, wot_g, 1)
        weight_grad(abuf, qkv, wqkv_g, 2)

        d_bias = jnp.sum(bsum[...], 0, keepdims=True)
        own_squares = own_squares + total(ssq[0] + ssq[2]) + total(d_bias * d_bias)
        shared = total(ssq[1] + fold(head_g[...] * head_g[...]))

        d_emb = ubuf
        for k in (0, 1):
            to_across(1, k).wait_recv()
            d_normed = chip[k] + r2[2 + k].astype(F32)
            normed = h0[rows(own0 + k), :]
            d_state = h1own[k] + norm_grad(d_normed, gain1, normed, inverses[2 + k])
            d_emb[rows(own0 + k), :] = d_state.astype(BF16)
            gradient_to_mate(d_emb, 1, own0 + k, k).start()
            vacc[3] = vacc[3] + fold(d_normed * normed)
            vacc[4] = vacc[4] + fold(d_normed)
            vacc[5] = vacc[5] + fold(jnp.where(row_id >= 1, d_state, 0.0))
            if k == 0:
                pos_g[...] = d_state
            else:
                pos_g[...] = pos_g[...] + d_state
                pos_to_mate().start()
                vec_to_mate().start()
            embedding_grad(own0 + k, d_emb, k == 1, False)
            remote(
                d_emb.at[sent_rows(oth0 + k)], d_emb.at[sent_rows(oth0 + k)],
                das.at[2 + k], dar.at[2 + k], mate,
            ).wait_recv()
            embedding_grad(oth0 + k, d_emb, True, k == 1)
        pos_to_mate().wait()
        vec_to_mate().wait()
        pos_g[...] = pos_g[...] + pos_r[...]
        sums = [jnp.sum(vacc[r] + vec_r[r], 0, keepdims=True) for r in range(6)]
        vec_g[0:1, :] = sums[3]
        vec_g[1:2, :] = sums[4]
        vec_g[2:3, :] = sums[0]
        vec_g[3:4, :] = sums[1]
        vec_g[6:7, :] = sums[5]
        vec_g[7:8, :] = sums[2]
        shared = (
            shared
            + total(ssq[3] + fold(pos_g[...] * pos_g[...]))
            + total(vec_g[...] * vec_g[...])
        )
        for message in range(6):
            o_to_mate(message).wait_send()
            o_across(message).wait_send()
            o_forward(message).wait_send()
        for k in (0, 1):
            to_mate(k).wait_send()
            to_across(1, k).wait_send()
            gradient_to_mate(datt, 0, own0 + k, k).wait_send()
            gradient_to_mate(d_emb, 1, own0 + k, k).wait_send()
        for shift in (1, 2, 3):
            spread(mx_s, mx_r, mxs, mxr, shift).wait_send()
        first_lane = lax.broadcasted_iota(jnp.int32, (8, 128), 1) < 64
        nx_s[...] = jnp.where(first_lane, own_squares + 0.25 * shared, loss_tile)
        for shift in (1, 2, 3):
            spread(nx_s, nx_r, nxs, nxr, shift).start()
        nx_r[me] = nx_s[...]

        @pl.when(step == steps - 1)
        def _():
            for which in (0, 1, 3, 4):
                load(which).start()

        for shift in (1, 2, 3):
            remote(
                nx_s, nx_r.at[lax.rem(me + 4 - shift, 4)], nxs.at[shift - 1], nxr.at[shift - 1], mate
            ).wait_recv()
        norm = jnp.sqrt((nx_r[0] + nx_r[1] + nx_r[2] + nx_r[3]))
        factor = live * (CLIP_LIMIT / jnp.maximum(norm, CLIP_LIMIT))
        norm_out[step] = live * norm
        loss_all[...] = loss_all[...] + nx_r[0]
        for shift in (1, 2, 3):
            spread(nx_s, nx_r, nxs, nxr, shift).wait_send()
        fac = factor[0:1, 0:1]

        low_row = lax.broadcasted_iota(jnp.int32, low_b.shape, 0) // SMALL
        low_b[...] = jnp.where(low_row == step, fac, rho * low_b[...])
        low_w[...] = low_w[...] + live * low_b[...]
        factors = (LOCAL_RATE * low_w[:, 0:1]) * low_a[...]
        factor_kept[...] = factor

        def small_update(full, mom, grad):
            mom[...] = rho * mom[...] + fac * grad
            full[...] = full[...] - (live * LOCAL_RATE) * mom[...]

        small_update(pos_f, pos_m, pos_g[...])
        small_update(vec_f, vec_m, vec_g[...])
        small_update(bias_f, bias_m, jnp.broadcast_to(d_bias, (8, width)))
        table = (
            (wqkv, wqkv_f, wqkv_m, wqkv_g),
            (w1, w1_f, w1_m, w1_g),
            (wot, wot_f, wot_m, wot_g),
            (wet, wet_f, wet_m, wet_g),
        )

        @pl.when(step < steps - 1)
        def _():
            load(2).start()
            update_rows((table[0], table[3]), rho, live, fac)

        @pl.when(step == steps - 1)
        def _():
            examples = jnp.full((1, 1), count_ref[0].astype(F32))
            factor_sum = jnp.zeros((), F32)
            for k in range(steps):
                worth = (1.0 - MOMENTUM_RHO ** (k + 1)) / (1.0 - MOMENTUM_RHO)
                factor_sum = factor_sum + jnp.where(k < taken, worth, 0.0)
            factor_sum = jnp.full((1, 1), factor_sum)
            share = examples / factor_sum
            for which in (0, 1, 3, 4):
                load(which).wait()

            def ended(at, full, mom, grad, lanes):
                m = rho * mom[at, lanes] + fac * grad[at, lanes]
                return full[at, lanes] - (live * LOCAL_RATE) * m

            outs = (
                (w1, main_out.at[:, 0:width]),
                (wet, table_out.at[:, 0:width]),
                (raw, main_out.at[:, width : 2 * width]),
                (rest, table_out.at[:, width : width + REST]),
            )
            copies = [
                pltpu.make_async_copy(src, dst, osem.at[i]) for i, (src, dst) in enumerate(outs)
            ]
            for i, (low, full, mom, grad) in enumerate((table[1], table[3])):

                def finish_square(j, carry):
                    at = pl.ds(pl.multiple_of(j * 64, 64), 64)
                    w = ended(at, full, mom, grad, slice(None))
                    low[at, :] = (share * (low[at, :].astype(F32) - w)).astype(BF16)
                    return carry

                lax.fori_loop(0, width // 64, finish_square, 0)
                copies[i].start()

            def finish(j, carry):
                at = pl.ds(pl.multiple_of(j * 64, 64), 64)
                three = tiles(ended(at, wqkv_f, wqkv_m, wqkv_g, slice(None)))
                _, full, mom, grad = table[2]
                wo_first = ended(at, full, mom, grad, pl.ds(pl.multiple_of(me * 128, 128), 128))
                wo_last = ended(
                    at, full, mom, grad, pl.ds(pl.multiple_of(4 * 128 + (me // 2) * 128, 128), 128)
                )
                wo_last = jnp.where(core == 1, swap(wo_last), wo_last)
                packed = join(
                    pack_two(three[0:2], three[2:4]) + pack_two(three[4:6], [wo_first, wo_last])
                )
                raw[at, :] = (share * (raw[at, :].astype(F32) - packed)).astype(BF16)
                return carry

            lax.fori_loop(0, width // 64, finish, 0)
            copies[2].start()
            small_update(head_f, head_m, head_g[...])
            h0[0:REST, :] = jnp.transpose(rest[...].astype(F32))
            for ref, begin, count in ((pos_f, 0, seq), (vec_f, vec_at, 9), (head_f, head_at, classes)):
                h0[begin : begin + count, :] = share * (h0[begin : begin + count, :] - ref[0:count, :])
            rest[...] = jnp.transpose(h0[0:REST, :]).astype(BF16)
            copies[3].start()
            d_bias_all = share * (bias_start[0:1, :] - bias_f[0:1, :])
            for r in range(width // 128):
                tile_out[r : r + 1, :] = d_bias_all[:, 128 * r : 128 * (r + 1)]
            lane = lax.broadcasted_iota(jnp.int32, (1, 128), 1)
            loss_sum = loss_all[0:1, 64:65]
            mean_loss = examples * loss_sum / jnp.full((1, 1), taken.astype(F32))
            scalars = jnp.where(lane == 0, examples, jnp.where(lane == 1, mean_loss, examples * factor_sum))
            tile_out[width // 128 : width // 128 + 1, :] = jnp.where(lane < 3, scalars, 0.0)
            tile_out[width // 128 + 1 :, :] = jnp.zeros((7 - width // 128, 128), F32)
            used = 4 * steps
            wanted_row = lax.broadcasted_iota(jnp.int32, (used, steps * SMALL), 0)
            wanted_row = (wanted_row // 4) * SMALL + lax.rem(wanted_row, 4)
            picker = (lax.broadcasted_iota(jnp.int32, (used, steps * SMALL), 1) == wanted_row).astype(BF16)
            low_left = nn(picker, (share * factors).astype(BF16)).astype(BF16)
            low_right = nn(picker, low_d[...])
            part = width // clients
            kept_lanes = lax.broadcasted_iota(jnp.int32, (used, 128), 1) < part
            for j in range(clients):
                low_out[j, :, 0:width] = low_left
                turned = pltpu.roll(low_right, (width - part * j) % width, 1) if j else low_right
                low_out[j, :, width : width + 128] = jnp.where(kept_lanes, turned[:, :128], 0.0).astype(BF16)
            for copy in copies:
                copy.wait()

        return carry

    lax.fori_loop(0, steps, one_step, 0)


def local_training(tau, counts, labels, index, patches, main, wo, table, bias, clients, pad, seq, classes):
    steps = patches.shape[0]
    width = main.shape[0]
    n_all = 4 * pad
    n_head = (classes + 127) // 128 * 128
    n_low = steps * SMALL
    vmem = pltpu.VMEM
    dma = pltpu.SemaphoreType.DMA
    anywhere = pl.BlockSpec(memory_space=pl.ANY)
    inside = pl.BlockSpec(memory_space=pltpu.VMEM)
    square = (width, width)
    out_shape = (
        jax.ShapeDtypeStruct((width, 2 * width), BF16),
        jax.ShapeDtypeStruct(table.shape, BF16),
        jax.ShapeDtypeStruct((clients, 4 * steps, width + 128), BF16),
        jax.ShapeDtypeStruct((8, 128), F32),
        jax.ShapeDtypeStruct((steps, 8, 128), F32),
    )
    scratch = [
        vmem(square, BF16), vmem(square, BF16), vmem(square, BF16), vmem(square, BF16),
        vmem(square, BF16), vmem((n_head, width), BF16),
    ]
    for _ in range(2):
        scratch += [
            vmem(square, F32), vmem(square, F32), vmem(square, F32), vmem(square, F32),
            vmem((pad, width), F32), vmem((n_head, width), F32), vmem((SMALL, width), F32),
            vmem((8, width), F32),
        ]
    scratch += [
        vmem(square, F32), vmem(square, F32), vmem(square, F32), vmem((pad, width), F32),
        vmem((n_head, width), F32), vmem((SMALL, width), F32),
        vmem((2, n_all, width), BF16), vmem((n_all, width), F32), vmem((n_all, width), F32),
        vmem((12, pad, pad), BF16), vmem((n_all, width), BF16), vmem((n_all, width), BF16),
        vmem((n_all, width), BF16), vmem((2, pad, 4 * 128), BF16), vmem((n_all, width), BF16),
        vmem((n_all, width), BF16), vmem((3, pad, width), F32), vmem((n_all, width), BF16),
        vmem((2, pad, width), F32), vmem((4, pad, 1), F32),
        vmem((4, 8, width), F32), vmem((4, 8, width), F32), vmem((SMALL, width), F32),
        vmem((8, width), F32), vmem((6, 8, width), F32), vmem((4, 8, width), F32),
        vmem((n_low, width), BF16), vmem((n_low, width), F32), vmem((n_low, 128), F32),
        vmem((n_low, 128), F32), vmem((8, 8, width), F32), vmem((8, 128), F32), vmem((8, 128), F32),
        vmem((8, LANE), F32), vmem((8, width), F32),
        vmem((2, pad, width), BF16), vmem((2, pad, width), BF16), vmem((2, pad, width), BF16),
        vmem((4, pad, width), BF16), vmem((8, width // 2), F32), vmem((4, 8, width // 2), F32),
        vmem((8, 128), F32), vmem((4, 8, 128), F32), vmem((pad, width), F32),
        vmem((6, 8, width), F32),
        dma((9,)), dma((2,)), dma((6,)), dma((6,)), dma((6,)), dma((6,)), dma((6,)), dma((6,)),
        dma((2,)), dma((2,)), dma((4,)), dma((4,)), dma((4,)), dma((4,)), dma((2,)), dma((2,)),
        dma((3,)), dma((3,)), dma((3,)), dma((3,)), dma((6,)),
    ]
    return pl.pallas_call(
        functools.partial(train_kernel, (steps, seq, pad, classes, clients)),
        out_shape=out_shape,
        in_specs=[pl.BlockSpec(memory_space=pltpu.SMEM)] * 4 + [anywhere] * 4 + [inside],
        out_specs=(anywhere,) * 2 + (inside,) * 3,
        scratch_shapes=scratch,
        compiler_params=pltpu.CompilerParams(
            collective_id=0, has_side_effects=True, vmem_limit_bytes=VMEM_LIMIT
        ),
        name="local_training",
    )(tau, counts, labels, index, patches, main, wo, table, bias)


def place_patches(chosen_ref, pool_ref, out_ref):
    seq_rows, width = pool_ref.shape[1], pool_ref.shape[2]
    pad = out_ref.shape[1]
    below = jnp.zeros((pad - 1 - seq_rows, width), F32)
    whole = jnp.concatenate([jnp.zeros((1, width), F32), pool_ref[0].astype(F32), below], 0)
    out_ref[0] = whole.astype(BF16)


def pick_patches(pool, chosen, pad):
    count = chosen.shape[0]
    _, patch_rows, width = pool.shape
    return pl.pallas_call(
        place_patches,
        out_shape=jax.ShapeDtypeStruct((count, pad, width), BF16),
        grid_spec=pltpu.PrefetchScalarGridSpec(
            num_scalar_prefetch=1,
            grid=(count,),
            in_specs=[pl.BlockSpec((1, patch_rows, width), lambda i, ids: (ids[i], 0, 0))],
            out_specs=pl.BlockSpec((1, pad, width), lambda i, ids: (i, 0, 0)),
        ),
        name="pick_patches",
    )(chosen, pool)


def ring_places(clients):
    depth = clients // 2
    client = lax.axis_index("client")
    member = lax.axis_index("tensor")
    core = lax.rem(member, 2)
    return (
        depth, client, client // 2, lax.rem(client, 2), member, core, member // 2,
        member + 1 - 2 * core, lax.rem(member + 2, 4),
    )


def send(src, dst, send_sem, recv_sem, client, member):
    return pltpu.make_async_remote_copy(
        src_ref=src, dst_ref=dst, send_sem=send_sem, recv_sem=recv_sem,
        device_id={"client": client, "tensor": member}, device_id_type=MESH,
    )


def span(start, size, unit):
    return pl.ds(pl.multiple_of(start, unit), size)


def gather_kernel(
    clients, index_ref, in_ref, out_ref, table_in, pool_ref, main_out, wo_out, table_out, x_out,
    main_ref, table_ref, wide_in, wide_out, pool_buf, x_buf, pool_sem, x_sem, up_s, up_r, down_s, down_r, y_s, y_r, mate_s, mate_r, x_s, x_r, on_s, on_r, own_sem, keep_sem,
):
    depth, client, z, y, member, core, chip_x, mate, across = ring_places(clients)
    block = main_ref.shape[0]
    half = block // 2
    columns = table_ref.shape[1] // 2
    peer = client + 1 - 2 * y

    wide = main_ref.shape[1]
    tail = wide - LANE

    def table_part(origin, who):
        return table_out.at[
            span(origin * block + (who // 2) * half, half, half),
            span(lax.rem(who, 2) * columns, columns, 128),
        ]

    def wo_part(origin, who):
        return wo_out.at[span(origin * block, block, block), span(who * LANE, LANE, LANE)]

    def shared(origin, who):
        return (wo_part(origin, who), table_part(origin, who))

    def main_part(origin, lanes):
        return main_out.at[span(origin * block, block, block), lanes]

    early, front, back = slice(0, 2 * wide // 9), slice(2 * wide // 9, 2 * wide // 3), slice(2 * wide // 3, wide)

    def beside(origin):
        return origin + 1 - 2 * lax.rem(origin, 2)

    def landed(origin):
        return (
            main_part(origin, back), table_part(origin, member), main_part(origin, front),
            main_part(origin, early), main_part(beside(origin), early),
        )

    own_table = table_ref.at[span(chip_x * half, half, half), span(core * columns, columns, 128)]
    own_pieces = (
        main_ref.at[:, back], own_table, main_ref.at[:, front], main_ref.at[:, early],
        main_part(peer, early),
    )

    def given(origin, mine):
        if mine:
            return (main_ref.at[:, tail:wide], own_table)
        return (main_part(origin, slice(tail, wide)), table_part(origin, member))

    def message(origin, mine, send_sem, recv_sem, index, to, part):
        sources = own_pieces if mine else landed(origin)
        return [
            send(src, dst, send_sem.at[p, index], recv_sem.at[p, index], to, member)
            for p, (src, dst) in enumerate(zip(sources, landed(origin)))
        ][part]

    first, second, third, over_all, crossing = slice(0, 2), slice(2, 3), slice(3, 5), slice(0, 3), slice(3, 4)

    def up(origin, i, part, mine=False):
        return message(origin, mine, up_s, up_r, i, client + 2, part)

    def down(origin, i, part, mine=False):
        return message(origin, mine, down_s, down_r, i, client - 2, part)

    def over(origin, part, mine=False):
        return message(origin, mine, y_s, y_r, origin // 2, peer, part)

    def give(origin, mine, send_sem, recv_sem, to):
        return [
            send(src, dst, send_sem.at[p, origin], recv_sem.at[p, origin], client, to)
            for p, (src, dst) in enumerate(zip(given(origin, mine), shared(origin, member)))
        ]

    def keep(origin, mine=False):
        return pltpu.make_async_copy(given(origin, mine)[0], wo_part(origin, member), keep_sem.at[origin])

    def share(origin, mine=False):
        return give(origin, mine, mate_s, mate_r, mate) + give(origin, mine, x_s, x_r, across)

    def from_across(origin):
        return [
            send(dst, dst, x_s.at[p, origin], x_r.at[p, origin], client, across)
            for p, dst in enumerate(shared(origin, across))
        ]

    def pass_on(origin):
        return [
            send(dst, dst, on_s.at[p, origin], on_r.at[p, origin], client, mate)
            for p, dst in enumerate(shared(origin, across))
        ]

    def start(copies):
        for copy in copies:
            copy.start()

    def arrived(copies):
        for copy in copies:
            copy.wait_recv()

    def sent(copies):
        for copy in copies:
            copy.wait_send()

    has_up, has_down = z < depth - 1, z > 0

    barrier = pltpu.get_barrier_semaphore()

    def hello(to_client, to_member):
        pl.semaphore_signal(
            barrier, inc=1, device_id={"client": to_client, "tensor": to_member}, device_id_type=MESH
        )

    hello(peer, member)
    for shift in (1, 2, 3):
        hello(client, lax.rem(member + shift, 4))
    for shift in range(1, depth):
        hello(2 * lax.rem(z + shift, depth) + y, member)
    wide_in[...] = jnp.zeros_like(wide_in)
    wide_out[...] = jnp.zeros_like(wide_out)
    table_ref[...] = jnp.zeros_like(table_ref)
    table_ref[:, 0 : table_in.shape[1]] = table_in[...]

    def in_slab(i):
        wide_in[i, :, 0 : in_ref.shape[2]] = in_ref[i].astype(F32)
        return tiles(wide_in[i])

    def out_slab(i):
        wide_out[i, 0 : out_ref.shape[1], 0:block] = out_ref[i].astype(F32)
        return tiles(jnp.transpose(wide_out[i])[:block])

    ordered = [in_slab(i) for i in (3, 4, 5, 6)] + [out_slab(i) for i in (1, 2, 3, 4)]
    ordered += [in_slab(i) for i in (0, 1, 2)] + [out_slab(0)]
    for i in range(0, 12, 2):
        packed = jnp.concatenate(pack_two(ordered[i], ordered[i + 1]), 1)
        main_ref[:, 192 * i : 192 * (i + 2)] = packed.astype(BF16)

    pl.semaphore_wait(barrier, 3 + depth)

    def line_start(part):
        @pl.when(has_up)
        def _():
            start(up(client, 0, part, True))

        @pl.when(has_down)
        def _():
            start(down(client, 0, part, True))

    start(over(client, crossing, True))
    start(over(client, first, True))
    line_start(first)
    start(over(client, second, True))
    line_start(second)
    start(share(client, True))
    keep(client, True).start()
    local = [
        pltpu.make_async_copy(src, dst, own_sem.at[p])
        for p, (src, dst) in enumerate(zip(own_pieces[:4], landed(client)))
    ]
    start(local)

    _, steps, each = index_ref.shape
    images = steps * each
    pool_size = pool_buf.shape[1] // 8
    patch_rows = pool_ref.shape[0] // pool_size
    pad = x_out.shape[1]

    def base(b):
        return lax.min(lax.max(8 * b - 1, 0), patch_rows - 8)

    deep = pool_buf.shape[0]

    def pool_load(b):
        k = lax.rem(b, deep)
        return pltpu.make_async_copy(
            pool_ref.at[span(base(b) * pool_size, 8 * pool_size, 32), :], pool_buf.at[k], pool_sem.at[k]
        )

    def x_store(b):
        k = lax.rem(b, deep)
        return pltpu.make_async_copy(x_buf.at[k], x_out.at[:, span(8 * b, 8, 8), :], x_sem.at[k])

    for b in range(deep - 1):
        pool_load(b).start()
    lane = lax.broadcasted_iota(jnp.int32, (8 * images, 8 * pool_size), 1)
    select_row = lax.broadcasted_iota(jnp.int32, (8 * images, 1), 0)
    line_row = lax.rem(select_row, 8)
    chosen = jnp.zeros((8 * images, 1), jnp.int32)
    for i in range(images):
        chosen = jnp.where(select_row // 8 == i, index_ref[0, i // each, i % each], chosen)

    def pick(b, carry):
        k = lax.rem(b, deep)
        pool_load(b).wait()

        @pl.when(b < pad // 8 - (deep - 1))
        def _():
            pool_load(b + deep - 1).start()

        wanted = (8 * b - 1 + line_row - base(b)) * pool_size + chosen
        picked = nn((lane == wanted).astype(BF16), pool_buf[k]).astype(BF16)

        @pl.when(b >= deep)
        def _():
            x_store(b - deep).wait()

        x_buf[k] = picked.reshape(images, 8, picked.shape[1])
        x_store(b).start()
        return carry

    lax.fori_loop(0, pad // 16, pick, 0)

    def line(d, act):
        @pl.when(z >= d)
        def _():
            act(client - 2 * d, True)

        @pl.when(z < depth - d)
        def _():
            act(client + 2 * d, False)

    def across_line(d, act):
        if d == 0:
            act(peer, True)
            return

        @pl.when(z >= d)
        def _():
            act(peer - 2 * d, True)

        @pl.when(z < depth - d)
        def _():
            act(peer + 2 * d, False)

    def line_in(d, part):
        def act(origin, below):
            line_s, line_r = (up_s, up_r) if below else (down_s, down_r)
            arrived(message(origin, False, line_s, line_r, d - 1, peer, part))
            if d < depth - 1:

                @pl.when(has_up if below else has_down)
                def _():
                    start(up(origin, d, part) if below else down(origin, d, part))

            if part is not third:
                start(over(origin, part))
            if part is first:
                start(share(origin))
                keep(origin).start()

        return act

    def y_in(origin, below):
        arrived(over(origin, first))
        start(share(origin))
        keep(origin).start()

    def forward(origin, below=True):
        arrived(from_across(origin))
        start(pass_on(origin))

    for d in range(1, depth + 1):
        if d < depth:
            line(d, line_in(d, first))
        across_line(d - 1, y_in)
        if d < depth:
            line(d, line_in(d, second))
        if d == 1:
            arrived(over(peer, crossing))
            line_start(third)
        else:
            line(d - 1, line_in(d - 1, third))
        if d == 1:
            lax.fori_loop(pad // 16, pad // 8, pick, 0)
            for b in range(pad // 8 - deep, pad // 8):
                x_store(b).wait()
            forward(client)
        else:
            line(d - 1, forward)
            across_line(d - 2, forward)
    across_line(depth - 1, forward)
    for d in range(depth):
        across_line(d, lambda origin, below: arrived(over(origin, second)))

    for copy in local:
        copy.wait()
    for origin in range(clients):
        sent(share(origin))
        sent(pass_on(origin))
        keep(origin).wait()
        arrived([
            send(dst, dst, mate_s.at[p, origin], mate_r.at[p, origin], client, mate)
            for p, dst in enumerate(shared(origin, mate))
        ])
        arrived([
            send(dst, dst, on_s.at[p, origin], on_r.at[p, origin], client, mate)
            for p, dst in enumerate(shared(origin, lax.rem(mate + 2, 4)))
        ])
    sent(over(client, crossing))
    for d in range(depth):
        sent(over(2 * d + y, over_all))

        @pl.when(has_up & (z >= d))
        def _():
            if d < depth - 1:
                sent(up(client - 2 * d, d, slice(0, 5)))

        @pl.when(has_down & (z < depth - d))
        def _():
            if d < depth - 1:
                sent(down(client + 2 * d, d, slice(0, 5)))


def gather_weights(clients, index, in_bf, out_bf, table_t, pool, pad):
    depth = clients // 2
    dma = pltpu.SemaphoreType.DMA
    anywhere = pl.BlockSpec(memory_space=pl.ANY)
    inside = pl.BlockSpec(memory_space=pltpu.VMEM)
    slabs, own, group = in_bf.shape
    width = own * clients
    packed = (slabs + out_bf.shape[0]) * group
    table_lanes = width + REST
    hops = depth - 1
    pool_size, patch_rows, features = pool.shape
    images = index.shape[1] * index.shape[2]
    rows = jnp.transpose(pool, (1, 0, 2)).reshape(patch_rows * pool_size, features)
    return pl.pallas_call(
        functools.partial(gather_kernel, clients),
        out_shape=(
            jax.ShapeDtypeStruct((width, packed), BF16),
            jax.ShapeDtypeStruct((width, 4 * LANE), BF16),
            jax.ShapeDtypeStruct((width, table_lanes), BF16),
            jax.ShapeDtypeStruct((images, pad, features), BF16),
        ),
        in_specs=[pl.BlockSpec(memory_space=pltpu.SMEM)] + [inside] * 3 + [anywhere],
        out_specs=(anywhere,) * 4,
        scratch_shapes=[
            pltpu.VMEM((own, packed), BF16), pltpu.VMEM((own, table_lanes), BF16),
            pltpu.VMEM((slabs, own, LANE), F32), pltpu.VMEM((out_bf.shape[0], LANE, 128), F32),
            pltpu.VMEM((6, 8 * pool_size, features), BF16), pltpu.VMEM((6, images, 8, features), BF16),
            dma((6,)), dma((6,)),
            dma((5, hops)), dma((5, hops)), dma((5, hops)), dma((5, hops)), dma((4, depth)),
            dma((4, depth)),
        ] + [dma((2, clients))] * 6 + [dma((4,)), dma((clients,))],
        compiler_params=pltpu.CompilerParams(collective_id=1, has_side_effects=True),
        name="gather_weights",
    )(index, in_bf, out_bf, table_t, rows)


def reduce_kernel(
    clients, main_in, table_in, low_in, tile_in, main_out, table_out, low_out, tile_out,
    own_main, own_table, y_main, y_table, zs_main, zs_table, zr_main, zr_table, rl_main, rl_table,
    whole, low_all, tile_all, own_sem, y_s, y_r, z_s, z_r, rl_s, rl_r, low_s, low_r, tile_s, tile_r, q_s, q_r, keep_sem,
):
    depth, client, z, y, member, core, chip_x, mate, across = ring_places(clients)
    block = own_main.shape[1]
    half, columns = own_table.shape[1], own_table.shape[2]
    peer = client + 1 - 2 * y
    cut = own_main.shape[2] // 2
    lanes = (None, slice(0, cut), slice(cut, 2 * cut))
    parts = (0, 1, 2)

    def source(owner, p):
        if p == 0:
            return table_in.at[
                span(owner * block + chip_x * half, half, half), span(core * columns, columns, 128)
            ]
        return main_in.at[span(owner * block, block, block), lanes[p]]

    def slot(table_ref, main_ref, i, p):
        return table_ref.at[i] if p == 0 else main_ref.at[i, :, lanes[p]]

    def own_load(level, p):
        return pltpu.make_async_copy(
            source(2 * level + y, p), slot(own_table, own_main, level, p), own_sem.at[p, level]
        )

    def over(level, p):
        return send(
            source(2 * level + 1 - y, p), slot(y_table, y_main, level, p),
            y_s.at[p, level], y_r.at[p, level], peer, member,
        )

    side = z // 2
    outer = z == 3 * side
    near = z + 1 - 2 * lax.rem(z, 2)
    levels = (3 * (1 - side), 2 - side, near, z)

    def relay(i, p):
        return send(
            slot(zs_table, zs_main, i, p), slot(rl_table, rl_main, i, p),
            rl_s.at[p, i], rl_r.at[p, i], 2 * near + y, member,
        )

    def onward(i, p):
        last = i // 2
        return send(
            slot(zs_table, zs_main, i, p), slot(zr_table, zr_main, last, p),
            z_s.at[p, i], z_r.at[p, last], 2 * levels[i] + y, member,
        )

    def came(last, p):
        return send(
            slot(zs_table, zs_main, 0, p), slot(zr_table, zr_main, last, p),
            z_s.at[p, 0], z_r.at[p, last], peer, member,
        )

    def small(shift):
        to = lax.rem(client + shift, clients)
        return [
            send(low_in.at[to], low_all.at[client], low_s.at[shift - 1], low_r.at[shift - 1], to, member),
            send(tile_in, tile_all.at[client], tile_s.at[shift - 1], tile_r.at[shift - 1], to, member),
        ]

    def small_from(shift):
        origin = lax.rem(client + clients - shift, clients)
        return [
            send(low_in.at[origin], low_all.at[origin], low_s.at[shift - 1], low_r.at[shift - 1], origin, member),
            send(tile_in, tile_all.at[origin], tile_s.at[shift - 1], tile_r.at[shift - 1], origin, member),
        ]

    def quarter(who):
        return whole.at[span((who // 2) * half, half, half), span(lax.rem(who, 2) * columns, columns, 128)]

    def pass_quarter(who, index, to):
        return send(quarter(who), quarter(who), q_s.at[index], q_r.at[index], client, to)

    barrier = pltpu.get_barrier_semaphore()
    for shift in range(1, clients):
        pl.semaphore_signal(
            barrier, inc=1,
            device_id={"client": lax.rem(client + shift, clients), "tensor": member}, device_id_type=MESH,
        )
    for shift in (1, 2, 3):
        pl.semaphore_signal(
            barrier, inc=1,
            device_id={"client": client, "tensor": lax.rem(member + shift, 4)}, device_id_type=MESH,
        )
    order = [(0, 1), (0, 2)] + [(i, 0) for i in range(depth)]
    order += [(i, p) for i in range(1, depth) for p in (1, 2)]
    for i, p in order:
        own_load(levels[i], p).start()
    own_small = [
        pltpu.make_async_copy(low_in.at[client], low_all.at[client], keep_sem.at[0]),
        pltpu.make_async_copy(tile_in, tile_all.at[client], keep_sem.at[1]),
    ]
    for copy in own_small:
        copy.start()
    pl.semaphore_wait(barrier, clients - 1 + 3)
    for i, p in order:
        over(levels[i], p).start()
    for shift in range(1, clients):
        for copy in small(shift):
            copy.start()

    def pair_up(i, p):
        level = levels[i]
        own_load(level, p).wait()
        over(level, p).wait_recv()
        pair = (
            slot(own_table, own_main, level, p)[...].astype(F32)
            + slot(y_table, y_main, level, p)[...].astype(F32)
        )
        if i == 3:
            if p == 0:
                quarter(member)[...] = pair
            else:
                main_out[:, lanes[p]] = pair
            return
        if i == 2:
            slot(zs_table, zs_main, i, p)[...] = pair.astype(BF16)
            onward(i, p).start()
            return

        @pl.when(outer)
        def _():
            slot(zs_table, zs_main, i, p)[...] = pair.astype(BF16)
            relay(i, p).start()

        @pl.when(z != 3 * side)
        def _():
            relay(i, p).wait_recv()
            both = pair + slot(rl_table, rl_main, i, p)[...].astype(F32)
            slot(zs_table, zs_main, i, p)[...] = both.astype(BF16)
            onward(i, p).start()

    pair_up(0, 1)
    pair_up(0, 2)
    for i in range(depth):
        pair_up(i, 0)
    pair_up(1, 1)
    pair_up(1, 2)
    mine = quarter(member)
    for last in (0, 1):
        came(last, 0).wait_recv()
        mine[...] = mine[...] + zr_table[last].astype(F32)
    to_others = [pass_quarter(member, 0, mate), pass_quarter(member, 1, across)]
    for copy in to_others:
        copy.start()
    pair_up(2, 1)
    pair_up(2, 2)
    pass_quarter(across, 1, across).wait_recv()
    second = pass_quarter(across, 2, mate)
    second.start()
    pair_up(3, 1)
    pair_up(3, 2)
    for shift in range(1, clients):
        for copy in small_from(shift):
            copy.wait_recv()
    for copy in own_small:
        copy.wait()
    low_out[...] = low_all[...]
    tile_out[...] = tile_all[...]
    pass_quarter(mate, 0, mate).wait_recv()
    pass_quarter(lax.rem(mate + 2, 4), 2, mate).wait_recv()
    table_out[...] = whole[...]
    for last in (1, 0):
        for p in (1, 2):
            came(last, p).wait_recv()
            main_out[:, lanes[p]] = main_out[:, lanes[p]] + zr_main[last, :, lanes[p]].astype(F32)
    for copy in to_others + [second]:
        copy.wait_send()
    for shift in range(1, clients):
        for copy in small(shift):
            copy.wait_send()
    for i in range(depth):
        for p in parts:
            over(i, p).wait_send()
    for p in parts:
        onward(2, p).wait_send()

    @pl.when(outer)
    def _():
        for i in (0, 1):
            for p in parts:
                relay(i, p).wait_send()

    @pl.when(z != 3 * side)
    def _():
        for i in (0, 1):
            for p in parts:
                onward(i, p).wait_send()


def reduce_deltas(clients, main, table, low, tile):
    depth = clients // 2
    dma = pltpu.SemaphoreType.DMA
    vmem = pltpu.VMEM
    anywhere = pl.BlockSpec(memory_space=pl.ANY)
    inside = pl.BlockSpec(memory_space=pltpu.VMEM)
    block = main.shape[0] // clients
    half, columns = block // 2, table.shape[1] // 2
    wide = main.shape[1]
    hops = depth - 1
    return pl.pallas_call(
        functools.partial(reduce_kernel, clients),
        out_shape=(
            jax.ShapeDtypeStruct((block, wide), F32),
            jax.ShapeDtypeStruct((block, table.shape[1]), F32),
            jax.ShapeDtypeStruct(low.shape, BF16),
            jax.ShapeDtypeStruct((clients,) + tile.shape, F32),
        ),
        in_specs=[anywhere] * 4,
        out_specs=(inside,) * 4,
        scratch_shapes=[
            vmem((depth, block, wide), BF16), vmem((depth, half, columns), BF16),
            vmem((depth, block, wide), BF16), vmem((depth, half, columns), BF16),
            vmem((hops, block, wide), BF16), vmem((hops, half, columns), BF16),
            vmem((2, block, wide), BF16), vmem((2, half, columns), BF16),
            vmem((2, block, wide), BF16), vmem((2, half, columns), BF16),
            vmem((block, table.shape[1]), F32), vmem(low.shape, BF16),
            vmem((clients,) + tile.shape, F32),
            dma((3, depth)), dma((3, depth)), dma((3, depth)), dma((3, hops)), dma((3, 2)),
            dma((3, 2)), dma((3, 2)),
            dma((clients - 1,)), dma((clients - 1,)), dma((clients - 1,)), dma((clients - 1,)),
            dma((3,)), dma((3,)), dma((2,)),
        ],
        compiler_params=pltpu.CompilerParams(
            collective_id=2, has_side_effects=True, vmem_limit_bytes=52 << 20
        ),
        name="reduce_deltas",
    )(main, table, low, tile)


def adam(master, first, second, grad):
    first2 = BETA_ONE * first + (1.0 - BETA_ONE) * grad
    second2 = BETA_TWO * second + (1.0 - BETA_TWO) * grad * grad
    moved = (
        first2 / (1.0 - BETA_ONE**ROUND) / (jnp.sqrt(second2 / (1.0 - BETA_TWO**ROUND)) + ADAM_EPS)
    )
    fresh = master - SERVER_RATE * (moved + WEIGHT_DECAY * master)
    return (fresh, first2, second2, fresh.astype(jnp.bfloat16))


def server_kernel(main_ref, table_ref, low_ref, tile_ref, norm_ref, *refs):
    masters, firsts, seconds = refs[0:4], refs[4:8], refs[8:12]
    loss_out, norms_out = refs[12:14]
    outs = [refs[14 + i : 30 : 4] for i in range(4)]
    own, group = masters[0].shape[1:]
    tile = jnp.sum(tile_ref[...], 0)
    row = main_ref.shape[1] // 256
    examples, weighted_loss, weighted_factor = (tile[row : row + 1, i : i + 1] for i in range(3))
    scale = weighted_factor / examples / examples
    loss_out[...] = weighted_loss / examples
    lane = lax.broadcasted_iota(jnp.int32, (1, 128), 1)
    norms = jnp.zeros((1, 128), F32)
    for i in range(norm_ref.shape[0]):
        norms = jnp.where(lane == i, norm_ref[i, 0:1, 0:1], norms)
    norms_out[...] = norms[:, 0 : norm_ref.shape[0]]

    def apply(which, at, delta):
        results = adam(
            masters[which][at], firsts[which][at], seconds[which][at], scale * delta
        )
        for ref, value in zip(outs[which], results):
            ref[at] = value

    def slab(pair):
        return jnp.concatenate(pair, 1)

    every = slice(None)
    packed = tiles(main_ref[...])
    slabs = []
    for i in range(0, len(packed), 3):
        slabs += [slab(pair) for pair in unpack_two(packed[i : i + 3])]
    for i, which in enumerate((3, 4, 5, 6, 0, 1, 2)):
        apply(0, (which, every, every), slabs[i][:, :group])
    wo_rows = jnp.concatenate([slabs[7], jnp.zeros((128 - own, LANE), F32)], 0)
    apply(1, (0, every, every), jnp.transpose(wo_rows)[:group, :own])
    width = low_ref.shape[2] - 128
    messages = low_ref[...].reshape(low_ref.shape[0] * low_ref.shape[1], low_ref.shape[2])
    moved = tn(messages[:, :width], messages[:, width:])
    for i in range(4):
        apply(1, (i + 1, every, every), moved[i * group : (i + 1) * group, :own])
    apply(2, (every, every), table_ref[:, 0 : masters[2].shape[1]])
    bias = [tile[i : i + 1, :] for i in range(row)]
    rows = []
    for i in range(0, row, 3):
        rows += [slab(pair) for pair in unpack_two(bias[i : i + 3])]
    for i in range(4):
        apply(3, (slice(i, i + 1), every), rows[i][:, :group])


def server_update(main, table, low, tile, norms, state):
    inside = pl.BlockSpec(memory_space=pltpu.VMEM)
    shapes = [value.shape for value in state[:4]]
    out_shape = [jax.ShapeDtypeStruct((1, 1), F32), jax.ShapeDtypeStruct((1, norms.shape[0]), F32)]
    for kind in (F32, F32, F32, BF16):
        out_shape += [jax.ShapeDtypeStruct(shape, kind) for shape in shapes]
    return pl.pallas_call(
        server_kernel,
        out_shape=tuple(out_shape),
        in_specs=[inside] * (5 + len(state)),
        out_specs=(inside,) * len(out_shape),
        compiler_params=pltpu.CompilerParams(vmem_limit_bytes=24 << 20),
        name="server_update",
    )(main, table, low, tile, norms, *state)


def on_device(
    pool, index, tau, counts, labels,
    in_bf, out_bf, table_bf, bias_bf,
    in_master, out_master, table_master, bias_master,
    in_first, out_first, table_first, bias_first,
    in_second, out_second, table_second, bias_second,
):
    clients = lax.axis_size("client")
    group = in_bf.shape[2]
    steps, images = index.shape[1], index.shape[2]
    patch_rows, features = pool.shape[1], pool.shape[2]
    seq = patch_rows + 1
    pad = (seq + 15) // 16 * 16
    own = in_bf.shape[1]
    rows_total = table_bf.shape[0]
    classes = rows_total - features - seq - 9
    table_t = table_bf.T
    direct = clients == 8
    if direct:
        main, wo_all, table, patches = gather_weights(
            clients, index, in_bf, out_bf, table_t, pool, pad
        )
    else:
        in_rows = jnp.transpose(in_bf, (1, 0, 2))
        out_rows = jnp.transpose(out_bf, (2, 0, 1))
        main_own = jnp.concatenate(
            [in_rows[:, 3:], out_rows[:, 1:], in_rows[:, :3], out_rows[:, :1]], 1
        ).reshape(own, 12 * group)
        table_own = jnp.pad(table_t, ((0, 0), (0, features + REST - rows_total)))
        main = lax.all_gather(main_own, "client", axis=0, tiled=True)
        table = lax.all_gather(table_own, "client", axis=0, tiled=True)
        wo_all = lax.all_gather(main[:, 12 * group - LANE :], "tensor", axis=1, tiled=True)
        patches = pick_patches(pool, index[0].reshape(steps * images), pad)
    patches = patches.reshape(steps, images * pad, features)
    d_main, d_table, low, tile, norms = local_training(
        tau, counts, labels, index, patches, main, wo_all, table, bias_bf, clients, pad, seq, classes
    )
    if direct:
        main_sum, table_sum, low_all, tile_all = reduce_deltas(clients, d_main, d_table, low, tile)
    else:
        tile_all = lax.psum(tile, "client")[None]
        main_sum = lax.psum_scatter(d_main, "client", scatter_dimension=0, tiled=True).astype(F32)
        first_member = lax.axis_index("tensor") == 0
        d_table = jnp.where(first_member, d_table, jnp.zeros_like(d_table))
        table_sum = lax.psum(
            lax.psum_scatter(d_table, "client", scatter_dimension=0, tiled=True).astype(F32), "tensor"
        )
        low_all = lax.all_to_all(low, "client", split_axis=0, concat_axis=0, tiled=True)
    state = (
        in_master, out_master, table_master.T, bias_master,
        in_first, out_first, table_first.T, bias_first,
        in_second, out_second, table_second.T, bias_second,
    )
    loss, norms, *fresh = server_update(main_sum, table_sum, low_all, tile_all, norms, state)
    fresh[2::4] = [value.T for value in fresh[2::4]]
    return (loss.reshape(()), norms, *fresh)


def solution(mesh):
    by_client = P("client", None, None)
    state = (P(None, "client", "tensor"), P(None, "tensor", "client"), P(None, "client"), P(None, "tensor"))
    in_specs = (by_client, by_client, P("client"), P("client"), P("client")) + state * 4
    out_specs = (P(), P("client", None)) + state * 4
    return jax.shard_map(
        on_device, mesh=mesh, in_specs=in_specs, out_specs=out_specs, check_vma=False
    )
```

```python
import functools

import jax
import jax.numpy as jnp
from jax import lax
from jax.experimental import pallas as pl
from jax.experimental.pallas import tpu as pltpu
from jax.sharding import PartitionSpec as P

HEAD_DIM = 64
ROUND = 5
EPS_NORM = 1e-06
MOMENTUM_RHO = 0.9
LOCAL_RATE = 0.05
CLIP_LIMIT = 1.0
BETA_ONE = 0.5
BETA_TWO = 0.7
ADAM_EPS = 1e-08
WEIGHT_DECAY = 0.05
SERVER_RATE = 0.05
SQRT_HALF = 0.7071067811865476
INV_ROOT_TAU = 0.3989422804014327
MESH = pl.DeviceIdType.MESH
F32 = jnp.float32
BF16 = jnp.bfloat16
NEG = -1e30
LANE = 256
SMALL = 16
REST = 512
VMEM_LIMIT = 67043328


def dot(left, right, dims):
    return lax.dot_general(left, right, (dims, ((), ())), preferred_element_type=F32)


def nn(left, right):
    return dot(left, right, ((1,), (0,)))


def nt(left, right):
    return dot(left, right, ((1,), (1,)))


def tn(left, right):
    return dot(left, right, ((0,), (0,)))


def fold(value):
    rows, width = value.shape
    return jnp.sum(value.reshape(rows // 8, 8, width), 0)


def total(value):
    return jnp.sum(jnp.sum(value, 1, keepdims=True), 0, keepdims=True)


def normalise(value):
    centre = value - jnp.mean(value, -1, keepdims=True)
    inverse = lax.rsqrt(jnp.mean(centre * centre, -1, keepdims=True) + EPS_NORM)
    return (centre * inverse, inverse)


def norm_grad(grad, gain, normed, inverse):
    scaled = grad * gain
    return inverse * (
        scaled
        - jnp.mean(scaled, -1, keepdims=True)
        - normed * jnp.mean(scaled * normed, -1, keepdims=True)
    )


def split_two(value):
    high = value.astype(BF16)
    return (high, (value - high.astype(F32)).astype(BF16))


def swap(tile):
    return pltpu.roll(tile, HEAD_DIM, 1)


def tiles(value):
    return [value[:, i : i + 128] for i in range(0, value.shape[1], 128)]


def low_half(shape):
    return lax.broadcasted_iota(jnp.int32, shape, 1) < HEAD_DIM


def pack_two(left, right):
    low = low_half(left[0].shape)
    return [
        left[0],
        jnp.where(low, left[1], swap(right[0])),
        jnp.where(low, swap(right[0]), swap(right[1])),
    ]


def unpack_two(packed):
    low = low_half(packed[0].shape)
    nothing = jnp.zeros_like(packed[0])
    middle, last = swap(packed[1]), swap(packed[2])
    return (
        [packed[0], jnp.where(low, packed[1], nothing)],
        [jnp.where(low, middle, last), jnp.where(low, last, nothing)],
    )


def train_kernel(
    sizes,
    tau_ref,
    count_ref,
    label_ref,
    index_ref,
    x_hbm,
    main_in,
    wo_in,
    table_in,
    bias_in,
    main_out,
    table_out,
    low_out,
    tile_out,
    norm_out,
    wqkv, w1, wot, w2t, wet, head,
    wqkv_f, w1_f, wot_f, wet_f, pos_f, head_f, vec_f, bias_f,
    wqkv_m, w1_m, wot_m, wet_m, pos_m, head_m, vec_m, bias_m,
    wqkv_g, wot_g, wet_g, pos_g, head_g, vec_g,
    xbuf, h0, slope, prob, abuf, qkv, oall, third, ubuf, dpre, h1own, datt, chip, inverses,
    hsum, asum, dact, bsum, vacc, ssq,
    low_d, low_a, low_b, low_w, scal, loss_all, factor_kept, bias_wide, bias_start,
    s1, r1, s2, r2, mx_s, mx_r, nx_s, nx_r, pos_r, vec_r,
    wsem, xsem, o_ps, o_xs, o_fs, o_pr, o_xr, o_fr,
    a1s, a1r, a2s, a2r, das, dar, pvs, pvr, mxs, mxr, nxs, nxr, osem,
):
    steps, seq, pad, classes, clients = sizes
    width = 768
    kept = (seq + 7) // 8 * 8
    me = lax.axis_index("tensor")
    core = lax.rem(me, 2)
    mate = me + 1 - 2 * core
    across = lax.rem(me + 2, 4)
    own0 = 2 * core
    oth0 = 2 - 2 * core

    def rows(n):
        return pl.ds(pl.multiple_of(n * pad, 16), pad)

    def sent_rows(n):
        return pl.ds(pl.multiple_of(n * pad, 16), kept)

    def remote(src, dst, send, recv, device):
        return pltpu.make_async_remote_copy(
            src_ref=src, dst_ref=dst, send_sem=send, recv_sem=recv,
            device_id={"tensor": device}, device_id_type=MESH,
        )

    rest = dpre.at[0:width, 0:REST]
    square_rows = pl.ds(0, width)
    raw = abuf.at[square_rows, :]
    wo_raw = [ubuf.at[square_rows, pl.ds(g * LANE, LANE)] for g in range(3)] + [
        qkv.at[square_rows, pl.ds(0, LANE)]
    ]
    weights_in = [
        main_in.at[:, 2 * width : 3 * width],
        main_in.at[:, 0:width],
        main_in.at[:, width : 2 * width],
        table_in.at[:, 0:width],
        table_in.at[:, width : width + REST],
    ] + [wo_in.at[:, g * LANE : (g + 1) * LANE] for g in range(4)]
    weights = [raw, w1, w2t, wet, rest] + wo_raw

    def load(which):
        return pltpu.make_async_copy(weights_in[which], weights[which], wsem.at[which])

    def fetch(step, slot):
        return pltpu.make_async_copy(x_hbm.at[step], xbuf.at[slot], xsem.at[slot])

    barrier = pltpu.get_barrier_semaphore()
    fetch(0, 0).start()
    for which in range(9):
        load(which).start()
    for zero in (r1, r2, oall, third, datt):
        zero[...] = jnp.zeros_like(zero)
    for shift in (1, 2, 3):
        pl.semaphore_signal(
            barrier, inc=1, device_id={"tensor": lax.rem(me + shift, 4)}, device_id_type=MESH
        )
    bias_wide[...] = jnp.zeros_like(bias_wide)
    bias_wide[0 : bias_in.shape[0], 0 : bias_in.shape[1]] = bias_in[...].astype(F32)
    slabs = [tiles(bias_wide[r : r + 1, :]) for r in range(4)]
    first_bias = jnp.concatenate(pack_two(slabs[0], slabs[1]) + pack_two(slabs[2], slabs[3]), 1)
    bias_start[...] = jnp.broadcast_to(first_bias, (8, width))
    bias_f[...] = bias_start[...]
    for zero in (pos_m, head_m, vec_m, bias_m, low_a, low_b, low_w, loss_all):
        zero[...] = jnp.zeros_like(zero)
    low_d[...] = jnp.zeros_like(low_d)
    for which in (0, 3, 4, 5, 6, 7, 8):
        load(which).wait()
    n_head = head.shape[0]
    vec_at, head_at = seq, seq + 9
    h0[0:REST, :] = jnp.transpose(rest[...].astype(F32))
    pos_rows = lax.broadcasted_iota(jnp.int32, (pad, 1), 0) < seq
    vec_rows = lax.broadcasted_iota(jnp.int32, (SMALL, 1), 0) < 9
    pos_f[...] = jnp.where(pos_rows, h0[0:pad, :], 0.0)
    vec_f[...] = jnp.where(vec_rows, h0[vec_at : vec_at + SMALL, :], 0.0)
    start_head = h0[head_at : head_at + n_head, :]
    head_f[...] = start_head
    head[...] = start_head.astype(BF16)
    taken = tau_ref[0]

    def join(parts):
        return jnp.concatenate(parts, 1)

    def start_rows(j, carry):
        at = pl.ds(pl.multiple_of(j * 64, 64), 64)
        packed = tiles(raw[at, :].astype(F32))
        q, k = unpack_two(packed[:3])
        v, _ = unpack_two(packed[3:])
        wqkv[at, :] = join(q + k + v).astype(BF16)
        pieces = [tiles(piece[at, :].astype(F32)) for piece in wo_raw]
        low = low_half((64, 128))
        first = [jnp.where(low, swap(p[0]), swap(p[1])) for p in pieces]
        last = [
            jnp.where(low, swap(pieces[g][1]), pieces[g + 1][1]) for g in (0, 2)
        ]
        wot[at, :] = join(first + last).astype(BF16)
        return carry

    lax.fori_loop(0, width // 64, start_rows, 0)
    pl.semaphore_wait(barrier, 3)

    row_id = lax.broadcasted_iota(jnp.int32, (pad, 1), 0)
    token = row_id < seq
    key_ok = lax.broadcasted_iota(jnp.int32, (1, pad), 1) < seq
    lane_head = lax.broadcasted_iota(jnp.int32, (1, LANE), 1) // HEAD_DIM
    small_ok = lax.broadcasted_iota(jnp.int32, (SMALL, 1), 0) < 4
    scale = HEAD_DIM ** (-0.5)

    def of_head(value, h):
        return jnp.where(lane_head == h, value, jnp.zeros_like(value))

    def o_part(message, group):
        lanes = pl.ds(pl.multiple_of(group * 128, 128), 128)
        pair, which = message // 3, message % 3
        if which == 2:
            return third.at[pair, 0:kept, lanes]
        return oall.at[pl.ds((2 * pair + which) * pad, kept), lanes]

    def o_to_mate(message):
        place = o_part(message, me)
        return remote(place, place, o_ps.at[message], o_pr.at[message], mate)

    def o_across(message):
        place = o_part(message, me)
        return remote(place, place, o_xs.at[message], o_xr.at[message], across)

    def o_forward(message):
        place = o_part(message, across)
        return remote(place, place, o_fs.at[message], o_fr.at[message], mate)

    def relay_o(message):
        place = o_part(message, across)
        remote(place, place, o_xs.at[message], o_xr.at[message], across).wait_recv()
        o_forward(message).start()

    def o_here(message):
        direct = o_part(message, mate)
        remote(direct, direct, o_ps.at[message], o_pr.at[message], mate).wait_recv()
        passed = o_part(message, lax.rem(mate + 2, 4))
        remote(passed, passed, o_fs.at[message], o_fr.at[message], mate).wait_recv()

    def to_mate(n):
        return remote(s1.at[n, 0:kept], r1.at[n, 0:kept], a1s.at[n], a1r.at[n], mate)

    def to_across(which, n):
        return remote(s2.at[n, 0:kept], r2.at[2 * which + n, 0:kept], a2s.at[2 * which + n], a2r.at[2 * which + n], across)

    def gradient_to_mate(buffer, which, image, k):
        return remote(
            buffer.at[sent_rows(image)], buffer.at[sent_rows(image)],
            das.at[2 * which + k], dar.at[2 * which + k], mate,
        )

    def pos_to_mate():
        return remote(pos_g, pos_r, pvs.at[0], pvr.at[0], mate)

    def vec_to_mate():
        return remote(vacc, vec_r, pvs.at[1], pvr.at[1], mate)

    def spread(src, dst, send, recv, shift):
        return remote(
            src, dst.at[me], send.at[shift - 1], recv.at[shift - 1], lax.rem(me + shift, 4)
        )

    def update_rows(entries, rho, live, fac):
        def update(j, carry):
            at = pl.ds(pl.multiple_of(j * 64, 64), 64)
            for low, full, mom, grad in entries:
                m = rho * mom[at, :] + fac * grad[at, :]
                mom[at, :] = m
                w = full[at, :] - (live * LOCAL_RATE) * m
                full[at, :] = w
                low[at, :] = w.astype(BF16)
            return carry

        lax.fori_loop(0, width // 64, update, 0)

    def one_step(step, carry):
        slot = lax.rem(step, 2)
        fetch(step, slot).wait()

        @pl.when(step < steps - 1)
        def _():
            fetch(step + 1, 1 - slot).start()

        gain1, shift1 = vec_f[0:1, :], vec_f[1:2, :]
        gain2, shift2 = vec_f[2:3, :], vec_f[3:4, :]
        gain3, shift3 = vec_f[4:5, :], vec_f[5:6, :]

        def attend(pair):
            two = slice(2 * pair * pad, 2 * (pair + 1) * pad)
            inside = (row_id >= 1) & token
            added = pos_f[...] + jnp.where(inside, vec_f[6:7, :], 0.0)
            state = nt(xbuf[slot, two, :], wet[...]) + jnp.concatenate([added, added], 0)
            h0[two, :] = state
            normed, _ = normalise(state)
            a = (normed * gain1 + shift1).astype(BF16)
            abuf[two, :] = a
            both = nn(a, wqkv[...]).astype(BF16)
            qkv[two, :] = both
            mine = pl.ds(pl.multiple_of(me * 128, 128), 128)
            thirds = []
            for i in range(2):
                projected = both[i * pad : (i + 1) * pad]
                q, k, v = projected[:, :LANE], projected[:, LANE : 2 * LANE], projected[:, 2 * LANE :]
                out = jnp.zeros((pad, LANE), F32)
                for h in range(3):
                    scores = jnp.where(key_ok, nt(of_head(q, h), k) * scale, NEG)
                    expd = jnp.exp(scores - jnp.max(scores, -1, keepdims=True))
                    p = (expd * (1.0 / jnp.sum(expd, -1, keepdims=True))).astype(BF16)
                    prob[(2 * pair + i) * 3 + h] = p
                    out = out + nn(p, of_head(v, h))
                oall[(2 * pair + i) * pad : (2 * pair + i + 1) * pad, mine] = out[:, :128].astype(BF16)
                thirds.append(out[:, 128:])
                o_to_mate(3 * pair + i).start()
                o_across(3 * pair + i).start()
            third[pair, :, mine] = (thirds[0] + swap(thirds[1])).astype(BF16)
            o_to_mate(3 * pair + 2).start()
            o_across(3 * pair + 2).start()

        attend(0)
        attend(1)

        @pl.when(step == 0)
        def _():
            load(1).wait()
            load(2).wait()

            def begin(j, carry):
                at = pl.ds(pl.multiple_of(j * 32, 32), 32)
                for low_ref, full, mom in (
                    (wqkv, wqkv_f, wqkv_m), (w1, w1_f, w1_m), (wot, wot_f, wot_m), (wet, wet_f, wet_m)
                ):
                    full[at, :] = low_ref[at, :].astype(F32)
                    mom[at, :] = jnp.zeros((32, width), F32)
                return carry

            lax.fori_loop(0, width // 32, begin, 0)

        @pl.when(step > 0)
        def _():
            was_live = jnp.where(step - 1 < taken, 1.0, 0.0)
            was_rho = jnp.where(step - 1 < taken, MOMENTUM_RHO, 1.0)
            was_fac = factor_kept[0:1, 0:1]
            update_rows(((w1, w1_f, w1_m, slope), (wot, wot_f, wot_m, wot_g)), was_rho, was_live, was_fac)
            head_m[...] = was_rho * head_m[...] + was_fac * head_g[...]
            head_f[...] = head_f[...] - (was_live * LOCAL_RATE) * head_m[...]
            head[...] = head_f[...].astype(BF16)
            moved_rows = (LOCAL_RATE * low_w[:, 0:1]) * low_a[...]
            low_hi, low_lo = split_two(moved_rows)
            pair_rows = jnp.concatenate([low_hi, low_lo], 0)
            load(2).wait()

            def low_rank(j, carry):
                at = pl.ds(pl.multiple_of(j * LANE, LANE), LANE)
                moved = tn(jnp.concatenate([low_d[:, at], low_d[:, at]], 0), pair_rows)
                w2t[at, :] = (w2t[at, :].astype(F32) - moved).astype(BF16)
                return carry

            lax.fori_loop(0, width // LANE, low_rank, 0)

        for message in range(3):
            relay_o(message)

        def feed(pair):
            for message in range(3):
                o_here(3 * pair + message)
            two = slice(2 * pair * pad, 2 * (pair + 1) * pad)
            side = tiles(third[pair].astype(F32))
            low = low_half((pad, 128))
            for i in range(2):
                for g in (0, 2):
                    if i == 0:
                        tile = jnp.where(low, side[g], swap(side[g + 1]))
                    else:
                        tile = jnp.where(low, swap(side[g]), side[g + 1])
                    at = 4 * 128 + g * HEAD_DIM
                    oall[(2 * pair + i) * pad : (2 * pair + i + 1) * pad, at : at + 128] = tile.astype(BF16)
            state = h0[two, :] + nt(oall[two, :], wot[...]) + vec_f[7:8, :]
            differs = (pair + core) - 2 * pair * core
            for i in range(2):
                part = state[i * pad : (i + 1) * pad]
                h1own[i * (1 - differs) + 2 * differs] = part
                hsum[2 * pair + i] = fold(jnp.where(token, part, 0.0))
            normed, _ = normalise(state)
            u = (normed * gain2 + shift2).astype(BF16)
            ubuf[two, :] = u
            if pair == 0:
                relay_o(3)
                relay_o(4)
            z = nn(u, w1[...]) + bias_f[0:1, :]
            cdf = 0.5 * (1.0 + lax.erf(z * SQRT_HALF))
            act = (z * cdf).astype(BF16).astype(F32)
            tail = cdf + z * jnp.exp(-0.5 * z * z) * INV_ROOT_TAU
            for i in range(2):
                part = slice(i * pad, (i + 1) * pad)
                asum[2 * pair + i] = fold(jnp.where(token, act[part], 0.0))
                slope[(2 * pair + i) * pad : (2 * pair + i + 1) * pad, :] = jnp.where(token, tail[part], 0.0)
            if pair == 0:
                relay_o(5)

        feed(0)
        feed(1)

        def stack(ref):
            parts = [jnp.sum(ref[n], 0, keepdims=True) for n in range(4)]
            return jnp.concatenate(parts + [jnp.zeros((SMALL - 4, width), F32)], 0)

        act_sum = stack(asum)
        act_hi, act_lo = split_two(act_sum)
        both = nt(jnp.concatenate([act_hi, act_lo], 0), w2t[...])
        folded = both[:4] + both[SMALL : SMALL + 4]
        mx_s[...] = jnp.concatenate([folded[:, : width // 2], folded[:, width // 2 :]], 0)
        for shift in (1, 2, 3):
            spread(mx_s, mx_r, mxs, mxr, shift).start()
        mx_r[me] = mx_s[...]
        h_mean = stack(hsum) * (1.0 / seq)
        for shift in (1, 2, 3):
            remote(
                mx_s, mx_r.at[lax.rem(me + 4 - shift, 4)], mxs.at[shift - 1], mxr.at[shift - 1], mate
            ).wait_recv()
        halves = mx_r[0] + mx_r[1] + mx_r[2] + mx_r[3]
        mlp = jnp.concatenate(
            [jnp.concatenate([halves[:4], halves[4:]], 1), jnp.zeros((SMALL - 4, width), F32)], 0
        )
        average = h_mean + mlp * (1.0 / seq) + vec_f[8:9, :]
        normed3, inverse3 = normalise(average)
        pooled = (normed3 * gain3 + shift3).astype(BF16)
        logits = nt(pooled, head[...])
        class_ok = lax.broadcasted_iota(jnp.int32, (1, head.shape[0]), 1) < classes
        logits = jnp.where(class_ok, logits, NEG)
        top = jnp.max(logits, -1, keepdims=True)
        exp_l = jnp.exp(logits - top)
        total_l = jnp.sum(exp_l, -1, keepdims=True)
        hot_row = lax.broadcasted_iota(jnp.int32, (SMALL, n_head), 0)
        hot_lane = lax.broadcasted_iota(jnp.int32, (SMALL, n_head), 1)
        hot = jnp.zeros((SMALL, n_head), F32)
        for n in range(4):
            label = label_ref[index_ref[0, step, n]]
            hot = jnp.where((hot_row == n) & (hot_lane == label), 1.0, hot)
        each = top + jnp.log(total_l) - jnp.sum(jnp.where(class_ok, logits, 0.0) * hot, -1, keepdims=True)
        loss = jnp.sum(jnp.where(small_ok, each, 0.0), 0, keepdims=True) * 0.25
        live = jnp.where(step < taken, 1.0, 0.0)
        rho = jnp.where(step < taken, MOMENTUM_RHO, 1.0)
        loss_tile = live * loss
        d_logits = jnp.where(small_ok, (exp_l / total_l - hot) * 0.25, 0.0).astype(BF16)
        d_head = tn(d_logits, pooled)
        head_g[...] = d_head
        d_pooled = nn(d_logits, head[...])
        d_average = norm_grad(d_pooled, gain3, normed3, inverse3)
        d_token = d_average * (1.0 / seq)
        d_mlp = d_token.astype(BF16)
        dact[...] = nn(d_mlp, w2t[...])
        for r in range(4):
            scal[r] = jnp.broadcast_to(d_token[r : r + 1, :], (8, width))
        vec_g[...] = jnp.zeros_like(vec_g)
        vec_g[4:5, :] = jnp.sum(d_pooled * normed3, 0, keepdims=True)
        vec_g[5:6, :] = jnp.sum(d_pooled, 0, keepdims=True)
        vec_g[8:9, :] = jnp.sum(d_average, 0, keepdims=True)
        low_at = pl.ds(pl.multiple_of(step * SMALL, SMALL), SMALL)
        low_d[low_at, :] = d_mlp
        low_a[low_at, :] = act_sum
        gram_d = nt(d_mlp, d_mlp)
        gram_a = nt(act_hi, act_hi) + nt(act_hi, act_lo) + nt(act_lo, act_hi)
        own_squares = total(gram_d * gram_a)

        for n in range(4):
            scal[4 + n] = jnp.broadcast_to(dact[n : n + 1, :], (8, width))
        bsum[...] = jnp.zeros_like(bsum)
        vacc[...] = jnp.zeros_like(vacc)

        def upper_partial(n):
            at = pl.ds(pl.multiple_of(n * pad, 16), 2 * pad)
            rate = jnp.concatenate(
                [jnp.broadcast_to(scal[4 + n + i][0:1, :], (pad, width)) for i in range(2)], 0
            )
            g = (rate * slope[at, :]).astype(BF16)
            dpre[at, :] = g
            bsum[...] = bsum[...] + fold(g.astype(F32))
            return nt(g, w1[...])

        other = upper_partial(oth0)
        for k in (0, 1):
            s1[k] = other[k * pad : (k + 1) * pad].astype(BF16)
            to_mate(k).start()
        own = upper_partial(own0)
        for k in (0, 1):
            to_mate(k).wait_recv()
            part = own[k * pad : (k + 1) * pad] + r1[k].astype(F32)
            chip[k] = part
            s2[k] = part.astype(BF16)
            to_across(0, k).start()

        ssq[...] = jnp.zeros_like(ssq)
        w1_g = slope

        def weight_grad(left, right, out, which):
            def tile(j, carry):
                at = pl.ds(pl.multiple_of(j * LANE, LANE), LANE)
                g = tn(left[:, at], right[...])
                out[at, :] = g
                ssq[which] = ssq[which] + fold(g * g)
                return carry

            lax.fori_loop(0, width // LANE, tile, 0)

        def embedding_grad(image, left, adds, last):
            def tile(j, carry):
                at = pl.ds(pl.multiple_of(j * LANE, LANE), LANE)
                g = tn(left[rows(image), at], xbuf[slot, rows(image), :])
                if adds:
                    g = g + wet_g[at, :]
                if last:
                    ssq[3] = ssq[3] + fold(g * g)
                wet_g[at, :] = g
                return carry

            lax.fori_loop(0, width // LANE, tile, 0)

        weight_grad(ubuf, dpre, w1_g, 0)

        for k in (0, 1):
            normed, inverse = normalise(h1own[k])
            h1own[k] = normed
            inverses[k] = inverse
            normed, inverse = normalise(h0[rows(own0 + k), :])
            h0[rows(own0 + k), :] = normed
            inverses[2 + k] = inverse

        def attention_partial(n):
            own_columns = jnp.concatenate(
                [
                    wot[:, pl.ds(pl.multiple_of(me * 128, 128), 128)],
                    wot[:, pl.ds(pl.multiple_of(4 * 128 + (me // 2) * 128, 128), 128)],
                ],
                1,
            )
            wide = nn(datt[rows(n), :], own_columns)
            thirds = jnp.where(core == 1, swap(wide[:, 128:]), wide[:, 128:])
            thirds = jnp.where(low_half((pad, 128)), thirds, 0.0)
            d_ctx = jnp.concatenate([wide[:, :128], thirds], 1).astype(BF16)
            projected = qkv[rows(n), :]
            q, k, v = projected[:, :LANE], projected[:, LANE : 2 * LANE], projected[:, 2 * LANE :]
            d_q = jnp.zeros((pad, LANE), F32)
            d_k = jnp.zeros((pad, LANE), F32)
            d_v = jnp.zeros((pad, LANE), F32)
            for h in range(3):
                part = of_head(d_ctx, h)
                p = prob[n * 3 + h]
                again = p.astype(F32)
                d_p = nt(part, v)
                inner = d_p - jnp.sum(d_p * again, -1, keepdims=True)
                d_s = (again * inner).astype(BF16)
                d_v = d_v + tn(p, part)
                d_q = d_q + nn(d_s, of_head(k, h))
                d_k = d_k + tn(d_s, of_head(q, h))
            d_all = jnp.concatenate([d_q * scale, d_k * scale, d_v], 1).astype(BF16)
            qkv[rows(n), :] = d_all
            return nt(d_all, wqkv[...])

        for k in (0, 1):
            to_across(0, k).wait_recv()
            d_upper = chip[k] + r2[k].astype(F32)
            normed = h1own[k]
            d_state = norm_grad(d_upper, gain2, normed, inverses[k]) + scal[own0 + k][0:1, :]
            d_state = jnp.where(token, d_state, 0.0)
            h1own[k] = d_state
            datt[rows(own0 + k), :] = d_state.astype(BF16)
            gradient_to_mate(datt, 0, own0 + k, k).start()
            vacc[0] = vacc[0] + fold(d_upper * normed)
            vacc[1] = vacc[1] + fold(d_upper)
            vacc[2] = vacc[2] + fold(d_state)
            own = attention_partial(own0 + k)
            remote(
                datt.at[sent_rows(oth0 + k)], datt.at[sent_rows(oth0 + k)], das.at[k], dar.at[k], mate
            ).wait_recv()
            other = attention_partial(oth0 + k)
            to_mate(k).wait_send()
            s1[k] = other.astype(BF16)
            to_mate(k).start()
            to_mate(k).wait_recv()
            own = own + r1[k].astype(F32)
            chip[k] = own
            to_across(0, k).wait_send()
            s2[k] = own.astype(BF16)
            to_across(1, k).start()

        weight_grad(datt, oall, wot_g, 1)
        weight_grad(abuf, qkv, wqkv_g, 2)

        d_bias = jnp.sum(bsum[...], 0, keepdims=True)
        own_squares = own_squares + total(ssq[0] + ssq[2]) + total(d_bias * d_bias)
        shared = total(ssq[1] + fold(head_g[...] * head_g[...]))

        d_emb = ubuf
        for k in (0, 1):
            to_across(1, k).wait_recv()
            d_normed = chip[k] + r2[2 + k].astype(F32)
            normed = h0[rows(own0 + k), :]
            d_state = h1own[k] + norm_grad(d_normed, gain1, normed, inverses[2 + k])
            d_emb[rows(own0 + k), :] = d_state.astype(BF16)
            gradient_to_mate(d_emb, 1, own0 + k, k).start()
            vacc[3] = vacc[3] + fold(d_normed * normed)
            vacc[4] = vacc[4] + fold(d_normed)
            vacc[5] = vacc[5] + fold(jnp.where(row_id >= 1, d_state, 0.0))
            if k == 0:
                pos_g[...] = d_state
            else:
                pos_g[...] = pos_g[...] + d_state
                pos_to_mate().start()
                vec_to_mate().start()
            embedding_grad(own0 + k, d_emb, k == 1, False)
            remote(
                d_emb.at[sent_rows(oth0 + k)], d_emb.at[sent_rows(oth0 + k)],
                das.at[2 + k], dar.at[2 + k], mate,
            ).wait_recv()
            embedding_grad(oth0 + k, d_emb, True, k == 1)
        pos_to_mate().wait()
        vec_to_mate().wait()
        pos_g[...] = pos_g[...] + pos_r[...]
        sums = [jnp.sum(vacc[r] + vec_r[r], 0, keepdims=True) for r in range(6)]
        vec_g[0:1, :] = sums[3]
        vec_g[1:2, :] = sums[4]
        vec_g[2:3, :] = sums[0]
        vec_g[3:4, :] = sums[1]
        vec_g[6:7, :] = sums[5]
        vec_g[7:8, :] = sums[2]
        shared = (
            shared
            + total(ssq[3] + fold(pos_g[...] * pos_g[...]))
            + total(vec_g[...] * vec_g[...])
        )
        for message in range(6):
            o_to_mate(message).wait_send()
            o_across(message).wait_send()
            o_forward(message).wait_send()
        for k in (0, 1):
            to_mate(k).wait_send()
            to_across(1, k).wait_send()
            gradient_to_mate(datt, 0, own0 + k, k).wait_send()
            gradient_to_mate(d_emb, 1, own0 + k, k).wait_send()
        for shift in (1, 2, 3):
            spread(mx_s, mx_r, mxs, mxr, shift).wait_send()
        first_lane = lax.broadcasted_iota(jnp.int32, (8, 128), 1) < 64
        nx_s[...] = jnp.where(first_lane, own_squares + 0.25 * shared, loss_tile)
        for shift in (1, 2, 3):
            spread(nx_s, nx_r, nxs, nxr, shift).start()
        nx_r[me] = nx_s[...]

        @pl.when(step == steps - 1)
        def _():
            for which in (0, 1, 3, 4):
                load(which).start()

        for shift in (1, 2, 3):
            remote(
                nx_s, nx_r.at[lax.rem(me + 4 - shift, 4)], nxs.at[shift - 1], nxr.at[shift - 1], mate
            ).wait_recv()
        norm = jnp.sqrt((nx_r[0] + nx_r[1] + nx_r[2] + nx_r[3]))
        factor = live * (CLIP_LIMIT / jnp.maximum(norm, CLIP_LIMIT))
        norm_out[step] = live * norm
        loss_all[...] = loss_all[...] + nx_r[0]
        for shift in (1, 2, 3):
            spread(nx_s, nx_r, nxs, nxr, shift).wait_send()
        fac = factor[0:1, 0:1]

        low_row = lax.broadcasted_iota(jnp.int32, low_b.shape, 0) // SMALL
        low_b[...] = jnp.where(low_row == step, fac, rho * low_b[...])
        low_w[...] = low_w[...] + live * low_b[...]
        factors = (LOCAL_RATE * low_w[:, 0:1]) * low_a[...]
        factor_kept[...] = factor

        def small_update(full, mom, grad):
            mom[...] = rho * mom[...] + fac * grad
            full[...] = full[...] - (live * LOCAL_RATE) * mom[...]

        small_update(pos_f, pos_m, pos_g[...])
        small_update(vec_f, vec_m, vec_g[...])
        small_update(bias_f, bias_m, jnp.broadcast_to(d_bias, (8, width)))
        table = (
            (wqkv, wqkv_f, wqkv_m, wqkv_g),
            (w1, w1_f, w1_m, w1_g),
            (wot, wot_f, wot_m, wot_g),
            (wet, wet_f, wet_m, wet_g),
        )

        @pl.when(step < steps - 1)
        def _():
            load(2).start()
            update_rows((table[0], table[3]), rho, live, fac)

        @pl.when(step == steps - 1)
        def _():
            examples = jnp.full((1, 1), count_ref[0].astype(F32))
            factor_sum = jnp.zeros((), F32)
            for k in range(steps):
                worth = (1.0 - MOMENTUM_RHO ** (k + 1)) / (1.0 - MOMENTUM_RHO)
                factor_sum = factor_sum + jnp.where(k < taken, worth, 0.0)
            factor_sum = jnp.full((1, 1), factor_sum)
            share = examples / factor_sum
            for which in (0, 1, 3, 4):
                load(which).wait()

            def ended(at, full, mom, grad, lanes):
                m = rho * mom[at, lanes] + fac * grad[at, lanes]
                return full[at, lanes] - (live * LOCAL_RATE) * m

            outs = (
                (w1, main_out.at[:, 0:width]),
                (wet, table_out.at[:, 0:width]),
                (raw, main_out.at[:, width : 2 * width]),
                (rest, table_out.at[:, width : width + REST]),
            )
            copies = [
                pltpu.make_async_copy(src, dst, osem.at[i]) for i, (src, dst) in enumerate(outs)
            ]
            for i, (low, full, mom, grad) in enumerate((table[1], table[3])):

                def finish_square(j, carry):
                    at = pl.ds(pl.multiple_of(j * 64, 64), 64)
                    w = ended(at, full, mom, grad, slice(None))
                    low[at, :] = (share * (low[at, :].astype(F32) - w)).astype(BF16)
                    return carry

                lax.fori_loop(0, width // 64, finish_square, 0)
                copies[i].start()

            def finish(j, carry):
                at = pl.ds(pl.multiple_of(j * 64, 64), 64)
                three = tiles(ended(at, wqkv_f, wqkv_m, wqkv_g, slice(None)))
                _, full, mom, grad = table[2]
                wo_first = ended(at, full, mom, grad, pl.ds(pl.multiple_of(me * 128, 128), 128))
                wo_last = ended(
                    at, full, mom, grad, pl.ds(pl.multiple_of(4 * 128 + (me // 2) * 128, 128), 128)
                )
                wo_last = jnp.where(core == 1, swap(wo_last), wo_last)
                packed = join(
                    pack_two(three[0:2], three[2:4]) + pack_two(three[4:6], [wo_first, wo_last])
                )
                raw[at, :] = (share * (raw[at, :].astype(F32) - packed)).astype(BF16)
                return carry

            lax.fori_loop(0, width // 64, finish, 0)
            copies[2].start()
            small_update(head_f, head_m, head_g[...])
            h0[0:REST, :] = jnp.transpose(rest[...].astype(F32))
            for ref, begin, count in ((pos_f, 0, seq), (vec_f, vec_at, 9), (head_f, head_at, classes)):
                h0[begin : begin + count, :] = share * (h0[begin : begin + count, :] - ref[0:count, :])
            rest[...] = jnp.transpose(h0[0:REST, :]).astype(BF16)
            copies[3].start()
            d_bias_all = share * (bias_start[0:1, :] - bias_f[0:1, :])
            for r in range(width // 128):
                tile_out[r : r + 1, :] = d_bias_all[:, 128 * r : 128 * (r + 1)]
            lane = lax.broadcasted_iota(jnp.int32, (1, 128), 1)
            loss_sum = loss_all[0:1, 64:65]
            mean_loss = examples * loss_sum / jnp.full((1, 1), taken.astype(F32))
            scalars = jnp.where(lane == 0, examples, jnp.where(lane == 1, mean_loss, examples * factor_sum))
            tile_out[width // 128 : width // 128 + 1, :] = jnp.where(lane < 3, scalars, 0.0)
            tile_out[width // 128 + 1 :, :] = jnp.zeros((7 - width // 128, 128), F32)
            used = 4 * steps
            wanted_row = lax.broadcasted_iota(jnp.int32, (used, steps * SMALL), 0)
            wanted_row = (wanted_row // 4) * SMALL + lax.rem(wanted_row, 4)
            picker = (lax.broadcasted_iota(jnp.int32, (used, steps * SMALL), 1) == wanted_row).astype(BF16)
            low_left = nn(picker, (share * factors).astype(BF16)).astype(BF16)
            low_right = nn(picker, low_d[...])
            part = width // clients
            kept_lanes = lax.broadcasted_iota(jnp.int32, (used, 128), 1) < part
            for j in range(clients):
                low_out[j, :, 0:width] = low_left
                turned = pltpu.roll(low_right, (width - part * j) % width, 1) if j else low_right
                low_out[j, :, width : width + 128] = jnp.where(kept_lanes, turned[:, :128], 0.0).astype(BF16)
            for copy in copies:
                copy.wait()

        return carry

    lax.fori_loop(0, steps, one_step, 0)


def local_training(tau, counts, labels, index, patches, main, wo, table, bias, clients, pad, seq, classes):
    steps = patches.shape[0]
    width = main.shape[0]
    n_all = 4 * pad
    n_head = (classes + 127) // 128 * 128
    n_low = steps * SMALL
    vmem = pltpu.VMEM
    dma = pltpu.SemaphoreType.DMA
    anywhere = pl.BlockSpec(memory_space=pl.ANY)
    inside = pl.BlockSpec(memory_space=pltpu.VMEM)
    square = (width, width)
    out_shape = (
        jax.ShapeDtypeStruct((width, 2 * width), BF16),
        jax.ShapeDtypeStruct(table.shape, BF16),
        jax.ShapeDtypeStruct((clients, 4 * steps, width + 128), BF16),
        jax.ShapeDtypeStruct((8, 128), F32),
        jax.ShapeDtypeStruct((steps, 8, 128), F32),
    )
    scratch = [
        vmem(square, BF16), vmem(square, BF16), vmem(square, BF16), vmem(square, BF16),
        vmem(square, BF16), vmem((n_head, width), BF16),
    ]
    for _ in range(2):
        scratch += [
            vmem(square, F32), vmem(square, F32), vmem(square, F32), vmem(square, F32),
            vmem((pad, width), F32), vmem((n_head, width), F32), vmem((SMALL, width), F32),
            vmem((8, width), F32),
        ]
    scratch += [
        vmem(square, F32), vmem(square, F32), vmem(square, F32), vmem((pad, width), F32),
        vmem((n_head, width), F32), vmem((SMALL, width), F32),
        vmem((2, n_all, width), BF16), vmem((n_all, width), F32), vmem((n_all, width), F32),
        vmem((12, pad, pad), BF16), vmem((n_all, width), BF16), vmem((n_all, width), BF16),
        vmem((n_all, width), BF16), vmem((2, pad, 4 * 128), BF16), vmem((n_all, width), BF16),
        vmem((n_all, width), BF16), vmem((3, pad, width), F32), vmem((n_all, width), BF16),
        vmem((2, pad, width), F32), vmem((4, pad, 1), F32),
        vmem((4, 8, width), F32), vmem((4, 8, width), F32), vmem((SMALL, width), F32),
        vmem((8, width), F32), vmem((6, 8, width), F32), vmem((4, 8, width), F32),
        vmem((n_low, width), BF16), vmem((n_low, width), F32), vmem((n_low, 128), F32),
        vmem((n_low, 128), F32), vmem((8, 8, width), F32), vmem((8, 128), F32), vmem((8, 128), F32),
        vmem((8, LANE), F32), vmem((8, width), F32),
        vmem((2, pad, width), BF16), vmem((2, pad, width), BF16), vmem((2, pad, width), BF16),
        vmem((4, pad, width), BF16), vmem((8, width // 2), F32), vmem((4, 8, width // 2), F32),
        vmem((8, 128), F32), vmem((4, 8, 128), F32), vmem((pad, width), F32),
        vmem((6, 8, width), F32),
        dma((9,)), dma((2,)), dma((6,)), dma((6,)), dma((6,)), dma((6,)), dma((6,)), dma((6,)),
        dma((2,)), dma((2,)), dma((4,)), dma((4,)), dma((4,)), dma((4,)), dma((2,)), dma((2,)),
        dma((3,)), dma((3,)), dma((3,)), dma((3,)), dma((6,)),
    ]
    return pl.pallas_call(
        functools.partial(train_kernel, (steps, seq, pad, classes, clients)),
        out_shape=out_shape,
        in_specs=[pl.BlockSpec(memory_space=pltpu.SMEM)] * 4 + [anywhere] * 4 + [inside],
        out_specs=(anywhere,) * 2 + (inside,) * 3,
        scratch_shapes=scratch,
        compiler_params=pltpu.CompilerParams(
            collective_id=0, has_side_effects=True, vmem_limit_bytes=VMEM_LIMIT
        ),
        name="local_training",
    )(tau, counts, labels, index, patches, main, wo, table, bias)


def place_patches(chosen_ref, pool_ref, out_ref):
    seq_rows, width = pool_ref.shape[1], pool_ref.shape[2]
    pad = out_ref.shape[1]
    below = jnp.zeros((pad - 1 - seq_rows, width), F32)
    whole = jnp.concatenate([jnp.zeros((1, width), F32), pool_ref[0].astype(F32), below], 0)
    out_ref[0] = whole.astype(BF16)


def pick_patches(pool, chosen, pad):
    count = chosen.shape[0]
    _, patch_rows, width = pool.shape
    return pl.pallas_call(
        place_patches,
        out_shape=jax.ShapeDtypeStruct((count, pad, width), BF16),
        grid_spec=pltpu.PrefetchScalarGridSpec(
            num_scalar_prefetch=1,
            grid=(count,),
            in_specs=[pl.BlockSpec((1, patch_rows, width), lambda i, ids: (ids[i], 0, 0))],
            out_specs=pl.BlockSpec((1, pad, width), lambda i, ids: (i, 0, 0)),
        ),
        name="pick_patches",
    )(chosen, pool)


def ring_places(clients):
    depth = clients // 2
    client = lax.axis_index("client")
    member = lax.axis_index("tensor")
    core = lax.rem(member, 2)
    return (
        depth, client, client // 2, lax.rem(client, 2), member, core, member // 2,
        member + 1 - 2 * core, lax.rem(member + 2, 4),
    )


def send(src, dst, send_sem, recv_sem, client, member):
    return pltpu.make_async_remote_copy(
        src_ref=src, dst_ref=dst, send_sem=send_sem, recv_sem=recv_sem,
        device_id={"client": client, "tensor": member}, device_id_type=MESH,
    )


def span(start, size, unit):
    return pl.ds(pl.multiple_of(start, unit), size)


def gather_kernel(
    clients, index_ref, in_ref, out_ref, table_in, pool_ref, main_out, wo_out, table_out, x_out,
    main_ref, table_ref, wide_in, wide_out, pool_buf, x_buf, pool_sem, x_sem, up_s, up_r, down_s, down_r, y_s, y_r, mate_s, mate_r, x_s, x_r, on_s, on_r, own_sem, keep_sem,
):
    depth, client, z, y, member, core, chip_x, mate, across = ring_places(clients)
    block = main_ref.shape[0]
    half = block // 2
    columns = table_ref.shape[1] // 2
    peer = client + 1 - 2 * y

    wide = main_ref.shape[1]
    tail = wide - LANE

    def table_part(origin, who):
        return table_out.at[
            span(origin * block + (who // 2) * half, half, half),
            span(lax.rem(who, 2) * columns, columns, 128),
        ]

    def wo_part(origin, who):
        return wo_out.at[span(origin * block, block, block), span(who * LANE, LANE, LANE)]

    def shared(origin, who):
        return (wo_part(origin, who), table_part(origin, who))

    def main_part(origin, lanes):
        return main_out.at[span(origin * block, block, block), lanes]

    early, front, back = slice(0, wide // 6), slice(wide // 6, 2 * wide // 3), slice(2 * wide // 3, wide)

    def beside(origin):
        return origin + 1 - 2 * lax.rem(origin, 2)

    def landed(origin):
        return (
            main_part(origin, back), table_part(origin, member), main_part(origin, front),
            main_part(origin, early), main_part(beside(origin), early),
        )

    own_table = table_ref.at[span(chip_x * half, half, half), span(core * columns, columns, 128)]
    own_pieces = (
        main_ref.at[:, back], own_table, main_ref.at[:, front], main_ref.at[:, early],
        main_part(peer, early),
    )

    def given(origin, mine):
        if mine:
            return (main_ref.at[:, tail:wide], own_table)
        return (main_part(origin, slice(tail, wide)), table_part(origin, member))

    def message(origin, mine, send_sem, recv_sem, index, to, part):
        sources = own_pieces if mine else landed(origin)
        return [
            send(src, dst, send_sem.at[p, index], recv_sem.at[p, index], to, member)
            for p, (src, dst) in enumerate(zip(sources, landed(origin)))
        ][part]

    first, second, third, over_all, crossing = slice(0, 2), slice(2, 3), slice(3, 5), slice(0, 3), slice(3, 4)

    def up(origin, i, part, mine=False):
        return message(origin, mine, up_s, up_r, i, client + 2, part)

    def down(origin, i, part, mine=False):
        return message(origin, mine, down_s, down_r, i, client - 2, part)

    def over(origin, part, mine=False):
        return message(origin, mine, y_s, y_r, origin // 2, peer, part)

    def give(origin, mine, send_sem, recv_sem, to):
        return [
            send(src, dst, send_sem.at[p, origin], recv_sem.at[p, origin], client, to)
            for p, (src, dst) in enumerate(zip(given(origin, mine), shared(origin, member)))
        ]

    def keep(origin, mine=False):
        return pltpu.make_async_copy(given(origin, mine)[0], wo_part(origin, member), keep_sem.at[origin])

    def share(origin, mine=False):
        return give(origin, mine, mate_s, mate_r, mate) + give(origin, mine, x_s, x_r, across)

    def from_across(origin):
        return [
            send(dst, dst, x_s.at[p, origin], x_r.at[p, origin], client, across)
            for p, dst in enumerate(shared(origin, across))
        ]

    def pass_on(origin):
        return [
            send(dst, dst, on_s.at[p, origin], on_r.at[p, origin], client, mate)
            for p, dst in enumerate(shared(origin, across))
        ]

    def start(copies):
        for copy in copies:
            copy.start()

    def arrived(copies):
        for copy in copies:
            copy.wait_recv()

    def sent(copies):
        for copy in copies:
            copy.wait_send()

    has_up, has_down = z < depth - 1, z > 0

    barrier = pltpu.get_barrier_semaphore()

    def hello(to_client, to_member):
        pl.semaphore_signal(
            barrier, inc=1, device_id={"client": to_client, "tensor": to_member}, device_id_type=MESH
        )

    hello(peer, member)
    for shift in (1, 2, 3):
        hello(client, lax.rem(member + shift, 4))
    for shift in range(1, depth):
        hello(2 * lax.rem(z + shift, depth) + y, member)
    wide_in[...] = jnp.zeros_like(wide_in)
    wide_out[...] = jnp.zeros_like(wide_out)
    table_ref[...] = jnp.zeros_like(table_ref)
    table_ref[:, 0 : table_in.shape[1]] = table_in[...]

    def in_slab(i):
        wide_in[i, :, 0 : in_ref.shape[2]] = in_ref[i].astype(F32)
        return tiles(wide_in[i])

    def out_slab(i):
        wide_out[i, 0 : out_ref.shape[1], 0:block] = out_ref[i].astype(F32)
        return tiles(jnp.transpose(wide_out[i])[:block])

    ordered = [in_slab(i) for i in (3, 4, 5, 6)] + [out_slab(i) for i in (1, 2, 3, 4)]
    ordered += [in_slab(i) for i in (0, 1, 2)] + [out_slab(0)]
    for i in range(0, 12, 2):
        packed = jnp.concatenate(pack_two(ordered[i], ordered[i + 1]), 1)
        main_ref[:, 192 * i : 192 * (i + 2)] = packed.astype(BF16)

    pl.semaphore_wait(barrier, 3 + depth)

    def line_start(part):
        @pl.when(has_up)
        def _():
            start(up(client, 0, part, True))

        @pl.when(has_down)
        def _():
            start(down(client, 0, part, True))

    start(over(client, crossing, True))
    start(over(client, first, True))
    line_start(first)
    start(over(client, second, True))
    line_start(second)
    start(share(client, True))
    keep(client, True).start()
    local = [
        pltpu.make_async_copy(src, dst, own_sem.at[p])
        for p, (src, dst) in enumerate(zip(own_pieces[:4], landed(client)))
    ]
    start(local)

    _, steps, each = index_ref.shape
    images = steps * each
    pool_size = pool_buf.shape[1] // 8
    patch_rows = pool_ref.shape[0] // pool_size
    pad = x_out.shape[1]

    def base(b):
        return lax.min(lax.max(8 * b - 1, 0), patch_rows - 8)

    deep = pool_buf.shape[0]

    def pool_load(b):
        k = lax.rem(b, deep)
        return pltpu.make_async_copy(
            pool_ref.at[span(base(b) * pool_size, 8 * pool_size, 32), :], pool_buf.at[k], pool_sem.at[k]
        )

    def x_store(b):
        k = lax.rem(b, deep)
        return pltpu.make_async_copy(x_buf.at[k], x_out.at[:, span(8 * b, 8, 8), :], x_sem.at[k])

    for b in range(deep - 1):
        pool_load(b).start()
    lane = lax.broadcasted_iota(jnp.int32, (8 * images, 8 * pool_size), 1)
    select_row = lax.broadcasted_iota(jnp.int32, (8 * images, 1), 0)
    line_row = lax.rem(select_row, 8)
    chosen = jnp.zeros((8 * images, 1), jnp.int32)
    for i in range(images):
        chosen = jnp.where(select_row // 8 == i, index_ref[0, i // each, i % each], chosen)

    def pick(b, carry):
        k = lax.rem(b, deep)
        pool_load(b).wait()

        @pl.when(b < pad // 8 - (deep - 1))
        def _():
            pool_load(b + deep - 1).start()

        wanted = (8 * b - 1 + line_row - base(b)) * pool_size + chosen
        picked = nn((lane == wanted).astype(BF16), pool_buf[k]).astype(BF16)

        @pl.when(b >= deep)
        def _():
            x_store(b - deep).wait()

        x_buf[k] = picked.reshape(images, 8, picked.shape[1])
        x_store(b).start()
        return carry

    lax.fori_loop(0, pad // 16, pick, 0)

    def line(d, act):
        @pl.when(z >= d)
        def _():
            act(client - 2 * d, True)

        @pl.when(z < depth - d)
        def _():
            act(client + 2 * d, False)

    def across_line(d, act):
        if d == 0:
            act(peer, True)
            return

        @pl.when(z >= d)
        def _():
            act(peer - 2 * d, True)

        @pl.when(z < depth - d)
        def _():
            act(peer + 2 * d, False)

    def line_in(d, part):
        def act(origin, below):
            line_s, line_r = (up_s, up_r) if below else (down_s, down_r)
            arrived(message(origin, False, line_s, line_r, d - 1, peer, part))
            if d < depth - 1:

                @pl.when(has_up if below else has_down)
                def _():
                    start(up(origin, d, part) if below else down(origin, d, part))

            if part is not third:
                start(over(origin, part))
            if part is first:
                start(share(origin))
                keep(origin).start()

        return act

    def y_in(origin, below):
        arrived(over(origin, first))
        start(share(origin))
        keep(origin).start()

    def forward(origin, below=True):
        arrived(from_across(origin))
        start(pass_on(origin))

    for d in range(1, depth + 1):
        if d < depth:
            line(d, line_in(d, first))
        across_line(d - 1, y_in)
        if d < depth:
            line(d, line_in(d, second))
        if d == 1:
            arrived(over(peer, crossing))
            line_start(third)
        else:
            line(d - 1, line_in(d - 1, third))
        if d == 1:
            lax.fori_loop(pad // 16, pad // 8, pick, 0)
            for b in range(pad // 8 - deep, pad // 8):
                x_store(b).wait()
            forward(client)
        else:
            line(d - 1, forward)
            across_line(d - 2, forward)
    across_line(depth - 1, forward)
    for d in range(depth):
        across_line(d, lambda origin, below: arrived(over(origin, second)))

    for copy in local:
        copy.wait()
    for origin in range(clients):
        sent(share(origin))
        sent(pass_on(origin))
        keep(origin).wait()
        arrived([
            send(dst, dst, mate_s.at[p, origin], mate_r.at[p, origin], client, mate)
            for p, dst in enumerate(shared(origin, mate))
        ])
        arrived([
            send(dst, dst, on_s.at[p, origin], on_r.at[p, origin], client, mate)
            for p, dst in enumerate(shared(origin, lax.rem(mate + 2, 4)))
        ])
    sent(over(client, crossing))
    for d in range(depth):
        sent(over(2 * d + y, over_all))

        @pl.when(has_up & (z >= d))
        def _():
            if d < depth - 1:
                sent(up(client - 2 * d, d, slice(0, 5)))

        @pl.when(has_down & (z < depth - d))
        def _():
            if d < depth - 1:
                sent(down(client + 2 * d, d, slice(0, 5)))


def gather_weights(clients, index, in_bf, out_bf, table_t, pool, pad):
    depth = clients // 2
    dma = pltpu.SemaphoreType.DMA
    anywhere = pl.BlockSpec(memory_space=pl.ANY)
    inside = pl.BlockSpec(memory_space=pltpu.VMEM)
    slabs, own, group = in_bf.shape
    width = own * clients
    packed = (slabs + out_bf.shape[0]) * group
    table_lanes = width + REST
    hops = depth - 1
    pool_size, patch_rows, features = pool.shape
    images = index.shape[1] * index.shape[2]
    rows = jnp.transpose(pool, (1, 0, 2)).reshape(patch_rows * pool_size, features)
    return pl.pallas_call(
        functools.partial(gather_kernel, clients),
        out_shape=(
            jax.ShapeDtypeStruct((width, packed), BF16),
            jax.ShapeDtypeStruct((width, 4 * LANE), BF16),
            jax.ShapeDtypeStruct((width, table_lanes), BF16),
            jax.ShapeDtypeStruct((images, pad, features), BF16),
        ),
        in_specs=[pl.BlockSpec(memory_space=pltpu.SMEM)] + [inside] * 3 + [anywhere],
        out_specs=(anywhere,) * 4,
        scratch_shapes=[
            pltpu.VMEM((own, packed), BF16), pltpu.VMEM((own, table_lanes), BF16),
            pltpu.VMEM((slabs, own, LANE), F32), pltpu.VMEM((out_bf.shape[0], LANE, 128), F32),
            pltpu.VMEM((6, 8 * pool_size, features), BF16), pltpu.VMEM((6, images, 8, features), BF16),
            dma((6,)), dma((6,)),
            dma((5, hops)), dma((5, hops)), dma((5, hops)), dma((5, hops)), dma((4, depth)),
            dma((4, depth)),
        ] + [dma((2, clients))] * 6 + [dma((4,)), dma((clients,))],
        compiler_params=pltpu.CompilerParams(collective_id=1, has_side_effects=True),
        name="gather_weights",
    )(index, in_bf, out_bf, table_t, rows)


def reduce_kernel(
    clients, main_in, table_in, low_in, tile_in, main_out, table_out, low_out, tile_out,
    own_main, own_table, y_main, y_table, zs_main, zs_table, zr_main, zr_table, rl_main, rl_table,
    whole, low_all, tile_all, own_sem, y_s, y_r, z_s, z_r, rl_s, rl_r, low_s, low_r, tile_s, tile_r, q_s, q_r, keep_sem,
):
    depth, client, z, y, member, core, chip_x, mate, across = ring_places(clients)
    block = own_main.shape[1]
    half, columns = own_table.shape[1], own_table.shape[2]
    peer = client + 1 - 2 * y
    cut = own_main.shape[2] // 2
    lanes = (None, slice(0, cut), slice(cut, 2 * cut))
    parts = (0, 1, 2)

    def source(owner, p):
        if p == 0:
            return table_in.at[
                span(owner * block + chip_x * half, half, half), span(core * columns, columns, 128)
            ]
        return main_in.at[span(owner * block, block, block), lanes[p]]

    def slot(table_ref, main_ref, i, p):
        return table_ref.at[i] if p == 0 else main_ref.at[i, :, lanes[p]]

    def own_load(level, p):
        return pltpu.make_async_copy(
            source(2 * level + y, p), slot(own_table, own_main, level, p), own_sem.at[p, level]
        )

    def over(level, p):
        return send(
            source(2 * level + 1 - y, p), slot(y_table, y_main, level, p),
            y_s.at[p, level], y_r.at[p, level], peer, member,
        )

    side = z // 2
    outer = z == 3 * side
    near = z + 1 - 2 * lax.rem(z, 2)
    levels = (3 * (1 - side), 2 - side, near, z)

    def relay(i, p):
        return send(
            slot(zs_table, zs_main, i, p), slot(rl_table, rl_main, i, p),
            rl_s.at[p, i], rl_r.at[p, i], 2 * near + y, member,
        )

    def onward(i, p):
        last = i // 2
        return send(
            slot(zs_table, zs_main, i, p), slot(zr_table, zr_main, last, p),
            z_s.at[p, i], z_r.at[p, last], 2 * levels[i] + y, member,
        )

    def came(last, p):
        return send(
            slot(zs_table, zs_main, 0, p), slot(zr_table, zr_main, last, p),
            z_s.at[p, 0], z_r.at[p, last], peer, member,
        )

    def small(shift):
        to = lax.rem(client + shift, clients)
        return [
            send(low_in.at[to], low_all.at[client], low_s.at[shift - 1], low_r.at[shift - 1], to, member),
            send(tile_in, tile_all.at[client], tile_s.at[shift - 1], tile_r.at[shift - 1], to, member),
        ]

    def small_from(shift):
        origin = lax.rem(client + clients - shift, clients)
        return [
            send(low_in.at[origin], low_all.at[origin], low_s.at[shift - 1], low_r.at[shift - 1], origin, member),
            send(tile_in, tile_all.at[origin], tile_s.at[shift - 1], tile_r.at[shift - 1], origin, member),
        ]

    def quarter(who):
        return whole.at[span((who // 2) * half, half, half), span(lax.rem(who, 2) * columns, columns, 128)]

    def pass_quarter(who, index, to):
        return send(quarter(who), quarter(who), q_s.at[index], q_r.at[index], client, to)

    barrier = pltpu.get_barrier_semaphore()
    for shift in range(1, clients):
        pl.semaphore_signal(
            barrier, inc=1,
            device_id={"client": lax.rem(client + shift, clients), "tensor": member}, device_id_type=MESH,
        )
    for shift in (1, 2, 3):
        pl.semaphore_signal(
            barrier, inc=1,
            device_id={"client": client, "tensor": lax.rem(member + shift, 4)}, device_id_type=MESH,
        )
    order = [(i, p) for i in (0, 1) for p in (1, 2)] + [(i, 0) for i in range(depth)]
    order += [(i, p) for i in range(2, depth) for p in (1, 2)]
    for i, p in order:
        own_load(levels[i], p).start()
    own_small = [
        pltpu.make_async_copy(low_in.at[client], low_all.at[client], keep_sem.at[0]),
        pltpu.make_async_copy(tile_in, tile_all.at[client], keep_sem.at[1]),
    ]
    for copy in own_small:
        copy.start()
    pl.semaphore_wait(barrier, clients - 1 + 3)
    for i, p in order:
        over(levels[i], p).start()
    for shift in range(1, clients):
        for copy in small(shift):
            copy.start()

    def pair_up(i, p):
        level = levels[i]
        own_load(level, p).wait()
        over(level, p).wait_recv()
        pair = (
            slot(own_table, own_main, level, p)[...].astype(F32)
            + slot(y_table, y_main, level, p)[...].astype(F32)
        )
        if i == 3:
            if p == 0:
                quarter(member)[...] = pair
            else:
                main_out[:, lanes[p]] = pair
            return
        if i == 2:
            slot(zs_table, zs_main, i, p)[...] = pair.astype(BF16)
            onward(i, p).start()
            return

        @pl.when(outer)
        def _():
            slot(zs_table, zs_main, i, p)[...] = pair.astype(BF16)
            relay(i, p).start()

        @pl.when(z != 3 * side)
        def _():
            relay(i, p).wait_recv()
            both = pair + slot(rl_table, rl_main, i, p)[...].astype(F32)
            slot(zs_table, zs_main, i, p)[...] = both.astype(BF16)
            onward(i, p).start()

    pair_up(0, 1)
    pair_up(0, 2)
    pair_up(1, 1)
    pair_up(1, 2)
    for i in range(depth):
        pair_up(i, 0)
    mine = quarter(member)
    for last in (0, 1):
        came(last, 0).wait_recv()
        mine[...] = mine[...] + zr_table[last].astype(F32)
    to_others = [pass_quarter(member, 0, mate), pass_quarter(member, 1, across)]
    for copy in to_others:
        copy.start()
    pair_up(2, 1)
    pair_up(2, 2)
    pass_quarter(across, 1, across).wait_recv()
    second = pass_quarter(across, 2, mate)
    second.start()
    pair_up(3, 1)
    pair_up(3, 2)
    for shift in range(1, clients):
        for copy in small_from(shift):
            copy.wait_recv()
    for copy in own_small:
        copy.wait()
    low_out[...] = low_all[...]
    tile_out[...] = tile_all[...]
    pass_quarter(mate, 0, mate).wait_recv()
    pass_quarter(lax.rem(mate + 2, 4), 2, mate).wait_recv()
    table_out[...] = whole[...]
    for last in (1, 0):
        for p in (1, 2):
            came(last, p).wait_recv()
            main_out[:, lanes[p]] = main_out[:, lanes[p]] + zr_main[last, :, lanes[p]].astype(F32)
    for copy in to_others + [second]:
        copy.wait_send()
    for shift in range(1, clients):
        for copy in small(shift):
            copy.wait_send()
    for i in range(depth):
        for p in parts:
            over(i, p).wait_send()
    for p in parts:
        onward(2, p).wait_send()

    @pl.when(outer)
    def _():
        for i in (0, 1):
            for p in parts:
                relay(i, p).wait_send()

    @pl.when(z != 3 * side)
    def _():
        for i in (0, 1):
            for p in parts:
                onward(i, p).wait_send()


def reduce_deltas(clients, main, table, low, tile):
    depth = clients // 2
    dma = pltpu.SemaphoreType.DMA
    vmem = pltpu.VMEM
    anywhere = pl.BlockSpec(memory_space=pl.ANY)
    inside = pl.BlockSpec(memory_space=pltpu.VMEM)
    block = main.shape[0] // clients
    half, columns = block // 2, table.shape[1] // 2
    wide = main.shape[1]
    hops = depth - 1
    return pl.pallas_call(
        functools.partial(reduce_kernel, clients),
        out_shape=(
            jax.ShapeDtypeStruct((block, wide), F32),
            jax.ShapeDtypeStruct((block, table.shape[1]), F32),
            jax.ShapeDtypeStruct(low.shape, BF16),
            jax.ShapeDtypeStruct((clients,) + tile.shape, F32),
        ),
        in_specs=[anywhere] * 4,
        out_specs=(inside,) * 4,
        scratch_shapes=[
            vmem((depth, block, wide), BF16), vmem((depth, half, columns), BF16),
            vmem((depth, block, wide), BF16), vmem((depth, half, columns), BF16),
            vmem((hops, block, wide), BF16), vmem((hops, half, columns), BF16),
            vmem((2, block, wide), BF16), vmem((2, half, columns), BF16),
            vmem((2, block, wide), BF16), vmem((2, half, columns), BF16),
            vmem((block, table.shape[1]), F32), vmem(low.shape, BF16),
            vmem((clients,) + tile.shape, F32),
            dma((3, depth)), dma((3, depth)), dma((3, depth)), dma((3, hops)), dma((3, 2)),
            dma((3, 2)), dma((3, 2)),
            dma((clients - 1,)), dma((clients - 1,)), dma((clients - 1,)), dma((clients - 1,)),
            dma((3,)), dma((3,)), dma((2,)),
        ],
        compiler_params=pltpu.CompilerParams(
            collective_id=2, has_side_effects=True, vmem_limit_bytes=52 << 20
        ),
        name="reduce_deltas",
    )(main, table, low, tile)


def adam(master, first, second, grad):
    first2 = BETA_ONE * first + (1.0 - BETA_ONE) * grad
    second2 = BETA_TWO * second + (1.0 - BETA_TWO) * grad * grad
    moved = (
        first2 / (1.0 - BETA_ONE**ROUND) / (jnp.sqrt(second2 / (1.0 - BETA_TWO**ROUND)) + ADAM_EPS)
    )
    fresh = master - SERVER_RATE * (moved + WEIGHT_DECAY * master)
    return (fresh, first2, second2, fresh.astype(jnp.bfloat16))


def server_kernel(main_ref, table_ref, low_ref, tile_ref, norm_ref, *refs):
    masters, firsts, seconds = refs[0:4], refs[4:8], refs[8:12]
    loss_out, norms_out = refs[12:14]
    outs = [refs[14 + i : 30 : 4] for i in range(4)]
    own, group = masters[0].shape[1:]
    tile = jnp.sum(tile_ref[...], 0)
    row = main_ref.shape[1] // 256
    examples, weighted_loss, weighted_factor = (tile[row : row + 1, i : i + 1] for i in range(3))
    scale = weighted_factor / examples / examples
    loss_out[...] = weighted_loss / examples
    lane = lax.broadcasted_iota(jnp.int32, (1, 128), 1)
    norms = jnp.zeros((1, 128), F32)
    for i in range(norm_ref.shape[0]):
        norms = jnp.where(lane == i, norm_ref[i, 0:1, 0:1], norms)
    norms_out[...] = norms[:, 0 : norm_ref.shape[0]]

    def apply(which, at, delta):
        results = adam(
            masters[which][at], firsts[which][at], seconds[which][at], scale * delta
        )
        for ref, value in zip(outs[which], results):
            ref[at] = value

    def slab(pair):
        return jnp.concatenate(pair, 1)

    every = slice(None)
    packed = tiles(main_ref[...])
    slabs = []
    for i in range(0, len(packed), 3):
        slabs += [slab(pair) for pair in unpack_two(packed[i : i + 3])]
    for i, which in enumerate((3, 4, 5, 6, 0, 1, 2)):
        apply(0, (which, every, every), slabs[i][:, :group])
    wo_rows = jnp.concatenate([slabs[7], jnp.zeros((128 - own, LANE), F32)], 0)
    apply(1, (0, every, every), jnp.transpose(wo_rows)[:group, :own])
    width = low_ref.shape[2] - 128
    messages = low_ref[...].reshape(low_ref.shape[0] * low_ref.shape[1], low_ref.shape[2])
    moved = tn(messages[:, :width], messages[:, width:])
    for i in range(4):
        apply(1, (i + 1, every, every), moved[i * group : (i + 1) * group, :own])
    apply(2, (every, every), table_ref[:, 0 : masters[2].shape[1]])
    bias = [tile[i : i + 1, :] for i in range(row)]
    rows = []
    for i in range(0, row, 3):
        rows += [slab(pair) for pair in unpack_two(bias[i : i + 3])]
    for i in range(4):
        apply(3, (slice(i, i + 1), every), rows[i][:, :group])


def server_update(main, table, low, tile, norms, state):
    inside = pl.BlockSpec(memory_space=pltpu.VMEM)
    shapes = [value.shape for value in state[:4]]
    out_shape = [jax.ShapeDtypeStruct((1, 1), F32), jax.ShapeDtypeStruct((1, norms.shape[0]), F32)]
    for kind in (F32, F32, F32, BF16):
        out_shape += [jax.ShapeDtypeStruct(shape, kind) for shape in shapes]
    return pl.pallas_call(
        server_kernel,
        out_shape=tuple(out_shape),
        in_specs=[inside] * (5 + len(state)),
        out_specs=(inside,) * len(out_shape),
        compiler_params=pltpu.CompilerParams(vmem_limit_bytes=24 << 20),
        name="server_update",
    )(main, table, low, tile, norms, *state)


def on_device(
    pool, index, tau, counts, labels,
    in_bf, out_bf, table_bf, bias_bf,
    in_master, out_master, table_master, bias_master,
    in_first, out_first, table_first, bias_first,
    in_second, out_second, table_second, bias_second,
):
    clients = lax.axis_size("client")
    group = in_bf.shape[2]
    steps, images = index.shape[1], index.shape[2]
    patch_rows, features = pool.shape[1], pool.shape[2]
    seq = patch_rows + 1
    pad = (seq + 15) // 16 * 16
    own = in_bf.shape[1]
    rows_total = table_bf.shape[0]
    classes = rows_total - features - seq - 9
    table_t = table_bf.T
    direct = clients == 8
    if direct:
        main, wo_all, table, patches = gather_weights(
            clients, index, in_bf, out_bf, table_t, pool, pad
        )
    else:
        in_rows = jnp.transpose(in_bf, (1, 0, 2))
        out_rows = jnp.transpose(out_bf, (2, 0, 1))
        main_own = jnp.concatenate(
            [in_rows[:, 3:], out_rows[:, 1:], in_rows[:, :3], out_rows[:, :1]], 1
        ).reshape(own, 12 * group)
        table_own = jnp.pad(table_t, ((0, 0), (0, features + REST - rows_total)))
        main = lax.all_gather(main_own, "client", axis=0, tiled=True)
        table = lax.all_gather(table_own, "client", axis=0, tiled=True)
        wo_all = lax.all_gather(main[:, 12 * group - LANE :], "tensor", axis=1, tiled=True)
        patches = pick_patches(pool, index[0].reshape(steps * images), pad)
    patches = patches.reshape(steps, images * pad, features)
    d_main, d_table, low, tile, norms = local_training(
        tau, counts, labels, index, patches, main, wo_all, table, bias_bf, clients, pad, seq, classes
    )
    if direct:
        main_sum, table_sum, low_all, tile_all = reduce_deltas(clients, d_main, d_table, low, tile)
    else:
        tile_all = lax.psum(tile, "client")[None]
        main_sum = lax.psum_scatter(d_main, "client", scatter_dimension=0, tiled=True).astype(F32)
        first_member = lax.axis_index("tensor") == 0
        d_table = jnp.where(first_member, d_table, jnp.zeros_like(d_table))
        table_sum = lax.psum(
            lax.psum_scatter(d_table, "client", scatter_dimension=0, tiled=True).astype(F32), "tensor"
        )
        low_all = lax.all_to_all(low, "client", split_axis=0, concat_axis=0, tiled=True)
    state = (
        in_master, out_master, table_master.T, bias_master,
        in_first, out_first, table_first.T, bias_first,
        in_second, out_second, table_second.T, bias_second,
    )
    loss, norms, *fresh = server_update(main_sum, table_sum, low_all, tile_all, norms, state)
    fresh[2::4] = [value.T for value in fresh[2::4]]
    return (loss.reshape(()), norms, *fresh)


def solution(mesh):
    by_client = P("client", None, None)
    state = (P(None, "client", "tensor"), P(None, "tensor", "client"), P(None, "client"), P(None, "tensor"))
    in_specs = (by_client, by_client, P("client"), P("client"), P("client")) + state * 4
    out_specs = (P(), P("client", None)) + state * 4
    return jax.shard_map(
        on_device, mesh=mesh, in_specs=in_specs, out_specs=out_specs, check_vma=False
    )
```
